32 devices in a mesh: dp: 2 (over y), fsdp: 16 (over z, x, core).
Axes of the slice: x: 2, y: 2, z: 4, core: 2. Of those that a mesh axis runs over, the one named last changes fastest.
Arguments:
- tokens: bfloat16 [65536, 768], P(('dp', 'fsdp')), may hold values from -12 to 12
- cotangent: bfloat16 [65536, 768], P(('dp', 'fsdp')), may hold values from -12 to 12
- segment_ids: int32 [65536], P(('dp', 'fsdp')), may hold values from 0 to 2687, as said below
- first_gain: bfloat16 [768], P('fsdp'), may hold values from 0.25 to 1.75
- first_shift: bfloat16 [768], P('fsdp'), may hold values from -1.75 to 1.75
- triple_weight: bfloat16 [768, 2304], P('fsdp'), may hold values from -0.3125 to 0.3125
- query_bias: bfloat16 [768], P('fsdp'), may hold values from -3 to 3
- value_bias: bfloat16 [768], P('fsdp'), may hold values from -1.75 to 1.75
- out_weight: bfloat16 [768, 768], P('fsdp'), may hold values from -0.875 to 0.875
- out_bias: bfloat16 [768], P('fsdp'), may hold values from -1.75 to 1.75
- second_gain: bfloat16 [768], P('fsdp'), may hold values from 0.25 to 1.75
- second_shift: bfloat16 [768], P('fsdp'), may hold values from -1.75 to 1.75
- up_weight: bfloat16 [768, 3072], P('fsdp'), may hold values from -0.21875 to 0.21875
- up_bias: bfloat16 [3072], P('fsdp'), may hold values from -3 to 3
- down_weight: bfloat16 [3072, 768], P('fsdp'), may hold values from -0.109375 to 0.109375
- down_bias: bfloat16 [768], P('fsdp'), may hold values from -1.75 to 1.75
Outputs:
- block_output: bfloat16 [65536, 768], P(('dp', 'fsdp'))
- tokens_gradient: bfloat16 [65536, 768], P(('dp', 'fsdp'))
- first_gain_gradient: float32 [768], P('fsdp')
- first_shift_gradient: float32 [768], P('fsdp')
- triple_weight_gradient: float32 [768, 2304], P('fsdp')
- query_bias_gradient: float32 [768], P('fsdp')
- value_bias_gradient: float32 [768], P('fsdp')
- out_weight_gradient: float32 [768, 768], P('fsdp')
- out_bias_gradient: float32 [768], P('fsdp')
- second_gain_gradient: float32 [768], P('fsdp')
- second_shift_gradient: float32 [768], P('fsdp')
- up_weight_gradient: float32 [768, 3072], P('fsdp')
- up_bias_gradient: float32 [3072], P('fsdp')
- down_weight_gradient: float32 [3072, 768], P('fsdp')
- down_bias_gradient: float32 [768], P('fsdp')
The draws below stay inside these ranges and needn't reach their ends.
Inputs may be any that keep to these rules, and one draw needn't show every extreme that they name: `segment_ids`: segment numbers never fall along the patches and no image spans two aligned blocks of 1024 patches; each image has 900 patches and begins its block, or has 1 to 64 patches; the first block begins with an image of 900 patches; the last patch carries exactly the largest number, 65536 // 1024 * (1024 // max(1, 25) + 2) - 1.
All inputs are finite; a program needn't handle non-finite values.
Results may differ from the reference program's by a relative error of at most 0.014.
Values may be sent and summed in bfloat16 or wider, within the bound.
A program may use at most 384 MiB of HBM per device.

```python
import jax
import jax.numpy as jnp
from jax import lax

D = 768
H = 12
HD = 64
FF = 3072
ROWS = 1024
LONG = 900
SHORT = 64
TOKENS = 65536


def draw_segment_ids(key, part):
    slot_count = TOKENS // ROWS
    low_len = max(1, SHORT * 25 // 64)
    small_count = ROWS // low_len + 1
    key_large, key_small = jax.random.split(jax.random.fold_in(key, 11))
    large_flag = jax.random.randint(key_large, (slot_count,), 0, 2).astype(jnp.int32)
    large_flag = large_flag.at[0].set(1)
    small_lengths = jax.random.randint(key_small, (slot_count, small_count), low_len, SHORT + 1).astype(jnp.int32)
    first_len = large_flag * LONG
    lengths = jnp.concatenate([first_len[:, None], small_lengths], axis=1)
    end_points = jnp.cumsum(lengths, axis=1)
    positions = jnp.arange(ROWS, dtype=jnp.int32)
    image_index = jnp.sum((end_points[:, None, :] <= positions[None, :, None]).astype(jnp.int32), axis=2)
    segments = image_index + jnp.arange(slot_count, dtype=jnp.int32)[:, None] * (small_count + 1)
    top_value = slot_count * (small_count + 1) - 1
    flat = segments.reshape(TOKENS).astype(jnp.int32)
    return flat.at[TOKENS - 1].set(top_value).astype(jnp.int32)


def spiked(values, stream_key, source, target, blocks, factor):
    owner, partner = [(jnp.arange(values.shape[position]) // (values.shape[position] // blocks)).reshape([-1 if axis == position else 1 for axis in range(values.ndim)]) for position in (source, target)]
    chosen = jax.random.permutation(stream_key, blocks)[partner]
    strong = (owner == chosen) | (owner == (partner + blocks // 2) % blocks)
    return jnp.where(strong, factor * values, values)


def shard_levels(rng, dims, pieces, least, high):
    level, own = 1.0, jax.random.fold_in(rng, 6)
    for dim, blocks in pieces:
        heights = jnp.exp(jax.random.uniform(jax.random.fold_in(own, dim), (blocks,), jnp.float32, least / len(pieces), high / len(pieces)))
        level = level * jnp.repeat(heights, dims[dim] // blocks).reshape([-1 if axis == dim else 1 for axis in range(len(dims))])
    return level


def normal_values(key, dims, spread, reach, shards=(), kind=jnp.bfloat16):
    values = jax.random.normal(key, dims, jnp.float32) * spread
    if len(shards) > 0:
        values = shard_levels(key, dims, shards, -0.22, 0.18) * values
    return jnp.clip(values, min=-reach, max=reach).astype(kind)


def bell_draw_with(rng, dims, width, reach, pieces, heavy, kind=jnp.bfloat16):
    values = width * jax.random.normal(rng, dims, jnp.float32)
    if pieces:
        values = values * shard_levels(rng, dims, pieces, -0.22, 0.18)
    return jnp.clip(spiked(values, jax.random.fold_in(rng, 3), *heavy), -reach, reach).astype(kind)


def setup_inputs(seed: int = 0) -> dict:
    streams_of = jax.random.split(jax.random.key(seed), 17)
    return {
        "tokens": bell_draw_with(streams_of[0], (TOKENS, D), 1.0, 12.0, ((0, 32),), (0, 1, 32, 2.75)),
        "cotangent": bell_draw_with(streams_of[1], (TOKENS, D), 1.0, 12.0, ((0, 32),), (0, 1, 32, 2.75)),
        "segment_ids": draw_segment_ids(jax.random.fold_in(streams_of[16], 71), 0),
        "first_gain": jnp.clip(1.0 + 0.15 * jax.random.normal(streams_of[3], (D,), jnp.float32), 0.25, 1.75).astype(jnp.bfloat16),
        "first_shift": normal_values(streams_of[4], (D,), 0.3, 1.75, ((0, 16),)),
        "triple_weight": normal_values(streams_of[5], (D, 3 * D), (D // 2) ** -0.5, 0.3125, ((0, 16),)),
        "query_bias": normal_values(streams_of[6], (D,), 0.5, 3.0, ((0, 16),)),
        "value_bias": normal_values(streams_of[7], (D,), 0.3, 1.75, ((0, 16),)),
        "out_weight": normal_values(streams_of[8], (D, D), (D // 16) ** -0.5, 0.875, ((0, 16),)),
        "out_bias": normal_values(streams_of[9], (D,), 0.3, 1.75, ((0, 16),)),
        "second_gain": jnp.clip(1.0 + 0.15 * jax.random.normal(streams_of[10], (D,), jnp.float32), 0.25, 1.75).astype(jnp.bfloat16),
        "second_shift": normal_values(streams_of[11], (D,), 0.3, 1.75, ((0, 16),)),
        "up_weight": normal_values(streams_of[12], (D, FF), D ** -0.5, 0.21875, ((0, 16),)),
        "up_bias": normal_values(streams_of[13], (FF,), 0.5, 3.0, ((0, 16),)),
        "down_weight": normal_values(streams_of[14], (FF, D), FF ** -0.5, 0.109375, ((0, 16),)),
        "down_bias": normal_values(streams_of[15], (D,), 0.3, 1.75, ((0, 16),)),
    }


norm_eps = 1e-06
highest = lax.Precision.HIGHEST

@jax.custom_vjp
def low(v):
    return lax.optimization_barrier(v.astype(jnp.bfloat16)).astype(jnp.float32)

@jax.custom_vjp
def low_back(v):
    return v

def low_keep(v):
    return (low(v), None)

def low_pass(kept, grad):
    return (grad,)

def back_keep(v):
    return (v, None)

def back_low(kept, grad):
    return (low(grad),)
low.defvjp(low_keep, low_pass)
low_back.defvjp(back_keep, back_low)

def norm_apply(values, gain, shift):
    mean_val = lax.optimization_barrier(jnp.mean(values, axis=-1, keepdims=True))
    centered = values - mean_val
    variance = lax.optimization_barrier(jnp.mean(centered * centered, axis=-1, keepdims=True))
    return centered * lax.rsqrt(variance + norm_eps) * gain + shift

def layer_slot(weights, rows_in, segments):
    first_gain, first_shift, triple_weight, query_bias, value_bias, out_weight, out_bias, second_gain, second_shift, up_weight, up_bias, down_weight, down_bias = weights
    first_in = low(norm_apply(rows_in, first_gain, first_shift))
    projected = jnp.dot(first_in, triple_weight, precision=highest)
    query = low(low_back(projected[:, :D] + query_bias)).reshape(ROWS, H, HD)
    keys = low(low_back(projected[:, D:2 * D])).reshape(ROWS, H, HD)
    value = low(low_back(projected[:, 2 * D:] + value_bias)).reshape(ROWS, H, HD)
    scores = jnp.einsum('qhd,khd->hqk', query, keys, precision=highest) * 0.125
    scores = low_back(scores)
    allowed = segments[:, None] == segments[None, :]
    scores = jnp.where(allowed[None], scores, -1e+30)
    soft = low(jax.nn.softmax(scores, axis=-1))
    attended = jnp.einsum('hqk,khd->qhd', soft, value, precision=highest).reshape(ROWS, D)
    mixed = low(low_back(attended))
    resid = rows_in + low_back(jnp.dot(mixed, out_weight, precision=highest)) + out_bias
    second_in = low(norm_apply(resid, second_gain, second_shift))
    upped = low_back(jnp.dot(second_in, up_weight, precision=highest)) + up_bias
    act = low(jax.nn.gelu(upped, approximate=False))
    return resid + low_back(jnp.dot(act, down_weight, precision=highest)) + down_bias

def reference(tokens, cotangent, segment_ids, first_gain, first_shift, triple_weight, query_bias, value_bias, out_weight, out_bias, second_gain, second_shift, up_weight, up_bias, down_weight, down_bias):
    slot_count = TOKENS // ROWS
    params = tuple((w.astype(jnp.float32) for w in (first_gain, first_shift, triple_weight, query_bias, value_bias, out_weight, out_bias, second_gain, second_shift, up_weight, up_bias, down_weight, down_bias)))
    segments = segment_ids.reshape(slot_count, ROWS).astype(jnp.int32)

    def forward(inputs, weights):

        def one_slot(item):
            return layer_slot(weights, item[0], item[1])
        results = lax.map(jax.checkpoint(one_slot), (inputs.reshape(slot_count, ROWS, D), segments))
        return results.reshape(TOKENS, D)
    result, pullback = jax.vjp(forward, tokens.astype(jnp.float32), params)
    grad_in, grads = pullback(cotangent.astype(jnp.float32))
    return (result.astype(jnp.bfloat16), grad_in.astype(jnp.bfloat16), grads[0], grads[1], grads[2], grads[3], grads[4], grads[5], grads[6], grads[7], grads[8], grads[9], grads[10], grads[11], grads[12])
```

```python
import functools

import jax
import jax.numpy as jnp
from jax import lax
from jax.experimental import pallas as pl
from jax.experimental.pallas import tpu as pltpu
from jax.sharding import PartitionSpec as P

H = 12
HD = 64
ROWS = 1024
EPS = 1e-06
F32 = jnp.float32
BF16 = jnp.bfloat16
VMEM_LIMIT = 60 * 1024 * 1024

ROOT_HALF = 0.7071067811865476
ROOT_INV_TWO_PI = 0.3989422804014327

NN = (((1,), (0,)), ((), ()))
NT = (((1,), (1,)), ((), ()))


def mm(a, b, dims=NN):
    return lax.dot_general(a, b, dims, preferred_element_type=F32)


def params(**kw):
    return pltpu.CompilerParams(vmem_limit_bytes=VMEM_LIMIT, **kw)


def norm_stats(x):
    mean = jnp.mean(x, axis=-1, keepdims=True)
    cen = x - mean
    var = jnp.mean(cen * cen, axis=-1, keepdims=True)
    inv = lax.rsqrt(var + EPS)
    return cen * inv, inv


def proj_body(x_ref, gain_ref, shift_ref, w_ref, bias_ref, scale_ref, qkv_ref):
    n, _ = norm_stats(x_ref[...].astype(F32))
    h = (n * gain_ref[...] + shift_ref[...]).astype(BF16)
    p = mm(h, w_ref[...])
    qkv_ref[...] = ((p + bias_ref[...]) * scale_ref[...]).astype(BF16)


def project(x, gain, shift, w, bias, scale):
    rows, d = x.shape
    cols = w.shape[1]
    tile = 512
    row = pl.BlockSpec((1, d), lambda i: (0, 0))
    wide = pl.BlockSpec((1, cols), lambda i: (0, 0))
    return pl.pallas_call(
        proj_body,
        grid=(rows // tile,),
        in_specs=[
            pl.BlockSpec((tile, d), lambda i: (i, 0)),
            row,
            row,
            pl.BlockSpec((d, cols), lambda i: (0, 0)),
            wide,
            wide,
        ],
        out_specs=pl.BlockSpec((tile, cols), lambda i: (i, 0)),
        out_shape=jax.ShapeDtypeStruct((rows, cols), BF16),
        compiler_params=params(),
        name="project",
        cost_estimate=pl.CostEstimate(
            flops=2 * rows * d * cols, bytes_accessed=2 * rows * (d + cols), transcendentals=0
        ),
    )(x, gain, shift, w, bias, scale)


QT = 256


def half_mask(value, hh):
    lane = lax.broadcasted_iota(jnp.int32, value.shape, 1)
    keep = lane < HD if hh == 0 else lane >= HD
    return jnp.where(keep, value, jnp.zeros_like(value))


def attend_body(q_ref, k_ref, v_ref, segc_ref, segr_ref, o_ref, p_ref, bias_ref):
    rows = q_ref.shape[0]

    @pl.when(pl.program_id(1) == 0)
    def _():
        bias_ref[...] = jnp.where(segc_ref[...] == segr_ref[...], 0.0, -1e30)

    k = k_ref[...]
    v = v_ref[...]
    for t in range(rows // QT):
        sl = pl.ds(t * QT, QT)
        out = None
        for hh in range(2):
            q = half_mask(q_ref[sl, :], hh)
            s = mm(q, k, NT) + bias_ref[sl, :]
            peak = jnp.max(s, axis=-1, keepdims=True)
            e = jnp.exp(s - peak)
            total = jnp.sum(e, axis=-1, keepdims=True)
            p = (e * (1.0 / total)).astype(BF16)
            p_ref[hh, sl, :] = p
            o = mm(p, v)
            if hh == 0:
                out = o
            else:
                lane = lax.broadcasted_iota(jnp.int32, o.shape, 1)
                out = jnp.where(lane < HD, out, o)
        o_ref[sl, :] = out.astype(BF16)


def attend(qkv, segc, segr):
    rows = qkv.shape[0]
    d = qkv.shape[1] // 3
    mb = rows // ROWS
    pairs = d // 128
    return pl.pallas_call(
        attend_body,
        grid=(mb, pairs),
        in_specs=[
            pl.BlockSpec((ROWS, 128), lambda m, h: (m, h)),
            pl.BlockSpec((ROWS, 128), lambda m, h: (m, pairs + h)),
            pl.BlockSpec((ROWS, 128), lambda m, h: (m, 2 * pairs + h)),
            pl.BlockSpec((ROWS, 1), lambda m, h: (m, 0)),
            pl.BlockSpec((None, 1, ROWS), lambda m, h: (m, 0, 0)),
        ],
        out_specs=[
            pl.BlockSpec((ROWS, 128), lambda m, h: (m, h)),
            pl.BlockSpec((None, 2, ROWS, ROWS), lambda m, h: (m, h, 0, 0)),
        ],
        out_shape=[
            jax.ShapeDtypeStruct((rows, d), BF16),
            jax.ShapeDtypeStruct((mb, 2 * pairs, ROWS, ROWS), BF16),
        ],
        scratch_shapes=[pltpu.VMEM((ROWS, ROWS), F32)],
        compiler_params=params(),
        name="attend",
        cost_estimate=pl.CostEstimate(
            flops=mb * pairs * 2 * 4 * ROWS * ROWS * 256,
            bytes_accessed=mb * pairs * 2 * ROWS * ROWS * 2,
            transcendentals=mb * pairs * 2 * ROWS * ROWS,
        ),
    )(qkv, qkv, qkv, segc, segr)


def attend_back_body(q_ref, k_ref, v_ref, p_ref, o_ref, g_ref, dq_ref, dk_ref, dv_ref, ds_ref):
    rows = q_ref.shape[0]
    k = k_ref[...]
    v = v_ref[...]
    q_t = q_ref[...].T
    g_t = g_ref[...].T
    prod = g_ref[...].astype(F32) * o_ref[...].astype(F32)
    dk_parts = []
    dv_parts = []
    dq_parts = []
    for hh in range(2):
        half = slice(hh * HD, (hh + 1) * HD)
        center = jnp.sum(half_mask(prod, hh), axis=-1, keepdims=True)
        for t in range(rows // QT):
            sl = pl.ds(t * QT, QT)
            ts = slice(t * QT, (t + 1) * QT)
            d_soft = mm(half_mask(g_ref[sl, :], hh), v, NT)
            ds = p_ref[hh, sl, :].astype(F32) * (d_soft - center[ts, :])
            ds_ref[hh, sl, :] = ds.astype(BF16)
        dv_parts.append(mm(g_t[half, :], p_ref[hh]))
        dk_parts.append(mm(q_t[half, :], ds_ref[hh]))
        dq_parts.append(mm(ds_ref[hh], k))
    lane = lax.broadcasted_iota(jnp.int32, dq_parts[0].shape, 1)
    dq_ref[...] = (jnp.where(lane < HD, dq_parts[0], dq_parts[1]) * 0.125).astype(BF16)
    dk_ref[...] = jnp.concatenate(dk_parts, axis=0).T.astype(BF16)
    dv_ref[...] = jnp.concatenate(dv_parts, axis=0).T.astype(BF16)


def attend_back(qkv, soft, mixed, d_mixed):
    rows = qkv.shape[0]
    d = qkv.shape[1] // 3
    mb = rows // ROWS
    pairs = d // 128
    blk = pl.BlockSpec((ROWS, 128), lambda m, h: (m, h))
    shape = jax.ShapeDtypeStruct((rows, d), BF16)
    return pl.pallas_call(
        attend_back_body,
        grid=(mb, pairs),
        in_specs=[
            blk,
            pl.BlockSpec((ROWS, 128), lambda m, h: (m, pairs + h)),
            pl.BlockSpec((ROWS, 128), lambda m, h: (m, 2 * pairs + h)),
            pl.BlockSpec((None, 2, ROWS, ROWS), lambda m, h: (m, h, 0, 0)),
            blk,
            blk,
        ],
        out_specs=[blk, blk, blk],
        out_shape=[shape, shape, shape],
        scratch_shapes=[pltpu.VMEM((2, ROWS, ROWS), BF16)],
        compiler_params=params(),
        name="attend_back",
        cost_estimate=pl.CostEstimate(
            flops=mb * pairs * 2 * 8 * ROWS * ROWS * 256,
            bytes_accessed=mb * pairs * 2 * ROWS * ROWS * 2,
            transcendentals=0,
        ),
    )(qkv, qkv, qkv, soft, mixed, d_mixed)


def out_body(x_ref, m_ref, w_ref, bias_ref, gain_ref, shift_ref, resid_ref, h_ref):
    resid = x_ref[...].astype(F32) + mm(m_ref[...], w_ref[...]) + bias_ref[...]
    resid_ref[...] = resid
    n, _ = norm_stats(resid)
    h_ref[...] = (n * gain_ref[...] + shift_ref[...]).astype(BF16)


def out_project(x, mixed, w, bias, gain, shift):
    rows, d = x.shape
    tile = 512
    blk = pl.BlockSpec((tile, d), lambda i: (i, 0))
    row = pl.BlockSpec((1, d), lambda i: (0, 0))
    return pl.pallas_call(
        out_body,
        grid=(rows // tile,),
        in_specs=[blk, blk, pl.BlockSpec((d, d), lambda i: (0, 0)), row, row, row],
        out_specs=[blk, blk],
        out_shape=[
            jax.ShapeDtypeStruct((rows, d), F32),
            jax.ShapeDtypeStruct((rows, d), BF16),
        ],
        compiler_params=params(),
        name="out_project",
        cost_estimate=pl.CostEstimate(
            flops=2 * rows * d * d, bytes_accessed=rows * d * 10, transcendentals=0
        ),
    )(x, mixed, w, bias, gain, shift)


FC = 512
RT = 512


def gelu_parts(u):
    cdf = 0.5 * (1.0 + lax.erf(u * ROOT_HALF))
    bell = jnp.exp(-0.5 * u * u) * ROOT_INV_TWO_PI
    return u * cdf, cdf + u * bell


def mlp_body(h_ref, ht_ref, g_ref, gt_ref, wu_ref, bu_ref, wd_ref, acc_ref, dh_ref, dwu_ref, dwd_ref, dbu_ref,
             act_ref, du_ref):
    rows = h_ref.shape[0]

    @pl.when(pl.program_id(0) == 0)
    def _():
        acc_ref[...] = jnp.zeros_like(acc_ref)
        dh_ref[...] = jnp.zeros_like(dh_ref)

    wu = wu_ref[...]
    wd = wd_ref[...]
    bias_sum = None
    for t in range(rows // RT):
        sl = pl.ds(t * RT, RT)
        u = mm(h_ref[sl, :], wu) + bu_ref[...]
        act, slope = gelu_parts(u)
        act_ref[sl, :] = act.astype(BF16)
        du = mm(g_ref[sl, :], wd, NT) * slope
        part = jnp.sum(du, axis=0, keepdims=True)
        bias_sum = part if bias_sum is None else bias_sum + part
        du_ref[sl, :] = du.astype(BF16)
        acc_ref[sl, :] += mm(act_ref[sl, :], wd)
        dh_ref[sl, :] += mm(du_ref[sl, :], wu, NT)
    dbu_ref[...] = bias_sum
    dwu_ref[...] = mm(ht_ref[...], du_ref[...]).astype(dwu_ref.dtype)
    dwd_ref[...] = mm(gt_ref[...], act_ref[...]).T.astype(dwd_ref.dtype)


def mlp(h, ht, g, gt, wu, bu, wd):
    rows, d = h.shape
    ff = wu.shape[1]
    one = pl.Buffered(1)
    whole = pl.BlockSpec((rows, d), lambda c: (0, 0), pipeline_mode=one)
    whole_t = pl.BlockSpec((d, rows), lambda c: (0, 0), pipeline_mode=one)
    return pl.pallas_call(
        mlp_body,
        grid=(ff // FC,),
        in_specs=[
            whole,
            whole_t,
            whole,
            whole_t,
            pl.BlockSpec((d, FC), lambda c: (0, c)),
            pl.BlockSpec((1, FC), lambda c: (0, c)),
            pl.BlockSpec((FC, d), lambda c: (c, 0)),
        ],
        out_specs=[
            whole,
            whole,
            pl.BlockSpec((d, FC), lambda c: (0, c)),
            pl.BlockSpec((FC, d), lambda c: (c, 0)),
            pl.BlockSpec((1, FC), lambda c: (0, c)),
        ],
        out_shape=[
            jax.ShapeDtypeStruct((rows, d), F32),
            jax.ShapeDtypeStruct((rows, d), F32),
            jax.ShapeDtypeStruct((d, ff), BF16),
            jax.ShapeDtypeStruct((ff, d), BF16),
            jax.ShapeDtypeStruct((1, ff), F32),
        ],
        scratch_shapes=[pltpu.VMEM((rows, FC), BF16), pltpu.VMEM((rows, FC), BF16)],
        compiler_params=params(),
        name="mlp",
        cost_estimate=pl.CostEstimate(
            flops=12 * rows * d * ff, bytes_accessed=rows * d * 20 + 8 * d * ff, transcendentals=3 * rows * ff
        ),
    )(h, ht, g, gt, wu, bu, wd)


def fold(ref, step, value):
    part = jnp.sum(value, axis=0, keepdims=True)

    @pl.when(step == 0)
    def _():
        ref[...] = part

    @pl.when(step != 0)
    def _():
        ref[...] += part


def norm_pull(grad, n, inv, gain):
    dn = grad * gain
    plain = jnp.mean(dn, axis=-1, keepdims=True)
    cross = jnp.mean(dn * n, axis=-1, keepdims=True)
    return inv * (dn - plain - n * cross)


def mid_body(resid_ref, acc_ref, dh_ref, g_ref, mixed_ref, w_ref, bias_ref, gain_ref,
             y_ref, dr_ref, dm_ref, dw_ref, dgain_ref, dshift_ref, dob_ref, ddb_ref, sum_ref):
    step = pl.program_id(0)
    resid = resid_ref[...]
    y_ref[...] = (resid + acc_ref[...] + bias_ref[...]).astype(BF16)
    g = g_ref[...].astype(F32)
    n, inv = norm_stats(resid)
    dh = dh_ref[...]
    fold(dgain_ref, step, dh * n)
    fold(dshift_ref, step, dh)
    fold(ddb_ref, step, g)
    dr = g + norm_pull(dh, n, inv, gain_ref[...])
    dr_ref[...] = dr
    fold(dob_ref, step, dr)
    low = dr.astype(BF16)
    dm_ref[...] = mm(low, w_ref[...], NT).astype(BF16)
    dw = mm(mixed_ref[...].T, low)

    @pl.when(step == 0)
    def _():
        sum_ref[...] = dw

    @pl.when(step != 0)
    def _():
        sum_ref[...] += dw

    @pl.when(step == pl.num_programs(0) - 1)
    def _():
        dw_ref[...] = sum_ref[...].astype(dw_ref.dtype)


def middle(resid, acc, dh, g, mixed, w, bias, gain):
    rows, d = resid.shape
    tile = 512
    blk = pl.BlockSpec((tile, d), lambda i: (i, 0))
    row = pl.BlockSpec((1, d), lambda i: (0, 0))
    mat = pl.BlockSpec((d, d), lambda i: (0, 0))
    vec = jax.ShapeDtypeStruct((1, d), F32)
    return pl.pallas_call(
        mid_body,
        grid=(rows // tile,),
        in_specs=[blk, blk, blk, blk, blk, mat, row, row],
        out_specs=[blk, blk, blk, mat, row, row, row, row],
        out_shape=[
            jax.ShapeDtypeStruct((rows, d), BF16),
            jax.ShapeDtypeStruct((rows, d), F32),
            jax.ShapeDtypeStruct((rows, d), BF16),
            jax.ShapeDtypeStruct((d, d), BF16),
            vec,
            vec,
            vec,
            vec,
        ],
        scratch_shapes=[pltpu.VMEM((d, d), F32)],
        compiler_params=params(),
        name="middle",
        cost_estimate=pl.CostEstimate(
            flops=4 * rows * d * d, bytes_accessed=rows * d * 24, transcendentals=0
        ),
    )(resid, acc, dh, g, mixed, w, bias, gain)


def last_body(x_ref, dr_ref, dq_ref, dk_ref, dv_ref, w_ref, gain_ref, shift_ref,
              dx_ref, dw_ref, dgain_ref, dshift_ref, dqb_ref, dvb_ref, sum_ref):
    step = pl.program_id(0)
    d = x_ref.shape[1]
    n, inv = norm_stats(x_ref[...].astype(F32))
    h_t = (n * gain_ref[...] + shift_ref[...]).astype(BF16).T
    dh = None
    for j, ref in enumerate((dq_ref, dk_ref, dv_ref)):
        cols = pl.ds(j * d, d)
        part = ref[...]
        term = mm(part, w_ref[:, cols], NT)
        dh = term if dh is None else dh + term
        dw = mm(h_t, part)

        @pl.when(step == 0)
        def _():
            sum_ref[:, cols] = dw

        @pl.when(step != 0)
        def _():
            sum_ref[:, cols] += dw

    fold(dqb_ref, step, dq_ref[...].astype(F32))
    fold(dvb_ref, step, dv_ref[...].astype(F32))
    fold(dgain_ref, step, dh * n)
    fold(dshift_ref, step, dh)
    dx_ref[...] = (dr_ref[...] + norm_pull(dh, n, inv, gain_ref[...])).astype(BF16)

    @pl.when(step == pl.num_programs(0) - 1)
    def _():
        dw_ref[...] = sum_ref[...].astype(dw_ref.dtype)


def last(x, dr, dq, dk, dv, w, gain, shift):
    rows, d = x.shape
    tile = 512
    blk = pl.BlockSpec((tile, d), lambda i: (i, 0))
    row = pl.BlockSpec((1, d), lambda i: (0, 0))
    mat = pl.BlockSpec((d, 3 * d), lambda i: (0, 0))
    vec = jax.ShapeDtypeStruct((1, d), F32)
    return pl.pallas_call(
        last_body,
        grid=(rows // tile,),
        in_specs=[blk, blk, blk, blk, blk, mat, row, row],
        out_specs=[blk, mat, row, row, row, row],
        out_shape=[
            jax.ShapeDtypeStruct((rows, d), BF16),
            jax.ShapeDtypeStruct((d, 3 * d), BF16),
            vec,
            vec,
            vec,
            vec,
        ],
        scratch_shapes=[pltpu.VMEM((d, 3 * d), F32)],
        compiler_params=params(),
        name="last",
        cost_estimate=pl.CostEstimate(
            flops=12 * rows * d * d, bytes_accessed=rows * d * 14, transcendentals=0
        ),
    )(x, dr, dq, dk, dv, w, gain, shift)


def layer(tokens, cotangent, segment_ids, full):
    (
        first_gain,
        first_shift,
        triple_weight,
        query_bias,
        value_bias,
        out_weight,
        out_bias,
        second_gain,
        second_shift,
        up_weight,
        up_bias,
        down_weight,
        down_bias,
    ) = full
    rows, d = tokens.shape
    row = lambda v: v.astype(F32).reshape(1, -1)
    zero = jnp.zeros((d,), BF16)
    bias = row(jnp.concatenate([query_bias, zero, value_bias]))
    scale = jnp.concatenate([jnp.full((1, d), 0.125, F32), jnp.ones((1, 2 * d), F32)], axis=1)
    segc = segment_ids.reshape(rows, 1)
    segr = segment_ids.reshape(rows // ROWS, 1, ROWS)
    qkv = project(tokens, row(first_gain), row(first_shift), triple_weight, bias, scale)
    mixed, soft = attend(qkv, segc, segr)
    resid, h = out_project(tokens, mixed, out_weight, row(out_bias), row(second_gain), row(second_shift))
    acc, dh, dwu, dwd, dbu = mlp(h, h.T, cotangent, cotangent.T, up_weight, row(up_bias), down_weight)
    y, dr, dm, dwo, dg2, ds2, dob, ddb = middle(
        resid, acc, dh, cotangent, mixed, out_weight, row(down_bias), row(second_gain)
    )
    dq, dk, dv = attend_back(qkv, soft, mixed, dm)
    dx, dwt, dg1, ds1, dqb, dvb = last(tokens, dr, dq, dk, dv, triple_weight, row(first_gain), row(first_shift))
    return y, dx, (dg1, ds1, dwt, dqb, dvb, dwo, dob, dg2, ds2, dwu, dbu, dwd, ddb)


def on_device(tokens, cotangent, segment_ids, *shards):
    gather = lambda s: lax.all_gather(s, "fsdp", axis=0, tiled=True)
    vectors = [s for s in shards if s.ndim == 1]
    n = lax.axis_size("fsdp")
    packed = gather(jnp.concatenate(vectors).reshape(1, -1))
    full = []
    at = 0
    for s in shards:
        if s.ndim == 1:
            full.append(packed[:, at : at + s.shape[0]].reshape(-1))
            at += s.shape[0]
        else:
            full.append(gather(s))
    y, dx, parts = layer(tokens, cotangent, segment_ids, full)
    small = jnp.concatenate([p.reshape(n, -1) for p, s in zip(parts, shards) if s.ndim == 1], axis=1)
    small = lax.psum_scatter(small, "fsdp", scatter_dimension=0, tiled=True).reshape(-1)
    small = lax.psum(small, "dp")
    grads = []
    at = 0
    for p, s in zip(parts, shards):
        if s.ndim == 1:
            grads.append(small[at : at + s.shape[0]])
            at += s.shape[0]
        else:
            one = lax.psum_scatter(p, "fsdp", scatter_dimension=0, tiled=True)
            grads.append(lax.psum(one, "dp").astype(F32))
    return (y, dx, *grads)


def solution(mesh):
    tok = P(("dp", "fsdp"), None)
    vec = P("fsdp")
    mat = P("fsdp", None)
    weights = (vec, vec, mat, vec, vec, mat, vec, vec, vec, mat, vec, mat, vec)
    return jax.shard_map(
        on_device,
        mesh=mesh,
        in_specs=(tok, tok, P(("dp", "fsdp")), *weights),
        out_specs=(tok, tok, *weights),
        check_vma=False,
    )
```

```python
import functools

import jax
import jax.numpy as jnp
from jax import lax
from jax.experimental import pallas as pl
from jax.experimental.pallas import tpu as pltpu
from jax.sharding import PartitionSpec as P

H = 12
HD = 64
ROWS = 1024
EPS = 1e-06
F32 = jnp.float32
BF16 = jnp.bfloat16
VMEM_LIMIT = 60 * 1024 * 1024

ROOT_HALF = 0.7071067811865476
ROOT_INV_TWO_PI = 0.3989422804014327

NN = (((1,), (0,)), ((), ()))
NT = (((1,), (1,)), ((), ()))


def mm(a, b, dims=NN):
    return lax.dot_general(a, b, dims, preferred_element_type=F32)


def params(**kw):
    return pltpu.CompilerParams(vmem_limit_bytes=VMEM_LIMIT, **kw)


def norm_stats(x):
    mean = jnp.mean(x, axis=-1, keepdims=True)
    cen = x - mean
    var = jnp.mean(cen * cen, axis=-1, keepdims=True)
    inv = lax.rsqrt(var + EPS)
    return cen * inv, inv


def proj_body(x_ref, gain_ref, shift_ref, w_ref, bias_ref, scale_ref, qkv_ref):
    n, _ = norm_stats(x_ref[...].astype(F32))
    h = (n * gain_ref[...] + shift_ref[...]).astype(BF16)
    p = mm(h, w_ref[...])
    qkv_ref[...] = ((p + bias_ref[...]) * scale_ref[...]).astype(BF16)


def project(x, gain, shift, w, bias, scale):
    rows, d = x.shape
    cols = w.shape[1]
    tile = 512
    row = pl.BlockSpec((1, d), lambda i: (0, 0))
    wide = pl.BlockSpec((1, cols), lambda i: (0, 0))
    return pl.pallas_call(
        proj_body,
        grid=(rows // tile,),
        in_specs=[
            pl.BlockSpec((tile, d), lambda i: (i, 0)),
            row,
            row,
            pl.BlockSpec((d, cols), lambda i: (0, 0)),
            wide,
            wide,
        ],
        out_specs=pl.BlockSpec((tile, cols), lambda i: (i, 0)),
        out_shape=jax.ShapeDtypeStruct((rows, cols), BF16),
        compiler_params=params(),
        name="project",
        cost_estimate=pl.CostEstimate(
            flops=2 * rows * d * cols, bytes_accessed=2 * rows * (d + cols), transcendentals=0
        ),
    )(x, gain, shift, w, bias, scale)


MESH = pl.DeviceIdType.MESH
ANY = pl.BlockSpec(memory_space=pl.ANY)
PER_UNIT = 23
OTHERS = [(0, 1), (0, 2), (0, 3), (1, 0), (1, 1), (1, 2), (1, 3)]


def whereabouts():
    y = lax.axis_index("dp")
    f = lax.axis_index("fsdp")
    return y, f // 4, (f // 2) % 2, f % 2


def spot(z, x, c):
    return z * 4 + x * 2 + c


def greet():
    y, z, x, c = whereabouts()
    barrier = pltpu.get_barrier_semaphore()
    peers = [(1 - y, spot(z, x, c)), (y, spot(z, 1 - x, c)), (y, spot(z, x, 1 - c))]
    peers += [(y, spot((z + d) % 4, x, c)) for d in (1, 2, 3)]
    for peer in peers:
        pl.semaphore_signal(barrier, inc=1, device_id=peer, device_id_type=MESH)
    pl.semaphore_wait(barrier, len(peers))


class Gather:
    def __init__(self, units, send, recv, local):
        self.units, self.send, self.recv, self.local = units, send, recv, local
        self.y, self.z, self.x, self.c = whereabouts()

    def rows(self, u, part, y):
        r = self.units[u][0].shape[0]
        if part == "all" or not self.units[u][5]:
            return 0, r
        third = r // 3
        return (y * third, 2 * third) if part == "wide" else (y * 2 * third, third)

    def mine(self, u, part):
        src, _, _, col, n, _ = self.units[u]
        lo, size = self.rows(u, part, self.y)
        return src.at[pl.ds(lo, size), pl.ds(col, n)]

    def there(self, u, part, y, z, x, c):
        src, dst, _, col, n, _ = self.units[u]
        lo, size = self.rows(u, part, y)
        return dst.at[pl.ds(spot(z, x, c) * src.shape[0] + lo, size), pl.ds(col, n)]

    def copy(self, u, slot, src, dst, peer):
        i = u * PER_UNIT + slot
        return pltpu.make_async_remote_copy(
            src_ref=src, dst_ref=dst, send_sem=self.send.at[i], recv_sem=self.recv.at[i],
            device_id=peer, device_id_type=MESH,
        )

    def along_z(self, u, d, out=True):
        y, z, x, c = self.y, self.z, self.x, self.c
        peer = (y, spot((z + d) % 4, x, c))
        dst = self.there(u, "wide", y, z if out else (z + 4 - d) % 4, x, c)
        return self.copy(u, d - 1, self.mine(u, "wide"), dst, peer)

    def along_x(self, u, d, out=True):
        y, z, x, c = self.y, self.z, self.x, self.c
        origin = (z + 4 - d) % 4
        dst = self.there(u, "wide", y, origin, x if out else 1 - x, c)
        src = self.mine(u, "wide") if d == 0 else self.there(u, "wide", y, origin, x, c)
        return self.copy(u, 3 + d, src, dst, (y, spot(z, 1 - x, c)))

    def along_y(self, u, k, d, out=True):
        y, z, x, c = self.y, self.z, self.x, self.c
        origin, column = (z + 4 - d) % 4, x if k == 0 else 1 - x
        dst = self.there(u, "thin", y if out else 1 - y, origin, column, c)
        src = self.there(u, "thin", y, origin, column, c)
        return self.copy(u, 7 + 4 * k + d, src, dst, (1 - y, spot(z, x, c)))

    def along_c(self, u, k, d, out=True):
        y, z, x, c = self.y, self.z, self.x, self.c
        origin, column = (z + 4 - d) % 4, x if k == 0 else 1 - x
        dst = self.there(u, "all", y, origin, column, c if out else 1 - c)
        src = self.mine(u, "all") if k == 0 and d == 0 else self.there(u, "all", y, origin, column, c)
        return self.copy(u, 15 + 4 * k + d, src, dst, (y, spot(z, x, 1 - c)))

    def load(self, u):
        _, _, hold, col, n, _ = self.units[u]
        return pltpu.make_async_copy(self.mine(u, "all"), hold.at[:, pl.ds(col, n)], self.local.at[2 * u])

    def store(self, u):
        _, _, hold, col, n, _ = self.units[u]
        dst = self.there(u, "all", self.y, self.z, self.x, self.c)
        return pltpu.make_async_copy(hold.at[:, pl.ds(col, n)], dst, self.local.at[2 * u + 1])

    def stage(self, s, u):
        split = self.units[u][5]
        if s == 0:
            for d in (1, 2, 3):
                self.along_z(u, d).start()
            self.along_x(u, 0).start()
            self.along_c(u, 0, 0).start()
            self.load(u).start()
        if s == 1:
            self.load(u).wait()
            self.store(u).start()
            for d in (1, 2, 3):
                self.along_z(u, d, False).wait_recv()
                self.along_x(u, d).start()
                (self.along_y if split else self.along_c)(u, 0, d).start()
        if s == 2:
            for d in range(4):
                self.along_x(u, d, False).wait_recv()
                (self.along_y if split else self.along_c)(u, 1, d).start()
        if s == 3 and split:
            for k, d in OTHERS:
                self.along_y(u, k, d, False).wait_recv()
                self.along_c(u, k, d).start()
        if s == 4:
            self.store(u).wait()
            for d in (1, 2, 3):
                self.along_z(u, d).wait_send()
            for d in range(4):
                self.along_x(u, d).wait_send()
            for k, d in [(0, 0)] + OTHERS:
                if split and (k, d) != (0, 0):
                    self.along_y(u, k, d).wait_send()
                self.along_c(u, k, d, False).wait_recv()
                self.along_c(u, k, d).wait_send()


STAGES = 5


def gather_scratch(shards, units):
    return [pltpu.VMEM(s.shape, s.dtype) for s in shards] + [
        pltpu.SemaphoreType.DMA((units * PER_UNIT,)),
        pltpu.SemaphoreType.DMA((units * PER_UNIT,)),
        pltpu.SemaphoreType.DMA((2 * units,)),
    ]


def whole(shard, n):
    return jax.ShapeDtypeStruct((shard.shape[0] * n, shard.shape[1]), shard.dtype)


def first_gather_body(t_ref, v_ref, tf_ref, vf_ref, th_ref, vh_ref, send, recv, local):
    third = t_ref.shape[1] // 3
    units = [(v_ref, vf_ref, vh_ref, 0, v_ref.shape[1], False)]
    units += [(t_ref, tf_ref, th_ref, j * third, third, True) for j in range(3)]
    greet()
    work = Gather(units, send, recv, local)
    for u in range(len(units)):
        work.stage(0, u)
    for k in range(len(units) + 3):
        for s in range(1, STAGES):
            if 0 <= k - s + 1 < len(units):
                work.stage(s, k - s + 1)


def first_gather(triple, vectors):
    return pl.pallas_call(
        first_gather_body,
        in_specs=[ANY, ANY],
        out_specs=[ANY, ANY],
        out_shape=[whole(triple, 16), whole(vectors, 16)],
        scratch_shapes=gather_scratch([triple, vectors], 4),
        compiler_params=params(collective_id=0, has_side_effects=True),
        name="first_gather",
    )(triple, vectors)


QT = 256


def half_mask(value, hh):
    lane = lax.broadcasted_iota(jnp.int32, value.shape, 1)
    keep = lane < HD if hh == 0 else lane >= HD
    return jnp.where(keep, value, jnp.zeros_like(value))


def attend_body(*refs):
    q_ref, k_ref, v_ref, segc_ref, segr_ref = refs[:5]
    if len(refs) == 8:
        o_ref, p_ref, bias_ref = refs[5:]
    else:
        out_ref, up_ref, down_ref, o_ref, p_ref, out_full, up_full, down_full, bias_ref = refs[5:14]
        out_hold, up_hold, down_hold, send, recv, local = refs[14:]
        units = [(out_ref, out_full, out_hold, 0, out_ref.shape[1], True)]
        for ref, full, hold in ((up_ref, up_full, up_hold), (down_ref, down_full, down_hold)):
            n = ref.shape[1] // 3
            units += [(ref, full, hold, j * n, n, True) for j in range(3)]
        work = Gather(units, send, recv, local)
        step = pl.program_id(0) * pl.num_programs(1) + pl.program_id(1)
        for k in range(len(units) + STAGES - 1):

            @pl.when(step == k)
            def _():
                if k == 0:
                    greet()
                for s in range(STAGES):
                    if 0 <= k - s < len(units):
                        work.stage(s, k - s)

    rows = q_ref.shape[0]

    @pl.when(pl.program_id(1) == 0)
    def _():
        bias_ref[...] = jnp.where(segc_ref[...] == segr_ref[...], 0.0, -1e30)

    k = k_ref[...]
    v = v_ref[...]
    for t in range(rows // QT):
        sl = pl.ds(t * QT, QT)
        out = None
        for hh in range(2):
            q = half_mask(q_ref[sl, :], hh)
            s = mm(q, k, NT) + bias_ref[sl, :]
            peak = jnp.max(s, axis=-1, keepdims=True)
            e = jnp.exp(s - peak)
            total = jnp.sum(e, axis=-1, keepdims=True)
            p = (e * (1.0 / total)).astype(BF16)
            p_ref[hh, sl, :] = p
            o = mm(p, v)
            if hh == 0:
                out = o
            else:
                lane = lax.broadcasted_iota(jnp.int32, o.shape, 1)
                out = jnp.where(lane < HD, out, o)
        o_ref[sl, :] = out.astype(BF16)


def attend(qkv, segc, segr, shards=()):
    rows = qkv.shape[0]
    d = qkv.shape[1] // 3
    mb = rows // ROWS
    pairs = d // 128
    extra = dict(collective_id=1, has_side_effects=True) if shards else {}
    return pl.pallas_call(
        attend_body,
        grid=(mb, pairs),
        in_specs=[
            pl.BlockSpec((ROWS, 128), lambda m, h: (m, h)),
            pl.BlockSpec((ROWS, 128), lambda m, h: (m, pairs + h)),
            pl.BlockSpec((ROWS, 128), lambda m, h: (m, 2 * pairs + h)),
            pl.BlockSpec((ROWS, 1), lambda m, h: (m, 0)),
            pl.BlockSpec((None, 1, ROWS), lambda m, h: (m, 0, 0)),
            *[ANY for _ in shards],
        ],
        out_specs=[
            pl.BlockSpec((ROWS, 128), lambda m, h: (m, h)),
            pl.BlockSpec((None, 2, ROWS, ROWS), lambda m, h: (m, h, 0, 0)),
            *[ANY for _ in shards],
        ],
        out_shape=[
            jax.ShapeDtypeStruct((rows, d), BF16),
            jax.ShapeDtypeStruct((mb, 2 * pairs, ROWS, ROWS), BF16),
            *[whole(s, 16) for s in shards],
        ],
        scratch_shapes=[pltpu.VMEM((ROWS, ROWS), F32)] + (gather_scratch(shards, 7) if shards else []),
        compiler_params=params(**extra),
        name="attend",
        cost_estimate=pl.CostEstimate(
            flops=mb * pairs * 2 * 4 * ROWS * ROWS * 256,
            bytes_accessed=mb * pairs * 2 * ROWS * ROWS * 2,
            transcendentals=mb * pairs * 2 * ROWS * ROWS,
        ),
    )(qkv, qkv, qkv, segc, segr, *shards)


def attend_back_body(q_ref, k_ref, v_ref, p_ref, o_ref, g_ref, dq_ref, dk_ref, dv_ref, ds_ref):
    rows = q_ref.shape[0]
    k = k_ref[...]
    v = v_ref[...]
    q_t = q_ref[...].T
    g_t = g_ref[...].T
    prod = g_ref[...].astype(F32) * o_ref[...].astype(F32)
    dk_parts = []
    dv_parts = []
    dq_parts = []
    for hh in range(2):
        half = slice(hh * HD, (hh + 1) * HD)
        center = jnp.sum(half_mask(prod, hh), axis=-1, keepdims=True)
        for t in range(rows // QT):
            sl = pl.ds(t * QT, QT)
            ts = slice(t * QT, (t + 1) * QT)
            d_soft = mm(half_mask(g_ref[sl, :], hh), v, NT)
            ds = p_ref[hh, sl, :].astype(F32) * (d_soft - center[ts, :])
            ds_ref[hh, sl, :] = ds.astype(BF16)
        dv_parts.append(mm(g_t[half, :], p_ref[hh]))
        dk_parts.append(mm(q_t[half, :], ds_ref[hh]))
        dq_parts.append(mm(ds_ref[hh], k))
    lane = lax.broadcasted_iota(jnp.int32, dq_parts[0].shape, 1)
    dq_ref[...] = (jnp.where(lane < HD, dq_parts[0], dq_parts[1]) * 0.125).astype(BF16)
    dk_ref[...] = jnp.concatenate(dk_parts, axis=0).T.astype(BF16)
    dv_ref[...] = jnp.concatenate(dv_parts, axis=0).T.astype(BF16)


def attend_back(qkv, soft, mixed, d_mixed):
    rows = qkv.shape[0]
    d = qkv.shape[1] // 3
    mb = rows // ROWS
    pairs = d // 128
    blk = pl.BlockSpec((ROWS, 128), lambda m, h: (m, h))
    shape = jax.ShapeDtypeStruct((rows, d), BF16)
    return pl.pallas_call(
        attend_back_body,
        grid=(mb, pairs),
        in_specs=[
            blk,
            pl.BlockSpec((ROWS, 128), lambda m, h: (m, pairs + h)),
            pl.BlockSpec((ROWS, 128), lambda m, h: (m, 2 * pairs + h)),
            pl.BlockSpec((None, 2, ROWS, ROWS), lambda m, h: (m, h, 0, 0)),
            blk,
            blk,
        ],
        out_specs=[blk, blk, blk],
        out_shape=[shape, shape, shape],
        scratch_shapes=[pltpu.VMEM((2, ROWS, ROWS), BF16)],
        compiler_params=params(),
        name="attend_back",
        cost_estimate=pl.CostEstimate(
            flops=mb * pairs * 2 * 8 * ROWS * ROWS * 256,
            bytes_accessed=mb * pairs * 2 * ROWS * ROWS * 2,
            transcendentals=0,
        ),
    )(qkv, qkv, qkv, soft, mixed, d_mixed)


def out_body(x_ref, m_ref, w_ref, bias_ref, gain_ref, shift_ref, resid_ref, h_ref):
    resid = x_ref[...].astype(F32) + mm(m_ref[...], w_ref[...]) + bias_ref[...]
    resid_ref[...] = resid
    n, _ = norm_stats(resid)
    h_ref[...] = (n * gain_ref[...] + shift_ref[...]).astype(BF16)


def out_project(x, mixed, w, bias, gain, shift):
    rows, d = x.shape
    tile = 512
    blk = pl.BlockSpec((tile, d), lambda i: (i, 0))
    row = pl.BlockSpec((1, d), lambda i: (0, 0))
    return pl.pallas_call(
        out_body,
        grid=(rows // tile,),
        in_specs=[blk, blk, pl.BlockSpec((d, d), lambda i: (0, 0)), row, row, row],
        out_specs=[blk, blk],
        out_shape=[
            jax.ShapeDtypeStruct((rows, d), F32),
            jax.ShapeDtypeStruct((rows, d), BF16),
        ],
        compiler_params=params(),
        name="out_project",
        cost_estimate=pl.CostEstimate(
            flops=2 * rows * d * d, bytes_accessed=rows * d * 10, transcendentals=0
        ),
    )(x, mixed, w, bias, gain, shift)


FC = 512
RT = 512


def gelu_parts(u):
    cdf = 0.5 * (1.0 + lax.erf(u * ROOT_HALF))
    bell = jnp.exp(-0.5 * u * u) * ROOT_INV_TWO_PI
    return u * cdf, cdf + u * bell


def mlp_body(h_ref, ht_ref, g_ref, gt_ref, wu_ref, bu_ref, wd_ref, acc_ref, dh_ref, dwu_ref, dwd_ref, dbu_ref,
             act_ref, du_ref):
    rows = h_ref.shape[0]

    @pl.when(pl.program_id(0) == 0)
    def _():
        acc_ref[...] = jnp.zeros_like(acc_ref)
        dh_ref[...] = jnp.zeros_like(dh_ref)

    wu = wu_ref[...]
    wd = wd_ref[...]
    bias_sum = None
    for t in range(rows // RT):
        sl = pl.ds(t * RT, RT)
        u = mm(h_ref[sl, :], wu) + bu_ref[...]
        act, slope = gelu_parts(u)
        act_ref[sl, :] = act.astype(BF16)
        du = mm(g_ref[sl, :], wd, NT) * slope
        part = jnp.sum(du, axis=0, keepdims=True)
        bias_sum = part if bias_sum is None else bias_sum + part
        du_ref[sl, :] = du.astype(BF16)
        acc_ref[sl, :] += mm(act_ref[sl, :], wd)
        dh_ref[sl, :] += mm(du_ref[sl, :], wu, NT)
    dbu_ref[...] = bias_sum
    dwu_ref[...] = mm(ht_ref[...], du_ref[...]).astype(dwu_ref.dtype)
    dwd_ref[...] = mm(gt_ref[...], act_ref[...]).T.astype(dwd_ref.dtype)


def mlp(h, ht, g, gt, wu, bu, wd):
    rows, d = h.shape
    ff = wu.shape[1]
    one = pl.Buffered(1)
    whole = pl.BlockSpec((rows, d), lambda c: (0, 0), pipeline_mode=one)
    whole_t = pl.BlockSpec((d, rows), lambda c: (0, 0), pipeline_mode=one)
    return pl.pallas_call(
        mlp_body,
        grid=(ff // FC,),
        in_specs=[
            whole,
            whole_t,
            whole,
            whole_t,
            pl.BlockSpec((d, FC), lambda c: (0, c)),
            pl.BlockSpec((1, FC), lambda c: (0, c)),
            pl.BlockSpec((FC, d), lambda c: (c, 0)),
        ],
        out_specs=[
            whole,
            whole,
            pl.BlockSpec((d, FC), lambda c: (0, c)),
            pl.BlockSpec((FC, d), lambda c: (c, 0)),
            pl.BlockSpec((1, FC), lambda c: (0, c)),
        ],
        out_shape=[
            jax.ShapeDtypeStruct((rows, d), F32),
            jax.ShapeDtypeStruct((rows, d), F32),
            jax.ShapeDtypeStruct((d, ff), BF16),
            jax.ShapeDtypeStruct((ff, d), BF16),
            jax.ShapeDtypeStruct((1, ff), F32),
        ],
        scratch_shapes=[pltpu.VMEM((rows, FC), BF16), pltpu.VMEM((rows, FC), BF16)],
        compiler_params=params(),
        name="mlp",
        cost_estimate=pl.CostEstimate(
            flops=12 * rows * d * ff, bytes_accessed=rows * d * 20 + 8 * d * ff, transcendentals=3 * rows * ff
        ),
    )(h, ht, g, gt, wu, bu, wd)


def fold(ref, step, value):
    part = jnp.sum(value, axis=0, keepdims=True)

    @pl.when(step == 0)
    def _():
        ref[...] = part

    @pl.when(step != 0)
    def _():
        ref[...] += part


def norm_pull(grad, n, inv, gain):
    dn = grad * gain
    plain = jnp.mean(dn, axis=-1, keepdims=True)
    cross = jnp.mean(dn * n, axis=-1, keepdims=True)
    return inv * (dn - plain - n * cross)


def mid_body(resid_ref, acc_ref, dh_ref, g_ref, mixed_ref, w_ref, bias_ref, gain_ref,
             y_ref, dr_ref, dm_ref, dw_ref, dgain_ref, dshift_ref, dob_ref, ddb_ref, sum_ref):
    step = pl.program_id(0)
    resid = resid_ref[...]
    y_ref[...] = (resid + acc_ref[...] + bias_ref[...]).astype(BF16)
    g = g_ref[...].astype(F32)
    n, inv = norm_stats(resid)
    dh = dh_ref[...]
    fold(dgain_ref, step, dh * n)
    fold(dshift_ref, step, dh)
    fold(ddb_ref, step, g)
    dr = g + norm_pull(dh, n, inv, gain_ref[...])
    dr_ref[...] = dr
    fold(dob_ref, step, dr)
    low = dr.astype(BF16)
    dm_ref[...] = mm(low, w_ref[...], NT).astype(BF16)
    dw = mm(mixed_ref[...].T, low)

    @pl.when(step == 0)
    def _():
        sum_ref[...] = dw

    @pl.when(step != 0)
    def _():
        sum_ref[...] += dw

    @pl.when(step == pl.num_programs(0) - 1)
    def _():
        dw_ref[...] = sum_ref[...].astype(dw_ref.dtype)


def middle(resid, acc, dh, g, mixed, w, bias, gain):
    rows, d = resid.shape
    tile = 512
    blk = pl.BlockSpec((tile, d), lambda i: (i, 0))
    row = pl.BlockSpec((1, d), lambda i: (0, 0))
    mat = pl.BlockSpec((d, d), lambda i: (0, 0))
    vec = jax.ShapeDtypeStruct((1, d), F32)
    return pl.pallas_call(
        mid_body,
        grid=(rows // tile,),
        in_specs=[blk, blk, blk, blk, blk, mat, row, row],
        out_specs=[blk, blk, blk, mat, row, row, row, row],
        out_shape=[
            jax.ShapeDtypeStruct((rows, d), BF16),
            jax.ShapeDtypeStruct((rows, d), F32),
            jax.ShapeDtypeStruct((rows, d), BF16),
            jax.ShapeDtypeStruct((d, d), BF16),
            vec,
            vec,
            vec,
            vec,
        ],
        scratch_shapes=[pltpu.VMEM((d, d), F32)],
        compiler_params=params(),
        name="middle",
        cost_estimate=pl.CostEstimate(
            flops=4 * rows * d * d, bytes_accessed=rows * d * 24, transcendentals=0
        ),
    )(resid, acc, dh, g, mixed, w, bias, gain)


def last_body(x_ref, dr_ref, dq_ref, dk_ref, dv_ref, w_ref, gain_ref, shift_ref,
              dx_ref, dw_ref, dgain_ref, dshift_ref, dqb_ref, dvb_ref, sum_ref):
    step = pl.program_id(0)
    d = x_ref.shape[1]
    n, inv = norm_stats(x_ref[...].astype(F32))
    h_t = (n * gain_ref[...] + shift_ref[...]).astype(BF16).T
    dh = None
    for j, ref in enumerate((dq_ref, dk_ref, dv_ref)):
        cols = pl.ds(j * d, d)
        part = ref[...]
        term = mm(part, w_ref[:, cols], NT)
        dh = term if dh is None else dh + term
        dw = mm(h_t, part)

        @pl.when(step == 0)
        def _():
            sum_ref[:, cols] = dw

        @pl.when(step != 0)
        def _():
            sum_ref[:, cols] += dw

    fold(dqb_ref, step, dq_ref[...].astype(F32))
    fold(dvb_ref, step, dv_ref[...].astype(F32))
    fold(dgain_ref, step, dh * n)
    fold(dshift_ref, step, dh)
    dx_ref[...] = (dr_ref[...] + norm_pull(dh, n, inv, gain_ref[...])).astype(BF16)

    @pl.when(step == pl.num_programs(0) - 1)
    def _():
        dw_ref[...] = sum_ref[...].astype(dw_ref.dtype)


def last(x, dr, dq, dk, dv, w, gain, shift):
    rows, d = x.shape
    tile = 512
    blk = pl.BlockSpec((tile, d), lambda i: (i, 0))
    row = pl.BlockSpec((1, d), lambda i: (0, 0))
    mat = pl.BlockSpec((d, 3 * d), lambda i: (0, 0))
    vec = jax.ShapeDtypeStruct((1, d), F32)
    return pl.pallas_call(
        last_body,
        grid=(rows // tile,),
        in_specs=[blk, blk, blk, blk, blk, mat, row, row],
        out_specs=[blk, mat, row, row, row, row],
        out_shape=[
            jax.ShapeDtypeStruct((rows, d), BF16),
            jax.ShapeDtypeStruct((d, 3 * d), BF16),
            vec,
            vec,
            vec,
            vec,
        ],
        scratch_shapes=[pltpu.VMEM((d, 3 * d), F32)],
        compiler_params=params(),
        name="last",
        cost_estimate=pl.CostEstimate(
            flops=12 * rows * d * d, bytes_accessed=rows * d * 14, transcendentals=0
        ),
    )(x, dr, dq, dk, dv, w, gain, shift)


def on_device(tokens, cotangent, segment_ids, *shards):
    gather = lambda s: lax.all_gather(s, "fsdp", axis=0, tiled=True)
    n = lax.axis_size("fsdp")
    near = n == 16 and lax.axis_size("dp") == 2
    triple_s, out_s, up_s, down_s = (s for s in shards if s.ndim == 2)
    vectors = [s for s in shards if s.ndim == 1]
    lane = jnp.concatenate(vectors)
    if near:
        tall = jnp.pad(lane, (0, 2048 - lane.shape[0])).reshape(16, 128)
        triple_weight, packed = first_gather(triple_s, tall)
        packed = packed.reshape(n, 2048)
    else:
        triple_weight = gather(triple_s)
        packed = gather(lane.reshape(1, -1))
    values = []
    at = 0
    for v in vectors:
        values.append(packed[:, at : at + v.shape[0]].astype(F32).reshape(1, -1))
        at += v.shape[0]
    (first_gain, first_shift, query_bias, value_bias, out_bias, second_gain, second_shift, up_bias, down_bias) = values

    rows, d = tokens.shape
    bias = jnp.concatenate([query_bias, jnp.zeros((1, d), F32), value_bias], axis=1)
    scale = jnp.concatenate([jnp.full((1, d), 0.125, F32), jnp.ones((1, 2 * d), F32)], axis=1)
    segc = segment_ids.reshape(rows, 1)
    segr = segment_ids.reshape(rows // ROWS, 1, ROWS)
    qkv = project(tokens, first_gain, first_shift, triple_weight, bias, scale)
    if near:
        mixed, soft, out_weight, up_weight, down_weight = attend(qkv, segc, segr, (out_s, up_s, down_s))
    else:
        mixed, soft = attend(qkv, segc, segr)
        out_weight, up_weight, down_weight = gather(out_s), gather(up_s), gather(down_s)
    resid, h = out_project(tokens, mixed, out_weight, out_bias, second_gain, second_shift)
    acc, dh, dwu, dwd, dbu = mlp(h, h.T, cotangent, cotangent.T, up_weight, up_bias, down_weight)
    y, dr, dm, dwo, dg2, ds2, dob, ddb = middle(resid, acc, dh, cotangent, mixed, out_weight, down_bias, second_gain)
    dq, dk, dv = attend_back(qkv, soft, mixed, dm)
    dx, dwt, dg1, ds1, dqb, dvb = last(tokens, dr, dq, dk, dv, triple_weight, first_gain, first_shift)

    parts = (dg1, ds1, dwt, dqb, dvb, dwo, dob, dg2, ds2, dwu, dbu, dwd, ddb)
    small = jnp.concatenate([p.reshape(n, -1) for p, s in zip(parts, shards) if s.ndim == 1], axis=1)
    small = lax.psum_scatter(small, "fsdp", scatter_dimension=0, tiled=True).reshape(-1)
    small = lax.psum(small, "dp")
    grads = []
    at = 0
    for p, s in zip(parts, shards):
        if s.ndim == 1:
            grads.append(small[at : at + s.shape[0]])
            at += s.shape[0]
        else:
            one = lax.psum_scatter(p, "fsdp", scatter_dimension=0, tiled=True)
            grads.append(lax.psum(one, "dp").astype(F32))
    return (y, dx, *grads)


def solution(mesh):
    tok = P(("dp", "fsdp"), None)
    vec = P("fsdp")
    mat = P("fsdp", None)
    weights = (vec, vec, mat, vec, vec, mat, vec, vec, vec, mat, vec, mat, vec)
    return jax.shard_map(
        on_device,
        mesh=mesh,
        in_specs=(tok, tok, P(("dp", "fsdp")), *weights),
        out_specs=(tok, tok, *weights),
        check_vma=False,
    )
```

```python
import functools

import jax
import jax.numpy as jnp
from jax import lax
from jax.experimental import pallas as pl
from jax.experimental.pallas import tpu as pltpu
from jax.sharding import PartitionSpec as P

H = 12
HD = 64
ROWS = 1024
EPS = 1e-06
F32 = jnp.float32
BF16 = jnp.bfloat16
VMEM_LIMIT = 60 * 1024 * 1024

ROOT_HALF = 0.7071067811865476
ROOT_INV_TWO_PI = 0.3989422804014327

NN = (((1,), (0,)), ((), ()))
NT = (((1,), (1,)), ((), ()))


def mm(a, b, dims=NN):
    return lax.dot_general(a, b, dims, preferred_element_type=F32)


def params(**kw):
    return pltpu.CompilerParams(vmem_limit_bytes=VMEM_LIMIT, **kw)


def norm_stats(x):
    mean = jnp.mean(x, axis=-1, keepdims=True)
    cen = x - mean
    var = jnp.mean(cen * cen, axis=-1, keepdims=True)
    inv = lax.rsqrt(var + EPS)
    return cen * inv, inv


def proj_body(x_ref, gain_ref, shift_ref, w_ref, bias_ref, scale_ref, qkv_ref):
    n, _ = norm_stats(x_ref[...].astype(F32))
    h = (n * gain_ref[...] + shift_ref[...]).astype(BF16)
    p = mm(h, w_ref[...])
    qkv_ref[...] = ((p + bias_ref[...]) * scale_ref[...]).astype(BF16)


def project(x, gain, shift, w, bias, scale):
    rows, d = x.shape
    cols = w.shape[1]
    tile = 512
    row = pl.BlockSpec((1, d), lambda i: (0, 0))
    wide = pl.BlockSpec((1, cols), lambda i: (0, 0))
    return pl.pallas_call(
        proj_body,
        grid=(rows // tile,),
        in_specs=[
            pl.BlockSpec((tile, d), lambda i: (i, 0)),
            row,
            row,
            pl.BlockSpec((d, cols), lambda i: (0, 0)),
            wide,
            wide,
        ],
        out_specs=pl.BlockSpec((tile, cols), lambda i: (i, 0)),
        out_shape=jax.ShapeDtypeStruct((rows, cols), BF16),
        compiler_params=params(),
        name="project",
        cost_estimate=pl.CostEstimate(
            flops=2 * rows * d * cols, bytes_accessed=2 * rows * (d + cols), transcendentals=0
        ),
    )(x, gain, shift, w, bias, scale)


MESH = pl.DeviceIdType.MESH
ANY = pl.BlockSpec(memory_space=pl.ANY)
PER_UNIT = 24
OTHERS = [(0, 1), (0, 2), (0, 3), (1, 0), (1, 1), (1, 2), (1, 3)]


def whereabouts():
    y = lax.axis_index("dp")
    f = lax.axis_index("fsdp")
    return y, f // 4, (f // 2) % 2, f % 2


def spot(z, x, c):
    return z * 4 + x * 2 + c


def greet():
    y, z, x, c = whereabouts()
    barrier = pltpu.get_barrier_semaphore()
    peers = [(1 - y, spot(z, x, c)), (y, spot(z, 1 - x, c)), (y, spot(z, x, 1 - c))]
    peers += [(y, spot((z + d) % 4, x, c)) for d in (1, 2, 3)]
    for peer in peers:
        pl.semaphore_signal(barrier, inc=1, device_id=peer, device_id_type=MESH)
    pl.semaphore_wait(barrier, len(peers))


class Gather:
    def __init__(self, units, send, recv, local):
        self.units, self.send, self.recv, self.local = units, send, recv, local
        self.y, self.z, self.x, self.c = whereabouts()

    def rows(self, u, part, y):
        r = self.units[u][0].shape[0]
        if part == "all" or not self.units[u][5]:
            return 0, r
        third = r // 3
        return (y * third, 2 * third) if part == "wide" else (y * 2 * third, third)

    def mine(self, u, part):
        src, _, _, col, n, _ = self.units[u]
        lo, size = self.rows(u, part, self.y)
        return src.at[pl.ds(lo, size), pl.ds(col, n)]

    def there(self, u, part, y, z, x, c):
        src, dst, _, col, n, _ = self.units[u]
        lo, size = self.rows(u, part, y)
        return dst.at[pl.ds(spot(z, x, c) * src.shape[0] + lo, size), pl.ds(col, n)]

    def copy(self, u, slot, src, dst, peer):
        i = u * PER_UNIT + slot
        return pltpu.make_async_remote_copy(
            src_ref=src, dst_ref=dst, send_sem=self.send.at[i], recv_sem=self.recv.at[i],
            device_id=peer, device_id_type=MESH,
        )

    def along_z(self, u, d, out=True):
        y, z, x, c = self.y, self.z, self.x, self.c
        peer = (y, spot((z + d) % 4, x, c))
        dst = self.there(u, "wide", y, z if out else (z + 4 - d) % 4, x, c)
        return self.copy(u, d - 1, self.mine(u, "wide"), dst, peer)

    def along_x(self, u, d, out=True):
        y, z, x, c = self.y, self.z, self.x, self.c
        origin = (z + 4 - d) % 4
        dst = self.there(u, "wide", y, origin, x if out else 1 - x, c)
        src = self.mine(u, "wide") if d == 0 else self.there(u, "wide", y, origin, x, c)
        return self.copy(u, 3 + d, src, dst, (y, spot(z, 1 - x, c)))

    def along_y(self, u, k, d, out=True):
        y, z, x, c = self.y, self.z, self.x, self.c
        origin, column = (z + 4 - d) % 4, x if k == 0 else 1 - x
        dst = self.there(u, "thin", y if out else 1 - y, origin, column, c)
        src = self.there(u, "thin", y, origin, column, c)
        return self.copy(u, 7 + 4 * k + d, src, dst, (1 - y, spot(z, x, c)))

    def along_c(self, u, k, d, out=True):
        y, z, x, c = self.y, self.z, self.x, self.c
        origin, column = (z + 4 - d) % 4, x if k == 0 else 1 - x
        dst = self.there(u, "all", y, origin, column, c if out else 1 - c)
        src = self.mine(u, "all") if k == 0 and d == 0 else self.there(u, "all", y, origin, column, c)
        return self.copy(u, 15 + 4 * k + d, src, dst, (y, spot(z, x, 1 - c)))

    def load(self, u):
        _, _, hold, col, n, _ = self.units[u]
        return pltpu.make_async_copy(self.mine(u, "all"), hold.at[:, pl.ds(col, n)], self.local.at[2 * u])

    def store(self, u):
        _, _, hold, col, n, _ = self.units[u]
        dst = self.there(u, "all", self.y, self.z, self.x, self.c)
        return pltpu.make_async_copy(hold.at[:, pl.ds(col, n)], dst, self.local.at[2 * u + 1])

    def stage(self, s, u):
        split = self.units[u][5]
        if s == 0:
            for d in (1, 2, 3):
                self.along_z(u, d).start()
            self.along_x(u, 0).start()
            self.along_c(u, 0, 0).start()
            self.load(u).start()
        if s == 1:
            self.load(u).wait()
            self.store(u).start()
            for d in (1, 2, 3):
                self.along_z(u, d, False).wait_recv()
                self.along_x(u, d).start()
                (self.along_y if split else self.along_c)(u, 0, d).start()
        if s == 2:
            for d in range(4):
                self.along_x(u, d, False).wait_recv()
                (self.along_y if split else self.along_c)(u, 1, d).start()
        if s == 3 and split:
            for k, d in OTHERS:
                self.along_y(u, k, d, False).wait_recv()
                self.along_c(u, k, d).start()
        if s == 4:
            self.store(u).wait()
            for d in (1, 2, 3):
                self.along_z(u, d).wait_send()
            for d in range(4):
                self.along_x(u, d).wait_send()
            for k, d in [(0, 0)] + OTHERS:
                if split and (k, d) != (0, 0):
                    self.along_y(u, k, d).wait_send()
                self.along_c(u, k, d, False).wait_recv()
                self.along_c(u, k, d).wait_send()


STAGES = 5


def gather_scratch(shards, units):
    return [pltpu.VMEM(s.shape, s.dtype) for s in shards] + [
        pltpu.SemaphoreType.DMA((units * PER_UNIT,)),
        pltpu.SemaphoreType.DMA((units * PER_UNIT,)),
        pltpu.SemaphoreType.DMA((2 * units,)),
    ]


def whole(shard, n):
    return jax.ShapeDtypeStruct((shard.shape[0] * n, shard.shape[1]), shard.dtype)


def first_gather_body(t_ref, v_ref, tf_ref, vf_ref, th_ref, vh_ref, send, recv, local):
    third = t_ref.shape[1] // 3
    units = [(v_ref, vf_ref, vh_ref, 0, v_ref.shape[1], False)]
    units += [(t_ref, tf_ref, th_ref, j * third, third, True) for j in range(3)]
    greet()
    work = Gather(units, send, recv, local)
    for u in range(len(units)):
        work.stage(0, u)
    for k in range(len(units) + 3):
        for s in range(1, STAGES):
            if 0 <= k - s + 1 < len(units):
                work.stage(s, k - s + 1)


def first_gather(triple, vectors):
    return pl.pallas_call(
        first_gather_body,
        in_specs=[ANY, ANY],
        out_specs=[ANY, ANY],
        out_shape=[whole(triple, 16), whole(vectors, 16)],
        scratch_shapes=gather_scratch([triple, vectors], 4),
        compiler_params=params(collective_id=0, has_side_effects=True),
        name="first_gather",
    )(triple, vectors)


class Reduce:
    def __init__(self, units, send, recv, local):
        self.units, self.send, self.recv, self.local = units, send, recv, local
        self.y, self.z, self.x, self.c = whereabouts()

    def size(self, u):
        return self.units[u][0].shape[0] // 16

    def wide(self, u, y):
        r = self.size(u)
        third = r // 3
        return pl.ds(pl.multiple_of(y * third, 8), 2 * third) if self.units[u][4] else pl.ds(0, r)

    def thin(self, u, y):
        third = self.size(u) // 3
        return pl.ds(pl.multiple_of(y * 2 * third, 8), third)

    def copy(self, u, slot, src, dst, peer):
        i = u * PER_UNIT + slot
        return pltpu.make_async_remote_copy(
            src_ref=src, dst_ref=dst, send_sem=self.send.at[i], recv_sem=self.recv.at[i],
            device_id=peer, device_id_type=MESH,
        )

    def partial(self, u, j, c):
        src, _, col, n, _, _ = self.units[u]
        r = self.size(u)
        return src.at[pl.ds(pl.multiple_of((2 * j + c) * r, 8), r), pl.ds(col, n)]

    def load(self, u, j):
        own = self.units[u][5][0]
        return pltpu.make_async_copy(self.partial(u, j, self.c), own.at[j], self.local.at[8 * u + j])

    def over_c(self, u, j):
        from_c = self.units[u][5][1]
        peer = (self.y, spot(self.z, self.x, 1 - self.c))
        return self.copy(u, j, self.partial(u, j, 1 - self.c), from_c.at[j], peer)

    def over_y(self, u, j):
        own, from_y = self.units[u][5][0], self.units[u][5][5]
        peer = (1 - self.y, spot(self.z, self.x, self.c))
        return self.copy(u, 8 + j, own.at[j, self.thin(u, 1 - self.y), :], from_y.at[j], peer)

    def over_x(self, u, k):
        own, from_x = self.units[u][5][0], self.units[u][5][2]
        peer = (self.y, spot(self.z, 1 - self.x, self.c))
        return self.copy(u, 16 + k, own.at[2 * k + 1 - self.x, self.wide(u, self.y), :], from_x.at[k], peer)

    def over_z(self, u, d):
        own, from_z = self.units[u][5][0], self.units[u][5][3]
        to = (self.z + d) % 4
        src = own.at[2 * to + self.x, self.wide(u, self.y), :]
        return self.copy(u, 19 + d, src, from_z.at[d - 1], (self.y, spot(to, self.x, self.c)))

    def over_last(self, u):
        last = self.units[u][5][4]
        peer = (1 - self.y, spot(self.z, self.x, self.c))
        return self.copy(u, 23, last.at[0], last.at[1], peer)

    def stage(self, s, u):
        _, out, col, n, split, (own, from_c, from_x, from_z, last, *rest) = self.units[u]
        y, z, x = self.y, self.z, self.x
        wide = self.wide(u, y)
        if s == 0:
            for j in range(8):
                self.over_c(u, j).start()
                self.load(u, j).start()
        if s == 1:
            for j in range(8):
                self.load(u, j).wait()
                self.over_c(u, j).wait_recv()
                own[j] = own[j] + from_c[j]
                if split:
                    self.over_y(u, j).start()
        if s == 2:
            if split:
                for j in range(8):
                    self.over_y(u, j).wait_recv()
                    rows = self.thin(u, y)
                    own[j, rows, :] = own[j, rows, :] + rest[0][j]
            for k in range(4):
                self.over_x(u, k).start()
        if s == 3:
            for k in range(4):
                self.over_x(u, k).wait_recv()
                own[2 * k + x, wide, :] = own[2 * k + x, wide, :] + from_x[k]
            for d in (1, 2, 3):
                self.over_z(u, d).start()
        if s == 4:
            total = own[2 * z + x, wide, :].astype(F32)
            for d in (1, 2, 3):
                self.over_z(u, d).wait_recv()
                total = total + from_z[d - 1].astype(F32)
            last[0] = total.astype(last.dtype)
            self.over_last(u).start()
        if s == 5:
            self.over_last(u).wait_recv()
            cols = pl.ds(col, n)
            if split:
                t = self.size(u) // 3
                at = lambda k: pl.ds(pl.multiple_of(k * t, 8), t)
                put = lambda k, v: out.__setitem__((at(k), cols), v.astype(F32))
                put(1, last[0, at(1 - y), :].astype(F32) + last[1, at(y), :].astype(F32))
                put(2 * y, last[0, at(y), :])
                put(2 * (1 - y), last[1, at(1 - y), :])
            else:
                out[:, cols] = last[0].astype(F32) + last[1].astype(F32)
        if s == 6:
            for j in range(8):
                self.over_c(u, j).wait_send()
                if split:
                    self.over_y(u, j).wait_send()
            for k in range(4):
                self.over_x(u, k).wait_send()
            for d in (1, 2, 3):
                self.over_z(u, d).wait_send()
            self.over_last(u).wait_send()


REDUCE_STAGES = 7


def reduce_buffers(r, n, dtype, split):
    wide = 2 * r // 3 if split else r
    shapes = [(8, r, n), (8, r, n), (4, wide, n), (3, wide, n), (2, wide, n)]
    if split:
        shapes.append((8, r // 3, n))
    return [pltpu.VMEM(shape, dtype) for shape in shapes]


def reduce_scratch(plan):
    flat = []
    for p in plan:
        flat += reduce_buffers(*p)
    units = len(plan)
    return flat + [
        pltpu.SemaphoreType.DMA((units * PER_UNIT,)),
        pltpu.SemaphoreType.DMA((units * PER_UNIT,)),
        pltpu.SemaphoreType.DMA((units * 8,)),
    ]


def reduce_work(plan, places, scratch):
    units = []
    at = 0
    for (r, n, _, split), (src, out, col) in zip(plan, places):
        count = 6 if split else 5
        units.append((src, out, col, n, split, scratch[at : at + count]))
        at += count
    return Reduce(units, *scratch[at:])


def last_reduce_body(plan, t_ref, v_ref, to_ref, vo_ref, *scratch):
    n = t_ref.shape[1] // 3
    places = [(t_ref, to_ref, j * n) for j in range(3)] + [(v_ref, vo_ref, 0)]
    greet()
    work = reduce_work(plan, places, scratch)
    for u in range(len(places)):
        work.stage(0, u)
    for k in range(len(places) + REDUCE_STAGES - 2):
        for s in range(1, REDUCE_STAGES):
            if 0 <= k - s + 1 < len(places):
                work.stage(s, k - s + 1)


def last_reduce(triple, vectors):
    r, n = triple.shape[0] // 16, triple.shape[1]
    v = vectors.shape[0] // 16
    plan = [(r, n // 3, BF16, True)] * 3 + [(v, vectors.shape[1], F32, False)]
    vmem = pl.BlockSpec(memory_space=pltpu.VMEM)
    return pl.pallas_call(
        functools.partial(last_reduce_body, plan),
        in_specs=[ANY, ANY],
        out_specs=[vmem, vmem],
        out_shape=[jax.ShapeDtypeStruct((r, n), F32), jax.ShapeDtypeStruct((v, vectors.shape[1]), F32)],
        scratch_shapes=reduce_scratch(plan),
        compiler_params=params(collective_id=3, has_side_effects=True),
        name="last_reduce",
    )(triple, vectors)


QT = 256


def half_mask(value, hh):
    lane = lax.broadcasted_iota(jnp.int32, value.shape, 1)
    keep = lane < HD if hh == 0 else lane >= HD
    return jnp.where(keep, value, jnp.zeros_like(value))


def attend_body(*refs):
    q_ref, k_ref, v_ref, segc_ref, segr_ref = refs[:5]
    if len(refs) == 8:
        o_ref, p_ref, bias_ref = refs[5:]
    else:
        out_ref, up_ref, down_ref, o_ref, p_ref, out_full, up_full, down_full, bias_ref = refs[5:14]
        out_hold, up_hold, down_hold, send, recv, local = refs[14:]
        units = [(out_ref, out_full, out_hold, 0, out_ref.shape[1], True)]
        for ref, full, hold in ((up_ref, up_full, up_hold), (down_ref, down_full, down_hold)):
            n = ref.shape[1] // 3
            units += [(ref, full, hold, j * n, n, True) for j in range(3)]
        work = Gather(units, send, recv, local)
        step = pl.program_id(0) * pl.num_programs(1) + pl.program_id(1)
        for k in range(len(units) + STAGES - 1):

            @pl.when(step == k)
            def _():
                if k == 0:
                    greet()
                for s in range(STAGES):
                    if 0 <= k - s < len(units):
                        work.stage(s, k - s)

    rows = q_ref.shape[0]

    @pl.when(pl.program_id(1) == 0)
    def _():
        bias_ref[...] = jnp.where(segc_ref[...] == segr_ref[...], 0.0, -1e30)

    k = k_ref[...]
    v = v_ref[...]
    for t in range(rows // QT):
        sl = pl.ds(t * QT, QT)
        out = None
        for hh in range(2):
            q = half_mask(q_ref[sl, :], hh)
            s = mm(q, k, NT) + bias_ref[sl, :]
            peak = jnp.max(s, axis=-1, keepdims=True)
            e = jnp.exp(s - peak)
            total = jnp.sum(e, axis=-1, keepdims=True)
            p = (e * (1.0 / total)).astype(BF16)
            p_ref[hh, sl, :] = p
            o = mm(p, v)
            if hh == 0:
                out = o
            else:
                lane = lax.broadcasted_iota(jnp.int32, o.shape, 1)
                out = jnp.where(lane < HD, out, o)
        o_ref[sl, :] = out.astype(BF16)


def attend(qkv, segc, segr, shards=()):
    rows = qkv.shape[0]
    d = qkv.shape[1] // 3
    mb = rows // ROWS
    pairs = d // 128
    extra = dict(collective_id=1, has_side_effects=True) if shards else {}
    return pl.pallas_call(
        attend_body,
        grid=(mb, pairs),
        in_specs=[
            pl.BlockSpec((ROWS, 128), lambda m, h: (m, h)),
            pl.BlockSpec((ROWS, 128), lambda m, h: (m, pairs + h)),
            pl.BlockSpec((ROWS, 128), lambda m, h: (m, 2 * pairs + h)),
            pl.BlockSpec((ROWS, 1), lambda m, h: (m, 0)),
            pl.BlockSpec((None, 1, ROWS), lambda m, h: (m, 0, 0)),
            *[ANY for _ in shards],
        ],
        out_specs=[
            pl.BlockSpec((ROWS, 128), lambda m, h: (m, h)),
            pl.BlockSpec((None, 2, ROWS, ROWS), lambda m, h: (m, h, 0, 0)),
            *[ANY for _ in shards],
        ],
        out_shape=[
            jax.ShapeDtypeStruct((rows, d), BF16),
            jax.ShapeDtypeStruct((mb, 2 * pairs, ROWS, ROWS), BF16),
            *[whole(s, 16) for s in shards],
        ],
        scratch_shapes=[pltpu.VMEM((ROWS, ROWS), F32)] + (gather_scratch(shards, 7) if shards else []),
        compiler_params=params(**extra),
        name="attend",
        cost_estimate=pl.CostEstimate(
            flops=mb * pairs * 2 * 4 * ROWS * ROWS * 256,
            bytes_accessed=mb * pairs * 2 * ROWS * ROWS * 2,
            transcendentals=mb * pairs * 2 * ROWS * ROWS,
        ),
    )(qkv, qkv, qkv, segc, segr, *shards)


def attend_back_body(plan, *refs):
    q_ref, k_ref, v_ref, p_ref, o_ref, g_ref = refs[:6]
    if plan is None:
        dq_ref, dk_ref, dv_ref, ds_ref = refs[6:]
    else:
        parts = refs[6:9]
        dq_ref, dk_ref, dv_ref = refs[9:12]
        results = refs[12:15]
        ds_ref = refs[15]
        places = []
        for part, result in zip(parts, results):
            n = plan[len(places)][1]
            places += [(part, result, col) for col in range(0, part.shape[1], n)]
        work = reduce_work(plan, places, refs[16:])
        step = pl.program_id(0) * pl.num_programs(1) + pl.program_id(1)
        for k in range(len(plan) + REDUCE_STAGES - 2):

            @pl.when(step == k)
            def _():
                if k == 0:
                    greet()
                for u in range(len(plan)):
                    s = k - max(0, u - 1)
                    if 0 <= s < REDUCE_STAGES:
                        work.stage(s, u)

    rows = q_ref.shape[0]
    k = k_ref[...]
    v = v_ref[...]
    q_t = q_ref[...].T
    g_t = g_ref[...].T
    prod = g_ref[...].astype(F32) * o_ref[...].astype(F32)
    dk_parts = []
    dv_parts = []
    dq_parts = []
    for hh in range(2):
        half = slice(hh * HD, (hh + 1) * HD)
        center = jnp.sum(half_mask(prod, hh), axis=-1, keepdims=True)
        for t in range(rows // QT):
            sl = pl.ds(t * QT, QT)
            ts = slice(t * QT, (t + 1) * QT)
            d_soft = mm(half_mask(g_ref[sl, :], hh), v, NT)
            ds = p_ref[hh, sl, :].astype(F32) * (d_soft - center[ts, :])
            ds_ref[hh, sl, :] = ds.astype(BF16)
        dv_parts.append(mm(g_t[half, :], p_ref[hh]))
        dk_parts.append(mm(q_t[half, :], ds_ref[hh]))
        dq_parts.append(mm(ds_ref[hh], k))
    lane = lax.broadcasted_iota(jnp.int32, dq_parts[0].shape, 1)
    dq_ref[...] = (jnp.where(lane < HD, dq_parts[0], dq_parts[1]) * 0.125).astype(BF16)
    dk_ref[...] = jnp.concatenate(dk_parts, axis=0).T.astype(BF16)
    dv_ref[...] = jnp.concatenate(dv_parts, axis=0).T.astype(BF16)


def attend_back(qkv, soft, mixed, d_mixed, grads=()):
    rows = qkv.shape[0]
    d = qkv.shape[1] // 3
    mb = rows // ROWS
    pairs = d // 128
    blk = pl.BlockSpec((ROWS, 128), lambda m, h: (m, h))
    shape = jax.ShapeDtypeStruct((rows, d), BF16)
    plan = None
    results = []
    extra = {}
    if grads:
        plan = []
        for i, g in enumerate(grads):
            pieces = 3 if i else 1
            plan += [(g.shape[0] // 16, g.shape[1] // pieces, BF16, True)] * pieces
        results = [jax.ShapeDtypeStruct((g.shape[0] // 16, g.shape[1]), F32) for g in grads]
        extra = dict(collective_id=2, has_side_effects=True)
    return pl.pallas_call(
        functools.partial(attend_back_body, plan),
        grid=(mb, pairs),
        in_specs=[
            blk,
            pl.BlockSpec((ROWS, 128), lambda m, h: (m, pairs + h)),
            pl.BlockSpec((ROWS, 128), lambda m, h: (m, 2 * pairs + h)),
            pl.BlockSpec((None, 2, ROWS, ROWS), lambda m, h: (m, h, 0, 0)),
            blk,
            blk,
            *[ANY for _ in grads],
        ],
        out_specs=[blk, blk, blk, *[pl.BlockSpec(r.shape, lambda m, h: (0, 0)) for r in results]],
        out_shape=[shape, shape, shape, *results],
        scratch_shapes=[pltpu.VMEM((2, ROWS, ROWS), BF16)] + (reduce_scratch(plan) if grads else []),
        compiler_params=params(**extra),
        name="attend_back",
        cost_estimate=pl.CostEstimate(
            flops=mb * pairs * 2 * 8 * ROWS * ROWS * 256,
            bytes_accessed=mb * pairs * 2 * ROWS * ROWS * 2,
            transcendentals=0,
        ),
    )(qkv, qkv, qkv, soft, mixed, d_mixed, *grads)


def out_body(x_ref, m_ref, w_ref, bias_ref, gain_ref, shift_ref, resid_ref, h_ref):
    resid = x_ref[...].astype(F32) + mm(m_ref[...], w_ref[...]) + bias_ref[...]
    resid_ref[...] = resid
    n, _ = norm_stats(resid)
    h_ref[...] = (n * gain_ref[...] + shift_ref[...]).astype(BF16)


def out_project(x, mixed, w, bias, gain, shift):
    rows, d = x.shape
    tile = 512
    blk = pl.BlockSpec((tile, d), lambda i: (i, 0))
    row = pl.BlockSpec((1, d), lambda i: (0, 0))
    return pl.pallas_call(
        out_body,
        grid=(rows // tile,),
        in_specs=[blk, blk, pl.BlockSpec((d, d), lambda i: (0, 0)), row, row, row],
        out_specs=[blk, blk],
        out_shape=[
            jax.ShapeDtypeStruct((rows, d), F32),
            jax.ShapeDtypeStruct((rows, d), BF16),
        ],
        compiler_params=params(),
        name="out_project",
        cost_estimate=pl.CostEstimate(
            flops=2 * rows * d * d, bytes_accessed=rows * d * 10, transcendentals=0
        ),
    )(x, mixed, w, bias, gain, shift)


FC = 512
RT = 512


def gelu_parts(u):
    cdf = 0.5 * (1.0 + lax.erf(u * ROOT_HALF))
    bell = jnp.exp(-0.5 * u * u) * ROOT_INV_TWO_PI
    return u * cdf, cdf + u * bell


def mlp_body(h_ref, ht_ref, g_ref, gt_ref, wu_ref, bu_ref, wd_ref, acc_ref, dh_ref, dwu_ref, dwd_ref, dbu_ref,
             act_ref, du_ref):
    rows = h_ref.shape[0]

    @pl.when(pl.program_id(0) == 0)
    def _():
        acc_ref[...] = jnp.zeros_like(acc_ref)
        dh_ref[...] = jnp.zeros_like(dh_ref)

    wu = wu_ref[...]
    wd = wd_ref[...]
    bias_sum = None
    for t in range(rows // RT):
        sl = pl.ds(t * RT, RT)
        u = mm(h_ref[sl, :], wu) + bu_ref[...]
        act, slope = gelu_parts(u)
        act_ref[sl, :] = act.astype(BF16)
        du = mm(g_ref[sl, :], wd, NT) * slope
        part = jnp.sum(du, axis=0, keepdims=True)
        bias_sum = part if bias_sum is None else bias_sum + part
        du_ref[sl, :] = du.astype(BF16)
        acc_ref[sl, :] += mm(act_ref[sl, :], wd)
        dh_ref[sl, :] += mm(du_ref[sl, :], wu, NT)
    dbu_ref[...] = bias_sum
    dwu_ref[...] = mm(ht_ref[...], du_ref[...]).astype(dwu_ref.dtype)
    dwd_ref[...] = mm(gt_ref[...], act_ref[...]).T.astype(dwd_ref.dtype)


def mlp(h, ht, g, gt, wu, bu, wd):
    rows, d = h.shape
    ff = wu.shape[1]
    one = pl.Buffered(1)
    whole = pl.BlockSpec((rows, d), lambda c: (0, 0), pipeline_mode=one)
    whole_t = pl.BlockSpec((d, rows), lambda c: (0, 0), pipeline_mode=one)
    return pl.pallas_call(
        mlp_body,
        grid=(ff // FC,),
        in_specs=[
            whole,
            whole_t,
            whole,
            whole_t,
            pl.BlockSpec((d, FC), lambda c: (0, c)),
            pl.BlockSpec((1, FC), lambda c: (0, c)),
            pl.BlockSpec((FC, d), lambda c: (c, 0)),
        ],
        out_specs=[
            whole,
            whole,
            pl.BlockSpec((d, FC), lambda c: (0, c)),
            pl.BlockSpec((FC, d), lambda c: (c, 0)),
            pl.BlockSpec((1, FC), lambda c: (0, c)),
        ],
        out_shape=[
            jax.ShapeDtypeStruct((rows, d), F32),
            jax.ShapeDtypeStruct((rows, d), F32),
            jax.ShapeDtypeStruct((d, ff), BF16),
            jax.ShapeDtypeStruct((ff, d), BF16),
            jax.ShapeDtypeStruct((1, ff), F32),
        ],
        scratch_shapes=[pltpu.VMEM((rows, FC), BF16), pltpu.VMEM((rows, FC), BF16)],
        compiler_params=params(),
        name="mlp",
        cost_estimate=pl.CostEstimate(
            flops=12 * rows * d * ff, bytes_accessed=rows * d * 20 + 8 * d * ff, transcendentals=3 * rows * ff
        ),
    )(h, ht, g, gt, wu, bu, wd)


def fold(ref, step, value):
    part = jnp.sum(value, axis=0, keepdims=True)

    @pl.when(step == 0)
    def _():
        ref[...] = part

    @pl.when(step != 0)
    def _():
        ref[...] += part


def norm_pull(grad, n, inv, gain):
    dn = grad * gain
    plain = jnp.mean(dn, axis=-1, keepdims=True)
    cross = jnp.mean(dn * n, axis=-1, keepdims=True)
    return inv * (dn - plain - n * cross)


def mid_body(resid_ref, acc_ref, dh_ref, g_ref, mixed_ref, w_ref, bias_ref, gain_ref,
             y_ref, dr_ref, dm_ref, dw_ref, dgain_ref, dshift_ref, dob_ref, ddb_ref, sum_ref):
    step = pl.program_id(0)
    resid = resid_ref[...]
    y_ref[...] = (resid + acc_ref[...] + bias_ref[...]).astype(BF16)
    g = g_ref[...].astype(F32)
    n, inv = norm_stats(resid)
    dh = dh_ref[...]
    fold(dgain_ref, step, dh * n)
    fold(dshift_ref, step, dh)
    fold(ddb_ref, step, g)
    dr = g + norm_pull(dh, n, inv, gain_ref[...])
    dr_ref[...] = dr
    fold(dob_ref, step, dr)
    low = dr.astype(BF16)
    dm_ref[...] = mm(low, w_ref[...], NT).astype(BF16)
    dw = mm(mixed_ref[...].T, low)

    @pl.when(step == 0)
    def _():
        sum_ref[...] = dw

    @pl.when(step != 0)
    def _():
        sum_ref[...] += dw

    @pl.when(step == pl.num_programs(0) - 1)
    def _():
        dw_ref[...] = sum_ref[...].astype(dw_ref.dtype)


def middle(resid, acc, dh, g, mixed, w, bias, gain):
    rows, d = resid.shape
    tile = 512
    blk = pl.BlockSpec((tile, d), lambda i: (i, 0))
    row = pl.BlockSpec((1, d), lambda i: (0, 0))
    mat = pl.BlockSpec((d, d), lambda i: (0, 0))
    vec = jax.ShapeDtypeStruct((1, d), F32)
    return pl.pallas_call(
        mid_body,
        grid=(rows // tile,),
        in_specs=[blk, blk, blk, blk, blk, mat, row, row],
        out_specs=[blk, blk, blk, mat, row, row, row, row],
        out_shape=[
            jax.ShapeDtypeStruct((rows, d), BF16),
            jax.ShapeDtypeStruct((rows, d), F32),
            jax.ShapeDtypeStruct((rows, d), BF16),
            jax.ShapeDtypeStruct((d, d), BF16),
            vec,
            vec,
            vec,
            vec,
        ],
        scratch_shapes=[pltpu.VMEM((d, d), F32)],
        compiler_params=params(),
        name="middle",
        cost_estimate=pl.CostEstimate(
            flops=4 * rows * d * d, bytes_accessed=rows * d * 24, transcendentals=0
        ),
    )(resid, acc, dh, g, mixed, w, bias, gain)


def last_body(x_ref, dr_ref, dq_ref, dk_ref, dv_ref, w_ref, gain_ref, shift_ref,
              dx_ref, dw_ref, dgain_ref, dshift_ref, dqb_ref, dvb_ref, sum_ref):
    step = pl.program_id(0)
    d = x_ref.shape[1]
    n, inv = norm_stats(x_ref[...].astype(F32))
    h_t = (n * gain_ref[...] + shift_ref[...]).astype(BF16).T
    dh = None
    for j, ref in enumerate((dq_ref, dk_ref, dv_ref)):
        cols = pl.ds(j * d, d)
        part = ref[...]
        term = mm(part, w_ref[:, cols], NT)
        dh = term if dh is None else dh + term
        dw = mm(h_t, part)

        @pl.when(step == 0)
        def _():
            sum_ref[:, cols] = dw

        @pl.when(step != 0)
        def _():
            sum_ref[:, cols] += dw

    fold(dqb_ref, step, dq_ref[...].astype(F32))
    fold(dvb_ref, step, dv_ref[...].astype(F32))
    fold(dgain_ref, step, dh * n)
    fold(dshift_ref, step, dh)
    dx_ref[...] = (dr_ref[...] + norm_pull(dh, n, inv, gain_ref[...])).astype(BF16)

    @pl.when(step == pl.num_programs(0) - 1)
    def _():
        dw_ref[...] = sum_ref[...].astype(dw_ref.dtype)


def last(x, dr, dq, dk, dv, w, gain, shift):
    rows, d = x.shape
    tile = 512
    blk = pl.BlockSpec((tile, d), lambda i: (i, 0))
    row = pl.BlockSpec((1, d), lambda i: (0, 0))
    mat = pl.BlockSpec((d, 3 * d), lambda i: (0, 0))
    vec = jax.ShapeDtypeStruct((1, d), F32)
    return pl.pallas_call(
        last_body,
        grid=(rows // tile,),
        in_specs=[blk, blk, blk, blk, blk, mat, row, row],
        out_specs=[blk, mat, row, row, row, row],
        out_shape=[
            jax.ShapeDtypeStruct((rows, d), BF16),
            jax.ShapeDtypeStruct((d, 3 * d), BF16),
            vec,
            vec,
            vec,
            vec,
        ],
        scratch_shapes=[pltpu.VMEM((d, 3 * d), F32)],
        compiler_params=params(),
        name="last",
        cost_estimate=pl.CostEstimate(
            flops=12 * rows * d * d, bytes_accessed=rows * d * 14, transcendentals=0
        ),
    )(x, dr, dq, dk, dv, w, gain, shift)


def on_device(tokens, cotangent, segment_ids, *shards):
    gather = lambda s: lax.all_gather(s, "fsdp", axis=0, tiled=True)
    n = lax.axis_size("fsdp")
    near = n == 16 and lax.axis_size("dp") == 2
    triple_s, out_s, up_s, down_s = (s for s in shards if s.ndim == 2)
    vectors = [s for s in shards if s.ndim == 1]
    lane = jnp.concatenate(vectors)
    if near:
        tall = jnp.pad(lane, (0, 2048 - lane.shape[0])).reshape(16, 128)
        triple_weight, packed = first_gather(triple_s, tall)
        packed = packed.reshape(n, 2048)
    else:
        triple_weight = gather(triple_s)
        packed = gather(lane.reshape(1, -1))
    values = []
    at = 0
    for v in vectors:
        values.append(packed[:, at : at + v.shape[0]].astype(F32).reshape(1, -1))
        at += v.shape[0]
    (first_gain, first_shift, query_bias, value_bias, out_bias, second_gain, second_shift, up_bias, down_bias) = values

    rows, d = tokens.shape
    bias = jnp.concatenate([query_bias, jnp.zeros((1, d), F32), value_bias], axis=1)
    scale = jnp.concatenate([jnp.full((1, d), 0.125, F32), jnp.ones((1, 2 * d), F32)], axis=1)
    segc = segment_ids.reshape(rows, 1)
    segr = segment_ids.reshape(rows // ROWS, 1, ROWS)
    qkv = project(tokens, first_gain, first_shift, triple_weight, bias, scale)
    if near:
        mixed, soft, out_weight, up_weight, down_weight = attend(qkv, segc, segr, (out_s, up_s, down_s))
    else:
        mixed, soft = attend(qkv, segc, segr)
        out_weight, up_weight, down_weight = gather(out_s), gather(up_s), gather(down_s)
    resid, h = out_project(tokens, mixed, out_weight, out_bias, second_gain, second_shift)
    acc, dh, dwu, dwd, dbu = mlp(h, h.T, cotangent, cotangent.T, up_weight, up_bias, down_weight)
    y, dr, dm, dwo, dg2, ds2, dob, ddb = middle(resid, acc, dh, cotangent, mixed, out_weight, down_bias, second_gain)
    if near:
        dq, dk, dv, out_grad, up_grad, down_grad = attend_back(qkv, soft, mixed, dm, (dwo, dwu, dwd))
    else:
        dq, dk, dv = attend_back(qkv, soft, mixed, dm)
    dx, dwt, dg1, ds1, dqb, dvb = last(tokens, dr, dq, dk, dv, triple_weight, first_gain, first_shift)

    small = jnp.concatenate([p.reshape(n, -1) for p in (dg1, ds1, dqb, dvb, dob, dg2, ds2, dbu, ddb)], axis=1)
    if near:
        tall = jnp.pad(small, ((0, 0), (0, 1024 - small.shape[1]))).reshape(n * 8, 128)
        triple_grad, small = last_reduce(dwt, tall)
        small = small.reshape(-1)
    else:
        small = lax.psum_scatter(small, "fsdp", scatter_dimension=0, tiled=True).reshape(-1)
        small = lax.psum(small, "dp")
        total = lambda p: lax.psum(lax.psum_scatter(p, "fsdp", scatter_dimension=0, tiled=True), "dp").astype(F32)
        triple_grad, out_grad, up_grad, down_grad = total(dwt), total(dwo), total(dwu), total(dwd)
    matrices = iter((triple_grad, out_grad, up_grad, down_grad))
    grads = []
    at = 0
    for s in shards:
        if s.ndim == 1:
            grads.append(small[at : at + s.shape[0]])
            at += s.shape[0]
        else:
            grads.append(next(matrices))
    return (y, dx, *grads)


def solution(mesh):
    tok = P(("dp", "fsdp"), None)
    vec = P("fsdp")
    mat = P("fsdp", None)
    weights = (vec, vec, mat, vec, vec, mat, vec, vec, vec, mat, vec, mat, vec)
    return jax.shard_map(
        on_device,
        mesh=mesh,
        in_specs=(tok, tok, P(("dp", "fsdp")), *weights),
        out_specs=(tok, tok, *weights),
        check_vma=False,
    )
```

```python
import functools

import jax
import jax.numpy as jnp
from jax import lax
from jax.experimental import pallas as pl
from jax.experimental.pallas import tpu as pltpu
from jax.sharding import PartitionSpec as P

H = 12
HD = 64
ROWS = 1024
EPS = 1e-06
F32 = jnp.float32
BF16 = jnp.bfloat16
VMEM_LIMIT = 60 * 1024 * 1024

ROOT_HALF = 0.7071067811865476
ROOT_INV_TWO_PI = 0.3989422804014327

NN = (((1,), (0,)), ((), ()))
NT = (((1,), (1,)), ((), ()))


def mm(a, b, dims=NN):
    return lax.dot_general(a, b, dims, preferred_element_type=F32)


def params(**kw):
    return pltpu.CompilerParams(vmem_limit_bytes=VMEM_LIMIT, **kw)


def norm_stats(x):
    mean = jnp.mean(x, axis=-1, keepdims=True)
    cen = x - mean
    var = jnp.mean(cen * cen, axis=-1, keepdims=True)
    inv = lax.rsqrt(var + EPS)
    return cen * inv, inv


MESH = pl.DeviceIdType.MESH
ANY = pl.BlockSpec(memory_space=pl.ANY)


def whereabouts():
    y = lax.axis_index("dp")
    f = lax.axis_index("fsdp")
    return y, f // 4, (f // 2) % 2, f % 2


def spot(z, x, c):
    return z * 4 + x * 2 + c


def greet():
    y, z, x, c = whereabouts()
    barrier = pltpu.get_barrier_semaphore()
    peers = [(1 - y, spot(z, x, c)), (y, spot(z, 1 - x, c)), (y, spot(z, x, 1 - c))]
    peers += [(y, spot((z + d) % 4, x, c)) for d in (1, 2, 3)]
    for peer in peers:
        pl.semaphore_signal(barrier, inc=1, device_id=peer, device_id_type=MESH)
    pl.semaphore_wait(barrier, len(peers))


class Mover:
    def __init__(self, send, recv, local, per):
        self.send, self.recv, self.local, self.per = send, recv, local, per
        self.y, self.z, self.x, self.c = whereabouts()

    def wide(self, r, split, y):
        return pl.ds(pl.multiple_of(y * (r // 3), 8), 2 * (r // 3)) if split else pl.ds(0, r)

    def thin(self, r, y):
        return pl.ds(pl.multiple_of(y * 2 * (r // 3), 8), r // 3)

    def copy(self, u, slot, src, dst, z=None, x=None, c=None, y=None):
        i = u * self.per + slot
        pick = lambda v, own: own if v is None else v
        peer = (pick(y, self.y), spot(pick(z, self.z), pick(x, self.x), pick(c, self.c)))
        return pltpu.make_async_remote_copy(
            src_ref=src, dst_ref=dst, send_sem=self.send.at[i], recv_sem=self.recv.at[i],
            device_id=peer, device_id_type=MESH,
        )


class Gather(Mover):
    def __init__(self, units, send, recv, local):
        super().__init__(send, recv, local, 6)
        self.units = units

    def mine(self, u):
        src, _, _, col, n, split = self.units[u]
        return src.at[self.wide(src.shape[0], split, self.y), pl.ds(col, n)]

    def held(self, u):
        src, _, hold, col, n, split = self.units[u]
        return hold.at[self.wide(src.shape[0], split, self.y), pl.ds(col, n)]

    def part(self, u, z, x, c, rows):
        _, dst, _, col, n, _ = self.units[u]
        every = slice(None)
        pick = lambda v: every if v is None else v
        return dst.at[pick(z), pick(x), pick(c), rows, pl.ds(col, n)]

    def broad(self, u):
        src, _, _, _, _, split = self.units[u]
        return self.wide(src.shape[0], split, self.y)

    def load(self, u):
        return pltpu.make_async_copy(self.mine(u), self.held(u), self.local.at[2 * u])

    def store(self, u):
        dst = self.part(u, self.z, self.x, self.c, self.broad(u))
        return pltpu.make_async_copy(self.held(u), dst, self.local.at[2 * u + 1])

    def along_z(self, u, d, out=True):
        here, there = (self.z + 4 - d) % 4, (self.z + d) % 4
        dst = self.part(u, self.z if out else here, self.x, self.c, self.broad(u))
        return self.copy(u, d - 1, self.mine(u), dst, z=there)

    def along_x(self, u, out=True):
        src = self.part(u, None, self.x, self.c, self.broad(u))
        dst = src if out else self.part(u, None, 1 - self.x, self.c, self.broad(u))
        return self.copy(u, 3, src, dst, x=1 - self.x)

    def along_y(self, u, out=True):
        r = self.units[u][0].shape[0]
        src = self.part(u, None, None, self.c, self.thin(r, self.y))
        dst = src if out else self.part(u, None, None, self.c, self.thin(r, 1 - self.y))
        return self.copy(u, 4, src, dst, y=1 - self.y)

    def along_c(self, u, out=True):
        every = pl.ds(0, self.units[u][0].shape[0])
        src = self.part(u, None, None, self.c, every)
        dst = src if out else self.part(u, None, None, 1 - self.c, every)
        return self.copy(u, 5, src, dst, c=1 - self.c)

    def stage(self, s, u):
        split = self.units[u][5]
        if s == 0:
            for d in (1, 2, 3):
                self.along_z(u, d).start()
            self.load(u).start()
        if s == 1:
            self.load(u).wait()
            self.store(u).start()
        if s == 2:
            self.store(u).wait()
            for d in (1, 2, 3):
                self.along_z(u, d, False).wait_recv()
            self.along_x(u).start()
        if s == 3:
            self.along_x(u, False).wait_recv()
            if split:
                self.along_y(u).start()
            else:
                self.along_c(u).start()
        if s == 4 and split:
            self.along_y(u, False).wait_recv()
            self.along_c(u).start()
        if s == 5:
            self.along_c(u, False).wait_recv()
            for d in (1, 2, 3):
                self.along_z(u, d).wait_send()
            self.along_x(u).wait_send()
            if split:
                self.along_y(u).wait_send()
            self.along_c(u).wait_send()


def gather_sems(units):
    return [
        pltpu.SemaphoreType.DMA((units * 6,)),
        pltpu.SemaphoreType.DMA((units * 6,)),
        pltpu.SemaphoreType.DMA((2 * units,)),
    ]


def whole(shard):
    return jax.ShapeDtypeStruct((4, 2, 2, *shard.shape), shard.dtype)


class Reduce(Mover):
    def __init__(self, units, send, recv, local):
        super().__init__(send, recv, local, 7)
        self.units = units

    def size(self, u):
        return self.units[u][0].shape[3]

    def partial(self, u, c):
        src, _, (col, _), n, _, _ = self.units[u]
        return src.at[:, :, c, :, pl.ds(col, n)]

    def load(self, u):
        return pltpu.make_async_copy(self.partial(u, self.c), self.units[u][5][0], self.local.at[u])

    def over_c(self, u):
        return self.copy(u, 0, self.partial(u, 1 - self.c), self.units[u][5][1], c=1 - self.c)

    def over_y(self, u):
        own, from_y = self.units[u][5][0], self.units[u][5][5]
        return self.copy(u, 1, own.at[:, :, self.thin(self.size(u), 1 - self.y), :], from_y, y=1 - self.y)

    def over_x(self, u):
        own, from_x = self.units[u][5][0], self.units[u][5][2]
        rows = self.wide(self.size(u), self.units[u][4], self.y)
        return self.copy(u, 2, own.at[:, 1 - self.x, rows, :], from_x, x=1 - self.x)

    def over_z(self, u, d):
        own, from_z = self.units[u][5][0], self.units[u][5][3]
        rows = self.wide(self.size(u), self.units[u][4], self.y)
        to = (self.z + d) % 4
        return self.copy(u, 2 + d, own.at[to, self.x, rows, :], from_z.at[d - 1], z=to)

    def over_last(self, u):
        last = self.units[u][5][4]
        return self.copy(u, 6, last.at[0], last.at[1], y=1 - self.y)

    def stage(self, s, u):
        _, out, (_, col), n, split, (own, from_c, from_x, from_z, last, *rest) = self.units[u]
        y, z, x = self.y, self.z, self.x
        r = self.size(u)
        rows = self.wide(r, split, y)
        if s == 0:
            self.over_c(u).start()
            self.load(u).start()
        if s == 1:
            self.load(u).wait()
            self.over_c(u).wait_recv()
            own[...] = own[...] + from_c[...]
            if split:
                self.over_y(u).start()
        if s == 2:
            if split:
                self.over_y(u).wait_recv()
                mine = self.thin(r, y)
                own[:, :, mine, :] = own[:, :, mine, :] + rest[0][...]
            self.over_x(u).start()
        if s == 3:
            self.over_x(u).wait_recv()
            for k in range(4):
                own[k, x, rows, :] = own[k, x, rows, :] + from_x[k]
            for d in (1, 2, 3):
                self.over_z(u, d).start()
        if s == 4:
            total = own[z, x, rows, :].astype(F32)
            for d in (1, 2, 3):
                self.over_z(u, d).wait_recv()
                total = total + from_z[d - 1].astype(F32)
            last[0] = total.astype(last.dtype)
            self.over_last(u).start()
        if s == 5:
            self.over_last(u).wait_recv()
            cols = pl.ds(col, n)
            if split:
                t = r // 3
                at = lambda k: pl.ds(pl.multiple_of(k * t, 8), t)
                put = lambda k, v: out.__setitem__((at(k), cols), v.astype(F32))
                put(1, last[0, at(1 - y), :].astype(F32) + last[1, at(y), :].astype(F32))
                put(2 * y, last[0, at(y), :])
                put(2 * (1 - y), last[1, at(1 - y), :])
            else:
                out[:, cols] = last[0].astype(F32) + last[1].astype(F32)
        if s == 6:
            self.over_c(u).wait_send()
            if split:
                self.over_y(u).wait_send()
            self.over_x(u).wait_send()
            for d in (1, 2, 3):
                self.over_z(u, d).wait_send()
            self.over_last(u).wait_send()


def reduce_buffers(r, n, dtype, split):
    wide = 2 * r // 3 if split else r
    shapes = [(4, 2, r, n), (4, 2, r, n), (4, wide, n), (3, wide, n), (2, wide, n)]
    if split:
        shapes.append((4, 2, r // 3, n))
    return [pltpu.VMEM(shape, dtype) for shape in shapes]


def reduce_scratch(plan):
    flat = []
    for p in plan:
        flat += reduce_buffers(*p)
    units = len(plan)
    return flat + [
        pltpu.SemaphoreType.DMA((units * 7,)),
        pltpu.SemaphoreType.DMA((units * 7,)),
        pltpu.SemaphoreType.DMA((units,)),
    ]


def reduce_work(plan, places, scratch):
    units = []
    at = 0
    for (_, n, _, split), (src, out, col) in zip(plan, places):
        count = 6 if split else 5
        units.append((src, out, col, n, split, scratch[at : at + count]))
        at += count
    return Reduce(units, *scratch[at:])


def at_hook(hook, moves, work):
    for u, hooks in enumerate(moves):
        for s, when in enumerate(hooks):
            if when == hook:
                work.stage(s, u)


def hooked(step, per_step, which, steps, moves, work):
    for k in range(steps):
        if any(k * per_step + which in hooks for hooks in moves):

            @pl.when(step == k)
            def _():
                if k == 0 and which == 0:
                    greet()
                at_hook(k * per_step + which, moves, work)


def unpack(vec_ref, ub_ref, tall_ref):
    d = vec_ref.shape[1] // 16
    f = ub_ref.shape[1] // 16
    for i in range(16):
        tile = tall_ref[i // 4, (i // 2) % 2, i % 2].astype(F32)
        vec_ref[:, i * d : (i + 1) * d] = tile[0:8, 0:d]
        ub_ref[:, i * f : i * f + 128] = tile[8:9, 0:128]
        ub_ref[:, i * f + 128 : (i + 1) * f] = tile[9:10, 0 : f - 128]


def first_gather_body(t_ref, v_ref, tf_ref, vec_ref, ub_ref, tall_ref, th_ref, vh_ref, *sems):
    n = t_ref.shape[1] // 6
    units = [(v_ref, tall_ref, vh_ref, 0, v_ref.shape[1], False)]
    units += [(t_ref, tf_ref, th_ref, j * n, n, True) for j in range(6)]
    greet()
    work = Gather(units, *sems)
    for u in range(len(units)):
        work.stage(0, u)
    for k in range(len(units) + 4):
        for s in range(1, 6):
            if 0 <= k - s + 1 < len(units):
                work.stage(s, k - s + 1)
    unpack(vec_ref, ub_ref, tall_ref)


def first_gather(triple, tall):
    d = triple.shape[0] * 16
    vmem = pl.BlockSpec(memory_space=pltpu.VMEM)
    return pl.pallas_call(
        first_gather_body,
        in_specs=[ANY, vmem],
        out_specs=[ANY, vmem, vmem],
        out_shape=[
            whole(triple),
            jax.ShapeDtypeStruct((8, d), F32),
            jax.ShapeDtypeStruct((1, 4 * d), F32),
        ],
        scratch_shapes=[
            pltpu.VMEM((4, 2, 2, *tall.shape), BF16),
            pltpu.VMEM(triple.shape, BF16),
            pltpu.VMEM(tall.shape, BF16),
            *gather_sems(7),
        ],
        compiler_params=params(collective_id=0, has_side_effects=True),
        name="first_gather",
    )(triple, tall)


def proj_body(x_ref, vec_ref, w_ref, qkv_ref, ht_ref):
    d = x_ref.shape[1]
    n, _ = norm_stats(x_ref[...].astype(F32))
    h = (n * vec_ref[0:1, :] + vec_ref[1:2, :]).astype(BF16)
    ht_ref[...] = h.T
    for j in range(3):
        cols = pl.ds(j * d, d)
        p = mm(h, w_ref[:, cols])
        if j == 0:
            p = (p + vec_ref[2:3, :]) * 0.125
        if j == 2:
            p = p + vec_ref[3:4, :]
        qkv_ref[:, cols] = p.astype(BF16)


def project(x, vec, w):
    rows, d = x.shape
    cols = w.shape[1]
    tile = 512
    return pl.pallas_call(
        proj_body,
        grid=(rows // tile,),
        in_specs=[
            pl.BlockSpec((tile, d), lambda i: (i, 0)),
            pl.BlockSpec((8, d), lambda i: (0, 0)),
            pl.BlockSpec((d, cols), lambda i: (0, 0)),
        ],
        out_specs=[
            pl.BlockSpec((tile, cols), lambda i: (i, 0)),
            pl.BlockSpec((d, tile), lambda i: (0, i)),
        ],
        out_shape=[jax.ShapeDtypeStruct((rows, cols), BF16), jax.ShapeDtypeStruct((d, rows), BF16)],
        compiler_params=params(),
        name="project",
        cost_estimate=pl.CostEstimate(
            flops=2 * rows * d * cols, bytes_accessed=2 * rows * (d + cols), transcendentals=0
        ),
    )(x, vec, w)


QT = 256


def half_mask(value, hh):
    lane = lax.broadcasted_iota(jnp.int32, value.shape, 1)
    keep = lane < HD if hh == 0 else lane >= HD
    return jnp.where(keep, value, jnp.zeros_like(value))


def unit_list(widths):
    units = [(0, 0, widths[0])]
    for i, w in enumerate(widths[1:]):
        units += [(i + 1, j * (w // 6), w // 6) for j in range(6)]
    return units


def attend_body(hosting, *refs):
    q_ref, k_ref, v_ref, seg_ref = refs[:4]
    if hosting:
        shards = refs[4:7]
        o_ref, p_ref = refs[7:9]
        full = refs[9:12]
        bias_ref = refs[12]
        hold = refs[13:16]
        units = [(shards[i], full[i], hold[i], col, n, True) for i, col, n in unit_list([s.shape[1] for s in shards])]
        work = Gather(units, *refs[16:])
        moves = [[u, u + 1, u + 2, u + 4, u + 6, u + 8] for u in range(len(units))]
    else:
        o_ref, p_ref, bias_ref = refs[4:]
    step = pl.program_id(0) * pl.num_programs(1) + pl.program_id(1)
    rows = q_ref.shape[0]

    @pl.when(pl.program_id(1) == 0)
    def _():
        seg = seg_ref[...].astype(F32)
        column = jnp.broadcast_to(seg, (8, rows)).T[:, 0:1]
        bias_ref[...] = jnp.where(column == seg, 0.0, -1e30)

    tiles = rows // QT
    for t in range(tiles):
        if hosting and t % (tiles // 2) == 0:
            hooked(step, 2, t // (tiles // 2), 12, moves, work)
        k = k_ref[...]
        v = v_ref[...]
        sl = pl.ds(t * QT, QT)
        out = None
        for hh in range(2):
            q = half_mask(q_ref[sl, :], hh)
            s = mm(q, k, NT) + bias_ref[sl, :]
            peak = jnp.max(s, axis=-1, keepdims=True)
            e = jnp.exp(s - peak)
            total = jnp.sum(e, axis=-1, keepdims=True)
            p = (e * (1.0 / total)).astype(BF16)
            p_ref[hh, sl, :] = p
            o = mm(p, v)
            if hh == 0:
                out = o
            else:
                lane = lax.broadcasted_iota(jnp.int32, o.shape, 1)
                out = jnp.where(lane < HD, out, o)
        o_ref[sl, :] = out.astype(BF16)


def attend(qkv, segr, shards=()):
    rows = qkv.shape[0]
    d = qkv.shape[1] // 3
    mb = rows // ROWS
    pairs = d // 128
    extra = dict(collective_id=1, has_side_effects=True) if shards else {}
    return pl.pallas_call(
        functools.partial(attend_body, bool(shards)),
        grid=(mb, pairs),
        in_specs=[
            pl.BlockSpec((ROWS, 128), lambda m, h: (m, h)),
            pl.BlockSpec((ROWS, 128), lambda m, h: (m, pairs + h)),
            pl.BlockSpec((ROWS, 128), lambda m, h: (m, 2 * pairs + h)),
            pl.BlockSpec((None, 1, ROWS), lambda m, h: (m, 0, 0)),
            *[ANY for _ in shards],
        ],
        out_specs=[
            pl.BlockSpec((ROWS, 128), lambda m, h: (m, h)),
            pl.BlockSpec((None, 2, ROWS, ROWS), lambda m, h: (m, h, 0, 0)),
            *[ANY for _ in shards],
        ],
        out_shape=[
            jax.ShapeDtypeStruct((rows, d), BF16),
            jax.ShapeDtypeStruct((mb, 2 * pairs, ROWS, ROWS), BF16),
            *[whole(s) for s in shards],
        ],
        scratch_shapes=[pltpu.VMEM((ROWS, ROWS), F32)]
        + ([pltpu.VMEM(s.shape, s.dtype) for s in shards] + gather_sems(13) if shards else []),
        compiler_params=params(**extra),
        name="attend",
        cost_estimate=pl.CostEstimate(
            flops=mb * pairs * 2 * 4 * ROWS * ROWS * 256,
            bytes_accessed=mb * pairs * 2 * ROWS * ROWS * 2,
            transcendentals=mb * pairs * 2 * ROWS * ROWS,
        ),
    )(qkv, qkv, qkv, segr, *shards)


def attend_back_body(plan, *refs):
    q_ref, k_ref, v_ref, p_ref, o_ref, g_ref = refs[:6]
    hosting = plan is not None
    if hosting:
        parts = refs[6:9]
        d_ref = refs[9]
        results = refs[10:13]
        ds_ref = refs[13]
        places = [(parts[i], results[i], (col, col)) for i, col, _ in unit_list([p.shape[4] for p in parts])]
        work = reduce_work(plan, places, refs[14:])
        moves = [[u, u + 1, u + 3, u + 5, u + 7, u + 9, u + 10] for u in range(len(places))]
    else:
        d_ref, ds_ref = refs[6:]
    step = pl.program_id(0) * pl.num_programs(1) + pl.program_id(1)
    rows = q_ref.shape[0]
    prod = None
    dk_parts = []
    dv_parts = []
    dq_parts = []
    for hh in range(2):
        if hosting:
            hooked(step, 2, hh, 12, moves, work)
        k = k_ref[...]
        v = v_ref[...]
        half = slice(hh * HD, (hh + 1) * HD)
        prod = g_ref[...].astype(F32) * o_ref[...].astype(F32)
        center = jnp.sum(half_mask(prod, hh), axis=-1, keepdims=True)
        for t in range(rows // QT):
            sl = pl.ds(t * QT, QT)
            ts = slice(t * QT, (t + 1) * QT)
            d_soft = mm(half_mask(g_ref[sl, :], hh), v, NT)
            ds = p_ref[hh, sl, :].astype(F32) * (d_soft - center[ts, :])
            ds_ref[hh, sl, :] = ds.astype(BF16)
        dv_parts.append(mm(g_ref[...].T[half, :], p_ref[hh]))
        dk_parts.append(mm(q_ref[...].T[half, :], ds_ref[hh]))
        dq_parts.append(mm(ds_ref[hh], k))
    lane = lax.broadcasted_iota(jnp.int32, dq_parts[0].shape, 1)
    d_ref[0] = (jnp.where(lane < HD, dq_parts[0], dq_parts[1]) * 0.125).astype(BF16)
    d_ref[1] = jnp.concatenate(dk_parts, axis=0).T.astype(BF16)
    d_ref[2] = jnp.concatenate(dv_parts, axis=0).T.astype(BF16)


def attend_back(qkv, soft, mixed, d_mixed, grads=()):
    rows = qkv.shape[0]
    d = qkv.shape[1] // 3
    mb = rows // ROWS
    pairs = d // 128
    blk = pl.BlockSpec((ROWS, 128), lambda m, h: (m, h))
    plan = None
    results = []
    extra = {}
    grads = [g.reshape(4, 2, 2, g.shape[0] // 16, g.shape[1]) for g in grads]
    if grads:
        plan = [(grads[i].shape[3], n, BF16, True) for i, _, n in unit_list([g.shape[4] for g in grads])]
        results = [jax.ShapeDtypeStruct(g.shape[3:], F32) for g in grads]
        extra = dict(collective_id=2, has_side_effects=True)
    return pl.pallas_call(
        functools.partial(attend_back_body, plan),
        grid=(mb, pairs),
        in_specs=[
            blk,
            pl.BlockSpec((ROWS, 128), lambda m, h: (m, pairs + h)),
            pl.BlockSpec((ROWS, 128), lambda m, h: (m, 2 * pairs + h)),
            pl.BlockSpec((None, 2, ROWS, ROWS), lambda m, h: (m, h, 0, 0)),
            blk,
            blk,
            *[ANY for _ in grads],
        ],
        out_specs=[
            pl.BlockSpec((3, ROWS, 128), lambda m, h: (0, m, h)),
            *[pl.BlockSpec(r.shape, lambda m, h: (0, 0)) for r in results],
        ],
        out_shape=[jax.ShapeDtypeStruct((3, rows, d), BF16), *results],
        scratch_shapes=[pltpu.VMEM((2, ROWS, ROWS), BF16)] + (reduce_scratch(plan) if grads else []),
        compiler_params=params(**extra),
        name="attend_back",
        cost_estimate=pl.CostEstimate(
            flops=mb * pairs * 2 * 8 * ROWS * ROWS * 256,
            bytes_accessed=mb * pairs * 2 * ROWS * ROWS * 2,
            transcendentals=0,
        ),
    )(qkv, qkv, qkv, soft, mixed, d_mixed, *grads)


def out_body(x_ref, m_ref, w_ref, vec_ref, resid_ref, h_ref, ht_ref):
    resid = x_ref[...].astype(F32) + mm(m_ref[...], w_ref[...]) + vec_ref[4:5, :]
    resid_ref[...] = resid
    n, _ = norm_stats(resid)
    h = (n * vec_ref[5:6, :] + vec_ref[6:7, :]).astype(BF16)
    h_ref[...] = h
    ht_ref[...] = h.T


def out_project(x, mixed, w, vec):
    rows, d = x.shape
    tile = 512
    blk = pl.BlockSpec((tile, d), lambda i: (i, 0))
    return pl.pallas_call(
        out_body,
        grid=(rows // tile,),
        in_specs=[blk, blk, pl.BlockSpec((d, d), lambda i: (0, 0)), pl.BlockSpec((8, d), lambda i: (0, 0))],
        out_specs=[blk, blk, pl.BlockSpec((d, tile), lambda i: (0, i))],
        out_shape=[
            jax.ShapeDtypeStruct((rows, d), F32),
            jax.ShapeDtypeStruct((rows, d), BF16),
            jax.ShapeDtypeStruct((d, rows), BF16),
        ],
        compiler_params=params(),
        name="out_project",
        cost_estimate=pl.CostEstimate(
            flops=2 * rows * d * d, bytes_accessed=rows * d * 12, transcendentals=0
        ),
    )(x, mixed, w, vec)


FC = 512
RT = 512


def gelu_parts(u):
    cdf = 0.5 * (1.0 + lax.erf(u * ROOT_HALF))
    bell = jnp.exp(-0.5 * u * u) * ROOT_INV_TWO_PI
    return u * cdf, cdf + u * bell


def mlp_body(h_ref, ht_ref, g_ref, gt_ref, wu_ref, bu_ref, wd_ref, acc_ref, dh_ref, dwu_ref, dwd_ref, dbu_ref,
             act_ref, du_ref):
    rows = h_ref.shape[0]

    @pl.when(pl.program_id(0) == 0)
    def _():
        acc_ref[...] = jnp.zeros_like(acc_ref)
        dh_ref[...] = jnp.zeros_like(dh_ref)

    wu = wu_ref[...]
    wd = wd_ref[...]
    bias_sum = None
    for t in range(rows // RT):
        sl = pl.ds(t * RT, RT)
        u = mm(h_ref[sl, :], wu) + bu_ref[...]
        act, slope = gelu_parts(u)
        act_ref[sl, :] = act.astype(BF16)
        du = mm(g_ref[sl, :], wd, NT) * slope
        part = jnp.sum(du, axis=0, keepdims=True)
        bias_sum = part if bias_sum is None else bias_sum + part
        du_ref[sl, :] = du.astype(BF16)
        acc_ref[sl, :] += mm(act_ref[sl, :], wd)
        dh_ref[sl, :] += mm(du_ref[sl, :], wu, NT)
    dbu_ref[...] = bias_sum
    dwu_ref[...] = mm(ht_ref[...], du_ref[...]).astype(dwu_ref.dtype)
    dwd_ref[...] = mm(gt_ref[...], act_ref[...]).T.astype(dwd_ref.dtype)


def mlp(h, ht, g, gt, wu, bu, wd):
    rows, d = h.shape
    ff = wu.shape[1]
    one = pl.Buffered(1)
    whole = pl.BlockSpec((rows, d), lambda c: (0, 0), pipeline_mode=one)
    whole_t = pl.BlockSpec((d, rows), lambda c: (0, 0), pipeline_mode=one)
    return pl.pallas_call(
        mlp_body,
        grid=(ff // FC,),
        in_specs=[
            whole,
            whole_t,
            whole,
            whole_t,
            pl.BlockSpec((d, FC), lambda c: (0, c)),
            pl.BlockSpec((1, FC), lambda c: (0, c)),
            pl.BlockSpec((FC, d), lambda c: (c, 0)),
        ],
        out_specs=[
            whole,
            whole,
            pl.BlockSpec((d, FC), lambda c: (0, c)),
            pl.BlockSpec((FC, d), lambda c: (c, 0)),
            pl.BlockSpec((1, FC), lambda c: (0, c)),
        ],
        out_shape=[
            jax.ShapeDtypeStruct((rows, d), F32),
            jax.ShapeDtypeStruct((rows, d), F32),
            jax.ShapeDtypeStruct((d, ff), BF16),
            jax.ShapeDtypeStruct((ff, d), BF16),
            jax.ShapeDtypeStruct((1, ff), F32),
        ],
        scratch_shapes=[pltpu.VMEM((rows, FC), BF16), pltpu.VMEM((rows, FC), BF16)],
        compiler_params=params(),
        name="mlp",
        cost_estimate=pl.CostEstimate(
            flops=12 * rows * d * ff, bytes_accessed=rows * d * 20 + 8 * d * ff, transcendentals=3 * rows * ff
        ),
    )(h, ht, g, gt, wu, bu, wd)


def fold(ref, row, step, value):
    part = jnp.sum(value, axis=0, keepdims=True)

    @pl.when(step == 0)
    def _():
        ref[row : row + 1, :] = part

    @pl.when(step != 0)
    def _():
        ref[row : row + 1, :] += part


def norm_pull(grad, n, inv, gain):
    dn = grad * gain
    plain = jnp.mean(dn, axis=-1, keepdims=True)
    cross = jnp.mean(dn * n, axis=-1, keepdims=True)
    return inv * (dn - plain - n * cross)


def mid_body(resid_ref, acc_ref, dh_ref, g_ref, mixed_ref, w_ref, vec_ref,
             y_ref, dr_ref, dm_ref, dw_ref, dvec_ref, sum_ref):
    step = pl.program_id(0)
    resid = resid_ref[...]
    y_ref[...] = (resid + acc_ref[...] + vec_ref[7:8, :]).astype(BF16)
    g = g_ref[...].astype(F32)
    n, inv = norm_stats(resid)
    dh = dh_ref[...]
    dr = g + norm_pull(dh, n, inv, vec_ref[5:6, :])
    dr_ref[...] = dr
    fold(dvec_ref, 4, step, dr)
    fold(dvec_ref, 5, step, dh * n)
    fold(dvec_ref, 6, step, dh)
    fold(dvec_ref, 7, step, g)
    low = dr.astype(BF16)
    dm_ref[...] = mm(low, w_ref[...], NT).astype(BF16)
    dw = mm(mixed_ref[...].T, low)

    @pl.when(step == 0)
    def _():
        sum_ref[...] = dw
        dvec_ref[0:4, :] = jnp.zeros((4, dvec_ref.shape[1]), F32)

    @pl.when(step != 0)
    def _():
        sum_ref[...] += dw

    @pl.when(step == pl.num_programs(0) - 1)
    def _():
        dw_ref[...] = sum_ref[...].astype(dw_ref.dtype)


def middle(resid, acc, dh, g, mixed, w, vec):
    rows, d = resid.shape
    tile = 512
    blk = pl.BlockSpec((tile, d), lambda i: (i, 0))
    mat = pl.BlockSpec((d, d), lambda i: (0, 0))
    eight = pl.BlockSpec((8, d), lambda i: (0, 0))
    return pl.pallas_call(
        mid_body,
        grid=(rows // tile,),
        in_specs=[blk, blk, blk, blk, blk, mat, eight],
        out_specs=[blk, blk, blk, mat, eight],
        out_shape=[
            jax.ShapeDtypeStruct((rows, d), BF16),
            jax.ShapeDtypeStruct((rows, d), F32),
            jax.ShapeDtypeStruct((rows, d), BF16),
            jax.ShapeDtypeStruct((d, d), BF16),
            jax.ShapeDtypeStruct((8, d), F32),
        ],
        scratch_shapes=[pltpu.VMEM((d, d), F32)],
        compiler_params=params(),
        name="middle",
        cost_estimate=pl.CostEstimate(
            flops=4 * rows * d * d, bytes_accessed=rows * d * 24, transcendentals=0
        ),
    )(resid, acc, dh, g, mixed, w, vec)


PHASES = 3
FINAL_TILE = 512


def finish_body(plan, plan_steps, ht_ref, part_ref, tile_ref, x_ref, dr_ref, w_hbm, vec_ref, dvec_ref, dbu_ref, dx_ref, *refs):
    step = pl.program_id(0)
    steps = pl.num_programs(0)
    d = x_ref.shape[1]
    if plan is None:
        dw_ref, sums_ref, w_ref, w_sem = refs
    else:
        out_ref, small_ref, w_ref, w_sem, sums_ref, grad_ref, tall_ref = refs[:7]
        places = [(grad_ref.at[j], out_ref, (0, j * d)) for j in range(PHASES)]
        places.append((tall_ref, small_ref, (0, 0)))
        work = reduce_work(plan, places, refs[7:])
        count = plan_steps
    fetch = pltpu.make_async_copy(w_hbm, w_ref, w_sem)

    @pl.when(step == 0)
    def _():
        if plan is not None:
            greet()
        fetch.start()
        sums_ref[...] = dvec_ref[...]

    @pl.when(step < PHASES)
    def _():
        part = part_ref[0]
        for j in range(d // 256):
            cols = pl.ds(j * 256, 256)
            dw = mm(ht_ref[...], part_ref[0, :, cols]).astype(BF16)
            if plan is None:
                dw_ref[:, cols] = dw
            else:
                grad_ref[step, :, :, :, :, cols] = dw.reshape(4, 2, 2, d // 16, 256)
        total = jnp.sum(part.astype(F32), axis=0, keepdims=True)

        @pl.when(step == 0)
        def _():
            sums_ref[2:3, :] = total

        @pl.when(step == 2)
        def _():
            sums_ref[3:4, :] = total

    @pl.when(step == PHASES)
    def _():
        fetch.wait()

    @pl.when(step >= PHASES)
    def _():
        n, inv = norm_stats(x_ref[...].astype(F32))
        dh = None
        for j in range(3):
            term = mm(tile_ref[j], w_ref[:, pl.ds(j * d, d)], NT)
            dh = term if dh is None else dh + term
        fold(sums_ref, 0, step - PHASES, dh * n)
        fold(sums_ref, 1, step - PHASES, dh)
        dx_ref[...] = (dr_ref[...] + norm_pull(dh, n, inv, vec_ref[0:1, :])).astype(BF16)

    if plan is not None:
        for k in range(count):

            @pl.when(step == k)
            def _():
                for u in range(PHASES):
                    s = k - u
                    if 0 <= s <= 6:
                        work.stage(s, u)
                if k == count - 1:
                    small = PHASES
                    pack(tall_ref, sums_ref, dbu_ref)
                    work.stage(0, small)
                    work.stage(1, small)
                    work.stage(2, small)
                    work.stage(5, 2)
                    work.stage(3, small)
                    work.stage(4, small)
                    work.stage(5, small)
                    for u in range(1, PHASES + 1):
                        work.stage(6, u)


def pack(tall_ref, sums_ref, dbu_ref):
    d = sums_ref.shape[1] // 16
    f = dbu_ref.shape[1] // 16
    for i in range(16):
        tile = tall_ref.at[i // 4, (i // 2) % 2, i % 2]
        tile[0:8, 0:d] = sums_ref[:, i * d : (i + 1) * d]
        tile[8:9, 0:128] = dbu_ref[:, i * f : i * f + 128]
        tile[9:10, 0 : f - 128] = dbu_ref[:, i * f + 128 : (i + 1) * f]


def finish(x, dr, ht, dqkv, w, vec, dvec, dbu, near):
    rows, d = x.shape
    tiles = rows // FINAL_TILE
    row = lambda s: jnp.maximum(s - PHASES, 0)
    one = pl.Buffered(1)
    eight = pl.BlockSpec((8, d), lambda s: (0, 0))
    if near:
        plan = [(d // 16, d, BF16, True)] * PHASES + [(16, 128, F32, False)]
        shapes = [jax.ShapeDtypeStruct((d // 16, 3 * d), F32), jax.ShapeDtypeStruct((16, 128), F32)]
        specs = [pl.BlockSpec(s.shape, lambda s: (0, 0)) for s in shapes]
        scratch = [
            pltpu.VMEM((8, d), F32),
            pltpu.VMEM((PHASES, 4, 2, 2, d // 16, d), BF16),
            pltpu.VMEM((4, 2, 2, 16, 128), F32),
        ] + reduce_scratch(plan)
        extra = dict(collective_id=3, has_side_effects=True)
    else:
        plan = None
        shapes = [jax.ShapeDtypeStruct((d, 3 * d), BF16), jax.ShapeDtypeStruct((8, d), F32)]
        specs = [pl.BlockSpec((d, d), lambda s: (0, jnp.minimum(s, PHASES - 1))), eight]
        scratch = []
        extra = {}
    return pl.pallas_call(
        functools.partial(finish_body, plan, PHASES + tiles),
        grid=(PHASES + tiles,),
        in_specs=[
            pl.BlockSpec((d, rows), lambda s: (0, 0), pipeline_mode=one),
            pl.BlockSpec((1, rows, d), lambda s: (jnp.minimum(s, PHASES - 1), 0, 0)),
            pl.BlockSpec((3, FINAL_TILE, d), lambda s: (0, row(s), 0)),
            pl.BlockSpec((FINAL_TILE, d), lambda s: (row(s), 0)),
            pl.BlockSpec((FINAL_TILE, d), lambda s: (row(s), 0)),
            ANY,
            eight,
            eight,
            pl.BlockSpec(dbu.shape, lambda s: (0, 0)),
        ],
        out_specs=[pl.BlockSpec((FINAL_TILE, d), lambda s: (row(s), 0)), *specs],
        out_shape=[jax.ShapeDtypeStruct((rows, d), BF16), *shapes],
        scratch_shapes=[pltpu.VMEM((d, 3 * d), BF16), pltpu.SemaphoreType.DMA(()), *scratch],
        compiler_params=params(**extra),
        name="finish",
        cost_estimate=pl.CostEstimate(
            flops=12 * rows * d * d, bytes_accessed=rows * d * 20, transcendentals=0
        ),
    )(ht, dqkv, dqkv, x, dr, w, vec, dvec, dbu)


def on_device(tokens, cotangent, segment_ids, *shards):
    gather = lambda s: lax.all_gather(s, "fsdp", axis=0, tiled=True)
    n = lax.axis_size("fsdp")
    near = n == 16 and lax.axis_size("dp") == 2
    triple_s, out_s, up_s, down_s = (s for s in shards if s.ndim == 2)
    rows, d = tokens.shape
    up_bias_s = shards[10]
    eights = [s for i, s in enumerate(shards) if s.ndim == 1 and i != 10]
    flat = lambda w: w.reshape(-1, w.shape[-1])
    if near:
        wide = [jnp.pad(v, (0, 128 - v.shape[0])) for v in eights]
        wide += [up_bias_s[:128], jnp.pad(up_bias_s[128:], (0, 256 - up_bias_s.shape[0]))]
        tall = jnp.pad(jnp.stack(wide), ((0, 6), (0, 0)))
        triple_weight, vec, up_bias = first_gather(triple_s, tall)
        triple_weight = flat(triple_weight)
    else:
        triple_weight = gather(triple_s)
        packed = gather(jnp.concatenate(eights + [up_bias_s]).reshape(1, -1)).astype(F32)
        m = eights[0].shape[0]
        vec = jnp.stack([packed[:, i * m : (i + 1) * m].reshape(-1) for i in range(8)])
        up_bias = packed[:, 8 * m :].reshape(1, -1)

    segr = segment_ids.reshape(rows // ROWS, 1, ROWS)
    qkv, first_t = project(tokens, vec, triple_weight)
    if near:
        mixed, soft, *full = attend(qkv, segr, (out_s, up_s, down_s))
        out_weight, up_weight, down_weight = (flat(w) for w in full)
    else:
        mixed, soft = attend(qkv, segr)
        out_weight, up_weight, down_weight = gather(out_s), gather(up_s), gather(down_s)
    resid, h, ht = out_project(tokens, mixed, out_weight, vec)
    acc, dh, dwu, dwd, dbu = mlp(h, ht, cotangent, cotangent.T, up_weight, up_bias, down_weight)
    y, dr, dm, dwo, dvec = middle(resid, acc, dh, cotangent, mixed, out_weight, vec)
    if near:
        dqkv, out_grad, up_grad, down_grad = attend_back(qkv, soft, mixed, dm, (dwo, dwu, dwd))
        dx, triple_grad, small = finish(tokens, dr, first_t, dqkv, triple_weight, vec, dvec, dbu, True)
        m = d // n
        small_grads = [small[i, :m] for i in range(8)]
        up_bias_grad = jnp.concatenate([small[8], small[9, : up_bias_s.shape[0] - 128]])
    else:
        (dqkv,) = attend_back(qkv, soft, mixed, dm)
        dx, dwt, dvec = finish(tokens, dr, first_t, dqkv, triple_weight, vec, dvec, dbu, False)
        small = jnp.concatenate([dvec[i].reshape(n, -1) for i in range(8)] + [dbu.reshape(n, -1)], axis=1)
        small = lax.psum_scatter(small, "fsdp", scatter_dimension=0, tiled=True).reshape(-1)
        small = lax.psum(small, "dp")
        total = lambda p: lax.psum(lax.psum_scatter(p, "fsdp", scatter_dimension=0, tiled=True), "dp").astype(F32)
        triple_grad, out_grad, up_grad, down_grad = total(dwt), total(dwo), total(dwu), total(dwd)
        m = d // n
        small_grads = [small[i * m : (i + 1) * m] for i in range(8)]
        up_bias_grad = small[8 * m :]
    dg1, ds1, dqb, dvb, dob, dg2, ds2, ddb = small_grads
    return (
        y, dx, dg1, ds1, triple_grad, dqb, dvb, out_grad, dob, dg2, ds2, up_grad, up_bias_grad, down_grad, ddb,
    )


def solution(mesh):
    tok = P(("dp", "fsdp"), None)
    vec = P("fsdp")
    mat = P("fsdp", None)
    weights = (vec, vec, mat, vec, vec, mat, vec, vec, vec, mat, vec, mat, vec)
    return jax.shard_map(
        on_device,
        mesh=mesh,
        in_specs=(tok, tok, P(("dp", "fsdp")), *weights),
        out_specs=(tok, tok, *weights),
        check_vma=False,
    )
```

```python
import functools

import jax
import jax.numpy as jnp
from jax import lax
from jax.experimental import pallas as pl
from jax.experimental.pallas import tpu as pltpu
from jax.sharding import PartitionSpec as P

H = 12
HD = 64
ROWS = 1024
EPS = 1e-06
F32 = jnp.float32
BF16 = jnp.bfloat16
VMEM_LIMIT = 60 * 1024 * 1024

ROOT_HALF = 0.7071067811865476
ROOT_INV_TWO_PI = 0.3989422804014327

NN = (((1,), (0,)), ((), ()))
NT = (((1,), (1,)), ((), ()))


def mm(a, b, dims=NN):
    return lax.dot_general(a, b, dims, preferred_element_type=F32)


def params(**kw):
    return pltpu.CompilerParams(vmem_limit_bytes=VMEM_LIMIT, **kw)


def norm_stats(x):
    mean = jnp.mean(x, axis=-1, keepdims=True)
    cen = x - mean
    var = jnp.mean(cen * cen, axis=-1, keepdims=True)
    inv = lax.rsqrt(var + EPS)
    return cen * inv, inv


MESH = pl.DeviceIdType.MESH
ANY = pl.BlockSpec(memory_space=pl.ANY)


def whereabouts():
    y = lax.axis_index("dp")
    f = lax.axis_index("fsdp")
    return y, f // 4, (f // 2) % 2, f % 2


def spot(z, x, c):
    return z * 4 + x * 2 + c


def greet():
    y, z, x, c = whereabouts()
    barrier = pltpu.get_barrier_semaphore()
    peers = [(1 - y, spot(z, x, c)), (y, spot(z, 1 - x, c)), (y, spot(z, x, 1 - c))]
    peers += [(y, spot((z + d) % 4, x, c)) for d in (1, 2, 3)]
    for peer in peers:
        pl.semaphore_signal(barrier, inc=1, device_id=peer, device_id_type=MESH)
    pl.semaphore_wait(barrier, len(peers))


class Mover:
    def __init__(self, send, recv, local, per):
        self.send, self.recv, self.local, self.per = send, recv, local, per
        self.y, self.z, self.x, self.c = whereabouts()

    def wide(self, r, split, y):
        return pl.ds(pl.multiple_of(y * (r // 3), 8), 2 * (r // 3)) if split else pl.ds(0, r)

    def thin(self, r, y):
        return pl.ds(pl.multiple_of(y * 2 * (r // 3), 8), r // 3)

    def copy(self, u, slot, src, dst, z=None, x=None, c=None, y=None):
        i = u * self.per + slot
        pick = lambda v, own: own if v is None else v
        peer = (pick(y, self.y), spot(pick(z, self.z), pick(x, self.x), pick(c, self.c)))
        return pltpu.make_async_remote_copy(
            src_ref=src, dst_ref=dst, send_sem=self.send.at[i], recv_sem=self.recv.at[i],
            device_id=peer, device_id_type=MESH,
        )


class Gather(Mover):
    def __init__(self, units, send, recv, local):
        super().__init__(send, recv, local, 6)
        self.units = units

    def mine(self, u):
        src, _, _, col, n, split = self.units[u]
        return src.at[self.wide(src.shape[0], split, self.y), pl.ds(col, n)]

    def held(self, u):
        src, _, hold, col, n, split = self.units[u]
        return hold.at[self.wide(src.shape[0], split, self.y), pl.ds(col, n)]

    def part(self, u, z, x, c, rows):
        _, dst, _, col, n, _ = self.units[u]
        every = slice(None)
        pick = lambda v: every if v is None else v
        return dst.at[pick(z), pick(x), pick(c), rows, pl.ds(col, n)]

    def broad(self, u):
        src, _, _, _, _, split = self.units[u]
        return self.wide(src.shape[0], split, self.y)

    def load(self, u):
        return pltpu.make_async_copy(self.mine(u), self.held(u), self.local.at[2 * u])

    def store(self, u):
        dst = self.part(u, self.z, self.x, self.c, self.broad(u))
        return pltpu.make_async_copy(self.held(u), dst, self.local.at[2 * u + 1])

    def along_z(self, u, d, out=True):
        here, there = (self.z + 4 - d) % 4, (self.z + d) % 4
        dst = self.part(u, self.z if out else here, self.x, self.c, self.broad(u))
        return self.copy(u, d - 1, self.mine(u), dst, z=there)

    def along_x(self, u, out=True):
        src = self.part(u, None, self.x, self.c, self.broad(u))
        dst = src if out else self.part(u, None, 1 - self.x, self.c, self.broad(u))
        return self.copy(u, 3, src, dst, x=1 - self.x)

    def along_y(self, u, out=True):
        r = self.units[u][0].shape[0]
        src = self.part(u, None, None, self.c, self.thin(r, self.y))
        dst = src if out else self.part(u, None, None, self.c, self.thin(r, 1 - self.y))
        return self.copy(u, 4, src, dst, y=1 - self.y)

    def along_c(self, u, out=True):
        every = pl.ds(0, self.units[u][0].shape[0])
        src = self.part(u, None, None, self.c, every)
        dst = src if out else self.part(u, None, None, 1 - self.c, every)
        return self.copy(u, 5, src, dst, c=1 - self.c)

    def stage(self, s, u):
        split = self.units[u][5]
        if s == 0:
            for d in (1, 2, 3):
                self.along_z(u, d).start()
            self.load(u).start()
        if s == 1:
            self.load(u).wait()
            self.store(u).start()
        if s == 2:
            self.store(u).wait()
            for d in (1, 2, 3):
                self.along_z(u, d, False).wait_recv()
            self.along_x(u).start()
        if s == 3:
            self.along_x(u, False).wait_recv()
            if split:
                self.along_y(u).start()
            else:
                self.along_c(u).start()
        if s == 4 and split:
            self.along_y(u, False).wait_recv()
            self.along_c(u).start()
        if s == 5:
            self.along_c(u, False).wait_recv()
            for d in (1, 2, 3):
                self.along_z(u, d).wait_send()
            self.along_x(u).wait_send()
            if split:
                self.along_y(u).wait_send()
            self.along_c(u).wait_send()


def gather_sems(units):
    return [
        pltpu.SemaphoreType.DMA((units * 6,)),
        pltpu.SemaphoreType.DMA((units * 6,)),
        pltpu.SemaphoreType.DMA((2 * units,)),
    ]


def whole(shard):
    return jax.ShapeDtypeStruct((4, 2, 2, *shard.shape), shard.dtype)


class Reduce(Mover):
    def __init__(self, units, send, recv, local):
        super().__init__(send, recv, local, 7)
        self.units = units

    def size(self, u):
        return self.units[u][0].shape[3]

    def partial(self, u, c):
        src, _, (col, _), n, _, _ = self.units[u]
        return src.at[:, :, c, :, pl.ds(col, n)]

    def load(self, u):
        return pltpu.make_async_copy(self.partial(u, self.c), self.units[u][5][0], self.local.at[u])

    def over_c(self, u):
        return self.copy(u, 0, self.partial(u, 1 - self.c), self.units[u][5][1], c=1 - self.c)

    def over_y(self, u):
        own, from_y = self.units[u][5][0], self.units[u][5][5]
        return self.copy(u, 1, own.at[:, :, self.thin(self.size(u), 1 - self.y), :], from_y, y=1 - self.y)

    def over_x(self, u):
        own, from_x = self.units[u][5][0], self.units[u][5][2]
        rows = self.wide(self.size(u), self.units[u][4], self.y)
        return self.copy(u, 2, own.at[:, 1 - self.x, rows, :], from_x, x=1 - self.x)

    def over_z(self, u, d):
        own, from_z = self.units[u][5][0], self.units[u][5][3]
        rows = self.wide(self.size(u), self.units[u][4], self.y)
        to = (self.z + d) % 4
        return self.copy(u, 2 + d, own.at[to, self.x, rows, :], from_z.at[d - 1], z=to)

    def over_last(self, u):
        last = self.units[u][5][4]
        return self.copy(u, 6, last.at[0], last.at[1], y=1 - self.y)

    def stage(self, s, u):
        _, out, (_, col), n, split, (own, from_c, from_x, from_z, last, *rest) = self.units[u]
        y, z, x = self.y, self.z, self.x
        r = self.size(u)
        rows = self.wide(r, split, y)
        if s == 0:
            self.over_c(u).start()
            self.load(u).start()
        if s == 1:
            self.load(u).wait()
            self.over_c(u).wait_recv()
            own[...] = own[...] + from_c[...]
            if split:
                self.over_y(u).start()
        if s == 2:
            if split:
                self.over_y(u).wait_recv()
                mine = self.thin(r, y)
                own[:, :, mine, :] = own[:, :, mine, :] + rest[0][...]
            self.over_x(u).start()
        if s == 3:
            self.over_x(u).wait_recv()
            for k in range(4):
                own[k, x, rows, :] = own[k, x, rows, :] + from_x[k]
            for d in (1, 2, 3):
                self.over_z(u, d).start()
        if s == 4:
            total = own[z, x, rows, :].astype(F32)
            for d in (1, 2, 3):
                self.over_z(u, d).wait_recv()
                total = total + from_z[d - 1].astype(F32)
            last[0] = total.astype(last.dtype)
            self.over_last(u).start()
        if s == 5:
            self.over_last(u).wait_recv()
            cols = pl.ds(col, n)
            if split:
                t = r // 3
                at = lambda k: pl.ds(pl.multiple_of(k * t, 8), t)
                put = lambda k, v: out.__setitem__((at(k), cols), v.astype(F32))
                put(1, last[0, at(1 - y), :].astype(F32) + last[1, at(y), :].astype(F32))
                put(2 * y, last[0, at(y), :])
                put(2 * (1 - y), last[1, at(1 - y), :])
            else:
                out[:, cols] = last[0].astype(F32) + last[1].astype(F32)
        if s == 6:
            self.over_c(u).wait_send()
            if split:
                self.over_y(u).wait_send()
            self.over_x(u).wait_send()
            for d in (1, 2, 3):
                self.over_z(u, d).wait_send()
            self.over_last(u).wait_send()


def reduce_buffers(r, n, dtype, split):
    wide = 2 * r // 3 if split else r
    shapes = [(4, 2, r, n), (4, 2, r, n), (4, wide, n), (3, wide, n), (2, wide, n)]
    if split:
        shapes.append((4, 2, r // 3, n))
    return [pltpu.VMEM(shape, dtype) for shape in shapes]


def reduce_scratch(plan):
    flat = []
    for p in plan:
        flat += reduce_buffers(*p)
    units = len(plan)
    return flat + [
        pltpu.SemaphoreType.DMA((units * 7,)),
        pltpu.SemaphoreType.DMA((units * 7,)),
        pltpu.SemaphoreType.DMA((units,)),
    ]


def reduce_work(plan, places, scratch):
    units = []
    at = 0
    for (_, n, _, split), (src, out, col) in zip(plan, places):
        count = 6 if split else 5
        units.append((src, out, col, n, split, scratch[at : at + count]))
        at += count
    return Reduce(units, *scratch[at:])


def at_hook(hook, moves, work):
    for u, hooks in enumerate(moves):
        for s, when in enumerate(hooks):
            if when == hook:
                work.stage(s, u)


def hooked(step, per_step, which, steps, moves, work):
    for k in range(steps):
        if any(k * per_step + which in hooks for hooks in moves):

            @pl.when(step == k)
            def _():
                if k == 0 and which == 0:
                    greet()
                at_hook(k * per_step + which, moves, work)


def unpack(vec_ref, ub_ref, tall_ref):
    d = vec_ref.shape[1] // 16
    f = ub_ref.shape[1] // 16
    for i in range(16):
        tile = tall_ref[i // 4, (i // 2) % 2, i % 2].astype(F32)
        vec_ref[:, i * d : (i + 1) * d] = tile[0:8, 0:d]
        ub_ref[:, i * f : i * f + 128] = tile[8:9, 0:128]
        ub_ref[:, i * f + 128 : (i + 1) * f] = tile[9:10, 0 : f - 128]


def first_gather_body(t_ref, v_ref, tf_ref, vec_ref, ub_ref, tall_ref, th_ref, vh_ref, *sems):
    n = t_ref.shape[1] // 6
    units = [(v_ref, tall_ref, vh_ref, 0, v_ref.shape[1], False)]
    units += [(t_ref, tf_ref, th_ref, j * n, n, True) for j in range(6)]
    greet()
    work = Gather(units, *sems)
    for u in range(len(units)):
        work.stage(0, u)
    for k in range(len(units) + 4):
        for s in range(1, 6):
            if 0 <= k - s + 1 < len(units):
                work.stage(s, k - s + 1)
    unpack(vec_ref, ub_ref, tall_ref)


def first_gather(triple, tall):
    d = triple.shape[0] * 16
    vmem = pl.BlockSpec(memory_space=pltpu.VMEM)
    return pl.pallas_call(
        first_gather_body,
        in_specs=[ANY, vmem],
        out_specs=[ANY, vmem, vmem],
        out_shape=[
            whole(triple),
            jax.ShapeDtypeStruct((8, d), F32),
            jax.ShapeDtypeStruct((1, 4 * d), F32),
        ],
        scratch_shapes=[
            pltpu.VMEM((4, 2, 2, *tall.shape), BF16),
            pltpu.VMEM(triple.shape, BF16),
            pltpu.VMEM(tall.shape, BF16),
            *gather_sems(7),
        ],
        compiler_params=params(collective_id=0, has_side_effects=True),
        name="first_gather",
    )(triple, tall)


def proj_body(x_ref, vec_ref, w_ref, qkv_ref, ht_ref):
    d = x_ref.shape[1]
    n, _ = norm_stats(x_ref[...].astype(F32))
    h = (n * vec_ref[0:1, :] + vec_ref[1:2, :]).astype(BF16)
    ht_ref[...] = h.T
    for j in range(3):
        cols = pl.ds(j * d, d)
        p = mm(h, w_ref[:, cols])
        if j == 0:
            p = (p + vec_ref[2:3, :]) * 0.125
        if j == 2:
            p = p + vec_ref[3:4, :]
        qkv_ref[:, cols] = p.astype(BF16)


def project(x, vec, w):
    rows, d = x.shape
    cols = w.shape[1]
    tile = 512
    return pl.pallas_call(
        proj_body,
        grid=(rows // tile,),
        in_specs=[
            pl.BlockSpec((tile, d), lambda i: (i, 0)),
            pl.BlockSpec((8, d), lambda i: (0, 0)),
            pl.BlockSpec((d, cols), lambda i: (0, 0)),
        ],
        out_specs=[
            pl.BlockSpec((tile, cols), lambda i: (i, 0)),
            pl.BlockSpec((d, tile), lambda i: (0, i)),
        ],
        out_shape=[jax.ShapeDtypeStruct((rows, cols), BF16), jax.ShapeDtypeStruct((d, rows), BF16)],
        compiler_params=params(),
        name="project",
        cost_estimate=pl.CostEstimate(
            flops=2 * rows * d * cols, bytes_accessed=2 * rows * (d + cols), transcendentals=0
        ),
    )(x, vec, w)


QT = 256
GATHER_LAGS = (0, 1, 3, 6, 9, 11)
REDUCE_LAGS = (0, 1, 3, 5, 7, 9, 10)


LOG2E = 1.4426950408889634


def swap(value):
    return jnp.concatenate([value[:, HD:], value[:, :HD]], axis=1)


def twice(value, own):
    return jnp.where(own, value, swap(value))


def unit_list(widths):
    units = [(0, 0, widths[0])]
    for i, w in enumerate(widths[1:]):
        units += [(i + 1, j * (w // 6), w // 6) for j in range(6)]
    return units


def attend_body(hosting, *refs):
    q_ref, k_ref, v_ref, seg_ref = refs[:4]
    if hosting:
        shards = refs[4:7]
        o_ref, p_ref, inv_ref = refs[7:10]
        full = refs[10:13]
        bias_ref, pair_ref = refs[13:15]
        hold = refs[15:18]
        units = [(shards[i], full[i], hold[i], col, n, True) for i, col, n in unit_list([s.shape[1] for s in shards])]
        work = Gather(units, *refs[18:])
        moves = [[u + lag for lag in GATHER_LAGS] for u in range(len(units))]
    else:
        o_ref, p_ref, inv_ref, bias_ref, pair_ref = refs[4:]
    step = pl.program_id(0) * pl.num_programs(1) + pl.program_id(1)
    rows = q_ref.shape[0]

    @pl.when(pl.program_id(1) == 0)
    def _():
        seg = seg_ref[...].astype(F32)
        column = jnp.broadcast_to(seg, (8, rows)).T[:, 0:1]
        bias_ref[...] = jnp.where(column == seg, 0.0, -1e30)

    lower = lax.broadcasted_iota(jnp.int32, (1, 128), 1) < HD
    lower = lax.broadcasted_iota(jnp.int32, (1, 128), 1) < HD
    lower = lax.broadcasted_iota(jnp.int32, (1, 128), 1) < HD
    sums = []
    for hh in range(2):
        if hosting:
            hooked(step, 2, hh, 12, moves, work)
        own = lower if hh == 0 else ~lower
        q = q_ref[...].astype(F32) * LOG2E
        high = q.astype(BF16)
        low = (q - high.astype(F32)).astype(BF16)
        pair_ref[0, hh] = jnp.where(own, high, swap(low))
        pair_ref[1, hh] = twice(k_ref[...], own)
        pair_ref[2, hh] = jnp.where(own, v_ref[...], jnp.ones_like(v_ref[...]))
        if hh == 1:
            sums.append(mm(p_ref[0], pair_ref[2, 0]))
        for t in range(rows // QT):
            sl = pl.ds(t * QT, QT)
            s = mm(pair_ref[0, hh, sl, :], pair_ref[1, hh], NT) + bias_ref[sl, :]
            p_ref[hh, sl, :] = jnp.exp2(s - jnp.max(s, axis=-1, keepdims=True)).astype(BF16)
    sums.append(mm(p_ref[1], pair_ref[2, 1]))
    inv = 1.0 / swap(jnp.where(lower, sums[1], sums[0]))
    inv_ref[...] = inv
    o_ref[...] = (jnp.where(lower, sums[0], sums[1]) * inv).astype(BF16)


def attend(qkv, segr, shards=()):
    rows = qkv.shape[0]
    d = qkv.shape[1] // 3
    mb = rows // ROWS
    pairs = d // 128
    extra = dict(collective_id=1, has_side_effects=True) if shards else {}
    return pl.pallas_call(
        functools.partial(attend_body, bool(shards)),
        grid=(mb, pairs),
        in_specs=[
            pl.BlockSpec((ROWS, 128), lambda m, h: (m, h)),
            pl.BlockSpec((ROWS, 128), lambda m, h: (m, pairs + h)),
            pl.BlockSpec((ROWS, 128), lambda m, h: (m, 2 * pairs + h)),
            pl.BlockSpec((None, 1, ROWS), lambda m, h: (m, 0, 0)),
            *[ANY for _ in shards],
        ],
        out_specs=[
            pl.BlockSpec((ROWS, 128), lambda m, h: (m, h)),
            pl.BlockSpec((None, 2, ROWS, ROWS), lambda m, h: (m, h, 0, 0)),
            pl.BlockSpec((ROWS, 128), lambda m, h: (m, h)),
            *[ANY for _ in shards],
        ],
        out_shape=[
            jax.ShapeDtypeStruct((rows, d), BF16),
            jax.ShapeDtypeStruct((mb, 2 * pairs, ROWS, ROWS), BF16),
            jax.ShapeDtypeStruct((rows, d), F32),
            *[whole(s) for s in shards],
        ],
        scratch_shapes=[pltpu.VMEM((ROWS, ROWS), F32), pltpu.VMEM((3, 2, ROWS, 128), BF16)]
        + ([pltpu.VMEM(s.shape, s.dtype) for s in shards] + gather_sems(13) if shards else []),
        compiler_params=params(**extra),
        name="attend",
        cost_estimate=pl.CostEstimate(
            flops=mb * pairs * 2 * 4 * ROWS * ROWS * 256,
            bytes_accessed=mb * pairs * 2 * ROWS * ROWS * 2,
            transcendentals=mb * pairs * 2 * ROWS * ROWS,
        ),
    )(qkv, qkv, qkv, segr, *shards)


def attend_back_body(plan, *refs):
    q_ref, k_ref, v_ref, p_ref, o_ref, g_ref, inv_ref = refs[:7]
    hosting = plan is not None
    if hosting:
        parts = refs[7:10]
        d_ref = refs[10]
        results = refs[11:14]
        ds_ref = refs[14]
        places = [(parts[i], results[i], (col, col)) for i, col, _ in unit_list([p.shape[4] for p in parts])]
        work = reduce_work(plan, places, refs[15:])
        moves = [[u + lag for lag in REDUCE_LAGS] for u in range(len(places))]
    else:
        d_ref, ds_ref = refs[7:]
    step = pl.program_id(0) * pl.num_programs(1) + pl.program_id(1)
    rows = q_ref.shape[0]
    lower = lax.broadcasted_iota(jnp.int32, (1, 128), 1) < HD
    dk_parts = []
    dv_parts = []
    dq_parts = []
    for hh in range(2):
        if hosting:
            hooked(step, 2, hh, 12, moves, work)
        own = lower if hh == 0 else ~lower
        half = slice(hh * HD, (hh + 1) * HD)
        g = g_ref[...].astype(F32) * inv_ref[...]
        high = g.astype(BF16)
        low = (g - high.astype(F32)).astype(BF16)
        pair = jnp.where(own, high, swap(low))
        center = jnp.sum(jnp.where(own, g * o_ref[...].astype(F32), 0.0), axis=-1, keepdims=True)
        v = twice(v_ref[...], own)
        for t in range(rows // QT):
            sl = pl.ds(t * QT, QT)
            ts = slice(t * QT, (t + 1) * QT)
            d_soft = mm(pair[ts, :], v, NT)
            ds_ref[hh, sl, :] = (p_ref[hh, sl, :].astype(F32) * (d_soft - center[ts, :])).astype(BF16)
        dv = mm(pair.T, p_ref[hh])
        dv_parts.append(dv[:HD, :] + dv[HD:, :])
        dk_parts.append(mm(q_ref[...].T[half, :], ds_ref[hh]))
        dq_parts.append(mm(ds_ref[hh], k_ref[...]))
    d_ref[0] = (jnp.where(lower, dq_parts[0], dq_parts[1]) * 0.125).astype(BF16)
    d_ref[1] = jnp.concatenate(dk_parts, axis=0).T.astype(BF16)
    d_ref[2] = jnp.concatenate(dv_parts, axis=0).T.astype(BF16)


def attend_back(qkv, soft, mixed, d_mixed, inv, grads=()):
    rows = qkv.shape[0]
    d = qkv.shape[1] // 3
    mb = rows // ROWS
    pairs = d // 128
    blk = pl.BlockSpec((ROWS, 128), lambda m, h: (m, h))
    plan = None
    results = []
    extra = {}
    grads = [g.reshape(4, 2, 2, g.shape[0] // 16, g.shape[1]) for g in grads]
    if grads:
        plan = [(grads[i].shape[3], n, BF16, True) for i, _, n in unit_list([g.shape[4] for g in grads])]
        results = [jax.ShapeDtypeStruct(g.shape[3:], F32) for g in grads]
        extra = dict(collective_id=2, has_side_effects=True)
    return pl.pallas_call(
        functools.partial(attend_back_body, plan),
        grid=(mb, pairs),
        in_specs=[
            blk,
            pl.BlockSpec((ROWS, 128), lambda m, h: (m, pairs + h)),
            pl.BlockSpec((ROWS, 128), lambda m, h: (m, 2 * pairs + h)),
            pl.BlockSpec((None, 2, ROWS, ROWS), lambda m, h: (m, h, 0, 0)),
            blk,
            blk,
            blk,
            *[ANY for _ in grads],
        ],
        out_specs=[
            pl.BlockSpec((3, ROWS, 128), lambda m, h: (0, m, h)),
            *[pl.BlockSpec(r.shape, lambda m, h: (0, 0)) for r in results],
        ],
        out_shape=[jax.ShapeDtypeStruct((3, rows, d), BF16), *results],
        scratch_shapes=[pltpu.VMEM((2, ROWS, ROWS), BF16)] + (reduce_scratch(plan) if grads else []),
        compiler_params=params(**extra),
        name="attend_back",
        cost_estimate=pl.CostEstimate(
            flops=mb * pairs * 2 * 8 * ROWS * ROWS * 256,
            bytes_accessed=mb * pairs * 2 * ROWS * ROWS * 2,
            transcendentals=0,
        ),
    )(qkv, qkv, qkv, soft, mixed, d_mixed, inv, *grads)


def out_body(x_ref, m_ref, w_ref, vec_ref, resid_ref, h_ref, ht_ref):
    resid = x_ref[...].astype(F32) + mm(m_ref[...], w_ref[...]) + vec_ref[4:5, :]
    resid_ref[...] = resid
    n, _ = norm_stats(resid)
    h = (n * vec_ref[5:6, :] + vec_ref[6:7, :]).astype(BF16)
    h_ref[...] = h
    ht_ref[...] = h.T


def out_project(x, mixed, w, vec):
    rows, d = x.shape
    tile = 512
    blk = pl.BlockSpec((tile, d), lambda i: (i, 0))
    return pl.pallas_call(
        out_body,
        grid=(rows // tile,),
        in_specs=[blk, blk, pl.BlockSpec((d, d), lambda i: (0, 0)), pl.BlockSpec((8, d), lambda i: (0, 0))],
        out_specs=[blk, blk, pl.BlockSpec((d, tile), lambda i: (0, i))],
        out_shape=[
            jax.ShapeDtypeStruct((rows, d), F32),
            jax.ShapeDtypeStruct((rows, d), BF16),
            jax.ShapeDtypeStruct((d, rows), BF16),
        ],
        compiler_params=params(),
        name="out_project",
        cost_estimate=pl.CostEstimate(
            flops=2 * rows * d * d, bytes_accessed=rows * d * 12, transcendentals=0
        ),
    )(x, mixed, w, vec)


FC = 512
RT = 512


def gelu_parts(u):
    cdf = 0.5 * (1.0 + lax.erf(u * ROOT_HALF))
    bell = jnp.exp(-0.5 * u * u) * ROOT_INV_TWO_PI
    return u * cdf, cdf + u * bell


def mlp_body(h_ref, ht_ref, g_ref, gt_ref, wu_ref, bu_ref, wd_ref, acc_ref, dh_ref, dwu_ref, dwd_ref, dbu_ref,
             act_ref, du_ref):
    rows = h_ref.shape[0]

    @pl.when(pl.program_id(0) == 0)
    def _():
        acc_ref[...] = jnp.zeros_like(acc_ref)
        dh_ref[...] = jnp.zeros_like(dh_ref)

    wu = wu_ref[...]
    wd = wd_ref[...]
    bias_sum = None
    for t in range(rows // RT):
        sl = pl.ds(t * RT, RT)
        u = mm(h_ref[sl, :], wu) + bu_ref[...]
        act, slope = gelu_parts(u)
        act_ref[sl, :] = act.astype(BF16)
        du = mm(g_ref[sl, :], wd, NT) * slope
        part = jnp.sum(du, axis=0, keepdims=True)
        bias_sum = part if bias_sum is None else bias_sum + part
        du_ref[sl, :] = du.astype(BF16)
        acc_ref[sl, :] += mm(act_ref[sl, :], wd)
        dh_ref[sl, :] += mm(du_ref[sl, :], wu, NT)
    dbu_ref[...] = bias_sum
    dwu_ref[...] = mm(ht_ref[...], du_ref[...]).astype(dwu_ref.dtype)
    dwd_ref[...] = mm(gt_ref[...], act_ref[...]).T.astype(dwd_ref.dtype)


def mlp(h, ht, g, gt, wu, bu, wd):
    rows, d = h.shape
    ff = wu.shape[1]
    one = pl.Buffered(1)
    whole = pl.BlockSpec((rows, d), lambda c: (0, 0), pipeline_mode=one)
    whole_t = pl.BlockSpec((d, rows), lambda c: (0, 0), pipeline_mode=one)
    return pl.pallas_call(
        mlp_body,
        grid=(ff // FC,),
        in_specs=[
            whole,
            whole_t,
            whole,
            whole_t,
            pl.BlockSpec((d, FC), lambda c: (0, c)),
            pl.BlockSpec((1, FC), lambda c: (0, c)),
            pl.BlockSpec((FC, d), lambda c: (c, 0)),
        ],
        out_specs=[
            whole,
            whole,
            pl.BlockSpec((d, FC), lambda c: (0, c)),
            pl.BlockSpec((FC, d), lambda c: (c, 0)),
            pl.BlockSpec((1, FC), lambda c: (0, c)),
        ],
        out_shape=[
            jax.ShapeDtypeStruct((rows, d), F32),
            jax.ShapeDtypeStruct((rows, d), F32),
            jax.ShapeDtypeStruct((d, ff), BF16),
            jax.ShapeDtypeStruct((ff, d), BF16),
            jax.ShapeDtypeStruct((1, ff), F32),
        ],
        scratch_shapes=[pltpu.VMEM((rows, FC), BF16), pltpu.VMEM((rows, FC), BF16)],
        compiler_params=params(),
        name="mlp",
        cost_estimate=pl.CostEstimate(
            flops=12 * rows * d * ff, bytes_accessed=rows * d * 20 + 8 * d * ff, transcendentals=3 * rows * ff
        ),
    )(h, ht, g, gt, wu, bu, wd)


def fold(ref, row, step, value):
    part = jnp.sum(value, axis=0, keepdims=True)

    @pl.when(step == 0)
    def _():
        ref[row : row + 1, :] = part

    @pl.when(step != 0)
    def _():
        ref[row : row + 1, :] += part


def norm_pull(grad, n, inv, gain):
    dn = grad * gain
    plain = jnp.mean(dn, axis=-1, keepdims=True)
    cross = jnp.mean(dn * n, axis=-1, keepdims=True)
    return inv * (dn - plain - n * cross)


def mid_body(resid_ref, acc_ref, dh_ref, g_ref, mixed_ref, w_ref, vec_ref,
             y_ref, dr_ref, dm_ref, dw_ref, dvec_ref, sum_ref):
    step = pl.program_id(0)
    resid = resid_ref[...]
    y_ref[...] = (resid + acc_ref[...] + vec_ref[7:8, :]).astype(BF16)
    g = g_ref[...].astype(F32)
    n, inv = norm_stats(resid)
    dh = dh_ref[...]
    dr = g + norm_pull(dh, n, inv, vec_ref[5:6, :])
    dr_ref[...] = dr
    fold(dvec_ref, 4, step, dr)
    fold(dvec_ref, 5, step, dh * n)
    fold(dvec_ref, 6, step, dh)
    fold(dvec_ref, 7, step, g)
    low = dr.astype(BF16)
    dm_ref[...] = mm(low, w_ref[...], NT).astype(BF16)
    dw = mm(mixed_ref[...].T, low)

    @pl.when(step == 0)
    def _():
        sum_ref[...] = dw
        dvec_ref[0:4, :] = jnp.zeros((4, dvec_ref.shape[1]), F32)

    @pl.when(step != 0)
    def _():
        sum_ref[...] += dw

    @pl.when(step == pl.num_programs(0) - 1)
    def _():
        dw_ref[...] = sum_ref[...].astype(dw_ref.dtype)


def middle(resid, acc, dh, g, mixed, w, vec):
    rows, d = resid.shape
    tile = 512
    blk = pl.BlockSpec((tile, d), lambda i: (i, 0))
    mat = pl.BlockSpec((d, d), lambda i: (0, 0))
    eight = pl.BlockSpec((8, d), lambda i: (0, 0))
    return pl.pallas_call(
        mid_body,
        grid=(rows // tile,),
        in_specs=[blk, blk, blk, blk, blk, mat, eight],
        out_specs=[blk, blk, blk, mat, eight],
        out_shape=[
            jax.ShapeDtypeStruct((rows, d), BF16),
            jax.ShapeDtypeStruct((rows, d), F32),
            jax.ShapeDtypeStruct((rows, d), BF16),
            jax.ShapeDtypeStruct((d, d), BF16),
            jax.ShapeDtypeStruct((8, d), F32),
        ],
        scratch_shapes=[pltpu.VMEM((d, d), F32)],
        compiler_params=params(),
        name="middle",
        cost_estimate=pl.CostEstimate(
            flops=4 * rows * d * d, bytes_accessed=rows * d * 24, transcendentals=0
        ),
    )(resid, acc, dh, g, mixed, w, vec)


PHASES = 3
FINAL_TILE = 512


def finish_body(plan, plan_steps, ht_ref, part_ref, tile_ref, x_ref, dr_ref, w_hbm, vec_ref, dvec_ref, dbu_ref, dx_ref, *refs):
    step = pl.program_id(0)
    steps = pl.num_programs(0)
    d = x_ref.shape[1]
    if plan is None:
        dw_ref, sums_ref, w_ref, w_sem = refs
    else:
        out_ref, small_ref, w_ref, w_sem, sums_ref, grad_ref, tall_ref = refs[:7]
        places = [(grad_ref.at[j], out_ref, (0, j * d)) for j in range(PHASES)]
        places.append((tall_ref, small_ref, (0, 0)))
        work = reduce_work(plan, places, refs[7:])
        count = plan_steps
    fetch = pltpu.make_async_copy(w_hbm, w_ref, w_sem)

    @pl.when(step == 0)
    def _():
        if plan is not None:
            greet()
        fetch.start()
        sums_ref[...] = dvec_ref[...]

    @pl.when(step < PHASES)
    def _():
        part = part_ref[0]
        for j in range(d // 256):
            cols = pl.ds(j * 256, 256)
            dw = mm(ht_ref[...], part_ref[0, :, cols]).astype(BF16)
            if plan is None:
                dw_ref[:, cols] = dw
            else:
                grad_ref[step, :, :, :, :, cols] = dw.reshape(4, 2, 2, d // 16, 256)
        total = jnp.sum(part.astype(F32), axis=0, keepdims=True)

        @pl.when(step == 0)
        def _():
            sums_ref[2:3, :] = total

        @pl.when(step == 2)
        def _():
            sums_ref[3:4, :] = total

    @pl.when(step == PHASES)
    def _():
        fetch.wait()

    @pl.when(step >= PHASES)
    def _():
        n, inv = norm_stats(x_ref[...].astype(F32))
        dh = None
        for j in range(3):
            term = mm(tile_ref[j], w_ref[:, pl.ds(j * d, d)], NT)
            dh = term if dh is None else dh + term
        fold(sums_ref, 0, step - PHASES, dh * n)
        fold(sums_ref, 1, step - PHASES, dh)
        dx_ref[...] = (dr_ref[...] + norm_pull(dh, n, inv, vec_ref[0:1, :])).astype(BF16)

    if plan is not None:
        for k in range(count):

            @pl.when(step == k)
            def _():
                for u in range(PHASES):
                    s = k - u
                    if 0 <= s <= 6:
                        work.stage(s, u)
                if k == count - 1:
                    small = PHASES
                    pack(tall_ref, sums_ref, dbu_ref)
                    work.stage(0, small)
                    work.stage(1, small)
                    work.stage(2, small)
                    work.stage(5, 2)
                    work.stage(3, small)
                    work.stage(4, small)
                    work.stage(5, small)
                    for u in range(1, PHASES + 1):
                        work.stage(6, u)


def pack(tall_ref, sums_ref, dbu_ref):
    d = sums_ref.shape[1] // 16
    f = dbu_ref.shape[1] // 16
    for i in range(16):
        tile = tall_ref.at[i // 4, (i // 2) % 2, i % 2]
        tile[0:8, 0:d] = sums_ref[:, i * d : (i + 1) * d]
        tile[8:9, 0:128] = dbu_ref[:, i * f : i * f + 128]
        tile[9:10, 0 : f - 128] = dbu_ref[:, i * f + 128 : (i + 1) * f]


def finish(x, dr, ht, dqkv, w, vec, dvec, dbu, near):
    rows, d = x.shape
    tiles = rows // FINAL_TILE
    row = lambda s: jnp.maximum(s - PHASES, 0)
    one = pl.Buffered(1)
    eight = pl.BlockSpec((8, d), lambda s: (0, 0))
    if near:
        plan = [(d // 16, d, BF16, True)] * PHASES + [(16, 128, F32, False)]
        shapes = [jax.ShapeDtypeStruct((d // 16, 3 * d), F32), jax.ShapeDtypeStruct((16, 128), F32)]
        specs = [pl.BlockSpec(s.shape, lambda s: (0, 0)) for s in shapes]
        scratch = [
            pltpu.VMEM((8, d), F32),
            pltpu.VMEM((PHASES, 4, 2, 2, d // 16, d), BF16),
            pltpu.VMEM((4, 2, 2, 16, 128), F32),
        ] + reduce_scratch(plan)
        extra = dict(collective_id=3, has_side_effects=True)
    else:
        plan = None
        shapes = [jax.ShapeDtypeStruct((d, 3 * d), BF16), jax.ShapeDtypeStruct((8, d), F32)]
        specs = [pl.BlockSpec((d, d), lambda s: (0, jnp.minimum(s, PHASES - 1))), eight]
        scratch = []
        extra = {}
    return pl.pallas_call(
        functools.partial(finish_body, plan, PHASES + tiles),
        grid=(PHASES + tiles,),
        in_specs=[
            pl.BlockSpec((d, rows), lambda s: (0, 0), pipeline_mode=one),
            pl.BlockSpec((1, rows, d), lambda s: (jnp.minimum(s, PHASES - 1), 0, 0)),
            pl.BlockSpec((3, FINAL_TILE, d), lambda s: (0, row(s), 0)),
            pl.BlockSpec((FINAL_TILE, d), lambda s: (row(s), 0)),
            pl.BlockSpec((FINAL_TILE, d), lambda s: (row(s), 0)),
            ANY,
            eight,
            eight,
            pl.BlockSpec(dbu.shape, lambda s: (0, 0)),
        ],
        out_specs=[pl.BlockSpec((FINAL_TILE, d), lambda s: (row(s), 0)), *specs],
        out_shape=[jax.ShapeDtypeStruct((rows, d), BF16), *shapes],
        scratch_shapes=[pltpu.VMEM((d, 3 * d), BF16), pltpu.SemaphoreType.DMA(()), *scratch],
        compiler_params=params(**extra),
        name="finish",
        cost_estimate=pl.CostEstimate(
            flops=12 * rows * d * d, bytes_accessed=rows * d * 20, transcendentals=0
        ),
    )(ht, dqkv, dqkv, x, dr, w, vec, dvec, dbu)


def on_device(tokens, cotangent, segment_ids, *shards):
    gather = lambda s: lax.all_gather(s, "fsdp", axis=0, tiled=True)
    n = lax.axis_size("fsdp")
    near = n == 16 and lax.axis_size("dp") == 2
    triple_s, out_s, up_s, down_s = (s for s in shards if s.ndim == 2)
    rows, d = tokens.shape
    up_bias_s = shards[10]
    eights = [s for i, s in enumerate(shards) if s.ndim == 1 and i != 10]
    flat = lambda w: w.reshape(-1, w.shape[-1])
    if near:
        wide = [jnp.pad(v, (0, 128 - v.shape[0])) for v in eights]
        wide += [up_bias_s[:128], jnp.pad(up_bias_s[128:], (0, 256 - up_bias_s.shape[0]))]
        tall = jnp.pad(jnp.stack(wide), ((0, 6), (0, 0)))
        triple_weight, vec, up_bias = first_gather(triple_s, tall)
        triple_weight = flat(triple_weight)
    else:
        triple_weight = gather(triple_s)
        packed = gather(jnp.concatenate(eights + [up_bias_s]).reshape(1, -1)).astype(F32)
        m = eights[0].shape[0]
        vec = jnp.stack([packed[:, i * m : (i + 1) * m].reshape(-1) for i in range(8)])
        up_bias = packed[:, 8 * m :].reshape(1, -1)

    segr = segment_ids.reshape(rows // ROWS, 1, ROWS)
    qkv, first_t = project(tokens, vec, triple_weight)
    if near:
        mixed, soft, inv, *full = attend(qkv, segr, (out_s, up_s, down_s))
        out_weight, up_weight, down_weight = (flat(w) for w in full)
    else:
        mixed, soft, inv = attend(qkv, segr)
        out_weight, up_weight, down_weight = gather(out_s), gather(up_s), gather(down_s)
    resid, h, ht = out_project(tokens, mixed, out_weight, vec)
    acc, dh, dwu, dwd, dbu = mlp(h, ht, cotangent, cotangent.T, up_weight, up_bias, down_weight)
    y, dr, dm, dwo, dvec = middle(resid, acc, dh, cotangent, mixed, out_weight, vec)
    if near:
        dqkv, out_grad, up_grad, down_grad = attend_back(qkv, soft, mixed, dm, inv, (dwo, dwu, dwd))
        dx, triple_grad, small = finish(tokens, dr, first_t, dqkv, triple_weight, vec, dvec, dbu, True)
        m = d // n
        small_grads = [small[i, :m] for i in range(8)]
        up_bias_grad = jnp.concatenate([small[8], small[9, : up_bias_s.shape[0] - 128]])
    else:
        (dqkv,) = attend_back(qkv, soft, mixed, dm, inv)
        dx, dwt, dvec = finish(tokens, dr, first_t, dqkv, triple_weight, vec, dvec, dbu, False)
        small = jnp.concatenate([dvec[i].reshape(n, -1) for i in range(8)] + [dbu.reshape(n, -1)], axis=1)
        small = lax.psum_scatter(small, "fsdp", scatter_dimension=0, tiled=True).reshape(-1)
        small = lax.psum(small, "dp")
        total = lambda p: lax.psum(lax.psum_scatter(p, "fsdp", scatter_dimension=0, tiled=True), "dp").astype(F32)
        triple_grad, out_grad, up_grad, down_grad = total(dwt), total(dwo), total(dwu), total(dwd)
        m = d // n
        small_grads = [small[i * m : (i + 1) * m] for i in range(8)]
        up_bias_grad = small[8 * m :]
    dg1, ds1, dqb, dvb, dob, dg2, ds2, ddb = small_grads
    return (
        y, dx, dg1, ds1, triple_grad, dqb, dvb, out_grad, dob, dg2, ds2, up_grad, up_bias_grad, down_grad, ddb,
    )


def solution(mesh):
    tok = P(("dp", "fsdp"), None)
    vec = P("fsdp")
    mat = P("fsdp", None)
    weights = (vec, vec, mat, vec, vec, mat, vec, vec, vec, mat, vec, mat, vec)
    return jax.shard_map(
        on_device,
        mesh=mesh,
        in_specs=(tok, tok, P(("dp", "fsdp")), *weights),
        out_specs=(tok, tok, *weights),
        check_vma=False,
    )
```

```python
import functools

import jax
import jax.numpy as jnp
from jax import lax
from jax.experimental import pallas as pl
from jax.experimental.pallas import tpu as pltpu
from jax.sharding import PartitionSpec as P

H = 12
HD = 64
ROWS = 1024
EPS = 1e-06
F32 = jnp.float32
BF16 = jnp.bfloat16
VMEM_LIMIT = 60 * 1024 * 1024

ROOT_HALF = 0.7071067811865476
ROOT_INV_TWO_PI = 0.3989422804014327

NN = (((1,), (0,)), ((), ()))
NT = (((1,), (1,)), ((), ()))


def mm(a, b, dims=NN):
    return lax.dot_general(a, b, dims, preferred_element_type=F32)


def params(**kw):
    return pltpu.CompilerParams(vmem_limit_bytes=VMEM_LIMIT, **kw)


def norm_stats(x):
    mean = jnp.mean(x, axis=-1, keepdims=True)
    cen = x - mean
    var = jnp.mean(cen * cen, axis=-1, keepdims=True)
    inv = lax.rsqrt(var + EPS)
    return cen * inv, inv


MESH = pl.DeviceIdType.MESH
ANY = pl.BlockSpec(memory_space=pl.ANY)


def whereabouts():
    y = lax.axis_index("dp")
    f = lax.axis_index("fsdp")
    return y, f // 4, (f // 2) % 2, f % 2


def spot(z, x, c):
    return z * 4 + x * 2 + c


def greet(signal=True, wait=True):
    y, z, x, c = whereabouts()
    barrier = pltpu.get_barrier_semaphore()
    peers = [(1 - y, spot(z, x, c)), (y, spot(z, 1 - x, c)), (y, spot(z, x, 1 - c))]
    peers += [(y, spot((z + d) % 4, x, c)) for d in (1, 2, 3)]
    if signal:
        for peer in peers:
            pl.semaphore_signal(barrier, inc=1, device_id=peer, device_id_type=MESH)
    if wait:
        pl.semaphore_wait(barrier, len(peers))


class Mover:
    def __init__(self, send, recv, local, per):
        self.send, self.recv, self.local, self.per = send, recv, local, per
        self.y, self.z, self.x, self.c = whereabouts()

    def wide(self, r, split, y):
        return pl.ds(pl.multiple_of(y * (r // 3), 8), 2 * (r // 3)) if split else pl.ds(0, r)

    def thin(self, r, y):
        return pl.ds(pl.multiple_of(y * 2 * (r // 3), 8), r // 3)

    def copy(self, u, slot, src, dst, z=None, x=None, c=None, y=None):
        i = u * self.per + slot
        pick = lambda v, own: own if v is None else v
        peer = (pick(y, self.y), spot(pick(z, self.z), pick(x, self.x), pick(c, self.c)))
        return pltpu.make_async_remote_copy(
            src_ref=src, dst_ref=dst, send_sem=self.send.at[i], recv_sem=self.recv.at[i],
            device_id=peer, device_id_type=MESH,
        )


class Gather(Mover):
    def __init__(self, units, send, recv, local):
        super().__init__(send, recv, local, 6)
        self.units = units

    def mine(self, u):
        src, _, _, col, n, split = self.units[u]
        return src.at[self.wide(src.shape[0], split, self.y), pl.ds(col, n)]

    def held(self, u):
        src, _, hold, col, n, split = self.units[u]
        return hold.at[self.wide(src.shape[0], split, self.y), pl.ds(col, n)]

    def part(self, u, z, x, c, rows):
        _, dst, _, col, n, _ = self.units[u]
        every = slice(None)
        pick = lambda v: every if v is None else v
        return dst.at[pick(z), pick(x), pick(c), rows, pl.ds(col, n)]

    def broad(self, u):
        src, _, _, _, _, split = self.units[u]
        return self.wide(src.shape[0], split, self.y)

    def load(self, u):
        return pltpu.make_async_copy(self.mine(u), self.held(u), self.local.at[2 * u])

    def store(self, u):
        dst = self.part(u, self.z, self.x, self.c, self.broad(u))
        return pltpu.make_async_copy(self.held(u), dst, self.local.at[2 * u + 1])

    def along_z(self, u, d, out=True):
        here, there = (self.z + 4 - d) % 4, (self.z + d) % 4
        dst = self.part(u, self.z if out else here, self.x, self.c, self.broad(u))
        return self.copy(u, d - 1, self.mine(u), dst, z=there)

    def along_x(self, u, out=True):
        src = self.part(u, None, self.x, self.c, self.broad(u))
        dst = src if out else self.part(u, None, 1 - self.x, self.c, self.broad(u))
        return self.copy(u, 3, src, dst, x=1 - self.x)

    def along_y(self, u, out=True):
        r = self.units[u][0].shape[0]
        src = self.part(u, None, None, self.c, self.thin(r, self.y))
        dst = src if out else self.part(u, None, None, self.c, self.thin(r, 1 - self.y))
        return self.copy(u, 4, src, dst, y=1 - self.y)

    def along_c(self, u, out=True):
        every = pl.ds(0, self.units[u][0].shape[0])
        src = self.part(u, None, None, self.c, every)
        dst = src if out else self.part(u, None, None, 1 - self.c, every)
        return self.copy(u, 5, src, dst, c=1 - self.c)

    def stage(self, s, u):
        split = self.units[u][5]
        if s == 0:
            for d in (1, 2, 3):
                self.along_z(u, d).start()
            self.load(u).start()
        if s == 1:
            self.load(u).wait()
            self.store(u).start()
        if s == 2:
            self.store(u).wait()
            for d in (1, 2, 3):
                self.along_z(u, d, False).wait_recv()
            self.along_x(u).start()
        if s == 3:
            self.along_x(u, False).wait_recv()
            if split:
                self.along_y(u).start()
            else:
                self.along_c(u).start()
        if s == 4 and split:
            self.along_y(u, False).wait_recv()
            self.along_c(u).start()
        if s == 5:
            self.along_c(u, False).wait_recv()
            for d in (1, 2, 3):
                self.along_z(u, d).wait_send()
            self.along_x(u).wait_send()
            if split:
                self.along_y(u).wait_send()
            self.along_c(u).wait_send()


def gather_sems(units):
    return [
        pltpu.SemaphoreType.DMA((units * 6,)),
        pltpu.SemaphoreType.DMA((units * 6,)),
        pltpu.SemaphoreType.DMA((2 * units,)),
    ]


def whole(shard):
    return jax.ShapeDtypeStruct((4, 2, 2, *shard.shape), shard.dtype)


class Reduce(Mover):
    def __init__(self, units, send, recv, local):
        super().__init__(send, recv, local, 7)
        self.units = units

    def size(self, u):
        return self.units[u][0].shape[3]

    def partial(self, u, c):
        src, _, (col, _), n, _, _ = self.units[u]
        return src.at[:, :, c, :, pl.ds(col, n)]

    def load(self, u):
        return pltpu.make_async_copy(self.partial(u, self.c), self.units[u][5][0], self.local.at[u])

    def over_c(self, u):
        return self.copy(u, 0, self.partial(u, 1 - self.c), self.units[u][5][1], c=1 - self.c)

    def over_y(self, u):
        own, from_y = self.units[u][5][0], self.units[u][5][5]
        return self.copy(u, 1, own.at[:, :, self.thin(self.size(u), 1 - self.y), :], from_y, y=1 - self.y)

    def over_x(self, u):
        own, from_x = self.units[u][5][0], self.units[u][5][2]
        rows = self.wide(self.size(u), self.units[u][4], self.y)
        return self.copy(u, 2, own.at[:, 1 - self.x, rows, :], from_x, x=1 - self.x)

    def over_z(self, u, d):
        own, from_z = self.units[u][5][0], self.units[u][5][3]
        rows = self.wide(self.size(u), self.units[u][4], self.y)
        to = (self.z + d) % 4
        return self.copy(u, 2 + d, own.at[to, self.x, rows, :], from_z.at[d - 1], z=to)

    def over_last(self, u):
        last = self.units[u][5][4]
        return self.copy(u, 6, last.at[0], last.at[1], y=1 - self.y)

    def stage(self, s, u):
        _, out, (_, col), n, split, (own, from_c, from_x, from_z, last, *rest) = self.units[u]
        y, z, x = self.y, self.z, self.x
        r = self.size(u)
        rows = self.wide(r, split, y)
        if s == 0:
            self.over_c(u).start()
            self.load(u).start()
        if s == 1:
            self.load(u).wait()
            self.over_c(u).wait_recv()
            own[...] = own[...] + from_c[...]
            if split:
                self.over_y(u).start()
        if s == 2:
            if split:
                self.over_y(u).wait_recv()
                mine = self.thin(r, y)
                own[:, :, mine, :] = own[:, :, mine, :] + rest[0][...]
            self.over_x(u).start()
        if s == 3:
            self.over_x(u).wait_recv()
            for k in range(4):
                own[k, x, rows, :] = own[k, x, rows, :] + from_x[k]
            for d in (1, 2, 3):
                self.over_z(u, d).start()
        if s == 4:
            total = own[z, x, rows, :].astype(F32)
            for d in (1, 2, 3):
                self.over_z(u, d).wait_recv()
                total = total + from_z[d - 1].astype(F32)
            last[0] = total.astype(last.dtype)
            self.over_last(u).start()
        if s == 5:
            self.over_last(u).wait_recv()
            cols = pl.ds(col, n)
            if split:
                t = r // 3
                at = lambda k: pl.ds(pl.multiple_of(k * t, 8), t)
                put = lambda k, v: out.__setitem__((at(k), cols), v.astype(F32))
                put(1, last[0, at(1 - y), :].astype(F32) + last[1, at(y), :].astype(F32))
                put(2 * y, last[0, at(y), :])
                put(2 * (1 - y), last[1, at(1 - y), :])
            else:
                out[:, cols] = last[0].astype(F32) + last[1].astype(F32)
        if s == 6:
            self.over_c(u).wait_send()
            if split:
                self.over_y(u).wait_send()
            self.over_x(u).wait_send()
            for d in (1, 2, 3):
                self.over_z(u, d).wait_send()
            self.over_last(u).wait_send()


def reduce_buffers(r, n, dtype, split):
    wide = 2 * r // 3 if split else r
    shapes = [(4, 2, r, n), (4, 2, r, n), (4, wide, n), (3, wide, n), (2, wide, n)]
    if split:
        shapes.append((4, 2, r // 3, n))
    return [pltpu.VMEM(shape, dtype) for shape in shapes]


def reduce_scratch(plan):
    flat = []
    for p in plan:
        flat += reduce_buffers(*p)
    units = len(plan)
    return flat + [
        pltpu.SemaphoreType.DMA((units * 7,)),
        pltpu.SemaphoreType.DMA((units * 7,)),
        pltpu.SemaphoreType.DMA((units,)),
    ]


def reduce_work(plan, places, scratch):
    units = []
    at = 0
    for (_, n, _, split), (src, out, col) in zip(plan, places):
        count = 6 if split else 5
        units.append((src, out, col, n, split, scratch[at : at + count]))
        at += count
    return Reduce(units, *scratch[at:])


def at_hook(hook, moves, work):
    for u, hooks in enumerate(moves):
        for s, when in enumerate(hooks):
            if when == hook:
                work.stage(s, u)


def hooked(step, per_step, which, steps, moves, work):
    if which == 0:

        @pl.when(step == 0)
        def _():
            greet(wait=False)

    for k in range(steps):
        if any(k * per_step + which in hooks for hooks in moves):

            @pl.when(step == k)
            def _():
                if k == 1 and which == 0:
                    greet(signal=False)
                at_hook(k * per_step + which, moves, work)


def unpack(vec_ref, ub_ref, tall_ref):
    d = vec_ref.shape[1] // 16
    f = ub_ref.shape[1] // 16
    for i in range(16):
        tile = tall_ref[i // 4, (i // 2) % 2, i % 2].astype(F32)
        vec_ref[:, i * d : (i + 1) * d] = tile[0:8, 0:d]
        ub_ref[:, i * f : i * f + 128] = tile[8:9, 0:128]
        ub_ref[:, i * f + 128 : (i + 1) * f] = tile[9:10, 0 : f - 128]


PIECES = ((0, 512), (512, 256))
FIRST_LAGS = (0, 1, 2, 4, 6, 8)


def first_body(*refs):
    vectors = refs[:9]
    t_ref, x_hbm, g_hbm = refs[9:12]
    w_hbm, vec_ref, ub_ref, qkv_hbm, ht_hbm, gt_hbm = refs[12:18]
    row_ref, tile_ref, tall_ref, vh_ref, w_ref, th_ref, x_ref, g_ref, h_ref, ht_ref, gt_ref, out_ref = refs[18:30]
    move_sem, out_sem, w_sem, *sems = refs[30:]
    rows, d = x_ref.shape
    columns = [(j, j * d + col, n) for j in range(3) for col, n in PIECES]
    units = [(tile_ref, tall_ref, vh_ref, 0, 128, False)]
    units += [(t_ref, w_ref, th_ref, col, n, True) for _, col, n in columns]
    work = Gather(units, *sems)
    moves = [[0, 1, 2, 3, 4, 5]] + [[u + lag for lag in FIRST_LAGS] for u in range(len(columns))]
    local = lambda i, src, dst: pltpu.make_async_copy(src, dst, move_sem.at[i])
    get_x, get_g = local(0, x_hbm, x_ref), local(1, g_hbm, g_ref)
    put_h, put_g = local(2, ht_ref, ht_hbm), local(3, gt_ref, gt_hbm)

    greet(wait=False)
    get_g.start()
    get_x.start()
    for i, ref in enumerate(vectors[:8]):
        row_ref[i : i + 1, 0 : ref.shape[0]] = ref[...].astype(F32).reshape(1, -1)
    up = vectors[8][...].astype(F32).reshape(1, -1)
    row_ref[8:9, :] = up[:, :128]
    row_ref[9:10, 0 : up.shape[1] - 128] = up[:, 128:]
    tile_ref[...] = row_ref[...].astype(BF16)
    greet(signal=False)
    at_hook(0, moves, work)
    get_g.wait()
    for t in range(4):
        part = slice(t * (rows // 4), (t + 1) * (rows // 4))
        gt_ref[:, part] = g_ref[part, :].T
        at_hook(1 + t, moves, work)
    put_g.start()
    get_x.wait()
    at_hook(5, moves, work)
    unpack(vec_ref, ub_ref, tall_ref)
    for t in range(4):
        part = slice(t * (rows // 4), (t + 1) * (rows // 4))
        n, _ = norm_stats(x_ref[part, :].astype(F32))
        h = (n * vec_ref[0:1, :] + vec_ref[1:2, :]).astype(BF16)
        h_ref[part, :] = h
        ht_ref[:, part] = h.T
        at_hook(6 + t, moves, work)
    put_h.start()

    def place(u):
        _, col, n = columns[u]
        return pltpu.make_async_copy(out_ref.at[u % 2, :, pl.ds(0, n)], qkv_hbm.at[:, pl.ds(col, n)], out_sem.at[u])

    def keep(u):
        _, col, n = columns[u]
        cols = pl.ds(col, n)
        return pltpu.make_async_copy(w_ref.at[:, :, :, :, cols], w_hbm.at[:, :, :, :, cols], w_sem.at[u])

    for u, (j, col, n) in enumerate(columns):
        if u:
            at_hook(9 + u, moves, work)
        keep(u).start()
        if u >= 2:
            place(u - 2).wait()
        own = slice(col - j * d, col - j * d + n)

        @pl.loop(0, 4)
        def _(t):
            part = pl.ds(pl.multiple_of(t * (rows // 4), 8), rows // 4)
            p = mm(h_ref[part, :], w_ref[:, :, :, :, col : col + n].reshape(d, n))
            if j == 0:
                p = (p + vec_ref[2:3, own]) * 0.125
            if j == 2:
                p = p + vec_ref[3:4, own]
            out_ref[u % 2, part, 0:n] = p.astype(BF16)

        place(u).start()
    put_g.wait()
    put_h.wait()
    for u in range(len(columns)):
        keep(u).wait()
        if u >= len(columns) - 2:
            place(u).wait()


def first(vectors, triple, x, g):
    rows, d = x.shape
    vmem = pl.BlockSpec(memory_space=pltpu.VMEM)
    across = pltpu.VMEM((d, rows), BF16)
    down = pltpu.VMEM((rows, d), BF16)
    pieces = 3 * len(PIECES)
    return pl.pallas_call(
        first_body,
        in_specs=[vmem] * 9 + [ANY] * 3,
        out_specs=[ANY, vmem, vmem, ANY, ANY, ANY],
        out_shape=[
            whole(triple),
            jax.ShapeDtypeStruct((8, d), F32),
            jax.ShapeDtypeStruct((1, 4 * d), F32),
            jax.ShapeDtypeStruct((rows, 3 * d), BF16),
            jax.ShapeDtypeStruct((d, rows), BF16),
            jax.ShapeDtypeStruct((d, rows), BF16),
        ],
        scratch_shapes=[
            pltpu.VMEM((16, 128), F32),
            pltpu.VMEM((16, 128), BF16),
            pltpu.VMEM((4, 2, 2, 16, 128), BF16),
            pltpu.VMEM((16, 128), BF16),
            pltpu.VMEM((4, 2, 2, *triple.shape), BF16),
            pltpu.VMEM(triple.shape, BF16),
            down,
            down,
            down,
            across,
            across,
            pltpu.VMEM((2, rows, PIECES[0][1]), BF16),
            pltpu.SemaphoreType.DMA((4,)),
            pltpu.SemaphoreType.DMA((pieces,)),
            pltpu.SemaphoreType.DMA((pieces,)),
            *gather_sems(1 + pieces),
        ],
        compiler_params=params(collective_id=0, has_side_effects=True),
        name="first",
    )(*vectors, triple, x, g)


def proj_body(x_ref, vec_ref, w_ref, qkv_ref, ht_ref):
    d = x_ref.shape[1]
    n, _ = norm_stats(x_ref[...].astype(F32))
    h = (n * vec_ref[0:1, :] + vec_ref[1:2, :]).astype(BF16)
    ht_ref[...] = h.T
    for j in range(3):
        cols = pl.ds(j * d, d)
        p = mm(h, w_ref[:, cols])
        if j == 0:
            p = (p + vec_ref[2:3, :]) * 0.125
        if j == 2:
            p = p + vec_ref[3:4, :]
        qkv_ref[:, cols] = p.astype(BF16)


def project(x, vec, w):
    rows, d = x.shape
    cols = w.shape[1]
    tile = 512
    return pl.pallas_call(
        proj_body,
        grid=(rows // tile,),
        in_specs=[
            pl.BlockSpec((tile, d), lambda i: (i, 0)),
            pl.BlockSpec((8, d), lambda i: (0, 0)),
            pl.BlockSpec((d, cols), lambda i: (0, 0)),
        ],
        out_specs=[
            pl.BlockSpec((tile, cols), lambda i: (i, 0)),
            pl.BlockSpec((d, tile), lambda i: (0, i)),
        ],
        out_shape=[jax.ShapeDtypeStruct((rows, cols), BF16), jax.ShapeDtypeStruct((d, rows), BF16)],
        compiler_params=params(),
        name="project",
        cost_estimate=pl.CostEstimate(
            flops=2 * rows * d * cols, bytes_accessed=2 * rows * (d + cols), transcendentals=0
        ),
    )(x, vec, w)


QT = 256
GATHER_LAGS = (0, 1, 3, 5, 7, 9)
REDUCE_LAGS = (0, 1, 3, 5, 7, 9, 10)


LOG2E = 1.4426950408889634


def swap(value):
    return jnp.concatenate([value[:, HD:], value[:, :HD]], axis=1)


def twice(value, own):
    return jnp.where(own, value, swap(value))


def unit_list(widths):
    units = [(0, 0, widths[0])]
    for i, w in enumerate(widths[1:]):
        units += [(i + 1, j * (w // 6), w // 6) for j in range(6)]
    return units


def attend_body(hosting, *refs):
    q_ref, k_ref, v_ref, seg_ref = refs[:4]
    if hosting:
        shards = refs[4:7]
        o_ref, p_ref, inv_ref = refs[7:10]
        full = refs[10:13]
        bias_ref, pair_ref = refs[13:15]
        hold = refs[15:18]
        units = [(shards[i], full[i], hold[i], col, n, True) for i, col, n in unit_list([s.shape[1] for s in shards])]
        work = Gather(units, *refs[18:])
        moves = [[2 + u + lag for lag in GATHER_LAGS] for u in range(len(units))]
    else:
        o_ref, p_ref, inv_ref, bias_ref, pair_ref = refs[4:]
    step = pl.program_id(0) * pl.num_programs(1) + pl.program_id(1)
    rows = q_ref.shape[0]

    @pl.when(pl.program_id(1) == 0)
    def _():
        seg = seg_ref[...].astype(F32)
        column = jnp.broadcast_to(seg, (8, rows)).T[:, 0:1]
        bias_ref[...] = jnp.where(column == seg, 0.0, -1e30)

    lower = lax.broadcasted_iota(jnp.int32, (1, 128), 1) < HD
    lower = lax.broadcasted_iota(jnp.int32, (1, 128), 1) < HD
    lower = lax.broadcasted_iota(jnp.int32, (1, 128), 1) < HD
    sums = []
    for hh in range(2):
        if hosting:
            hooked(step, 2, hh, 12, moves, work)
        own = lower if hh == 0 else ~lower
        q = q_ref[...].astype(F32) * LOG2E
        high = q.astype(BF16)
        low = (q - high.astype(F32)).astype(BF16)
        pair_ref[0, hh] = jnp.where(own, high, swap(low))
        pair_ref[1, hh] = twice(k_ref[...], own)
        pair_ref[2, hh] = jnp.where(own, v_ref[...], jnp.ones_like(v_ref[...]))
        if hh == 1:
            sums.append(mm(p_ref[0], pair_ref[2, 0]))
        for t in range(rows // QT):
            sl = pl.ds(t * QT, QT)
            s = mm(pair_ref[0, hh, sl, :], pair_ref[1, hh], NT) + bias_ref[sl, :]
            p_ref[hh, sl, :] = jnp.exp2(s - jnp.max(s, axis=-1, keepdims=True)).astype(BF16)
    sums.append(mm(p_ref[1], pair_ref[2, 1]))
    inv = 1.0 / swap(jnp.where(lower, sums[1], sums[0]))
    inv_ref[...] = inv
    o_ref[...] = (jnp.where(lower, sums[0], sums[1]) * inv).astype(BF16)


def attend(qkv, segr, shards=()):
    rows = qkv.shape[0]
    d = qkv.shape[1] // 3
    mb = rows // ROWS
    pairs = d // 128
    extra = dict(collective_id=1, has_side_effects=True) if shards else {}
    return pl.pallas_call(
        functools.partial(attend_body, bool(shards)),
        grid=(mb, pairs),
        in_specs=[
            pl.BlockSpec((ROWS, 128), lambda m, h: (m, h)),
            pl.BlockSpec((ROWS, 128), lambda m, h: (m, pairs + h)),
            pl.BlockSpec((ROWS, 128), lambda m, h: (m, 2 * pairs + h)),
            pl.BlockSpec((None, 1, ROWS), lambda m, h: (m, 0, 0)),
            *[ANY for _ in shards],
        ],
        out_specs=[
            pl.BlockSpec((ROWS, 128), lambda m, h: (m, h)),
            pl.BlockSpec((None, 2, ROWS, ROWS), lambda m, h: (m, h, 0, 0)),
            pl.BlockSpec((ROWS, 128), lambda m, h: (m, h)),
            *[ANY for _ in shards],
        ],
        out_shape=[
            jax.ShapeDtypeStruct((rows, d), BF16),
            jax.ShapeDtypeStruct((mb, 2 * pairs, ROWS, ROWS), BF16),
            jax.ShapeDtypeStruct((rows, d), F32),
            *[whole(s) for s in shards],
        ],
        scratch_shapes=[pltpu.VMEM((ROWS, ROWS), F32), pltpu.VMEM((3, 2, ROWS, 128), BF16)]
        + ([pltpu.VMEM(s.shape, s.dtype) for s in shards] + gather_sems(13) if shards else []),
        compiler_params=params(**extra),
        name="attend",
        cost_estimate=pl.CostEstimate(
            flops=mb * pairs * 2 * 4 * ROWS * ROWS * 256,
            bytes_accessed=mb * pairs * 2 * ROWS * ROWS * 2,
            transcendentals=mb * pairs * 2 * ROWS * ROWS,
        ),
    )(qkv, qkv, qkv, segr, *shards)


def attend_back_body(plan, *refs):
    q_ref, k_ref, v_ref, p_ref, o_ref, g_ref, inv_ref = refs[:7]
    hosting = plan is not None
    if hosting:
        parts = refs[7:10]
        d_ref = refs[10]
        results = refs[11:14]
        ds_ref = refs[14]
        places = [(parts[i], results[i], (col, col)) for i, col, _ in unit_list([p.shape[4] for p in parts])]
        work = reduce_work(plan, places, refs[15:])
        moves = [[2 + max(0, u - 1) + lag for lag in REDUCE_LAGS] for u in range(len(places))]
    else:
        d_ref, ds_ref = refs[7:]
    step = pl.program_id(0) * pl.num_programs(1) + pl.program_id(1)
    rows = q_ref.shape[0]
    lower = lax.broadcasted_iota(jnp.int32, (1, 128), 1) < HD
    dk_parts = []
    dv_parts = []
    dq_parts = []
    for hh in range(2):
        if hosting:
            hooked(step, 2, hh, 12, moves, work)
        own = lower if hh == 0 else ~lower
        half = slice(hh * HD, (hh + 1) * HD)
        g = g_ref[...].astype(F32) * inv_ref[...]
        high = g.astype(BF16)
        low = (g - high.astype(F32)).astype(BF16)
        pair = jnp.where(own, high, swap(low))
        center = jnp.sum(jnp.where(own, g * o_ref[...].astype(F32), 0.0), axis=-1, keepdims=True)
        v = twice(v_ref[...], own)
        for t in range(rows // QT):
            sl = pl.ds(t * QT, QT)
            ts = slice(t * QT, (t + 1) * QT)
            d_soft = mm(pair[ts, :], v, NT)
            ds_ref[hh, sl, :] = (p_ref[hh, sl, :].astype(F32) * (d_soft - center[ts, :])).astype(BF16)
        dv = mm(pair.T, p_ref[hh])
        dv_parts.append(dv[:HD, :] + dv[HD:, :])
        dk_parts.append(mm(q_ref[...].T[half, :], ds_ref[hh]))
        dq_parts.append(mm(ds_ref[hh], k_ref[...]))
    d_ref[0] = (jnp.where(lower, dq_parts[0], dq_parts[1]) * 0.125).astype(BF16)
    d_ref[1] = jnp.concatenate(dk_parts, axis=0).T.astype(BF16)
    d_ref[2] = jnp.concatenate(dv_parts, axis=0).T.astype(BF16)


def attend_back(qkv, soft, mixed, d_mixed, inv, grads=()):
    rows = qkv.shape[0]
    d = qkv.shape[1] // 3
    mb = rows // ROWS
    pairs = d // 128
    blk = pl.BlockSpec((ROWS, 128), lambda m, h: (m, h))
    plan = None
    results = []
    extra = {}
    grads = [g.reshape(4, 2, 2, g.shape[0] // 16, g.shape[1]) for g in grads]
    if grads:
        plan = [(grads[i].shape[3], n, BF16, True) for i, _, n in unit_list([g.shape[4] for g in grads])]
        results = [jax.ShapeDtypeStruct(g.shape[3:], F32) for g in grads]
        extra = dict(collective_id=2, has_side_effects=True)
    return pl.pallas_call(
        functools.partial(attend_back_body, plan),
        grid=(mb, pairs),
        in_specs=[
            blk,
            pl.BlockSpec((ROWS, 128), lambda m, h: (m, pairs + h)),
            pl.BlockSpec((ROWS, 128), lambda m, h: (m, 2 * pairs + h)),
            pl.BlockSpec((None, 2, ROWS, ROWS), lambda m, h: (m, h, 0, 0)),
            blk,
            blk,
            blk,
            *[ANY for _ in grads],
        ],
        out_specs=[
            pl.BlockSpec((3, ROWS, 128), lambda m, h: (0, m, h)),
            *[pl.BlockSpec(r.shape, lambda m, h: (0, 0)) for r in results],
        ],
        out_shape=[jax.ShapeDtypeStruct((3, rows, d), BF16), *results],
        scratch_shapes=[pltpu.VMEM((2, ROWS, ROWS), BF16)] + (reduce_scratch(plan) if grads else []),
        compiler_params=params(**extra),
        name="attend_back",
        cost_estimate=pl.CostEstimate(
            flops=mb * pairs * 2 * 8 * ROWS * ROWS * 256,
            bytes_accessed=mb * pairs * 2 * ROWS * ROWS * 2,
            transcendentals=0,
        ),
    )(qkv, qkv, qkv, soft, mixed, d_mixed, inv, *grads)


def out_body(x_ref, m_ref, w_ref, vec_ref, resid_ref, h_ref, ht_ref):
    resid = x_ref[...].astype(F32) + mm(m_ref[...], w_ref[...]) + vec_ref[4:5, :]
    resid_ref[...] = resid
    n, _ = norm_stats(resid)
    h = (n * vec_ref[5:6, :] + vec_ref[6:7, :]).astype(BF16)
    h_ref[...] = h
    ht_ref[...] = h.T


def out_project(x, mixed, w, vec):
    rows, d = x.shape
    tile = 512
    blk = pl.BlockSpec((tile, d), lambda i: (i, 0))
    return pl.pallas_call(
        out_body,
        grid=(rows // tile,),
        in_specs=[blk, blk, pl.BlockSpec((d, d), lambda i: (0, 0)), pl.BlockSpec((8, d), lambda i: (0, 0))],
        out_specs=[blk, blk, pl.BlockSpec((d, tile), lambda i: (0, i))],
        out_shape=[
            jax.ShapeDtypeStruct((rows, d), F32),
            jax.ShapeDtypeStruct((rows, d), BF16),
            jax.ShapeDtypeStruct((d, rows), BF16),
        ],
        compiler_params=params(),
        name="out_project",
        cost_estimate=pl.CostEstimate(
            flops=2 * rows * d * d, bytes_accessed=rows * d * 12, transcendentals=0
        ),
    )(x, mixed, w, vec)


FC = 512
RT = 512


def gelu_parts(u):
    cdf = 0.5 * (1.0 + lax.erf(u * ROOT_HALF))
    bell = jnp.exp(-0.5 * u * u) * ROOT_INV_TWO_PI
    return u * cdf, cdf + u * bell


def mlp_body(h_ref, ht_ref, g_ref, gt_ref, wu_ref, bu_ref, wd_ref, acc_ref, dh_ref, dwu_ref, dwd_ref, dbu_ref,
             act_ref, du_ref):
    rows = h_ref.shape[0]

    @pl.when(pl.program_id(0) == 0)
    def _():
        acc_ref[...] = jnp.zeros_like(acc_ref)
        dh_ref[...] = jnp.zeros_like(dh_ref)

    wu = wu_ref[...]
    wd = wd_ref[...]
    bias_sum = None
    for t in range(rows // RT):
        sl = pl.ds(t * RT, RT)
        u = mm(h_ref[sl, :], wu) + bu_ref[...]
        act, slope = gelu_parts(u)
        act_ref[sl, :] = act.astype(BF16)
        du = mm(g_ref[sl, :], wd, NT) * slope
        part = jnp.sum(du, axis=0, keepdims=True)
        bias_sum = part if bias_sum is None else bias_sum + part
        du_ref[sl, :] = du.astype(BF16)
        acc_ref[sl, :] += mm(act_ref[sl, :], wd)
        dh_ref[sl, :] += mm(du_ref[sl, :], wu, NT)
    dbu_ref[...] = bias_sum
    dwu_ref[...] = mm(ht_ref[...], du_ref[...]).astype(dwu_ref.dtype)
    dwd_ref[...] = mm(gt_ref[...], act_ref[...]).T.astype(dwd_ref.dtype)


def mlp(h, ht, g, gt, wu, bu, wd):
    rows, d = h.shape
    ff = wu.shape[1]
    one = pl.Buffered(1)
    whole = pl.BlockSpec((rows, d), lambda c: (0, 0), pipeline_mode=one)
    whole_t = pl.BlockSpec((d, rows), lambda c: (0, 0), pipeline_mode=one)
    return pl.pallas_call(
        mlp_body,
        grid=(ff // FC,),
        in_specs=[
            whole,
            whole_t,
            whole,
            whole_t,
            pl.BlockSpec((d, FC), lambda c: (0, c)),
            pl.BlockSpec((1, FC), lambda c: (0, c)),
            pl.BlockSpec((FC, d), lambda c: (c, 0)),
        ],
        out_specs=[
            whole,
            whole,
            pl.BlockSpec((d, FC), lambda c: (0, c)),
            pl.BlockSpec((FC, d), lambda c: (c, 0)),
            pl.BlockSpec((1, FC), lambda c: (0, c)),
        ],
        out_shape=[
            jax.ShapeDtypeStruct((rows, d), F32),
            jax.ShapeDtypeStruct((rows, d), F32),
            jax.ShapeDtypeStruct((d, ff), BF16),
            jax.ShapeDtypeStruct((ff, d), BF16),
            jax.ShapeDtypeStruct((1, ff), F32),
        ],
        scratch_shapes=[pltpu.VMEM((rows, FC), BF16), pltpu.VMEM((rows, FC), BF16)],
        compiler_params=params(),
        name="mlp",
        cost_estimate=pl.CostEstimate(
            flops=12 * rows * d * ff, bytes_accessed=rows * d * 20 + 8 * d * ff, transcendentals=3 * rows * ff
        ),
    )(h, ht, g, gt, wu, bu, wd)


def fold(ref, row, step, value):
    part = jnp.sum(value, axis=0, keepdims=True)

    @pl.when(step == 0)
    def _():
        ref[row : row + 1, :] = part

    @pl.when(step != 0)
    def _():
        ref[row : row + 1, :] += part


def norm_pull(grad, n, inv, gain):
    dn = grad * gain
    plain = jnp.mean(dn, axis=-1, keepdims=True)
    cross = jnp.mean(dn * n, axis=-1, keepdims=True)
    return inv * (dn - plain - n * cross)


def mid_body(resid_ref, acc_ref, dh_ref, g_ref, mixed_ref, w_ref, vec_ref,
             y_ref, dr_ref, dm_ref, dw_ref, dvec_ref, sum_ref):
    step = pl.program_id(0)
    resid = resid_ref[...]
    y_ref[...] = (resid + acc_ref[...] + vec_ref[7:8, :]).astype(BF16)
    g = g_ref[...].astype(F32)
    n, inv = norm_stats(resid)
    dh = dh_ref[...]
    dr = g + norm_pull(dh, n, inv, vec_ref[5:6, :])
    dr_ref[...] = dr
    fold(dvec_ref, 4, step, dr)
    fold(dvec_ref, 5, step, dh * n)
    fold(dvec_ref, 6, step, dh)
    fold(dvec_ref, 7, step, g)
    low = dr.astype(BF16)
    dm_ref[...] = mm(low, w_ref[...], NT).astype(BF16)
    dw = mm(mixed_ref[...].T, low)

    @pl.when(step == 0)
    def _():
        sum_ref[...] = dw
        dvec_ref[0:4, :] = jnp.zeros((4, dvec_ref.shape[1]), F32)

    @pl.when(step != 0)
    def _():
        sum_ref[...] += dw

    @pl.when(step == pl.num_programs(0) - 1)
    def _():
        dw_ref[...] = sum_ref[...].astype(dw_ref.dtype)


def middle(resid, acc, dh, g, mixed, w, vec):
    rows, d = resid.shape
    tile = 512
    blk = pl.BlockSpec((tile, d), lambda i: (i, 0))
    mat = pl.BlockSpec((d, d), lambda i: (0, 0))
    eight = pl.BlockSpec((8, d), lambda i: (0, 0))
    return pl.pallas_call(
        mid_body,
        grid=(rows // tile,),
        in_specs=[blk, blk, blk, blk, blk, mat, eight],
        out_specs=[blk, blk, blk, mat, eight],
        out_shape=[
            jax.ShapeDtypeStruct((rows, d), BF16),
            jax.ShapeDtypeStruct((rows, d), F32),
            jax.ShapeDtypeStruct((rows, d), BF16),
            jax.ShapeDtypeStruct((d, d), BF16),
            jax.ShapeDtypeStruct((8, d), F32),
        ],
        scratch_shapes=[pltpu.VMEM((d, d), F32)],
        compiler_params=params(),
        name="middle",
        cost_estimate=pl.CostEstimate(
            flops=4 * rows * d * d, bytes_accessed=rows * d * 24, transcendentals=0
        ),
    )(resid, acc, dh, g, mixed, w, vec)


PHASES = 3
FINAL_TILE = 256


def finish_body(plan, ht_ref, part_ref, tile_ref, x_ref, dr_ref, w_hbm, vec_ref, dvec_ref, dbu_ref, dx_ref, *refs):
    step = pl.program_id(0)
    d = x_ref.shape[1]
    if plan is None:
        dw_ref, sums_ref, w_ref, w_sem = refs
    else:
        out_ref, small_ref, w_ref, w_sem, sums_ref, grad_ref, tall_ref = refs[:7]
        places = [(grad_ref.at[j], out_ref, (col, j * d + col)) for j in range(PHASES) for col, _ in PIECES]
        places.append((tall_ref, small_ref, (0, 0)))
        work = reduce_work(plan, places, refs[7:])
        vectors = len(places) - 1
        last = vectors - 1 + len_tiles(ht_ref)
        moves = [[u + lag for lag in FINISH_LAGS] for u in range(vectors)]
        moves.append([last, last + 1, last + 1, last + 2, last + 3, last + 4, last + 5])

    fetch = pltpu.make_async_copy(w_hbm, w_ref, w_sem)

    @pl.when(step == 0)
    def _():
        if plan is not None:
            greet(wait=False)
        fetch.start()
        sums_ref[...] = dvec_ref[...]

    for i, (col, n) in enumerate(PIECES):
        for j in range(PHASES):

            @pl.when(step == j)
            def _():
                cols = pl.ds(col, n)
                dw = mm(ht_ref[...], part_ref[0, :, cols]).astype(BF16)
                if plan is None:
                    dw_ref[:, cols] = dw
                else:
                    grad_ref[j, :, :, :, :, cols] = dw.reshape(4, 2, 2, d // 16, n)
                    if i == 0 and j == 0:
                        greet(signal=False)
                    at_hook(2 * j + i, moves, work)
                if i == 1 and j != 1:
                    row = 2 if j == 0 else 3
                    sums_ref[row : row + 1, :] = jnp.sum(part_ref[0].astype(F32), axis=0, keepdims=True)

    @pl.when(step == PHASES)
    def _():
        fetch.wait()

    @pl.when(step >= PHASES)
    def _():
        n, inv = norm_stats(x_ref[...].astype(F32))
        dh = None
        for j in range(3):
            term = mm(tile_ref[j], w_ref[:, pl.ds(j * d, d)], NT)
            dh = term if dh is None else dh + term
        fold(sums_ref, 0, step - PHASES, dh * n)
        fold(sums_ref, 1, step - PHASES, dh)
        dx_ref[...] = (dr_ref[...] + norm_pull(dh, n, inv, vec_ref[0:1, :])).astype(BF16)

    if plan is not None:
        for k in range(2 * PHASES, last + 1):

            @pl.when(step == k - PHASES)
            def _():
                if k == last:
                    pack(tall_ref, sums_ref, dbu_ref)
                    for hook in range(last, 1 + max(max(m) for m in moves)):
                        at_hook(hook, moves, work)
                else:
                    at_hook(k, moves, work)


FINISH_LAGS = (0, 1, 3, 5, 7, 9, 10)


def len_tiles(ht_ref):
    return ht_ref.shape[1] // FINAL_TILE


def pack(tall_ref, sums_ref, dbu_ref):
    d = sums_ref.shape[1] // 16
    f = dbu_ref.shape[1] // 16
    for i in range(16):
        tile = tall_ref.at[i // 4, (i // 2) % 2, i % 2]
        tile[0:8, 0:d] = sums_ref[:, i * d : (i + 1) * d]
        tile[8:9, 0:128] = dbu_ref[:, i * f : i * f + 128]
        tile[9:10, 0 : f - 128] = dbu_ref[:, i * f + 128 : (i + 1) * f]


def finish(x, dr, ht, dqkv, w, vec, dvec, dbu, near):
    rows, d = x.shape
    tiles = rows // FINAL_TILE
    row = lambda s: jnp.maximum(s - PHASES, 0)
    one = pl.Buffered(1)
    eight = pl.BlockSpec((8, d), lambda s: (0, 0))
    if near:
        plan = [(d // 16, n, BF16, True) for _ in range(PHASES) for _, n in PIECES] + [(16, 128, F32, False)]
        shapes = [jax.ShapeDtypeStruct((d // 16, 3 * d), F32), jax.ShapeDtypeStruct((16, 128), F32)]
        specs = [pl.BlockSpec(s.shape, lambda s: (0, 0)) for s in shapes]
        scratch = [
            pltpu.VMEM((8, d), F32),
            pltpu.VMEM((PHASES, 4, 2, 2, d // 16, d), BF16),
            pltpu.VMEM((4, 2, 2, 16, 128), F32),
        ] + reduce_scratch(plan)
        extra = dict(collective_id=3, has_side_effects=True)
    else:
        plan = None
        shapes = [jax.ShapeDtypeStruct((d, 3 * d), BF16), jax.ShapeDtypeStruct((8, d), F32)]
        specs = [pl.BlockSpec((d, d), lambda s: (0, jnp.minimum(s, PHASES - 1))), eight]
        scratch = []
        extra = {}
    return pl.pallas_call(
        functools.partial(finish_body, plan),
        grid=(PHASES + tiles,),
        in_specs=[
            pl.BlockSpec((d, rows), lambda s: (0, 0), pipeline_mode=one),
            pl.BlockSpec((1, rows, d), lambda s: (jnp.minimum(s, PHASES - 1), 0, 0)),
            pl.BlockSpec((3, FINAL_TILE, d), lambda s: (0, row(s), 0)),
            pl.BlockSpec((FINAL_TILE, d), lambda s: (row(s), 0)),
            pl.BlockSpec((FINAL_TILE, d), lambda s: (row(s), 0)),
            ANY,
            eight,
            eight,
            pl.BlockSpec(dbu.shape, lambda s: (0, 0)),
        ],
        out_specs=[pl.BlockSpec((FINAL_TILE, d), lambda s: (row(s), 0)), *specs],
        out_shape=[jax.ShapeDtypeStruct((rows, d), BF16), *shapes],
        scratch_shapes=[pltpu.VMEM((d, 3 * d), BF16), pltpu.SemaphoreType.DMA(()), *scratch],
        compiler_params=params(**extra),
        name="finish",
        cost_estimate=pl.CostEstimate(
            flops=12 * rows * d * d, bytes_accessed=rows * d * 20, transcendentals=0
        ),
    )(ht, dqkv, dqkv, x, dr, w, vec, dvec, dbu)


def on_device(tokens, cotangent, segment_ids, *shards):
    gather = lambda s: lax.all_gather(s, "fsdp", axis=0, tiled=True)
    n = lax.axis_size("fsdp")
    near = n == 16 and lax.axis_size("dp") == 2
    triple_s, out_s, up_s, down_s = (s for s in shards if s.ndim == 2)
    rows, d = tokens.shape
    up_bias_s = shards[10]
    eights = [s for i, s in enumerate(shards) if s.ndim == 1 and i != 10]
    flat = lambda w: w.reshape(-1, w.shape[-1])
    if near:
        triple_weight, vec, up_bias, qkv, first_t, cot_t = first(eights + [up_bias_s], triple_s, tokens, cotangent)
        triple_weight = flat(triple_weight)
    else:
        triple_weight = gather(triple_s)
        packed = gather(jnp.concatenate(eights + [up_bias_s]).reshape(1, -1)).astype(F32)
        m = eights[0].shape[0]
        vec = jnp.stack([packed[:, i * m : (i + 1) * m].reshape(-1) for i in range(8)])
        up_bias = packed[:, 8 * m :].reshape(1, -1)
        qkv, first_t = project(tokens, vec, triple_weight)
        cot_t = cotangent.T

    segr = segment_ids.reshape(rows // ROWS, 1, ROWS)
    if near:
        mixed, soft, inv, *full = attend(qkv, segr, (out_s, up_s, down_s))
        out_weight, up_weight, down_weight = (flat(w) for w in full)
    else:
        mixed, soft, inv = attend(qkv, segr)
        out_weight, up_weight, down_weight = gather(out_s), gather(up_s), gather(down_s)
    resid, h, ht = out_project(tokens, mixed, out_weight, vec)
    acc, dh, dwu, dwd, dbu = mlp(h, ht, cotangent, cot_t, up_weight, up_bias, down_weight)
    y, dr, dm, dwo, dvec = middle(resid, acc, dh, cotangent, mixed, out_weight, vec)
    if near:
        dqkv, out_grad, up_grad, down_grad = attend_back(qkv, soft, mixed, dm, inv, (dwo, dwu, dwd))
        dx, triple_grad, small = finish(tokens, dr, first_t, dqkv, triple_weight, vec, dvec, dbu, True)
        m = d // n
        small_grads = [small[i, :m] for i in range(8)]
        up_bias_grad = jnp.concatenate([small[8], small[9, : up_bias_s.shape[0] - 128]])
    else:
        (dqkv,) = attend_back(qkv, soft, mixed, dm, inv)
        dx, dwt, dvec = finish(tokens, dr, first_t, dqkv, triple_weight, vec, dvec, dbu, False)
        small = jnp.concatenate([dvec[i].reshape(n, -1) for i in range(8)] + [dbu.reshape(n, -1)], axis=1)
        small = lax.psum_scatter(small, "fsdp", scatter_dimension=0, tiled=True).reshape(-1)
        small = lax.psum(small, "dp")
        total = lambda p: lax.psum(lax.psum_scatter(p, "fsdp", scatter_dimension=0, tiled=True), "dp").astype(F32)
        triple_grad, out_grad, up_grad, down_grad = total(dwt), total(dwo), total(dwu), total(dwd)
        m = d // n
        small_grads = [small[i * m : (i + 1) * m] for i in range(8)]
        up_bias_grad = small[8 * m :]
    dg1, ds1, dqb, dvb, dob, dg2, ds2, ddb = small_grads
    return (
        y, dx, dg1, ds1, triple_grad, dqb, dvb, out_grad, dob, dg2, ds2, up_grad, up_bias_grad, down_grad, ddb,
    )


def solution(mesh):
    tok = P(("dp", "fsdp"), None)
    vec = P("fsdp")
    mat = P("fsdp", None)
    weights = (vec, vec, mat, vec, vec, mat, vec, vec, vec, mat, vec, mat, vec)
    return jax.shard_map(
        on_device,
        mesh=mesh,
        in_specs=(tok, tok, P(("dp", "fsdp")), *weights),
        out_specs=(tok, tok, *weights),
        check_vma=False,
    )
```

```python
import functools

import jax
import jax.numpy as jnp
from jax import lax
from jax.experimental import pallas as pl
from jax.experimental.pallas import tpu as pltpu
from jax.sharding import PartitionSpec as P

H = 12
HD = 64
ROWS = 1024
EPS = 1e-06
F32 = jnp.float32
BF16 = jnp.bfloat16
VMEM_LIMIT = 60 * 1024 * 1024

ROOT_HALF = 0.7071067811865476
ROOT_INV_TWO_PI = 0.3989422804014327

NN = (((1,), (0,)), ((), ()))
NT = (((1,), (1,)), ((), ()))


def mm(a, b, dims=NN):
    return lax.dot_general(a, b, dims, preferred_element_type=F32)


def params(**kw):
    return pltpu.CompilerParams(vmem_limit_bytes=VMEM_LIMIT, **kw)


def norm_stats(x):
    mean = jnp.mean(x, axis=-1, keepdims=True)
    cen = x - mean
    var = jnp.mean(cen * cen, axis=-1, keepdims=True)
    inv = lax.rsqrt(var + EPS)
    return cen * inv, inv


MESH = pl.DeviceIdType.MESH
ANY = pl.BlockSpec(memory_space=pl.ANY)


def whereabouts():
    y = lax.axis_index("dp")
    f = lax.axis_index("fsdp")
    return y, f // 4, (f // 2) % 2, f % 2


def spot(z, x, c):
    return z * 4 + x * 2 + c


def greet(signal=True, wait=True):
    y, z, x, c = whereabouts()
    barrier = pltpu.get_barrier_semaphore()
    peers = [(1 - y, spot(z, x, c)), (y, spot(z, 1 - x, c)), (y, spot(z, x, 1 - c))]
    peers += [(y, spot((z + d) % 4, x, c)) for d in (1, 2, 3)]
    if signal:
        for peer in peers:
            pl.semaphore_signal(barrier, inc=1, device_id=peer, device_id_type=MESH)
    if wait:
        pl.semaphore_wait(barrier, len(peers))


class Mover:
    def __init__(self, send, recv, local, per):
        self.send, self.recv, self.local, self.per = send, recv, local, per
        self.y, self.z, self.x, self.c = whereabouts()

    def wide(self, r, split, y):
        return pl.ds(pl.multiple_of(y * (r // 3), 8), 2 * (r // 3)) if split else pl.ds(0, r)

    def thin(self, r, y):
        return pl.ds(pl.multiple_of(y * 2 * (r // 3), 8), r // 3)

    def copy(self, u, slot, src, dst, z=None, x=None, c=None, y=None):
        i = u * self.per + slot
        pick = lambda v, own: own if v is None else v
        peer = (pick(y, self.y), spot(pick(z, self.z), pick(x, self.x), pick(c, self.c)))
        return pltpu.make_async_remote_copy(
            src_ref=src, dst_ref=dst, send_sem=self.send.at[i], recv_sem=self.recv.at[i],
            device_id=peer, device_id_type=MESH,
        )


class Gather(Mover):
    def __init__(self, units, send, recv, local):
        super().__init__(send, recv, local, 6)
        self.units = units

    def mine(self, u):
        src, _, _, col, n, split = self.units[u]
        return src.at[self.wide(src.shape[0], split, self.y), pl.ds(col, n)]

    def held(self, u):
        src, _, hold, col, n, split = self.units[u]
        return hold.at[self.wide(src.shape[0], split, self.y), pl.ds(col, n)]

    def part(self, u, z, x, c, rows):
        _, dst, _, col, n, _ = self.units[u]
        every = slice(None)
        pick = lambda v: every if v is None else v
        return dst.at[pick(z), pick(x), pick(c), rows, pl.ds(col, n)]

    def broad(self, u):
        src, _, _, _, _, split = self.units[u]
        return self.wide(src.shape[0], split, self.y)

    def load(self, u):
        return pltpu.make_async_copy(self.mine(u), self.held(u), self.local.at[2 * u])

    def store(self, u):
        dst = self.part(u, self.z, self.x, self.c, self.broad(u))
        return pltpu.make_async_copy(self.held(u), dst, self.local.at[2 * u + 1])

    def along_z(self, u, d, out=True):
        here, there = (self.z + 4 - d) % 4, (self.z + d) % 4
        dst = self.part(u, self.z if out else here, self.x, self.c, self.broad(u))
        return self.copy(u, d - 1, self.mine(u), dst, z=there)

    def along_x(self, u, out=True):
        src = self.part(u, None, self.x, self.c, self.broad(u))
        dst = src if out else self.part(u, None, 1 - self.x, self.c, self.broad(u))
        return self.copy(u, 3, src, dst, x=1 - self.x)

    def along_y(self, u, out=True):
        r = self.units[u][0].shape[0]
        src = self.part(u, None, None, self.c, self.thin(r, self.y))
        dst = src if out else self.part(u, None, None, self.c, self.thin(r, 1 - self.y))
        return self.copy(u, 4, src, dst, y=1 - self.y)

    def along_c(self, u, out=True):
        every = pl.ds(0, self.units[u][0].shape[0])
        src = self.part(u, None, None, self.c, every)
        dst = src if out else self.part(u, None, None, 1 - self.c, every)
        return self.copy(u, 5, src, dst, c=1 - self.c)

    def stage(self, s, u):
        split = self.units[u][5]
        if s == 0:
            for d in (1, 2, 3):
                self.along_z(u, d).start()
            self.load(u).start()
        if s == 1:
            self.load(u).wait()
            self.store(u).start()
        if s == 2:
            self.store(u).wait()
            for d in (1, 2, 3):
                self.along_z(u, d, False).wait_recv()
            self.along_x(u).start()
        if s == 3:
            self.along_x(u, False).wait_recv()
            if split:
                self.along_y(u).start()
            else:
                self.along_c(u).start()
        if s == 4 and split:
            self.along_y(u, False).wait_recv()
            self.along_c(u).start()
        if s == 5:
            self.along_c(u, False).wait_recv()
            for d in (1, 2, 3):
                self.along_z(u, d).wait_send()
            self.along_x(u).wait_send()
            if split:
                self.along_y(u).wait_send()
            self.along_c(u).wait_send()


def gather_sems(units):
    return [
        pltpu.SemaphoreType.DMA((units * 6,)),
        pltpu.SemaphoreType.DMA((units * 6,)),
        pltpu.SemaphoreType.DMA((2 * units,)),
    ]


def whole(shard):
    return jax.ShapeDtypeStruct((4, 2, 2, *shard.shape), shard.dtype)


class Reduce(Mover):
    def __init__(self, units, send, recv, local):
        super().__init__(send, recv, local, 7)
        self.units = units

    def size(self, u):
        return self.units[u][0].shape[3]

    def partial(self, u, c):
        src, _, (col, _), n, _, _ = self.units[u]
        return src.at[:, :, c, :, pl.ds(col, n)]

    def load(self, u):
        return pltpu.make_async_copy(self.partial(u, self.c), self.units[u][5][0], self.local.at[u])

    def over_c(self, u):
        return self.copy(u, 0, self.partial(u, 1 - self.c), self.units[u][5][1], c=1 - self.c)

    def over_y(self, u):
        own, from_y = self.units[u][5][0], self.units[u][5][5]
        return self.copy(u, 1, own.at[:, :, self.thin(self.size(u), 1 - self.y), :], from_y, y=1 - self.y)

    def over_x(self, u):
        own, from_x = self.units[u][5][0], self.units[u][5][2]
        rows = self.wide(self.size(u), self.units[u][4], self.y)
        return self.copy(u, 2, own.at[:, 1 - self.x, rows, :], from_x, x=1 - self.x)

    def over_z(self, u, d):
        own, from_z = self.units[u][5][0], self.units[u][5][3]
        rows = self.wide(self.size(u), self.units[u][4], self.y)
        to = (self.z + d) % 4
        return self.copy(u, 2 + d, own.at[to, self.x, rows, :], from_z.at[d - 1], z=to)

    def over_last(self, u):
        last = self.units[u][5][4]
        return self.copy(u, 6, last.at[0], last.at[1], y=1 - self.y)

    def stage(self, s, u):
        _, out, (_, col), n, split, (own, from_c, from_x, from_z, last, *rest) = self.units[u]
        y, z, x = self.y, self.z, self.x
        r = self.size(u)
        rows = self.wide(r, split, y)
        if s == 0:
            self.over_c(u).start()
            self.load(u).start()
        if s == 1:
            self.load(u).wait()
            self.over_c(u).wait_recv()
            own[...] = own[...] + from_c[...]
            if split:
                self.over_y(u).start()
        if s == 2:
            if split:
                self.over_y(u).wait_recv()
                mine = self.thin(r, y)
                own[:, :, mine, :] = own[:, :, mine, :] + rest[0][...]
            self.over_x(u).start()
        if s == 3:
            self.over_x(u).wait_recv()
            for k in range(4):
                own[k, x, rows, :] = own[k, x, rows, :] + from_x[k]
            for d in (1, 2, 3):
                self.over_z(u, d).start()
        if s == 4:
            total = own[z, x, rows, :].astype(F32)
            for d in (1, 2, 3):
                self.over_z(u, d).wait_recv()
                total = total + from_z[d - 1].astype(F32)
            last[0] = total.astype(last.dtype)
            self.over_last(u).start()
        if s == 5:
            self.over_last(u).wait_recv()
            cols = pl.ds(col, n)
            if split:
                t = r // 3
                at = lambda k: pl.ds(pl.multiple_of(k * t, 8), t)
                put = lambda k, v: out.__setitem__((at(k), cols), v.astype(F32))
                put(1, last[0, at(1 - y), :].astype(F32) + last[1, at(y), :].astype(F32))
                put(2 * y, last[0, at(y), :])
                put(2 * (1 - y), last[1, at(1 - y), :])
            else:
                out[:, cols] = last[0].astype(F32) + last[1].astype(F32)
        if s == 6:
            self.over_c(u).wait_send()
            if split:
                self.over_y(u).wait_send()
            self.over_x(u).wait_send()
            for d in (1, 2, 3):
                self.over_z(u, d).wait_send()
            self.over_last(u).wait_send()


def reduce_buffers(r, n, dtype, split):
    wide = 2 * r // 3 if split else r
    shapes = [(4, 2, r, n), (4, 2, r, n), (4, wide, n), (3, wide, n), (2, wide, n)]
    if split:
        shapes.append((4, 2, r // 3, n))
    return [pltpu.VMEM(shape, dtype) for shape in shapes]


def reduce_scratch(plan):
    flat = []
    for p in plan:
        flat += reduce_buffers(*p)
    units = len(plan)
    return flat + [
        pltpu.SemaphoreType.DMA((units * 7,)),
        pltpu.SemaphoreType.DMA((units * 7,)),
        pltpu.SemaphoreType.DMA((units,)),
    ]


def reduce_work(plan, places, scratch):
    units = []
    at = 0
    for (_, n, _, split), (src, out, col) in zip(plan, places):
        count = 6 if split else 5
        units.append((src, out, col, n, split, scratch[at : at + count]))
        at += count
    return Reduce(units, *scratch[at:])


def at_hook(hook, moves, work, newest=False):
    for u, hooks in list(enumerate(moves))[:: -1 if newest else 1]:
        for s, when in enumerate(hooks):
            if when == hook:
                work.stage(s, u)


def hooked(step, per_step, which, steps, moves, work, late=False):
    if late and which == 0:

        @pl.when(step == 0)
        def _():
            greet(wait=False)

    for k in range(steps):
        if any(k * per_step + which in hooks for hooks in moves):

            @pl.when(step == k)
            def _():
                if which == 0 and k == late:
                    greet(signal=not late)
                at_hook(k * per_step + which, moves, work)


def unpack(vec_ref, ub_ref, tall_ref):
    d = vec_ref.shape[1] // 16
    f = ub_ref.shape[1] // 16
    for i in range(16):
        tile = tall_ref[i // 4, (i // 2) % 2, i % 2].astype(F32)
        vec_ref[:, i * d : (i + 1) * d] = tile[0:8, 0:d]
        ub_ref[:, i * f : i * f + 128] = tile[8:9, 0:128]
        ub_ref[:, i * f + 128 : (i + 1) * f] = tile[9:10, 0 : f - 128]


PIECES = ((0, 512), (512, 256))
FIRST_LAGS = (0, 1, 2, 4, 6, 8)


def first_body(*refs):
    vectors = refs[:9]
    t_ref, x_hbm, g_hbm = refs[9:12]
    w_hbm, vec_ref, ub_ref, qkv_hbm, ht_hbm, gt_hbm = refs[12:18]
    row_ref, tile_ref, tall_ref, vh_ref, w_ref, th_ref, x_ref, g_ref, h_ref, ht_ref, gt_ref, out_ref = refs[18:30]
    move_sem, out_sem, w_sem, *sems = refs[30:]
    rows, d = x_ref.shape
    columns = [(j, j * d + col, n) for j in range(3) for col, n in PIECES]
    units = [(tile_ref, tall_ref, vh_ref, 0, 128, False)]
    units += [(t_ref, w_ref, th_ref, col, n, True) for _, col, n in columns]
    work = Gather(units, *sems)
    moves = [[0, 1, 2, 3, 4, 5]] + [[u + lag for lag in FIRST_LAGS] for u in range(len(columns))]
    local = lambda i, src, dst: pltpu.make_async_copy(src, dst, move_sem.at[i])
    get_x, get_g = local(0, x_hbm, x_ref), local(1, g_hbm, g_ref)
    put_h, put_g = local(2, ht_ref, ht_hbm), local(3, gt_ref, gt_hbm)

    greet(wait=False)
    get_g.start()
    get_x.start()
    for i, ref in enumerate(vectors[:8]):
        row_ref[i : i + 1, 0 : ref.shape[0]] = ref[...].astype(F32).reshape(1, -1)
    up = vectors[8][...].astype(F32).reshape(1, -1)
    row_ref[8:9, :] = up[:, :128]
    row_ref[9:10, 0 : up.shape[1] - 128] = up[:, 128:]
    tile_ref[...] = row_ref[...].astype(BF16)
    greet(signal=False)
    at_hook(0, moves, work)
    get_g.wait()
    for t in range(4):
        part = slice(t * (rows // 4), (t + 1) * (rows // 4))
        gt_ref[:, part] = g_ref[part, :].T
        at_hook(1 + t, moves, work)
    put_g.start()
    get_x.wait()
    at_hook(5, moves, work)
    unpack(vec_ref, ub_ref, tall_ref)
    for t in range(4):
        part = slice(t * (rows // 4), (t + 1) * (rows // 4))
        n, _ = norm_stats(x_ref[part, :].astype(F32))
        h = (n * vec_ref[0:1, :] + vec_ref[1:2, :]).astype(BF16)
        h_ref[part, :] = h
        ht_ref[:, part] = h.T
        at_hook(6 + t, moves, work)
    put_h.start()

    def place(u):
        _, col, n = columns[u]
        return pltpu.make_async_copy(out_ref.at[u % 2, :, pl.ds(0, n)], qkv_hbm.at[:, pl.ds(col, n)], out_sem.at[u])

    def keep(u):
        _, col, n = columns[u]
        cols = pl.ds(col, n)
        return pltpu.make_async_copy(w_ref.at[:, :, :, :, cols], w_hbm.at[:, :, :, :, cols], w_sem.at[u])

    for u, (j, col, n) in enumerate(columns):
        if u:
            at_hook(9 + u, moves, work)
        keep(u).start()
        if u >= 2:
            place(u - 2).wait()
        own = slice(col - j * d, col - j * d + n)

        @pl.loop(0, 4)
        def _(t):
            part = pl.ds(pl.multiple_of(t * (rows // 4), 8), rows // 4)
            p = mm(h_ref[part, :], w_ref[:, :, :, :, col : col + n].reshape(d, n))
            if j == 0:
                p = (p + vec_ref[2:3, own]) * 0.125
            if j == 2:
                p = p + vec_ref[3:4, own]
            out_ref[u % 2, part, 0:n] = p.astype(BF16)

        place(u).start()
    put_g.wait()
    put_h.wait()
    for u in range(len(columns)):
        keep(u).wait()
        if u >= len(columns) - 2:
            place(u).wait()


def first(vectors, triple, x, g):
    rows, d = x.shape
    vmem = pl.BlockSpec(memory_space=pltpu.VMEM)
    across = pltpu.VMEM((d, rows), BF16)
    down = pltpu.VMEM((rows, d), BF16)
    pieces = 3 * len(PIECES)
    return pl.pallas_call(
        first_body,
        in_specs=[vmem] * 9 + [ANY] * 3,
        out_specs=[ANY, vmem, vmem, ANY, ANY, ANY],
        out_shape=[
            whole(triple),
            jax.ShapeDtypeStruct((8, d), F32),
            jax.ShapeDtypeStruct((1, 4 * d), F32),
            jax.ShapeDtypeStruct((rows, 3 * d), BF16),
            jax.ShapeDtypeStruct((d, rows), BF16),
            jax.ShapeDtypeStruct((d, rows), BF16),
        ],
        scratch_shapes=[
            pltpu.VMEM((16, 128), F32),
            pltpu.VMEM((16, 128), BF16),
            pltpu.VMEM((4, 2, 2, 16, 128), BF16),
            pltpu.VMEM((16, 128), BF16),
            pltpu.VMEM((4, 2, 2, *triple.shape), BF16),
            pltpu.VMEM(triple.shape, BF16),
            down,
            down,
            down,
            across,
            across,
            pltpu.VMEM((2, rows, PIECES[0][1]), BF16),
            pltpu.SemaphoreType.DMA((4,)),
            pltpu.SemaphoreType.DMA((pieces,)),
            pltpu.SemaphoreType.DMA((pieces,)),
            *gather_sems(1 + pieces),
        ],
        compiler_params=params(collective_id=0, has_side_effects=True),
        name="first",
    )(*vectors, triple, x, g)


def proj_body(x_ref, vec_ref, w_ref, qkv_ref, ht_ref):
    d = x_ref.shape[1]
    n, _ = norm_stats(x_ref[...].astype(F32))
    h = (n * vec_ref[0:1, :] + vec_ref[1:2, :]).astype(BF16)
    ht_ref[...] = h.T
    for j in range(3):
        cols = pl.ds(j * d, d)
        p = mm(h, w_ref[:, cols])
        if j == 0:
            p = (p + vec_ref[2:3, :]) * 0.125
        if j == 2:
            p = p + vec_ref[3:4, :]
        qkv_ref[:, cols] = p.astype(BF16)


def project(x, vec, w):
    rows, d = x.shape
    cols = w.shape[1]
    tile = 512
    return pl.pallas_call(
        proj_body,
        grid=(rows // tile,),
        in_specs=[
            pl.BlockSpec((tile, d), lambda i: (i, 0)),
            pl.BlockSpec((8, d), lambda i: (0, 0)),
            pl.BlockSpec((d, cols), lambda i: (0, 0)),
        ],
        out_specs=[
            pl.BlockSpec((tile, cols), lambda i: (i, 0)),
            pl.BlockSpec((d, tile), lambda i: (0, i)),
        ],
        out_shape=[jax.ShapeDtypeStruct((rows, cols), BF16), jax.ShapeDtypeStruct((d, rows), BF16)],
        compiler_params=params(),
        name="project",
        cost_estimate=pl.CostEstimate(
            flops=2 * rows * d * cols, bytes_accessed=2 * rows * (d + cols), transcendentals=0
        ),
    )(x, vec, w)


QT = 256
GATHER_CUT = 6
REDUCE_CUT = 3
GATHER_LAGS = (0, 1, 3, 5, 7, 9)
REDUCE_LAGS = (0, 1, 4, 7, 10, 12, 12)


LOG2E = 1.4426950408889634


def swap(value):
    return jnp.concatenate([value[:, HD:], value[:, :HD]], axis=1)


def twice(value, own):
    return jnp.where(own, value, swap(value))


def unit_list(widths, cut):
    units = [(0, 0, widths[0])]
    for i, w in enumerate(widths[1:]):
        units += [(i + 1, j * (w // cut), w // cut) for j in range(cut)]
    return units


def attend_body(hosting, *refs):
    q_ref, k_ref, v_ref, seg_ref = refs[:4]
    if hosting:
        shards = refs[4:7]
        o_ref, p_ref, inv_ref = refs[7:10]
        full = refs[10:13]
        bias_ref, pair_ref = refs[13:15]
        hold = refs[15:18]
        units = [(shards[i], full[i], hold[i], col, n, True) for i, col, n in unit_list([s.shape[1] for s in shards], GATHER_CUT)]
        work = Gather(units, *refs[18:])
        moves = [[2 + u + lag for lag in GATHER_LAGS] for u in range(len(units))]
    else:
        o_ref, p_ref, inv_ref, bias_ref, pair_ref = refs[4:]
    step = pl.program_id(0) * pl.num_programs(1) + pl.program_id(1)
    rows = q_ref.shape[0]

    @pl.when(pl.program_id(1) == 0)
    def _():
        seg = seg_ref[...].astype(F32)
        column = jnp.broadcast_to(seg, (8, rows)).T[:, 0:1]
        bias_ref[...] = jnp.where(column == seg, 0.0, -1e30)

    lower = lax.broadcasted_iota(jnp.int32, (1, 128), 1) < HD
    lower = lax.broadcasted_iota(jnp.int32, (1, 128), 1) < HD
    lower = lax.broadcasted_iota(jnp.int32, (1, 128), 1) < HD
    sums = []
    for hh in range(2):
        if hosting:
            hooked(step, 2, hh, 12, moves, work, True)
        own = lower if hh == 0 else ~lower
        q = q_ref[...].astype(F32) * LOG2E
        high = q.astype(BF16)
        low = (q - high.astype(F32)).astype(BF16)
        pair_ref[0, hh] = jnp.where(own, high, swap(low))
        pair_ref[1, hh] = twice(k_ref[...], own)
        pair_ref[2, hh] = jnp.where(own, v_ref[...], jnp.ones_like(v_ref[...]))
        if hh == 1:
            sums.append(mm(p_ref[0], pair_ref[2, 0]))
        for t in range(rows // QT):
            sl = pl.ds(t * QT, QT)
            s = mm(pair_ref[0, hh, sl, :], pair_ref[1, hh], NT) + bias_ref[sl, :]
            p_ref[hh, sl, :] = jnp.exp2(s - jnp.max(s, axis=-1, keepdims=True)).astype(BF16)
    sums.append(mm(p_ref[1], pair_ref[2, 1]))
    inv = 1.0 / swap(jnp.where(lower, sums[1], sums[0]))
    inv_ref[...] = inv
    o_ref[...] = (jnp.where(lower, sums[0], sums[1]) * inv).astype(BF16)


def attend(qkv, segr, shards=()):
    rows = qkv.shape[0]
    d = qkv.shape[1] // 3
    mb = rows // ROWS
    pairs = d // 128
    extra = dict(collective_id=1, has_side_effects=True) if shards else {}
    return pl.pallas_call(
        functools.partial(attend_body, bool(shards)),
        grid=(mb, pairs),
        in_specs=[
            pl.BlockSpec((ROWS, 128), lambda m, h: (m, h)),
            pl.BlockSpec((ROWS, 128), lambda m, h: (m, pairs + h)),
            pl.BlockSpec((ROWS, 128), lambda m, h: (m, 2 * pairs + h)),
            pl.BlockSpec((None, 1, ROWS), lambda m, h: (m, 0, 0)),
            *[ANY for _ in shards],
        ],
        out_specs=[
            pl.BlockSpec((ROWS, 128), lambda m, h: (m, h)),
            pl.BlockSpec((None, 2, ROWS, ROWS), lambda m, h: (m, h, 0, 0)),
            pl.BlockSpec((ROWS, 128), lambda m, h: (m, h)),
            *[ANY for _ in shards],
        ],
        out_shape=[
            jax.ShapeDtypeStruct((rows, d), BF16),
            jax.ShapeDtypeStruct((mb, 2 * pairs, ROWS, ROWS), BF16),
            jax.ShapeDtypeStruct((rows, d), F32),
            *[whole(s) for s in shards],
        ],
        scratch_shapes=[pltpu.VMEM((ROWS, ROWS), F32), pltpu.VMEM((3, 2, ROWS, 128), BF16)]
        + ([pltpu.VMEM(s.shape, s.dtype) for s in shards] + gather_sems(1 + 2 * GATHER_CUT) if shards else []),
        compiler_params=params(**extra),
        name="attend",
        cost_estimate=pl.CostEstimate(
            flops=mb * pairs * 2 * 4 * ROWS * ROWS * 256,
            bytes_accessed=mb * pairs * 2 * ROWS * ROWS * 2,
            transcendentals=mb * pairs * 2 * ROWS * ROWS,
        ),
    )(qkv, qkv, qkv, segr, *shards)


def attend_back_body(plan, *refs):
    q_ref, k_ref, v_ref, p_ref, o_ref, g_ref, inv_ref = refs[:7]
    hosting = plan is not None
    if hosting:
        parts = refs[7:10]
        d_ref = refs[10]
        results = refs[11:14]
        ds_ref = refs[14]
        places = [(parts[i], results[i], (col, col)) for i, col, _ in unit_list([p.shape[4] for p in parts], REDUCE_CUT)]
        work = reduce_work(plan, places, refs[15:])
        moves = [[max(0, 2 * u - 1) + lag for lag in REDUCE_LAGS] for u in range(len(places))]
    else:
        d_ref, ds_ref = refs[7:]
    step = pl.program_id(0) * pl.num_programs(1) + pl.program_id(1)
    rows = q_ref.shape[0]
    lower = lax.broadcasted_iota(jnp.int32, (1, 128), 1) < HD
    dk_parts = []
    dv_parts = []
    dq_parts = []
    for hh in range(2):
        if hosting:
            hooked(step, 2, hh, 12, moves, work)
        own = lower if hh == 0 else ~lower
        half = slice(hh * HD, (hh + 1) * HD)
        g = g_ref[...].astype(F32) * inv_ref[...]
        high = g.astype(BF16)
        low = (g - high.astype(F32)).astype(BF16)
        pair = jnp.where(own, high, swap(low))
        center = jnp.sum(jnp.where(own, g * o_ref[...].astype(F32), 0.0), axis=-1, keepdims=True)
        v = twice(v_ref[...], own)
        for t in range(rows // QT):
            sl = pl.ds(t * QT, QT)
            ts = slice(t * QT, (t + 1) * QT)
            d_soft = mm(pair[ts, :], v, NT)
            ds_ref[hh, sl, :] = (p_ref[hh, sl, :].astype(F32) * (d_soft - center[ts, :])).astype(BF16)
        dv = mm(pair.T, p_ref[hh])
        dv_parts.append(dv[:HD, :] + dv[HD:, :])
        dk_parts.append(mm(q_ref[...].T[half, :], ds_ref[hh]))
        dq_parts.append(mm(ds_ref[hh], k_ref[...]))
    d_ref[0] = (jnp.where(lower, dq_parts[0], dq_parts[1]) * 0.125).astype(BF16)
    d_ref[1] = jnp.concatenate(dk_parts, axis=0).T.astype(BF16)
    d_ref[2] = jnp.concatenate(dv_parts, axis=0).T.astype(BF16)


def attend_back(qkv, soft, mixed, d_mixed, inv, grads=()):
    rows = qkv.shape[0]
    d = qkv.shape[1] // 3
    mb = rows // ROWS
    pairs = d // 128
    blk = pl.BlockSpec((ROWS, 128), lambda m, h: (m, h))
    plan = None
    results = []
    extra = {}
    grads = [g.reshape(4, 2, 2, g.shape[0] // 16, g.shape[1]) for g in grads]
    if grads:
        plan = [(grads[i].shape[3], n, BF16, True) for i, _, n in unit_list([g.shape[4] for g in grads], REDUCE_CUT)]
        results = [jax.ShapeDtypeStruct(g.shape[3:], F32) for g in grads]
        extra = dict(collective_id=2, has_side_effects=True)
    return pl.pallas_call(
        functools.partial(attend_back_body, plan),
        grid=(mb, pairs),
        in_specs=[
            blk,
            pl.BlockSpec((ROWS, 128), lambda m, h: (m, pairs + h)),
            pl.BlockSpec((ROWS, 128), lambda m, h: (m, 2 * pairs + h)),
            pl.BlockSpec((None, 2, ROWS, ROWS), lambda m, h: (m, h, 0, 0)),
            blk,
            blk,
            blk,
            *[ANY for _ in grads],
        ],
        out_specs=[
            pl.BlockSpec((3, ROWS, 128), lambda m, h: (0, m, h)),
            *[pl.BlockSpec(r.shape, lambda m, h: (0, 0)) for r in results],
        ],
        out_shape=[jax.ShapeDtypeStruct((3, rows, d), BF16), *results],
        scratch_shapes=[pltpu.VMEM((2, ROWS, ROWS), BF16)] + (reduce_scratch(plan) if grads else []),
        compiler_params=params(**extra),
        name="attend_back",
        cost_estimate=pl.CostEstimate(
            flops=mb * pairs * 2 * 8 * ROWS * ROWS * 256,
            bytes_accessed=mb * pairs * 2 * ROWS * ROWS * 2,
            transcendentals=0,
        ),
    )(qkv, qkv, qkv, soft, mixed, d_mixed, inv, *grads)


def out_body(x_ref, m_ref, w_ref, vec_ref, resid_ref, h_ref, ht_ref):
    resid = x_ref[...].astype(F32) + mm(m_ref[...], w_ref[...]) + vec_ref[4:5, :]
    resid_ref[...] = resid
    n, _ = norm_stats(resid)
    h = (n * vec_ref[5:6, :] + vec_ref[6:7, :]).astype(BF16)
    h_ref[...] = h
    ht_ref[...] = h.T


def out_project(x, mixed, w, vec):
    rows, d = x.shape
    tile = 512
    blk = pl.BlockSpec((tile, d), lambda i: (i, 0))
    return pl.pallas_call(
        out_body,
        grid=(rows // tile,),
        in_specs=[blk, blk, pl.BlockSpec((d, d), lambda i: (0, 0)), pl.BlockSpec((8, d), lambda i: (0, 0))],
        out_specs=[blk, blk, pl.BlockSpec((d, tile), lambda i: (0, i))],
        out_shape=[
            jax.ShapeDtypeStruct((rows, d), F32),
            jax.ShapeDtypeStruct((rows, d), BF16),
            jax.ShapeDtypeStruct((d, rows), BF16),
        ],
        compiler_params=params(),
        name="out_project",
        cost_estimate=pl.CostEstimate(
            flops=2 * rows * d * d, bytes_accessed=rows * d * 12, transcendentals=0
        ),
    )(x, mixed, w, vec)


FC = 512
RT = 1024


def gelu_parts(u):
    cdf = 0.5 * (1.0 + lax.erf(u * ROOT_HALF))
    bell = jnp.exp(-0.5 * u * u) * ROOT_INV_TWO_PI
    return u * cdf, cdf + u * bell


def mlp_body(h_ref, ht_ref, g_ref, gt_ref, wu_ref, bu_ref, wd_ref, acc_ref, dh_ref, dwu_ref, dwd_ref, dbu_ref,
             act_ref, du_ref):
    rows = h_ref.shape[0]

    @pl.when(pl.program_id(0) == 0)
    def _():
        acc_ref[...] = jnp.zeros_like(acc_ref)
        dh_ref[...] = jnp.zeros_like(dh_ref)

    wu = wu_ref[...]
    wd = wd_ref[...]
    dbu_ref[...] = jnp.zeros_like(dbu_ref)

    @pl.loop(0, rows // RT)
    def _(t):
        sl = pl.ds(pl.multiple_of(t * RT, RT), RT)
        u = mm(h_ref[sl, :], wu) + bu_ref[...]
        act, slope = gelu_parts(u)
        act_ref[sl, :] = act.astype(BF16)
        du = mm(g_ref[sl, :], wd, NT) * slope
        dbu_ref[...] += jnp.sum(du, axis=0, keepdims=True)
        du_ref[sl, :] = du.astype(BF16)
        acc_ref[sl, :] += mm(act_ref[sl, :], wd)
        dh_ref[sl, :] += mm(du_ref[sl, :], wu, NT)

    dwu_ref[...] = mm(ht_ref[...], du_ref[...]).astype(dwu_ref.dtype)
    dwd_ref[...] = mm(gt_ref[...], act_ref[...]).T.astype(dwd_ref.dtype)


def mlp(h, ht, g, gt, wu, bu, wd):
    rows, d = h.shape
    ff = wu.shape[1]
    one = pl.Buffered(1)
    whole = pl.BlockSpec((rows, d), lambda c: (0, 0), pipeline_mode=one)
    whole_t = pl.BlockSpec((d, rows), lambda c: (0, 0), pipeline_mode=one)
    return pl.pallas_call(
        mlp_body,
        grid=(ff // FC,),
        in_specs=[
            whole,
            whole_t,
            whole,
            whole_t,
            pl.BlockSpec((d, FC), lambda c: (0, c)),
            pl.BlockSpec((1, FC), lambda c: (0, c)),
            pl.BlockSpec((FC, d), lambda c: (c, 0)),
        ],
        out_specs=[
            whole,
            whole,
            pl.BlockSpec((d, FC), lambda c: (0, c)),
            pl.BlockSpec((FC, d), lambda c: (c, 0)),
            pl.BlockSpec((1, FC), lambda c: (0, c)),
        ],
        out_shape=[
            jax.ShapeDtypeStruct((rows, d), F32),
            jax.ShapeDtypeStruct((rows, d), F32),
            jax.ShapeDtypeStruct((d, ff), BF16),
            jax.ShapeDtypeStruct((ff, d), BF16),
            jax.ShapeDtypeStruct((1, ff), F32),
        ],
        scratch_shapes=[pltpu.VMEM((rows, FC), BF16), pltpu.VMEM((rows, FC), BF16)],
        compiler_params=params(),
        name="mlp",
        cost_estimate=pl.CostEstimate(
            flops=12 * rows * d * ff, bytes_accessed=rows * d * 20 + 8 * d * ff, transcendentals=3 * rows * ff
        ),
    )(h, ht, g, gt, wu, bu, wd)


def fold(ref, row, step, value):
    part = jnp.sum(value, axis=0, keepdims=True)

    @pl.when(step == 0)
    def _():
        ref[row : row + 1, :] = part

    @pl.when(step != 0)
    def _():
        ref[row : row + 1, :] += part


def norm_pull(grad, n, inv, gain):
    dn = grad * gain
    plain = jnp.mean(dn, axis=-1, keepdims=True)
    cross = jnp.mean(dn * n, axis=-1, keepdims=True)
    return inv * (dn - plain - n * cross)


def mid_body(resid_ref, acc_ref, dh_ref, g_ref, mixed_ref, w_ref, vec_ref,
             y_ref, dr_ref, dm_ref, dw_ref, dvec_ref, sum_ref):
    step = pl.program_id(0)
    resid = resid_ref[...]
    y_ref[...] = (resid + acc_ref[...] + vec_ref[7:8, :]).astype(BF16)
    g = g_ref[...].astype(F32)
    n, inv = norm_stats(resid)
    dh = dh_ref[...]
    dr = g + norm_pull(dh, n, inv, vec_ref[5:6, :])
    dr_ref[...] = dr
    fold(dvec_ref, 4, step, dr)
    fold(dvec_ref, 5, step, dh * n)
    fold(dvec_ref, 6, step, dh)
    fold(dvec_ref, 7, step, g)
    low = dr.astype(BF16)
    dm_ref[...] = mm(low, w_ref[...], NT).astype(BF16)
    dw = mm(mixed_ref[...].T, low)

    @pl.when(step == 0)
    def _():
        sum_ref[...] = dw
        dvec_ref[0:4, :] = jnp.zeros((4, dvec_ref.shape[1]), F32)

    @pl.when(step != 0)
    def _():
        sum_ref[...] += dw

    @pl.when(step == pl.num_programs(0) - 1)
    def _():
        dw_ref[...] = sum_ref[...].astype(dw_ref.dtype)


def middle(resid, acc, dh, g, mixed, w, vec):
    rows, d = resid.shape
    tile = 512
    blk = pl.BlockSpec((tile, d), lambda i: (i, 0))
    mat = pl.BlockSpec((d, d), lambda i: (0, 0))
    eight = pl.BlockSpec((8, d), lambda i: (0, 0))
    return pl.pallas_call(
        mid_body,
        grid=(rows // tile,),
        in_specs=[blk, blk, blk, blk, blk, mat, eight],
        out_specs=[blk, blk, blk, mat, eight],
        out_shape=[
            jax.ShapeDtypeStruct((rows, d), BF16),
            jax.ShapeDtypeStruct((rows, d), F32),
            jax.ShapeDtypeStruct((rows, d), BF16),
            jax.ShapeDtypeStruct((d, d), BF16),
            jax.ShapeDtypeStruct((8, d), F32),
        ],
        scratch_shapes=[pltpu.VMEM((d, d), F32)],
        compiler_params=params(),
        name="middle",
        cost_estimate=pl.CostEstimate(
            flops=4 * rows * d * d, bytes_accessed=rows * d * 24, transcendentals=0
        ),
    )(resid, acc, dh, g, mixed, w, vec)


PHASES = 3
FINAL_TILE = 256


def finish_body(plan, ht_ref, part_ref, tile_ref, x_ref, dr_ref, w_hbm, vec_ref, dvec_ref, dbu_ref, dx_ref, *refs):
    step = pl.program_id(0)
    d = x_ref.shape[1]
    if plan is None:
        dw_ref, sums_ref, w_ref, w_sem = refs
    else:
        out_ref, small_ref, w_ref, w_sem, sums_ref, grad_ref, tall_ref = refs[:7]
        places = [(grad_ref.at[j], out_ref, (col, j * d + col)) for j in range(PHASES) for col, _ in PIECES]
        places.append((tall_ref, small_ref, (0, 0)))
        work = reduce_work(plan, places, refs[7:])
        vectors = len(places) - 1
        last = vectors - 1 + ht_ref.shape[1] // FINAL_TILE
        moves = FINISH_MOVES

    fetch = pltpu.make_async_copy(w_hbm, w_ref, w_sem)

    @pl.when(step == 0)
    def _():
        if plan is not None:
            greet(wait=False)
        fetch.start()
        sums_ref[...] = dvec_ref[...]

    for i, (col, n) in enumerate(PIECES):

        @pl.when(step < PHASES)
        def _():
            cols = pl.ds(col, n)
            dw = mm(ht_ref[...], part_ref[0, :, cols]).astype(BF16)
            if plan is None:
                dw_ref[:, cols] = dw
            else:
                grad_ref[step, :, :, :, :, cols] = dw.reshape(4, 2, 2, d // 16, n)

        if plan is not None:
            for j in range(PHASES):

                @pl.when(step == j)
                def _():
                    if i == 0 and j == 0:
                        greet(signal=False)
                    at_hook(2 * j + i, moves, work, True)

    for j, row in ((0, 2), (2, 3)):

        @pl.when(step == j)
        def _():
            sums_ref[row : row + 1, :] = jnp.sum(part_ref[0].astype(F32), axis=0, keepdims=True)

    @pl.when(step == PHASES)
    def _():
        fetch.wait()

    @pl.when(step >= PHASES)
    def _():
        n, inv = norm_stats(x_ref[...].astype(F32))
        dh = None
        for j in range(3):
            term = mm(tile_ref[j], w_ref[:, pl.ds(j * d, d)], NT)
            dh = term if dh is None else dh + term
        fold(sums_ref, 0, step - PHASES, dh * n)
        fold(sums_ref, 1, step - PHASES, dh)
        dx_ref[...] = (dr_ref[...] + norm_pull(dh, n, inv, vec_ref[0:1, :])).astype(BF16)

    if plan is not None:
        for k in range(2 * PHASES, last + 1):

            @pl.when(step == k - PHASES)
            def _():
                if k == last:
                    pack(tall_ref, sums_ref, dbu_ref)
                    for hook in range(last, 1 + max(max(m) for m in moves)):
                        at_hook(hook, moves, work, True)
                else:
                    at_hook(k, moves, work, True)


FINISH_MOVES = [
    [0, 1, 5, 8, 12, 14, 18],
    [1, 2, 6, 9, 12, 14, 18],
    [2, 3, 7, 10, 13, 15, 18],
    [3, 4, 8, 11, 14, 16, 18],
    [4, 5, 9, 12, 14, 16, 18],
    [5, 6, 11, 13, 15, 17, 18],
    [13, 14, 14, 15, 16, 17, 18],
]


def pack(tall_ref, sums_ref, dbu_ref):
    d = sums_ref.shape[1] // 16
    f = dbu_ref.shape[1] // 16
    for i in range(16):
        tile = tall_ref.at[i // 4, (i // 2) % 2, i % 2]
        tile[0:8, 0:d] = sums_ref[:, i * d : (i + 1) * d]
        tile[8:9, 0:128] = dbu_ref[:, i * f : i * f + 128]
        tile[9:10, 0 : f - 128] = dbu_ref[:, i * f + 128 : (i + 1) * f]


def finish(x, dr, ht, dqkv, w, vec, dvec, dbu, near):
    rows, d = x.shape
    tiles = rows // FINAL_TILE
    row = lambda s: jnp.maximum(s - PHASES, 0)
    one = pl.Buffered(1)
    eight = pl.BlockSpec((8, d), lambda s: (0, 0))
    if near:
        plan = [(d // 16, n, BF16, True) for _ in range(PHASES) for _, n in PIECES] + [(16, 128, F32, False)]
        shapes = [jax.ShapeDtypeStruct((d // 16, 3 * d), F32), jax.ShapeDtypeStruct((16, 128), F32)]
        specs = [pl.BlockSpec(s.shape, lambda s: (0, 0)) for s in shapes]
        scratch = [
            pltpu.VMEM((8, d), F32),
            pltpu.VMEM((PHASES, 4, 2, 2, d // 16, d), BF16),
            pltpu.VMEM((4, 2, 2, 16, 128), F32),
        ] + reduce_scratch(plan)
        extra = dict(collective_id=3, has_side_effects=True)
    else:
        plan = None
        shapes = [jax.ShapeDtypeStruct((d, 3 * d), BF16), jax.ShapeDtypeStruct((8, d), F32)]
        specs = [pl.BlockSpec((d, d), lambda s: (0, jnp.minimum(s, PHASES - 1))), eight]
        scratch = []
        extra = {}
    return pl.pallas_call(
        functools.partial(finish_body, plan),
        grid=(PHASES + tiles,),
        in_specs=[
            pl.BlockSpec((d, rows), lambda s: (0, 0), pipeline_mode=one),
            pl.BlockSpec((1, rows, d), lambda s: (jnp.minimum(s, PHASES - 1), 0, 0)),
            pl.BlockSpec((3, FINAL_TILE, d), lambda s: (0, row(s), 0)),
            pl.BlockSpec((FINAL_TILE, d), lambda s: (row(s), 0)),
            pl.BlockSpec((FINAL_TILE, d), lambda s: (row(s), 0)),
            ANY,
            eight,
            eight,
            pl.BlockSpec(dbu.shape, lambda s: (0, 0)),
        ],
        out_specs=[pl.BlockSpec((FINAL_TILE, d), lambda s: (row(s), 0)), *specs],
        out_shape=[jax.ShapeDtypeStruct((rows, d), BF16), *shapes],
        scratch_shapes=[pltpu.VMEM((d, 3 * d), BF16), pltpu.SemaphoreType.DMA(()), *scratch],
        compiler_params=params(**extra),
        name="finish",
        cost_estimate=pl.CostEstimate(
            flops=12 * rows * d * d, bytes_accessed=rows * d * 20, transcendentals=0
        ),
    )(ht, dqkv, dqkv, x, dr, w, vec, dvec, dbu)


def on_device(tokens, cotangent, segment_ids, *shards):
    gather = lambda s: lax.all_gather(s, "fsdp", axis=0, tiled=True)
    n = lax.axis_size("fsdp")
    near = n == 16 and lax.axis_size("dp") == 2
    triple_s, out_s, up_s, down_s = (s for s in shards if s.ndim == 2)
    rows, d = tokens.shape
    up_bias_s = shards[10]
    eights = [s for i, s in enumerate(shards) if s.ndim == 1 and i != 10]
    flat = lambda w: w.reshape(-1, w.shape[-1])
    if near:
        triple_weight, vec, up_bias, qkv, first_t, cot_t = first(eights + [up_bias_s], triple_s, tokens, cotangent)
        triple_weight = flat(triple_weight)
    else:
        triple_weight = gather(triple_s)
        packed = gather(jnp.concatenate(eights + [up_bias_s]).reshape(1, -1)).astype(F32)
        m = eights[0].shape[0]
        vec = jnp.stack([packed[:, i * m : (i + 1) * m].reshape(-1) for i in range(8)])
        up_bias = packed[:, 8 * m :].reshape(1, -1)
        qkv, first_t = project(tokens, vec, triple_weight)
        cot_t = cotangent.T

    segr = segment_ids.reshape(rows // ROWS, 1, ROWS)
    if near:
        mixed, soft, inv, *full = attend(qkv, segr, (out_s, up_s, down_s))
        out_weight, up_weight, down_weight = (flat(w) for w in full)
    else:
        mixed, soft, inv = attend(qkv, segr)
        out_weight, up_weight, down_weight = gather(out_s), gather(up_s), gather(down_s)
    resid, h, ht = out_project(tokens, mixed, out_weight, vec)
    acc, dh, dwu, dwd, dbu = mlp(h, ht, cotangent, cot_t, up_weight, up_bias, down_weight)
    y, dr, dm, dwo, dvec = middle(resid, acc, dh, cotangent, mixed, out_weight, vec)
    if near:
        dqkv, out_grad, up_grad, down_grad = attend_back(qkv, soft, mixed, dm, inv, (dwo, dwu, dwd))
        dx, triple_grad, small = finish(tokens, dr, first_t, dqkv, triple_weight, vec, dvec, dbu, True)
        m = d // n
        small_grads = [small[i, :m] for i in range(8)]
        up_bias_grad = jnp.concatenate([small[8], small[9, : up_bias_s.shape[0] - 128]])
    else:
        (dqkv,) = attend_back(qkv, soft, mixed, dm, inv)
        dx, dwt, dvec = finish(tokens, dr, first_t, dqkv, triple_weight, vec, dvec, dbu, False)
        small = jnp.concatenate([dvec[i].reshape(n, -1) for i in range(8)] + [dbu.reshape(n, -1)], axis=1)
        small = lax.psum_scatter(small, "fsdp", scatter_dimension=0, tiled=True).reshape(-1)
        small = lax.psum(small, "dp")
        total = lambda p: lax.psum(lax.psum_scatter(p, "fsdp", scatter_dimension=0, tiled=True), "dp").astype(F32)
        triple_grad, out_grad, up_grad, down_grad = total(dwt), total(dwo), total(dwu), total(dwd)
        m = d // n
        small_grads = [small[i * m : (i + 1) * m] for i in range(8)]
        up_bias_grad = small[8 * m :]
    dg1, ds1, dqb, dvb, dob, dg2, ds2, ddb = small_grads
    return (
        y, dx, dg1, ds1, triple_grad, dqb, dvb, out_grad, dob, dg2, ds2, up_grad, up_bias_grad, down_grad, ddb,
    )


def solution(mesh):
    tok = P(("dp", "fsdp"), None)
    vec = P("fsdp")
    mat = P("fsdp", None)
    weights = (vec, vec, mat, vec, vec, mat, vec, vec, vec, mat, vec, mat, vec)
    return jax.shard_map(
        on_device,
        mesh=mesh,
        in_specs=(tok, tok, P(("dp", "fsdp")), *weights),
        out_specs=(tok, tok, *weights),
        check_vma=False,
    )
```

```python
import functools

import jax
import jax.numpy as jnp
from jax import lax
from jax.experimental import pallas as pl
from jax.experimental.pallas import tpu as pltpu
from jax.sharding import PartitionSpec as P

H = 12
HD = 64
ROWS = 1024
EPS = 1e-06
F32 = jnp.float32
BF16 = jnp.bfloat16
VMEM_LIMIT = 60 * 1024 * 1024

ROOT_HALF = 0.7071067811865476
ROOT_INV_TWO_PI = 0.3989422804014327

NN = (((1,), (0,)), ((), ()))
NT = (((1,), (1,)), ((), ()))


def mm(a, b, dims=NN):
    return lax.dot_general(a, b, dims, preferred_element_type=F32)


def params(**kw):
    return pltpu.CompilerParams(vmem_limit_bytes=VMEM_LIMIT, **kw)


def norm_stats(x):
    mean = jnp.mean(x, axis=-1, keepdims=True)
    cen = x - mean
    var = jnp.mean(cen * cen, axis=-1, keepdims=True)
    inv = lax.rsqrt(var + EPS)
    return cen * inv, inv


MESH = pl.DeviceIdType.MESH
ANY = pl.BlockSpec(memory_space=pl.ANY)


def whereabouts():
    y = lax.axis_index("dp")
    f = lax.axis_index("fsdp")
    return y, f // 4, (f // 2) % 2, f % 2


def spot(z, x, c):
    return z * 4 + x * 2 + c


def greet(signal=True, wait=True):
    y, z, x, c = whereabouts()
    barrier = pltpu.get_barrier_semaphore()
    peers = [(1 - y, spot(z, x, c)), (y, spot(z, 1 - x, c)), (y, spot(z, x, 1 - c))]
    peers += [(y, spot((z + d) % 4, x, c)) for d in (1, 2, 3)]
    if signal:
        for peer in peers:
            pl.semaphore_signal(barrier, inc=1, device_id=peer, device_id_type=MESH)
    if wait:
        pl.semaphore_wait(barrier, len(peers))


class Mover:
    def __init__(self, send, recv, local, per):
        self.send, self.recv, self.local, self.per = send, recv, local, per
        self.y, self.z, self.x, self.c = whereabouts()

    def wide(self, r, split, y):
        return pl.ds(pl.multiple_of(y * (r // 3), 8), 2 * (r // 3)) if split else pl.ds(0, r)

    def thin(self, r, y):
        return pl.ds(pl.multiple_of(y * 2 * (r // 3), 8), r // 3)

    def copy(self, u, slot, src, dst, z=None, x=None, c=None, y=None):
        i = u * self.per + slot
        pick = lambda v, own: own if v is None else v
        peer = (pick(y, self.y), spot(pick(z, self.z), pick(x, self.x), pick(c, self.c)))
        return pltpu.make_async_remote_copy(
            src_ref=src, dst_ref=dst, send_sem=self.send.at[i], recv_sem=self.recv.at[i],
            device_id=peer, device_id_type=MESH,
        )


class Gather(Mover):
    def __init__(self, units, send, recv, local):
        super().__init__(send, recv, local, 6)
        self.units = units

    def mine(self, u):
        src, _, _, col, n, split = self.units[u]
        return src.at[self.wide(src.shape[0], split, self.y), pl.ds(col, n)]

    def held(self, u):
        src, _, hold, col, n, split = self.units[u]
        return hold.at[self.wide(src.shape[0], split, self.y), pl.ds(col, n)]

    def part(self, u, z, x, c, rows):
        _, dst, _, col, n, _ = self.units[u]
        every = slice(None)
        pick = lambda v: every if v is None else v
        return dst.at[pick(z), pick(x), pick(c), rows, pl.ds(col, n)]

    def broad(self, u):
        src, _, _, _, _, split = self.units[u]
        return self.wide(src.shape[0], split, self.y)

    def load(self, u):
        return pltpu.make_async_copy(self.mine(u), self.held(u), self.local.at[2 * u])

    def store(self, u):
        dst = self.part(u, self.z, self.x, self.c, self.broad(u))
        return pltpu.make_async_copy(self.held(u), dst, self.local.at[2 * u + 1])

    def along_z(self, u, d, out=True):
        here, there = (self.z + 4 - d) % 4, (self.z + d) % 4
        dst = self.part(u, self.z if out else here, self.x, self.c, self.broad(u))
        return self.copy(u, d - 1, self.mine(u), dst, z=there)

    def along_x(self, u, out=True):
        src = self.part(u, None, self.x, self.c, self.broad(u))
        dst = src if out else self.part(u, None, 1 - self.x, self.c, self.broad(u))
        return self.copy(u, 3, src, dst, x=1 - self.x)

    def along_y(self, u, out=True):
        r = self.units[u][0].shape[0]
        src = self.part(u, None, None, self.c, self.thin(r, self.y))
        dst = src if out else self.part(u, None, None, self.c, self.thin(r, 1 - self.y))
        return self.copy(u, 4, src, dst, y=1 - self.y)

    def along_c(self, u, out=True):
        every = pl.ds(0, self.units[u][0].shape[0])
        src = self.part(u, None, None, self.c, every)
        dst = src if out else self.part(u, None, None, 1 - self.c, every)
        return self.copy(u, 5, src, dst, c=1 - self.c)

    def stage(self, s, u):
        split = self.units[u][5]
        if s == 0:
            for d in (1, 2, 3):
                self.along_z(u, d).start()
            self.load(u).start()
        if s == 1:
            self.load(u).wait()
            self.store(u).start()
        if s == 2:
            self.store(u).wait()
            for d in (1, 2, 3):
                self.along_z(u, d, False).wait_recv()
            self.along_x(u).start()
        if s == 3:
            self.along_x(u, False).wait_recv()
            if split:
                self.along_y(u).start()
            else:
                self.along_c(u).start()
        if s == 4 and split:
            self.along_y(u, False).wait_recv()
            self.along_c(u).start()
        if s == 5:
            self.along_c(u, False).wait_recv()
            for d in (1, 2, 3):
                self.along_z(u, d).wait_send()
            self.along_x(u).wait_send()
            if split:
                self.along_y(u).wait_send()
            self.along_c(u).wait_send()


def gather_sems(units):
    return [
        pltpu.SemaphoreType.DMA((units * 6,)),
        pltpu.SemaphoreType.DMA((units * 6,)),
        pltpu.SemaphoreType.DMA((2 * units,)),
    ]


def whole(shard):
    return jax.ShapeDtypeStruct((4, 2, 2, *shard.shape), shard.dtype)


class Reduce(Mover):
    def __init__(self, units, send, recv, local):
        super().__init__(send, recv, local, 7)
        self.units = units

    def size(self, u):
        return self.units[u][0].shape[3]

    def partial(self, u, c):
        src, _, (col, _), n, _, _ = self.units[u]
        return src.at[:, :, c, :, pl.ds(col, n)]

    def load(self, u):
        return pltpu.make_async_copy(self.partial(u, self.c), self.units[u][5][0], self.local.at[u])

    def over_c(self, u):
        return self.copy(u, 0, self.partial(u, 1 - self.c), self.units[u][5][1], c=1 - self.c)

    def over_y(self, u):
        own, from_y = self.units[u][5][0], self.units[u][5][5]
        return self.copy(u, 1, own.at[:, :, self.thin(self.size(u), 1 - self.y), :], from_y, y=1 - self.y)

    def over_x(self, u):
        own, from_x = self.units[u][5][0], self.units[u][5][2]
        rows = self.wide(self.size(u), self.units[u][4], self.y)
        return self.copy(u, 2, own.at[:, 1 - self.x, rows, :], from_x, x=1 - self.x)

    def over_z(self, u, d):
        own, from_z = self.units[u][5][0], self.units[u][5][3]
        rows = self.wide(self.size(u), self.units[u][4], self.y)
        to = (self.z + d) % 4
        return self.copy(u, 2 + d, own.at[to, self.x, rows, :], from_z.at[d - 1], z=to)

    def over_last(self, u):
        last = self.units[u][5][4]
        return self.copy(u, 6, last.at[0], last.at[1], y=1 - self.y)

    def stage(self, s, u):
        _, out, (_, col), n, split, (own, from_c, from_x, from_z, last, *rest) = self.units[u]
        y, z, x = self.y, self.z, self.x
        r = self.size(u)
        rows = self.wide(r, split, y)
        if s == 0:
            self.over_c(u).start()
            self.load(u).start()
        if s == 1:
            self.load(u).wait()
            self.over_c(u).wait_recv()
            own[...] = own[...] + from_c[...]
            if split:
                self.over_y(u).start()
        if s == 2:
            if split:
                self.over_y(u).wait_recv()
                mine = self.thin(r, y)
                own[:, :, mine, :] = own[:, :, mine, :] + rest[0][...]
            self.over_x(u).start()
        if s == 3:
            self.over_x(u).wait_recv()
            for k in range(4):
                own[k, x, rows, :] = own[k, x, rows, :] + from_x[k]
            for d in (1, 2, 3):
                self.over_z(u, d).start()
        if s == 4:
            total = own[z, x, rows, :].astype(F32)
            for d in (1, 2, 3):
                self.over_z(u, d).wait_recv()
                total = total + from_z[d - 1].astype(F32)
            last[0] = total.astype(last.dtype)
            self.over_last(u).start()
        if s == 5:
            self.over_last(u).wait_recv()
            cols = pl.ds(col, n)
            if split:
                t = r // 3
                at = lambda k: pl.ds(pl.multiple_of(k * t, 8), t)
                put = lambda k, v: out.__setitem__((at(k), cols), v.astype(F32))
                put(1, last[0, at(1 - y), :].astype(F32) + last[1, at(y), :].astype(F32))
                put(2 * y, last[0, at(y), :])
                put(2 * (1 - y), last[1, at(1 - y), :])
            else:
                out[:, cols] = last[0].astype(F32) + last[1].astype(F32)
        if s == 6:
            self.over_c(u).wait_send()
            if split:
                self.over_y(u).wait_send()
            self.over_x(u).wait_send()
            for d in (1, 2, 3):
                self.over_z(u, d).wait_send()
            self.over_last(u).wait_send()


def reduce_buffers(r, n, dtype, split):
    wide = 2 * r // 3 if split else r
    shapes = [(4, 2, r, n), (4, 2, r, n), (4, wide, n), (3, wide, n), (2, wide, n)]
    if split:
        shapes.append((4, 2, r // 3, n))
    return [pltpu.VMEM(shape, dtype) for shape in shapes]


def reduce_scratch(plan):
    flat = []
    for p in plan:
        flat += reduce_buffers(*p)
    units = len(plan)
    return flat + [
        pltpu.SemaphoreType.DMA((units * 7,)),
        pltpu.SemaphoreType.DMA((units * 7,)),
        pltpu.SemaphoreType.DMA((units,)),
    ]


def reduce_work(plan, places, scratch):
    units = []
    at = 0
    for (_, n, _, split), (src, out, col) in zip(plan, places):
        count = 6 if split else 5
        units.append((src, out, col, n, split, scratch[at : at + count]))
        at += count
    return Reduce(units, *scratch[at:])


def at_hook(hook, moves, work, newest=False):
    for u, hooks in list(enumerate(moves))[:: -1 if newest else 1]:
        for s, when in enumerate(hooks):
            if when == hook:
                work.stage(s, u)


def hooked(step, per_step, which, steps, moves, work, late=False):
    if late and which == 0:

        @pl.when(step == 0)
        def _():
            greet(wait=False)

    for k in range(steps):
        if any(k * per_step + which in hooks for hooks in moves):

            @pl.when(step == k)
            def _():
                if which == 0 and k == late:
                    greet(signal=not late)
                at_hook(k * per_step + which, moves, work)


def unpack(vec_ref, ub_ref, tall_ref):
    d = vec_ref.shape[1] // 16
    f = ub_ref.shape[1] // 16
    for i in range(16):
        tile = tall_ref[i // 4, (i // 2) % 2, i % 2].astype(F32)
        vec_ref[:, i * d : (i + 1) * d] = tile[0:8, 0:d]
        ub_ref[:, i * f : i * f + 128] = tile[8:9, 0:128]
        ub_ref[:, i * f + 128 : (i + 1) * f] = tile[9:10, 0 : f - 128]


PIECES = ((0, 512), (512, 256))
FIRST_LAGS = (0, 1, 2, 4, 6, 8)


def first_body(*refs):
    vectors = refs[:9]
    t_ref, x_hbm, g_hbm = refs[9:12]
    w_hbm, vec_ref, ub_ref, qkv_hbm, ht_hbm, gt_hbm = refs[12:18]
    row_ref, tile_ref, tall_ref, vh_ref, w_ref, th_ref, x_ref, g_ref, h_ref, ht_ref, gt_ref, out_ref = refs[18:30]
    move_sem, out_sem, w_sem, *sems = refs[30:]
    rows, d = x_ref.shape
    columns = [(j, j * d + col, n) for j in range(3) for col, n in PIECES]
    units = [(tile_ref, tall_ref, vh_ref, 0, 128, False)]
    units += [(t_ref, w_ref, th_ref, col, n, True) for _, col, n in columns]
    work = Gather(units, *sems)
    moves = [[0, 1, 2, 3, 4, 5]] + [[u + lag for lag in FIRST_LAGS] for u in range(len(columns))]
    local = lambda i, src, dst: pltpu.make_async_copy(src, dst, move_sem.at[i])
    get_x, get_g = local(0, x_hbm, x_ref), local(1, g_hbm, g_ref)
    put_h, put_g = local(2, ht_ref, ht_hbm), local(3, gt_ref, gt_hbm)

    greet(wait=False)
    get_g.start()
    get_x.start()
    for i, ref in enumerate(vectors[:8]):
        row_ref[i : i + 1, 0 : ref.shape[0]] = ref[...].astype(F32).reshape(1, -1)
    up = vectors[8][...].astype(F32).reshape(1, -1)
    row_ref[8:9, :] = up[:, :128]
    row_ref[9:10, 0 : up.shape[1] - 128] = up[:, 128:]
    tile_ref[...] = row_ref[...].astype(BF16)
    greet(signal=False)
    at_hook(0, moves, work)
    get_g.wait()
    for t in range(4):
        part = slice(t * (rows // 4), (t + 1) * (rows // 4))
        gt_ref[:, part] = g_ref[part, :].T
        at_hook(1 + t, moves, work)
    put_g.start()
    get_x.wait()
    at_hook(5, moves, work)
    unpack(vec_ref, ub_ref, tall_ref)
    for t in range(4):
        part = slice(t * (rows // 4), (t + 1) * (rows // 4))
        n, _ = norm_stats(x_ref[part, :].astype(F32))
        h = (n * vec_ref[0:1, :] + vec_ref[1:2, :]).astype(BF16)
        h_ref[part, :] = h
        ht_ref[:, part] = h.T
        at_hook(6 + t, moves, work)
    put_h.start()

    def place(u):
        _, col, n = columns[u]
        return pltpu.make_async_copy(out_ref.at[u % 2, :, pl.ds(0, n)], qkv_hbm.at[:, pl.ds(col, n)], out_sem.at[u])

    def keep(u):
        _, col, n = columns[u]
        cols = pl.ds(col, n)
        return pltpu.make_async_copy(w_ref.at[:, :, :, :, cols], w_hbm.at[:, :, :, :, cols], w_sem.at[u])

    for u, (j, col, n) in enumerate(columns):
        if u:
            at_hook(9 + u, moves, work)
        keep(u).start()
        if u >= 2:
            place(u - 2).wait()
        own = slice(col - j * d, col - j * d + n)

        @pl.loop(0, 4)
        def _(t):
            part = pl.ds(pl.multiple_of(t * (rows // 4), 8), rows // 4)
            p = mm(h_ref[part, :], w_ref[:, :, :, :, col : col + n].reshape(d, n))
            if j == 0:
                p = (p + vec_ref[2:3, own]) * 0.125
            if j == 2:
                p = p + vec_ref[3:4, own]
            out_ref[u % 2, part, 0:n] = p.astype(BF16)

        place(u).start()
    put_g.wait()
    put_h.wait()
    for u in range(len(columns)):
        keep(u).wait()
        if u >= len(columns) - 2:
            place(u).wait()


def first(vectors, triple, x, g):
    rows, d = x.shape
    vmem = pl.BlockSpec(memory_space=pltpu.VMEM)
    across = pltpu.VMEM((d, rows), BF16)
    down = pltpu.VMEM((rows, d), BF16)
    pieces = 3 * len(PIECES)
    return pl.pallas_call(
        first_body,
        in_specs=[vmem] * 9 + [ANY] * 3,
        out_specs=[ANY, vmem, vmem, ANY, ANY, ANY],
        out_shape=[
            whole(triple),
            jax.ShapeDtypeStruct((8, d), F32),
            jax.ShapeDtypeStruct((1, 4 * d), F32),
            jax.ShapeDtypeStruct((rows, 3 * d), BF16),
            jax.ShapeDtypeStruct((d, rows), BF16),
            jax.ShapeDtypeStruct((d, rows), BF16),
        ],
        scratch_shapes=[
            pltpu.VMEM((16, 128), F32),
            pltpu.VMEM((16, 128), BF16),
            pltpu.VMEM((4, 2, 2, 16, 128), BF16),
            pltpu.VMEM((16, 128), BF16),
            pltpu.VMEM((4, 2, 2, *triple.shape), BF16),
            pltpu.VMEM(triple.shape, BF16),
            down,
            down,
            down,
            across,
            across,
            pltpu.VMEM((2, rows, PIECES[0][1]), BF16),
            pltpu.SemaphoreType.DMA((4,)),
            pltpu.SemaphoreType.DMA((pieces,)),
            pltpu.SemaphoreType.DMA((pieces,)),
            *gather_sems(1 + pieces),
        ],
        compiler_params=params(collective_id=0, has_side_effects=True),
        name="first",
    )(*vectors, triple, x, g)


def proj_body(x_ref, vec_ref, w_ref, qkv_ref, ht_ref):
    d = x_ref.shape[1]
    n, _ = norm_stats(x_ref[...].astype(F32))
    h = (n * vec_ref[0:1, :] + vec_ref[1:2, :]).astype(BF16)
    ht_ref[...] = h.T
    for j in range(3):
        cols = pl.ds(j * d, d)
        p = mm(h, w_ref[:, cols])
        if j == 0:
            p = (p + vec_ref[2:3, :]) * 0.125
        if j == 2:
            p = p + vec_ref[3:4, :]
        qkv_ref[:, cols] = p.astype(BF16)


def project(x, vec, w):
    rows, d = x.shape
    cols = w.shape[1]
    tile = 512
    return pl.pallas_call(
        proj_body,
        grid=(rows // tile,),
        in_specs=[
            pl.BlockSpec((tile, d), lambda i: (i, 0)),
            pl.BlockSpec((8, d), lambda i: (0, 0)),
            pl.BlockSpec((d, cols), lambda i: (0, 0)),
        ],
        out_specs=[
            pl.BlockSpec((tile, cols), lambda i: (i, 0)),
            pl.BlockSpec((d, tile), lambda i: (0, i)),
        ],
        out_shape=[jax.ShapeDtypeStruct((rows, cols), BF16), jax.ShapeDtypeStruct((d, rows), BF16)],
        compiler_params=params(),
        name="project",
        cost_estimate=pl.CostEstimate(
            flops=2 * rows * d * cols, bytes_accessed=2 * rows * (d + cols), transcendentals=0
        ),
    )(x, vec, w)


QT = 256
GATHER_CUT = (2, 8, 6)
REDUCE_CUT = (1, 3, 3)
GATHER_LAGS = (0, 1, 2, 4, 6, 8)
REDUCE_LAGS = (0, 1, 4, 7, 10, 12, 12)


LOG2E = 1.4426950408889634


def swap(value):
    return jnp.concatenate([value[:, HD:], value[:, :HD]], axis=1)


def twice(value, own):
    return jnp.where(own, value, swap(value))


def unit_list(widths, cuts):
    return [(i, j * (w // cut), w // cut) for i, (w, cut) in enumerate(zip(widths, cuts)) for j in range(cut)]


def attend_body(hosting, *refs):
    q_ref, k_ref, v_ref, seg_ref = refs[:4]
    if hosting:
        shards = refs[4:7]
        o_ref, p_ref, inv_ref = refs[7:10]
        full = refs[10:13]
        bias_ref, pair_ref = refs[13:15]
        hold = refs[15:18]
        units = [(shards[i], full[i], hold[i], col, n, True) for i, col, n in unit_list([s.shape[1] for s in shards], GATHER_CUT)]
        work = Gather(units, *refs[18:])
        moves = [[u + lag for lag in GATHER_LAGS] for u in range(len(units))]
    else:
        o_ref, p_ref, inv_ref, bias_ref, pair_ref = refs[4:]
    step = pl.program_id(0) * pl.num_programs(1) + pl.program_id(1)
    rows = q_ref.shape[0]

    @pl.when(pl.program_id(1) == 0)
    def _():
        seg = seg_ref[...].astype(F32)
        column = jnp.broadcast_to(seg, (8, rows)).T[:, 0:1]
        bias_ref[...] = jnp.where(column == seg, 0.0, -1e30)

    lower = lax.broadcasted_iota(jnp.int32, (1, 128), 1) < HD
    lower = lax.broadcasted_iota(jnp.int32, (1, 128), 1) < HD
    lower = lax.broadcasted_iota(jnp.int32, (1, 128), 1) < HD
    sums = []
    for hh in range(2):
        if hosting:
            hooked(step, 2, hh, 12, moves, work)
        own = lower if hh == 0 else ~lower
        q = q_ref[...].astype(F32) * LOG2E
        high = q.astype(BF16)
        low = (q - high.astype(F32)).astype(BF16)
        pair_ref[0, hh] = jnp.where(own, high, swap(low))
        pair_ref[1, hh] = twice(k_ref[...], own)
        pair_ref[2, hh] = jnp.where(own, v_ref[...], jnp.ones_like(v_ref[...]))
        if hh == 1:
            sums.append(mm(p_ref[0], pair_ref[2, 0]))
        for t in range(rows // QT):
            sl = pl.ds(t * QT, QT)
            s = mm(pair_ref[0, hh, sl, :], pair_ref[1, hh], NT) + bias_ref[sl, :]
            p_ref[hh, sl, :] = jnp.exp2(s - jnp.max(s, axis=-1, keepdims=True)).astype(BF16)
    sums.append(mm(p_ref[1], pair_ref[2, 1]))
    inv = 1.0 / swap(jnp.where(lower, sums[1], sums[0]))
    inv_ref[...] = inv
    o_ref[...] = (jnp.where(lower, sums[0], sums[1]) * inv).astype(BF16)


def attend(qkv, segr, shards=()):
    rows = qkv.shape[0]
    d = qkv.shape[1] // 3
    mb = rows // ROWS
    pairs = d // 128
    extra = dict(collective_id=1, has_side_effects=True) if shards else {}
    return pl.pallas_call(
        functools.partial(attend_body, bool(shards)),
        grid=(mb, pairs),
        in_specs=[
            pl.BlockSpec((ROWS, 128), lambda m, h: (m, h)),
            pl.BlockSpec((ROWS, 128), lambda m, h: (m, pairs + h)),
            pl.BlockSpec((ROWS, 128), lambda m, h: (m, 2 * pairs + h)),
            pl.BlockSpec((None, 1, ROWS), lambda m, h: (m, 0, 0)),
            *[ANY for _ in shards],
        ],
        out_specs=[
            pl.BlockSpec((ROWS, 128), lambda m, h: (m, h)),
            pl.BlockSpec((None, 2, ROWS, ROWS), lambda m, h: (m, h, 0, 0)),
            pl.BlockSpec((ROWS, 128), lambda m, h: (m, h)),
            *[ANY for _ in shards],
        ],
        out_shape=[
            jax.ShapeDtypeStruct((rows, d), BF16),
            jax.ShapeDtypeStruct((mb, 2 * pairs, ROWS, ROWS), BF16),
            jax.ShapeDtypeStruct((rows, d), F32),
            *[whole(s) for s in shards],
        ],
        scratch_shapes=[pltpu.VMEM((ROWS, ROWS), F32), pltpu.VMEM((3, 2, ROWS, 128), BF16)]
        + ([pltpu.VMEM(s.shape, s.dtype) for s in shards] + gather_sems(sum(GATHER_CUT)) if shards else []),
        compiler_params=params(**extra),
        name="attend",
        cost_estimate=pl.CostEstimate(
            flops=mb * pairs * 2 * 4 * ROWS * ROWS * 256,
            bytes_accessed=mb * pairs * 2 * ROWS * ROWS * 2,
            transcendentals=mb * pairs * 2 * ROWS * ROWS,
        ),
    )(qkv, qkv, qkv, segr, *shards)


def attend_back_body(plan, *refs):
    q_ref, k_ref, v_ref, p_ref, o_ref, g_ref, inv_ref = refs[:7]
    hosting = plan is not None
    if hosting:
        parts = refs[7:10]
        d_ref = refs[10]
        results = refs[11:14]
        ds_ref = refs[14]
        places = [(parts[i], results[i], (col, col)) for i, col, _ in unit_list([p.shape[4] for p in parts], REDUCE_CUT)]
        work = reduce_work(plan, places, refs[15:])
        moves = [[max(0, 2 * u - 1) + lag for lag in REDUCE_LAGS] for u in range(len(places))]
    else:
        d_ref, ds_ref = refs[7:]
    step = pl.program_id(0) * pl.num_programs(1) + pl.program_id(1)
    rows = q_ref.shape[0]
    lower = lax.broadcasted_iota(jnp.int32, (1, 128), 1) < HD
    dk_parts = []
    dv_parts = []
    dq_parts = []
    for hh in range(2):
        if hosting:
            hooked(step, 2, hh, 12, moves, work)
        own = lower if hh == 0 else ~lower
        half = slice(hh * HD, (hh + 1) * HD)
        g = g_ref[...].astype(F32) * inv_ref[...]
        high = g.astype(BF16)
        low = (g - high.astype(F32)).astype(BF16)
        pair = jnp.where(own, high, swap(low))
        center = jnp.sum(jnp.where(own, g * o_ref[...].astype(F32), 0.0), axis=-1, keepdims=True)
        v = twice(v_ref[...], own)
        for t in range(rows // QT):
            sl = pl.ds(t * QT, QT)
            ts = slice(t * QT, (t + 1) * QT)
            d_soft = mm(pair[ts, :], v, NT)
            ds_ref[hh, sl, :] = (p_ref[hh, sl, :].astype(F32) * (d_soft - center[ts, :])).astype(BF16)
        dv = mm(pair.T, p_ref[hh])
        dv_parts.append(dv[:HD, :] + dv[HD:, :])
        dk_parts.append(mm(q_ref[...].T[half, :], ds_ref[hh]))
        dq_parts.append(mm(ds_ref[hh], k_ref[...]))
    d_ref[0] = (jnp.where(lower, dq_parts[0], dq_parts[1]) * 0.125).astype(BF16)
    d_ref[1] = jnp.concatenate(dk_parts, axis=0).T.astype(BF16)
    d_ref[2] = jnp.concatenate(dv_parts, axis=0).T.astype(BF16)


def attend_back(qkv, soft, mixed, d_mixed, inv, grads=()):
    rows = qkv.shape[0]
    d = qkv.shape[1] // 3
    mb = rows // ROWS
    pairs = d // 128
    blk = pl.BlockSpec((ROWS, 128), lambda m, h: (m, h))
    plan = None
    results = []
    extra = {}
    grads = [g.reshape(4, 2, 2, g.shape[0] // 16, g.shape[1]) for g in grads]
    if grads:
        plan = [(grads[i].shape[3], n, BF16, True) for i, _, n in unit_list([g.shape[4] for g in grads], REDUCE_CUT)]
        results = [jax.ShapeDtypeStruct(g.shape[3:], F32) for g in grads]
        extra = dict(collective_id=2, has_side_effects=True)
    return pl.pallas_call(
        functools.partial(attend_back_body, plan),
        grid=(mb, pairs),
        in_specs=[
            blk,
            pl.BlockSpec((ROWS, 128), lambda m, h: (m, pairs + h)),
            pl.BlockSpec((ROWS, 128), lambda m, h: (m, 2 * pairs + h)),
            pl.BlockSpec((None, 2, ROWS, ROWS), lambda m, h: (m, h, 0, 0)),
            blk,
            blk,
            blk,
            *[ANY for _ in grads],
        ],
        out_specs=[
            pl.BlockSpec((3, ROWS, 128), lambda m, h: (0, m, h)),
            *[pl.BlockSpec(r.shape, lambda m, h: (0, 0)) for r in results],
        ],
        out_shape=[jax.ShapeDtypeStruct((3, rows, d), BF16), *results],
        scratch_shapes=[pltpu.VMEM((2, ROWS, ROWS), BF16)] + (reduce_scratch(plan) if grads else []),
        compiler_params=params(**extra),
        name="attend_back",
        cost_estimate=pl.CostEstimate(
            flops=mb * pairs * 2 * 8 * ROWS * ROWS * 256,
            bytes_accessed=mb * pairs * 2 * ROWS * ROWS * 2,
            transcendentals=0,
        ),
    )(qkv, qkv, qkv, soft, mixed, d_mixed, inv, *grads)


def out_body(x_ref, m_ref, w_ref, vec_ref, resid_ref, h_ref, ht_ref):
    resid = x_ref[...].astype(F32) + mm(m_ref[...], w_ref[...]) + vec_ref[4:5, :]
    resid_ref[...] = resid
    n, _ = norm_stats(resid)
    h = (n * vec_ref[5:6, :] + vec_ref[6:7, :]).astype(BF16)
    h_ref[...] = h
    ht_ref[...] = h.T


def out_project(x, mixed, w, vec):
    rows, d = x.shape
    tile = 512
    blk = pl.BlockSpec((tile, d), lambda i: (i, 0))
    return pl.pallas_call(
        out_body,
        grid=(rows // tile,),
        in_specs=[blk, blk, pl.BlockSpec((d, d), lambda i: (0, 0)), pl.BlockSpec((8, d), lambda i: (0, 0))],
        out_specs=[blk, blk, pl.BlockSpec((d, tile), lambda i: (0, i))],
        out_shape=[
            jax.ShapeDtypeStruct((rows, d), F32),
            jax.ShapeDtypeStruct((rows, d), BF16),
            jax.ShapeDtypeStruct((d, rows), BF16),
        ],
        compiler_params=params(),
        name="out_project",
        cost_estimate=pl.CostEstimate(
            flops=2 * rows * d * d, bytes_accessed=rows * d * 12, transcendentals=0
        ),
    )(x, mixed, w, vec)


FC = 512
RT = 1024


def gelu_parts(u):
    cdf = 0.5 * (1.0 + lax.erf(u * ROOT_HALF))
    bell = jnp.exp(-0.5 * u * u) * ROOT_INV_TWO_PI
    return u * cdf, cdf + u * bell


def mlp_body(h_ref, ht_ref, g_ref, gt_ref, wu_ref, bu_ref, wd_ref, acc_ref, dh_ref, dwu_ref, dwd_ref, dbu_ref,
             act_ref, du_ref):
    rows = h_ref.shape[0]

    @pl.when(pl.program_id(0) == 0)
    def _():
        acc_ref[...] = jnp.zeros_like(acc_ref)
        dh_ref[...] = jnp.zeros_like(dh_ref)

    wu = wu_ref[...]
    wd = wd_ref[...]
    dbu_ref[...] = jnp.zeros_like(dbu_ref)

    @pl.loop(0, rows // RT)
    def _(t):
        sl = pl.ds(pl.multiple_of(t * RT, RT), RT)
        u = mm(h_ref[sl, :], wu) + bu_ref[...]
        act, slope = gelu_parts(u)
        act_ref[sl, :] = act.astype(BF16)
        du = mm(g_ref[sl, :], wd, NT) * slope
        dbu_ref[...] += jnp.sum(du, axis=0, keepdims=True)
        du_ref[sl, :] = du.astype(BF16)
        acc_ref[sl, :] += mm(act_ref[sl, :], wd)
        dh_ref[sl, :] += mm(du_ref[sl, :], wu, NT)

    dwu_ref[...] = mm(ht_ref[...], du_ref[...]).astype(dwu_ref.dtype)
    dwd_ref[...] = mm(gt_ref[...], act_ref[...]).T.astype(dwd_ref.dtype)


def mlp(h, ht, g, gt, wu, bu, wd):
    rows, d = h.shape
    ff = wu.shape[1]
    one = pl.Buffered(1)
    whole = pl.BlockSpec((rows, d), lambda c: (0, 0), pipeline_mode=one)
    whole_t = pl.BlockSpec((d, rows), lambda c: (0, 0), pipeline_mode=one)
    return pl.pallas_call(
        mlp_body,
        grid=(ff // FC,),
        in_specs=[
            whole,
            whole_t,
            whole,
            whole_t,
            pl.BlockSpec((d, FC), lambda c: (0, c)),
            pl.BlockSpec((1, FC), lambda c: (0, c)),
            pl.BlockSpec((FC, d), lambda c: (c, 0)),
        ],
        out_specs=[
            whole,
            whole,
            pl.BlockSpec((d, FC), lambda c: (0, c)),
            pl.BlockSpec((FC, d), lambda c: (c, 0)),
            pl.BlockSpec((1, FC), lambda c: (0, c)),
        ],
        out_shape=[
            jax.ShapeDtypeStruct((rows, d), F32),
            jax.ShapeDtypeStruct((rows, d), F32),
            jax.ShapeDtypeStruct((d, ff), BF16),
            jax.ShapeDtypeStruct((ff, d), BF16),
            jax.ShapeDtypeStruct((1, ff), F32),
        ],
        scratch_shapes=[pltpu.VMEM((rows, FC), BF16), pltpu.VMEM((rows, FC), BF16)],
        compiler_params=params(),
        name="mlp",
        cost_estimate=pl.CostEstimate(
            flops=12 * rows * d * ff, bytes_accessed=rows * d * 20 + 8 * d * ff, transcendentals=3 * rows * ff
        ),
    )(h, ht, g, gt, wu, bu, wd)


def fold(ref, row, step, value):
    part = jnp.sum(value, axis=0, keepdims=True)

    @pl.when(step == 0)
    def _():
        ref[row : row + 1, :] = part

    @pl.when(step != 0)
    def _():
        ref[row : row + 1, :] += part


def norm_pull(grad, n, inv, gain):
    dn = grad * gain
    plain = jnp.mean(dn, axis=-1, keepdims=True)
    cross = jnp.mean(dn * n, axis=-1, keepdims=True)
    return inv * (dn - plain - n * cross)


def mid_body(resid_ref, acc_ref, dh_ref, g_ref, mixed_ref, w_ref, vec_ref,
             y_ref, dr_ref, dm_ref, dw_ref, dvec_ref, sum_ref, low_ref):
    step = pl.program_id(0)

    @pl.when(step == 0)
    def _():
        dvec_ref[...] = jnp.zeros_like(dvec_ref)

    size = 128
    for t in range(resid_ref.shape[0] // size):
        sl = pl.ds(t * size, size)
        resid = resid_ref[sl, :]
        y_ref[sl, :] = (resid + acc_ref[sl, :] + vec_ref[7:8, :]).astype(BF16)
        g = g_ref[sl, :].astype(F32)
        n, inv = norm_stats(resid)
        dh = dh_ref[sl, :]
        dr = g + norm_pull(dh, n, inv, vec_ref[5:6, :])
        dr_ref[sl, :] = dr
        for row, value in ((4, dr), (5, dh * n), (6, dh), (7, g)):
            dvec_ref[row : row + 1, :] += jnp.sum(value, axis=0, keepdims=True)
        low_ref[sl, :] = dr.astype(BF16)
        dm_ref[sl, :] = mm(low_ref[sl, :], w_ref[...], NT).astype(BF16)
    low = low_ref[...]
    dw = mm(mixed_ref[...].T, low)

    @pl.when(step == 0)
    def _():
        sum_ref[...] = dw

    @pl.when(step != 0)
    def _():
        sum_ref[...] += dw

    @pl.when(step == pl.num_programs(0) - 1)
    def _():
        dw_ref[...] = sum_ref[...].astype(dw_ref.dtype)


def middle(resid, acc, dh, g, mixed, w, vec):
    rows, d = resid.shape
    tile = 512
    blk = pl.BlockSpec((tile, d), lambda i: (i, 0))
    mat = pl.BlockSpec((d, d), lambda i: (0, 0))
    eight = pl.BlockSpec((8, d), lambda i: (0, 0))
    return pl.pallas_call(
        mid_body,
        grid=(rows // tile,),
        in_specs=[blk, blk, blk, blk, blk, mat, eight],
        out_specs=[blk, blk, blk, mat, eight],
        out_shape=[
            jax.ShapeDtypeStruct((rows, d), BF16),
            jax.ShapeDtypeStruct((rows, d), F32),
            jax.ShapeDtypeStruct((rows, d), BF16),
            jax.ShapeDtypeStruct((d, d), BF16),
            jax.ShapeDtypeStruct((8, d), F32),
        ],
        scratch_shapes=[pltpu.VMEM((d, d), F32), pltpu.VMEM((tile, d), BF16)],
        compiler_params=params(),
        name="middle",
        cost_estimate=pl.CostEstimate(
            flops=4 * rows * d * d, bytes_accessed=rows * d * 24, transcendentals=0
        ),
    )(resid, acc, dh, g, mixed, w, vec)


PHASES = 3
FINAL_TILE = 256


def finish_body(plan, ht_ref, part_ref, tile_ref, x_ref, dr_ref, w_hbm, vec_ref, dvec_ref, dbu_ref, dx_ref, *refs):
    step = pl.program_id(0)
    d = x_ref.shape[1]
    if plan is None:
        dw_ref, sums_ref, w_ref, w_sem = refs
    else:
        out_ref, small_ref, w_ref, w_sem, sums_ref, grad_ref, tall_ref = refs[:7]
        places = [(grad_ref.at[j], out_ref, (col, j * d + col)) for j in range(PHASES) for col, _ in PIECES]
        places.append((tall_ref, small_ref, (0, 0)))
        work = reduce_work(plan, places, refs[7:])
        vectors = len(places) - 1
        last = vectors - 1 + ht_ref.shape[1] // FINAL_TILE
        moves = FINISH_MOVES

    fetch = pltpu.make_async_copy(w_hbm, w_ref, w_sem)

    @pl.when(step == 0)
    def _():
        if plan is not None:
            greet(wait=False)
        fetch.start()
        sums_ref[...] = dvec_ref[...]

    for i, (col, n) in enumerate(PIECES):

        @pl.when(step < PHASES)
        def _():
            cols = pl.ds(col, n)
            dw = mm(ht_ref[...], part_ref[0, :, cols]).astype(BF16)
            if plan is None:
                dw_ref[:, cols] = dw
            else:
                grad_ref[step, :, :, :, :, cols] = dw.reshape(4, 2, 2, d // 16, n)

        if plan is not None:
            for j in range(PHASES):

                @pl.when(step == j)
                def _():
                    if i == 0 and j == 0:
                        greet(signal=False)
                    at_hook(2 * j + i, moves, work, True)

    for j, row in ((0, 2), (2, 3)):

        @pl.when(step == j)
        def _():
            sums_ref[row : row + 1, :] = jnp.sum(part_ref[0].astype(F32), axis=0, keepdims=True)

    @pl.when(step == PHASES)
    def _():
        fetch.wait()

    @pl.when(step >= PHASES)
    def _():
        n, inv = norm_stats(x_ref[...].astype(F32))
        dh = None
        for j in range(3):
            term = mm(tile_ref[j], w_ref[:, pl.ds(j * d, d)], NT)
            dh = term if dh is None else dh + term
        fold(sums_ref, 0, step - PHASES, dh * n)
        fold(sums_ref, 1, step - PHASES, dh)
        dx_ref[...] = (dr_ref[...] + norm_pull(dh, n, inv, vec_ref[0:1, :])).astype(BF16)

    if plan is not None:
        for k in range(2 * PHASES, last + 1):

            @pl.when(step == k - PHASES)
            def _():
                if k == last:
                    pack(tall_ref, sums_ref, dbu_ref)
                    for hook in range(last, 1 + max(max(m) for m in moves)):
                        at_hook(hook, moves, work, True)
                else:
                    at_hook(k, moves, work, True)


FINISH_MOVES = [
    [0, 1, 5, 8, 12, 14, 18],
    [1, 2, 6, 9, 12, 14, 18],
    [2, 3, 7, 10, 13, 15, 18],
    [3, 4, 8, 11, 14, 16, 18],
    [4, 5, 9, 12, 14, 16, 18],
    [5, 6, 11, 13, 15, 17, 18],
    [13, 14, 14, 15, 16, 17, 18],
]


def pack(tall_ref, sums_ref, dbu_ref):
    d = sums_ref.shape[1] // 16
    f = dbu_ref.shape[1] // 16
    for i in range(16):
        tile = tall_ref.at[i // 4, (i // 2) % 2, i % 2]
        tile[0:8, 0:d] = sums_ref[:, i * d : (i + 1) * d]
        tile[8:9, 0:128] = dbu_ref[:, i * f : i * f + 128]
        tile[9:10, 0 : f - 128] = dbu_ref[:, i * f + 128 : (i + 1) * f]


def finish(x, dr, ht, dqkv, w, vec, dvec, dbu, near):
    rows, d = x.shape
    tiles = rows // FINAL_TILE
    row = lambda s: jnp.maximum(s - PHASES, 0)
    one = pl.Buffered(1)
    eight = pl.BlockSpec((8, d), lambda s: (0, 0))
    if near:
        plan = [(d // 16, n, BF16, True) for _ in range(PHASES) for _, n in PIECES] + [(16, 128, F32, False)]
        shapes = [jax.ShapeDtypeStruct((d // 16, 3 * d), F32), jax.ShapeDtypeStruct((16, 128), F32)]
        specs = [pl.BlockSpec(s.shape, lambda s: (0, 0)) for s in shapes]
        scratch = [
            pltpu.VMEM((8, d), F32),
            pltpu.VMEM((PHASES, 4, 2, 2, d // 16, d), BF16),
            pltpu.VMEM((4, 2, 2, 16, 128), F32),
        ] + reduce_scratch(plan)
        extra = dict(collective_id=3, has_side_effects=True)
    else:
        plan = None
        shapes = [jax.ShapeDtypeStruct((d, 3 * d), BF16), jax.ShapeDtypeStruct((8, d), F32)]
        specs = [pl.BlockSpec((d, d), lambda s: (0, jnp.minimum(s, PHASES - 1))), eight]
        scratch = []
        extra = {}
    return pl.pallas_call(
        functools.partial(finish_body, plan),
        grid=(PHASES + tiles,),
        in_specs=[
            pl.BlockSpec((d, rows), lambda s: (0, 0), pipeline_mode=one),
            pl.BlockSpec((1, rows, d), lambda s: (jnp.minimum(s, PHASES - 1), 0, 0)),
            pl.BlockSpec((3, FINAL_TILE, d), lambda s: (0, row(s), 0)),
            pl.BlockSpec((FINAL_TILE, d), lambda s: (row(s), 0)),
            pl.BlockSpec((FINAL_TILE, d), lambda s: (row(s), 0)),
            ANY,
            eight,
            eight,
            pl.BlockSpec(dbu.shape, lambda s: (0, 0)),
        ],
        out_specs=[pl.BlockSpec((FINAL_TILE, d), lambda s: (row(s), 0)), *specs],
        out_shape=[jax.ShapeDtypeStruct((rows, d), BF16), *shapes],
        scratch_shapes=[pltpu.VMEM((d, 3 * d), BF16), pltpu.SemaphoreType.DMA(()), *scratch],
        compiler_params=params(**extra),
        name="finish",
        cost_estimate=pl.CostEstimate(
            flops=12 * rows * d * d, bytes_accessed=rows * d * 20, transcendentals=0
        ),
    )(ht, dqkv, dqkv, x, dr, w, vec, dvec, dbu)


def publish_body(splits, small_ref, *refs):
    n = len(splits)
    arrays, outs = refs[:n], refs[n : 2 * n]
    vectors = refs[2 * n : 2 * n + 9]
    holds = refs[2 * n + 9 : 3 * n + 9]
    get_sem, put_sem = refs[3 * n + 9 :]
    gets, puts = [], []
    for src, out, hold, parts in zip(arrays, outs, holds, splits):
        size = src.shape[0] // parts
        for p in range(parts):
            rows = pl.ds(p * size, size)
            i = len(gets)
            gets.append(pltpu.make_async_copy(src.at[rows], hold.at[rows], get_sem.at[i]))
            puts.append(pltpu.make_async_copy(hold.at[rows], out.at[rows], put_sem.at[i]))
    for get in gets:
        get.start()
    for i, ref in enumerate(vectors[:8]):
        ref[...] = small_ref[i, 0 : ref.shape[0]]
    up = vectors[8]
    up[0:128] = small_ref[8, :]
    up[128:] = small_ref[9, 0 : up.shape[0] - 128]
    for get, put in zip(gets, puts):
        get.wait()
        put.start()
    for put in puts:
        put.wait()


def publish(small, lengths, arrays):
    splits = [8 if a.dtype == BF16 else 2 for a in arrays]
    total = sum(splits)
    vmem = pl.BlockSpec(memory_space=pltpu.VMEM)
    return pl.pallas_call(
        functools.partial(publish_body, splits),
        in_specs=[vmem] + [ANY] * len(arrays),
        out_specs=[ANY] * len(arrays) + [vmem] * 9,
        out_shape=[jax.ShapeDtypeStruct(a.shape, a.dtype) for a in arrays]
        + [jax.ShapeDtypeStruct((n,), F32) for n in lengths],
        scratch_shapes=[pltpu.VMEM(a.shape, a.dtype) for a in arrays]
        + [pltpu.SemaphoreType.DMA((total,)), pltpu.SemaphoreType.DMA((total,))],
        compiler_params=params(),
        name="publish",
    )(small, *arrays)


def on_device(tokens, cotangent, segment_ids, *shards):
    gather = lambda s: lax.all_gather(s, "fsdp", axis=0, tiled=True)
    n = lax.axis_size("fsdp")
    near = n == 16 and lax.axis_size("dp") == 2
    triple_s, out_s, up_s, down_s = (s for s in shards if s.ndim == 2)
    rows, d = tokens.shape
    up_bias_s = shards[10]
    eights = [s for i, s in enumerate(shards) if s.ndim == 1 and i != 10]
    flat = lambda w: w.reshape(-1, w.shape[-1])
    if near:
        triple_weight, vec, up_bias, qkv, first_t, cot_t = first(eights + [up_bias_s], triple_s, tokens, cotangent)
        triple_weight = flat(triple_weight)
    else:
        triple_weight = gather(triple_s)
        packed = gather(jnp.concatenate(eights + [up_bias_s]).reshape(1, -1)).astype(F32)
        m = eights[0].shape[0]
        vec = jnp.stack([packed[:, i * m : (i + 1) * m].reshape(-1) for i in range(8)])
        up_bias = packed[:, 8 * m :].reshape(1, -1)
        qkv, first_t = project(tokens, vec, triple_weight)
        cot_t = cotangent.T

    segr = segment_ids.reshape(rows // ROWS, 1, ROWS)
    if near:
        mixed, soft, inv, *full = attend(qkv, segr, (out_s, up_s, down_s))
        out_weight, up_weight, down_weight = (flat(w) for w in full)
    else:
        mixed, soft, inv = attend(qkv, segr)
        out_weight, up_weight, down_weight = gather(out_s), gather(up_s), gather(down_s)
    resid, h, ht = out_project(tokens, mixed, out_weight, vec)
    acc, dh, dwu, dwd, dbu = mlp(h, ht, cotangent, cot_t, up_weight, up_bias, down_weight)
    y, dr, dm, dwo, dvec = middle(resid, acc, dh, cotangent, mixed, out_weight, vec)
    if near:
        dqkv, out_grad, up_grad, down_grad = attend_back(qkv, soft, mixed, dm, inv, (dwo, dwu, dwd))
        dx, triple_grad, small = finish(tokens, dr, first_t, dqkv, triple_weight, vec, dvec, dbu, True)
        lengths = [d // n] * 8 + [up_bias_s.shape[0]]
        dx, triple_grad, out_grad, up_grad, down_grad, *small_grads, up_bias_grad = publish(
            small, lengths, (dx, triple_grad, out_grad, up_grad, down_grad)
        )
    else:
        (dqkv,) = attend_back(qkv, soft, mixed, dm, inv)
        dx, dwt, dvec = finish(tokens, dr, first_t, dqkv, triple_weight, vec, dvec, dbu, False)
        small = jnp.concatenate([dvec[i].reshape(n, -1) for i in range(8)] + [dbu.reshape(n, -1)], axis=1)
        small = lax.psum_scatter(small, "fsdp", scatter_dimension=0, tiled=True).reshape(-1)
        small = lax.psum(small, "dp")
        total = lambda p: lax.psum(lax.psum_scatter(p, "fsdp", scatter_dimension=0, tiled=True), "dp").astype(F32)
        triple_grad, out_grad, up_grad, down_grad = total(dwt), total(dwo), total(dwu), total(dwd)
        m = d // n
        small_grads = [small[i * m : (i + 1) * m] for i in range(8)]
        up_bias_grad = small[8 * m :]
    dg1, ds1, dqb, dvb, dob, dg2, ds2, ddb = small_grads
    return (
        y, dx, dg1, ds1, triple_grad, dqb, dvb, out_grad, dob, dg2, ds2, up_grad, up_bias_grad, down_grad, ddb,
    )


def solution(mesh):
    tok = P(("dp", "fsdp"), None)
    vec = P("fsdp")
    mat = P("fsdp", None)
    weights = (vec, vec, mat, vec, vec, mat, vec, vec, vec, mat, vec, mat, vec)
    return jax.shard_map(
        on_device,
        mesh=mesh,
        in_specs=(tok, tok, P(("dp", "fsdp")), *weights),
        out_specs=(tok, tok, *weights),
        check_vma=False,
    )
```

```python
import functools

import jax
import jax.numpy as jnp
from jax import lax
from jax.experimental import pallas as pl
from jax.experimental.pallas import tpu as pltpu
from jax.sharding import PartitionSpec as P

H = 12
HD = 64
ROWS = 1024
EPS = 1e-06
F32 = jnp.float32
BF16 = jnp.bfloat16
VMEM_LIMIT = 60 * 1024 * 1024

ROOT_HALF = 0.7071067811865476
ROOT_INV_TWO_PI = 0.3989422804014327

NN = (((1,), (0,)), ((), ()))
NT = (((1,), (1,)), ((), ()))


def mm(a, b, dims=NN):
    return lax.dot_general(a, b, dims, preferred_element_type=F32)


def params(**kw):
    return pltpu.CompilerParams(vmem_limit_bytes=VMEM_LIMIT, **kw)


def norm_stats(x):
    mean = jnp.mean(x, axis=-1, keepdims=True)
    cen = x - mean
    var = jnp.mean(cen * cen, axis=-1, keepdims=True)
    inv = lax.rsqrt(var + EPS)
    return cen * inv, inv


MESH = pl.DeviceIdType.MESH
ANY = pl.BlockSpec(memory_space=pl.ANY)


def whereabouts():
    y = lax.axis_index("dp")
    f = lax.axis_index("fsdp")
    return y, f // 4, (f // 2) % 2, f % 2


def spot(z, x, c):
    return z * 4 + x * 2 + c


def greet(signal=True, wait=True):
    y, z, x, c = whereabouts()
    barrier = pltpu.get_barrier_semaphore()
    peers = [(1 - y, spot(z, x, c)), (y, spot(z, 1 - x, c)), (y, spot(z, x, 1 - c))]
    peers += [(y, spot((z + d) % 4, x, c)) for d in (1, 2, 3)]
    if signal:
        for peer in peers:
            pl.semaphore_signal(barrier, inc=1, device_id=peer, device_id_type=MESH)
    if wait:
        pl.semaphore_wait(barrier, len(peers))


class Mover:
    def __init__(self, send, recv, local, per):
        self.send, self.recv, self.local, self.per = send, recv, local, per
        self.y, self.z, self.x, self.c = whereabouts()

    def wide(self, r, split, y):
        return pl.ds(pl.multiple_of(y * (r // 3), 8), 2 * (r // 3)) if split else pl.ds(0, r)

    def thin(self, r, y):
        return pl.ds(pl.multiple_of(y * 2 * (r // 3), 8), r // 3)

    def copy(self, u, slot, src, dst, z=None, x=None, c=None, y=None):
        i = u * self.per + slot
        pick = lambda v, own: own if v is None else v
        peer = (pick(y, self.y), spot(pick(z, self.z), pick(x, self.x), pick(c, self.c)))
        return pltpu.make_async_remote_copy(
            src_ref=src, dst_ref=dst, send_sem=self.send.at[i], recv_sem=self.recv.at[i],
            device_id=peer, device_id_type=MESH,
        )


class Gather(Mover):
    def __init__(self, units, send, recv, local):
        super().__init__(send, recv, local, 6)
        self.units = units

    def mine(self, u):
        src, _, _, col, n, split = self.units[u]
        return src.at[self.wide(src.shape[0], split, self.y), pl.ds(col, n)]

    def held(self, u):
        src, _, hold, col, n, split = self.units[u]
        return hold.at[self.wide(src.shape[0], split, self.y), pl.ds(col, n)]

    def part(self, u, z, x, c, rows):
        _, dst, _, col, n, _ = self.units[u]
        every = slice(None)
        pick = lambda v: every if v is None else v
        return dst.at[pick(z), pick(x), pick(c), rows, pl.ds(col, n)]

    def broad(self, u):
        src, _, _, _, _, split = self.units[u]
        return self.wide(src.shape[0], split, self.y)

    def load(self, u):
        return pltpu.make_async_copy(self.mine(u), self.held(u), self.local.at[2 * u])

    def store(self, u):
        dst = self.part(u, self.z, self.x, self.c, self.broad(u))
        return pltpu.make_async_copy(self.held(u), dst, self.local.at[2 * u + 1])

    def along_z(self, u, d, out=True):
        here, there = (self.z + 4 - d) % 4, (self.z + d) % 4
        dst = self.part(u, self.z if out else here, self.x, self.c, self.broad(u))
        return self.copy(u, d - 1, self.mine(u), dst, z=there)

    def along_x(self, u, out=True):
        src = self.part(u, None, self.x, self.c, self.broad(u))
        dst = src if out else self.part(u, None, 1 - self.x, self.c, self.broad(u))
        return self.copy(u, 3, src, dst, x=1 - self.x)

    def along_y(self, u, out=True):
        r = self.units[u][0].shape[0]
        src = self.part(u, None, None, self.c, self.thin(r, self.y))
        dst = src if out else self.part(u, None, None, self.c, self.thin(r, 1 - self.y))
        return self.copy(u, 4, src, dst, y=1 - self.y)

    def along_c(self, u, out=True):
        every = pl.ds(0, self.units[u][0].shape[0])
        src = self.part(u, None, None, self.c, every)
        dst = src if out else self.part(u, None, None, 1 - self.c, every)
        return self.copy(u, 5, src, dst, c=1 - self.c)

    def stage(self, s, u):
        split = self.units[u][5]
        if s == 0:
            for d in (1, 2, 3):
                self.along_z(u, d).start()
            self.load(u).start()
        if s == 1:
            self.load(u).wait()
            self.store(u).start()
        if s == 2:
            self.store(u).wait()
            for d in (1, 2, 3):
                self.along_z(u, d, False).wait_recv()
            self.along_x(u).start()
        if s == 3:
            self.along_x(u, False).wait_recv()
            if split:
                self.along_y(u).start()
            else:
                self.along_c(u).start()
        if s == 4 and split:
            self.along_y(u, False).wait_recv()
            self.along_c(u).start()
        if s == 5:
            self.along_c(u, False).wait_recv()
            for d in (1, 2, 3):
                self.along_z(u, d).wait_send()
            self.along_x(u).wait_send()
            if split:
                self.along_y(u).wait_send()
            self.along_c(u).wait_send()


def gather_sems(units):
    return [
        pltpu.SemaphoreType.DMA((units * 6,)),
        pltpu.SemaphoreType.DMA((units * 6,)),
        pltpu.SemaphoreType.DMA((2 * units,)),
    ]


def whole(shard):
    return jax.ShapeDtypeStruct((4, 2, 2, *shard.shape), shard.dtype)


class Reduce(Mover):
    def __init__(self, units, send, recv, local):
        super().__init__(send, recv, local, 7)
        self.units = units

    def size(self, u):
        return self.units[u][0].shape[3]

    def partial(self, u, c):
        src, _, (col, _), n, _, _ = self.units[u]
        return src.at[:, :, c, :, pl.ds(col, n)]

    def load(self, u):
        return pltpu.make_async_copy(self.partial(u, self.c), self.units[u][5][0], self.local.at[u])

    def over_c(self, u):
        return self.copy(u, 0, self.partial(u, 1 - self.c), self.units[u][5][1], c=1 - self.c)

    def over_y(self, u):
        own, from_y = self.units[u][5][0], self.units[u][5][5]
        return self.copy(u, 1, own.at[:, :, self.thin(self.size(u), 1 - self.y), :], from_y, y=1 - self.y)

    def over_x(self, u):
        own, from_x = self.units[u][5][0], self.units[u][5][2]
        rows = self.wide(self.size(u), self.units[u][4], self.y)
        return self.copy(u, 2, own.at[:, 1 - self.x, rows, :], from_x, x=1 - self.x)

    def over_z(self, u, d):
        own, from_z = self.units[u][5][0], self.units[u][5][3]
        rows = self.wide(self.size(u), self.units[u][4], self.y)
        to = (self.z + d) % 4
        return self.copy(u, 2 + d, own.at[to, self.x, rows, :], from_z.at[d - 1], z=to)

    def over_last(self, u):
        last = self.units[u][5][4]
        return self.copy(u, 6, last.at[0], last.at[1], y=1 - self.y)

    def stage(self, s, u):
        _, out, (_, col), n, split, (own, from_c, from_x, from_z, last, *rest) = self.units[u]
        y, z, x = self.y, self.z, self.x
        r = self.size(u)
        rows = self.wide(r, split, y)
        if s == 0:
            self.over_c(u).start()
            self.load(u).start()
        if s == 1:
            self.load(u).wait()
            self.over_c(u).wait_recv()
            own[...] = own[...] + from_c[...]
            if split:
                self.over_y(u).start()
        if s == 2:
            if split:
                self.over_y(u).wait_recv()
                mine = self.thin(r, y)
                own[:, :, mine, :] = own[:, :, mine, :] + rest[0][...]
            self.over_x(u).start()
        if s == 3:
            self.over_x(u).wait_recv()
            for k in range(4):
                own[k, x, rows, :] = own[k, x, rows, :] + from_x[k]
            for d in (1, 2, 3):
                self.over_z(u, d).start()
        if s == 4:
            total = own[z, x, rows, :].astype(F32)
            for d in (1, 2, 3):
                self.over_z(u, d).wait_recv()
                total = total + from_z[d - 1].astype(F32)
            last[0] = total.astype(last.dtype)
            self.over_last(u).start()
        if s == 5:
            self.over_last(u).wait_recv()
            cols = pl.ds(col, n)
            if split:
                t = r // 3
                at = lambda k: pl.ds(pl.multiple_of(k * t, 8), t)
                put = lambda k, v: out.__setitem__((at(k), cols), v.astype(F32))
                put(1, last[0, at(1 - y), :].astype(F32) + last[1, at(y), :].astype(F32))
                put(2 * y, last[0, at(y), :])
                put(2 * (1 - y), last[1, at(1 - y), :])
            else:
                out[:, cols] = last[0].astype(F32) + last[1].astype(F32)
        if s == 6:
            self.over_c(u).wait_send()
            if split:
                self.over_y(u).wait_send()
            self.over_x(u).wait_send()
            for d in (1, 2, 3):
                self.over_z(u, d).wait_send()
            self.over_last(u).wait_send()


def reduce_buffers(r, n, dtype, split):
    wide = 2 * r // 3 if split else r
    shapes = [(4, 2, r, n), (4, 2, r, n), (4, wide, n), (3, wide, n), (2, wide, n)]
    if split:
        shapes.append((4, 2, r // 3, n))
    return [pltpu.VMEM(shape, dtype) for shape in shapes]


def reduce_scratch(plan):
    flat = []
    for p in plan:
        flat += reduce_buffers(*p)
    units = len(plan)
    return flat + [
        pltpu.SemaphoreType.DMA((units * 7,)),
        pltpu.SemaphoreType.DMA((units * 7,)),
        pltpu.SemaphoreType.DMA((units,)),
    ]


def reduce_work(plan, places, scratch):
    units = []
    at = 0
    for (_, n, _, split), (src, out, col) in zip(plan, places):
        count = 6 if split else 5
        units.append((src, out, col, n, split, scratch[at : at + count]))
        at += count
    return Reduce(units, *scratch[at:])


def at_hook(hook, moves, work, newest=False):
    for u, hooks in list(enumerate(moves))[:: -1 if newest else 1]:
        for s, when in enumerate(hooks):
            if when == hook:
                work.stage(s, u)


def hooked(step, per_step, which, steps, moves, work, late=False):
    if late and which == 0:

        @pl.when(step == 0)
        def _():
            greet(wait=False)

    for k in range(steps):
        if any(k * per_step + which in hooks for hooks in moves):

            @pl.when(step == k)
            def _():
                if which == 0 and k == late:
                    greet(signal=not late)
                at_hook(k * per_step + which, moves, work)


def unpack(vec_ref, ub_ref, tall_ref):
    d = vec_ref.shape[1] // 16
    f = ub_ref.shape[1] // 16
    for i in range(16):
        tile = tall_ref[i // 4, (i // 2) % 2, i % 2].astype(F32)
        vec_ref[:, i * d : (i + 1) * d] = tile[0:8, 0:d]
        ub_ref[:, i * f : i * f + 128] = tile[8:9, 0:128]
        ub_ref[:, i * f + 128 : (i + 1) * f] = tile[9:10, 0 : f - 128]


PIECES = ((0, 512), (512, 256))
FIRST_LAGS = (0, 1, 2, 4, 6, 8)


def first_body(*refs):
    vectors = refs[:9]
    t_ref, x_hbm, g_hbm = refs[9:12]
    w_hbm, vec_ref, ub_ref, qkv_hbm, ht_hbm, gt_hbm = refs[12:18]
    row_ref, tile_ref, tall_ref, vh_ref, w_ref, th_ref, x_ref, g_ref, h_ref, ht_ref, gt_ref, out_ref = refs[18:30]
    move_sem, out_sem, w_sem, *sems = refs[30:]
    rows, d = x_ref.shape
    columns = [(j, j * d + col, n) for j in range(3) for col, n in PIECES]
    units = [(tile_ref, tall_ref, vh_ref, 0, 128, False)]
    units += [(t_ref, w_ref, th_ref, col, n, True) for _, col, n in columns]
    work = Gather(units, *sems)
    moves = [[0, 1, 2, 3, 4, 5]] + [[u + lag for lag in FIRST_LAGS] for u in range(len(columns))]
    local = lambda i, src, dst: pltpu.make_async_copy(src, dst, move_sem.at[i])
    get_x, get_g = local(0, x_hbm, x_ref), local(1, g_hbm, g_ref)
    put_h, put_g = local(2, ht_ref, ht_hbm), local(3, gt_ref, gt_hbm)

    greet(wait=False)
    get_g.start()
    get_x.start()
    for i, ref in enumerate(vectors[:8]):
        row_ref[i : i + 1, 0 : ref.shape[0]] = ref[...].astype(F32).reshape(1, -1)
    up = vectors[8][...].astype(F32).reshape(1, -1)
    row_ref[8:9, :] = up[:, :128]
    row_ref[9:10, 0 : up.shape[1] - 128] = up[:, 128:]
    tile_ref[...] = row_ref[...].astype(BF16)
    greet(signal=False)
    at_hook(0, moves, work)
    get_g.wait()
    for t in range(4):

        @pl.loop(0, rows // 4 // 128)
        def _(i):
            part = pl.ds(pl.multiple_of(t * (rows // 4) + i * 128, 128), 128)
            gt_ref[:, part] = g_ref[part, :].T

        at_hook(1 + t, moves, work)
    put_g.start()
    get_x.wait()
    at_hook(5, moves, work)
    unpack(vec_ref, ub_ref, tall_ref)
    for t in range(4):

        @pl.loop(0, rows // 4 // 128)
        def _(i):
            part = pl.ds(pl.multiple_of(t * (rows // 4) + i * 128, 128), 128)
            n, _ = norm_stats(x_ref[part, :].astype(F32))
            h = (n * vec_ref[0:1, :] + vec_ref[1:2, :]).astype(BF16)
            h_ref[part, :] = h
            ht_ref[:, part] = h.T

        at_hook(6 + t, moves, work)
    put_h.start()

    def place(u):
        _, col, n = columns[u]
        return pltpu.make_async_copy(out_ref.at[u % 2, :, pl.ds(0, n)], qkv_hbm.at[:, pl.ds(col, n)], out_sem.at[u])

    def keep(u):
        _, col, n = columns[u]
        cols = pl.ds(col, n)
        return pltpu.make_async_copy(w_ref.at[:, :, :, :, cols], w_hbm.at[:, :, :, :, cols], w_sem.at[u])

    for u, (j, col, n) in enumerate(columns):
        if u:
            at_hook(9 + u, moves, work)
        keep(u).start()
        if u >= 2:
            place(u - 2).wait()
        own = slice(col - j * d, col - j * d + n)

        @pl.loop(0, 4)
        def _(t):
            part = pl.ds(pl.multiple_of(t * (rows // 4), 8), rows // 4)
            p = mm(h_ref[part, :], w_ref[:, :, :, :, col : col + n].reshape(d, n))
            if j == 0:
                p = (p + vec_ref[2:3, own]) * 0.125
            if j == 2:
                p = p + vec_ref[3:4, own]
            out_ref[u % 2, part, 0:n] = p.astype(BF16)

        place(u).start()
    put_g.wait()
    put_h.wait()
    for u in range(len(columns)):
        keep(u).wait()
        if u >= len(columns) - 2:
            place(u).wait()


def first(vectors, triple, x, g):
    rows, d = x.shape
    vmem = pl.BlockSpec(memory_space=pltpu.VMEM)
    across = pltpu.VMEM((d, rows), BF16)
    down = pltpu.VMEM((rows, d), BF16)
    pieces = 3 * len(PIECES)
    return pl.pallas_call(
        first_body,
        in_specs=[vmem] * 9 + [ANY] * 3,
        out_specs=[ANY, vmem, vmem, ANY, ANY, ANY],
        out_shape=[
            whole(triple),
            jax.ShapeDtypeStruct((8, d), F32),
            jax.ShapeDtypeStruct((1, 4 * d), F32),
            jax.ShapeDtypeStruct((rows, 3 * d), BF16),
            jax.ShapeDtypeStruct((d, rows), BF16),
            jax.ShapeDtypeStruct((d, rows), BF16),
        ],
        scratch_shapes=[
            pltpu.VMEM((16, 128), F32),
            pltpu.VMEM((16, 128), BF16),
            pltpu.VMEM((4, 2, 2, 16, 128), BF16),
            pltpu.VMEM((16, 128), BF16),
            pltpu.VMEM((4, 2, 2, *triple.shape), BF16),
            pltpu.VMEM(triple.shape, BF16),
            down,
            down,
            down,
            across,
            across,
            pltpu.VMEM((2, rows, PIECES[0][1]), BF16),
            pltpu.SemaphoreType.DMA((4,)),
            pltpu.SemaphoreType.DMA((pieces,)),
            pltpu.SemaphoreType.DMA((pieces,)),
            *gather_sems(1 + pieces),
        ],
        compiler_params=params(collective_id=0, has_side_effects=True),
        name="first",
    )(*vectors, triple, x, g)


def proj_body(x_ref, vec_ref, w_ref, qkv_ref, ht_ref):
    d = x_ref.shape[1]
    n, _ = norm_stats(x_ref[...].astype(F32))
    h = (n * vec_ref[0:1, :] + vec_ref[1:2, :]).astype(BF16)
    ht_ref[...] = h.T
    for j in range(3):
        cols = pl.ds(j * d, d)
        p = mm(h, w_ref[:, cols])
        if j == 0:
            p = (p + vec_ref[2:3, :]) * 0.125
        if j == 2:
            p = p + vec_ref[3:4, :]
        qkv_ref[:, cols] = p.astype(BF16)


def project(x, vec, w):
    rows, d = x.shape
    cols = w.shape[1]
    tile = 512
    return pl.pallas_call(
        proj_body,
        grid=(rows // tile,),
        in_specs=[
            pl.BlockSpec((tile, d), lambda i: (i, 0)),
            pl.BlockSpec((8, d), lambda i: (0, 0)),
            pl.BlockSpec((d, cols), lambda i: (0, 0)),
        ],
        out_specs=[
            pl.BlockSpec((tile, cols), lambda i: (i, 0)),
            pl.BlockSpec((d, tile), lambda i: (0, i)),
        ],
        out_shape=[jax.ShapeDtypeStruct((rows, cols), BF16), jax.ShapeDtypeStruct((d, rows), BF16)],
        compiler_params=params(),
        name="project",
        cost_estimate=pl.CostEstimate(
            flops=2 * rows * d * cols, bytes_accessed=2 * rows * (d + cols), transcendentals=0
        ),
    )(x, vec, w)


QT = 256
GATHER_CUT = (2, 8, 6)
REDUCE_CUT = (1, 3, 3)
GATHER_LAGS = (0, 1, 2, 4, 6, 8)
REDUCE_LAGS = (0, 1, 4, 7, 10, 12, 12)


LOG2E = 1.4426950408889634


def swap(value):
    return jnp.concatenate([value[:, HD:], value[:, :HD]], axis=1)


def twice(value, own):
    return jnp.where(own, value, swap(value))


def unit_list(widths, cuts):
    return [(i, j * (w // cut), w // cut) for i, (w, cut) in enumerate(zip(widths, cuts)) for j in range(cut)]


def attend_body(hosting, *refs):
    q_ref, k_ref, v_ref, seg_ref = refs[:4]
    if hosting:
        shards = refs[4:7]
        o_ref, p_ref, inv_ref = refs[7:10]
        full = refs[10:13]
        bias_ref, pair_ref = refs[13:15]
        hold = refs[15:18]
        units = [(shards[i], full[i], hold[i], col, n, True) for i, col, n in unit_list([s.shape[1] for s in shards], GATHER_CUT)]
        work = Gather(units, *refs[18:])
        moves = [[u + lag for lag in GATHER_LAGS] for u in range(len(units))]
    else:
        o_ref, p_ref, inv_ref, bias_ref, pair_ref = refs[4:]
    step = pl.program_id(0) * pl.num_programs(1) + pl.program_id(1)
    rows = q_ref.shape[0]

    @pl.when(pl.program_id(1) == 0)
    def _():
        seg = seg_ref[...].astype(F32)
        column = jnp.broadcast_to(seg, (8, rows)).T[:, 0:1]
        bias_ref[...] = jnp.where(column == seg, 0.0, -1e30)

    lower = lax.broadcasted_iota(jnp.int32, (1, 128), 1) < HD
    lower = lax.broadcasted_iota(jnp.int32, (1, 128), 1) < HD
    lower = lax.broadcasted_iota(jnp.int32, (1, 128), 1) < HD
    sums = []
    for hh in range(2):
        if hosting:
            hooked(step, 2, hh, 12, moves, work)
        own = lower if hh == 0 else ~lower
        q = q_ref[...].astype(F32) * LOG2E
        high = q.astype(BF16)
        low = (q - high.astype(F32)).astype(BF16)
        pair_ref[0, hh] = jnp.where(own, high, swap(low))
        pair_ref[1, hh] = twice(k_ref[...], own)
        pair_ref[2, hh] = jnp.where(own, v_ref[...], jnp.ones_like(v_ref[...]))
        if hh == 1:
            sums.append(mm(p_ref[0], pair_ref[2, 0]))
        for t in range(rows // QT):
            sl = pl.ds(t * QT, QT)
            s = mm(pair_ref[0, hh, sl, :], pair_ref[1, hh], NT) + bias_ref[sl, :]
            p_ref[hh, sl, :] = jnp.exp2(s - jnp.max(s, axis=-1, keepdims=True)).astype(BF16)
    sums.append(mm(p_ref[1], pair_ref[2, 1]))
    inv = 1.0 / swap(jnp.where(lower, sums[1], sums[0]))
    inv_ref[...] = inv
    o_ref[...] = (jnp.where(lower, sums[0], sums[1]) * inv).astype(BF16)


def attend(qkv, segr, shards=()):
    rows = qkv.shape[0]
    d = qkv.shape[1] // 3
    mb = rows // ROWS
    pairs = d // 128
    extra = dict(collective_id=1, has_side_effects=True) if shards else {}
    return pl.pallas_call(
        functools.partial(attend_body, bool(shards)),
        grid=(mb, pairs),
        in_specs=[
            pl.BlockSpec((ROWS, 128), lambda m, h: (m, h)),
            pl.BlockSpec((ROWS, 128), lambda m, h: (m, pairs + h)),
            pl.BlockSpec((ROWS, 128), lambda m, h: (m, 2 * pairs + h)),
            pl.BlockSpec((None, 1, ROWS), lambda m, h: (m, 0, 0)),
            *[ANY for _ in shards],
        ],
        out_specs=[
            pl.BlockSpec((ROWS, 128), lambda m, h: (m, h)),
            pl.BlockSpec((None, 2, ROWS, ROWS), lambda m, h: (m, h, 0, 0)),
            pl.BlockSpec((ROWS, 128), lambda m, h: (m, h)),
            *[ANY for _ in shards],
        ],
        out_shape=[
            jax.ShapeDtypeStruct((rows, d), BF16),
            jax.ShapeDtypeStruct((mb, 2 * pairs, ROWS, ROWS), BF16),
            jax.ShapeDtypeStruct((rows, d), F32),
            *[whole(s) for s in shards],
        ],
        scratch_shapes=[pltpu.VMEM((ROWS, ROWS), F32), pltpu.VMEM((3, 2, ROWS, 128), BF16)]
        + ([pltpu.VMEM(s.shape, s.dtype) for s in shards] + gather_sems(sum(GATHER_CUT)) if shards else []),
        compiler_params=params(**extra),
        name="attend",
        cost_estimate=pl.CostEstimate(
            flops=mb * pairs * 2 * 4 * ROWS * ROWS * 256,
            bytes_accessed=mb * pairs * 2 * ROWS * ROWS * 2,
            transcendentals=mb * pairs * 2 * ROWS * ROWS,
        ),
    )(qkv, qkv, qkv, segr, *shards)


def attend_back_body(plan, *refs):
    q_ref, k_ref, v_ref, p_ref, o_ref, g_ref, inv_ref = refs[:7]
    hosting = plan is not None
    if hosting:
        parts = refs[7:10]
        d_ref = refs[10]
        results = refs[11:14]
        ds_ref = refs[14]
        places = [(parts[i], results[i], (col, col)) for i, col, _ in unit_list([p.shape[4] for p in parts], REDUCE_CUT)]
        work = reduce_work(plan, places, refs[15:])
        moves = [[max(0, 2 * u - 1) + lag for lag in REDUCE_LAGS] for u in range(len(places))]
    else:
        d_ref, ds_ref = refs[7:]
    step = pl.program_id(0) * pl.num_programs(1) + pl.program_id(1)
    rows = q_ref.shape[0]
    lower = lax.broadcasted_iota(jnp.int32, (1, 128), 1) < HD
    dk_parts = []
    dv_parts = []
    dq_parts = []
    for hh in range(2):
        if hosting:
            hooked(step, 2, hh, 12, moves, work)
        own = lower if hh == 0 else ~lower
        half = slice(hh * HD, (hh + 1) * HD)
        g = g_ref[...].astype(F32) * inv_ref[...]
        high = g.astype(BF16)
        low = (g - high.astype(F32)).astype(BF16)
        pair = jnp.where(own, high, swap(low))
        center = jnp.sum(jnp.where(own, g * o_ref[...].astype(F32), 0.0), axis=-1, keepdims=True)
        v = twice(v_ref[...], own)
        for t in range(rows // QT):
            sl = pl.ds(t * QT, QT)
            ts = slice(t * QT, (t + 1) * QT)
            d_soft = mm(pair[ts, :], v, NT)
            ds_ref[hh, sl, :] = (p_ref[hh, sl, :].astype(F32) * (d_soft - center[ts, :])).astype(BF16)
        dv = mm(pair.T, p_ref[hh])
        dv_parts.append(dv[:HD, :] + dv[HD:, :])
        dk_parts.append(mm(q_ref[...].T[half, :], ds_ref[hh]))
        dq_parts.append(mm(ds_ref[hh], k_ref[...]))
    d_ref[0] = (jnp.where(lower, dq_parts[0], dq_parts[1]) * 0.125).astype(BF16)
    d_ref[1] = jnp.concatenate(dk_parts, axis=0).T.astype(BF16)
    d_ref[2] = jnp.concatenate(dv_parts, axis=0).T.astype(BF16)


def attend_back(qkv, soft, mixed, d_mixed, inv, grads=()):
    rows = qkv.shape[0]
    d = qkv.shape[1] // 3
    mb = rows // ROWS
    pairs = d // 128
    blk = pl.BlockSpec((ROWS, 128), lambda m, h: (m, h))
    plan = None
    results = []
    extra = {}
    grads = [g.reshape(4, 2, 2, g.shape[0] // 16, g.shape[1]) for g in grads]
    if grads:
        plan = [(grads[i].shape[3], n, BF16, True) for i, _, n in unit_list([g.shape[4] for g in grads], REDUCE_CUT)]
        results = [jax.ShapeDtypeStruct(g.shape[3:], F32) for g in grads]
        extra = dict(collective_id=2, has_side_effects=True)
    return pl.pallas_call(
        functools.partial(attend_back_body, plan),
        grid=(mb, pairs),
        in_specs=[
            blk,
            pl.BlockSpec((ROWS, 128), lambda m, h: (m, pairs + h)),
            pl.BlockSpec((ROWS, 128), lambda m, h: (m, 2 * pairs + h)),
            pl.BlockSpec((None, 2, ROWS, ROWS), lambda m, h: (m, h, 0, 0)),
            blk,
            blk,
            blk,
            *[ANY for _ in grads],
        ],
        out_specs=[
            pl.BlockSpec((3, ROWS, 128), lambda m, h: (0, m, h)),
            *[pl.BlockSpec(r.shape, lambda m, h: (0, 0)) for r in results],
        ],
        out_shape=[jax.ShapeDtypeStruct((3, rows, d), BF16), *results],
        scratch_shapes=[pltpu.VMEM((2, ROWS, ROWS), BF16)] + (reduce_scratch(plan) if grads else []),
        compiler_params=params(**extra),
        name="attend_back",
        cost_estimate=pl.CostEstimate(
            flops=mb * pairs * 2 * 8 * ROWS * ROWS * 256,
            bytes_accessed=mb * pairs * 2 * ROWS * ROWS * 2,
            transcendentals=0,
        ),
    )(qkv, qkv, qkv, soft, mixed, d_mixed, inv, *grads)


def out_body(x_ref, m_ref, w_ref, vec_ref, resid_ref, h_ref, ht_ref):
    resid = x_ref[...].astype(F32) + mm(m_ref[...], w_ref[...]) + vec_ref[4:5, :]
    resid_ref[...] = resid
    n, _ = norm_stats(resid)
    h = (n * vec_ref[5:6, :] + vec_ref[6:7, :]).astype(BF16)
    h_ref[...] = h
    ht_ref[...] = h.T


def out_project(x, mixed, w, vec):
    rows, d = x.shape
    tile = 512
    blk = pl.BlockSpec((tile, d), lambda i: (i, 0))
    return pl.pallas_call(
        out_body,
        grid=(rows // tile,),
        in_specs=[blk, blk, pl.BlockSpec((d, d), lambda i: (0, 0)), pl.BlockSpec((8, d), lambda i: (0, 0))],
        out_specs=[blk, blk, pl.BlockSpec((d, tile), lambda i: (0, i))],
        out_shape=[
            jax.ShapeDtypeStruct((rows, d), F32),
            jax.ShapeDtypeStruct((rows, d), BF16),
            jax.ShapeDtypeStruct((d, rows), BF16),
        ],
        compiler_params=params(),
        name="out_project",
        cost_estimate=pl.CostEstimate(
            flops=2 * rows * d * d, bytes_accessed=rows * d * 12, transcendentals=0
        ),
    )(x, mixed, w, vec)


FC = 512
RT = 1024


def gelu_parts(u):
    cdf = 0.5 * (1.0 + lax.erf(u * ROOT_HALF))
    bell = jnp.exp(-0.5 * u * u) * ROOT_INV_TWO_PI
    return u * cdf, cdf + u * bell


def mlp_body(h_ref, ht_ref, g_ref, gt_ref, wu_ref, bu_ref, wd_ref, acc_ref, dh_ref, dwu_ref, dwd_ref, dbu_ref,
             act_ref, du_ref):
    rows = h_ref.shape[0]

    @pl.when(pl.program_id(0) == 0)
    def _():
        acc_ref[...] = jnp.zeros_like(acc_ref)
        dh_ref[...] = jnp.zeros_like(dh_ref)

    wu = wu_ref[...]
    wd = wd_ref[...]
    bias_sum = None
    for t in range(rows // RT):
        sl = pl.ds(t * RT, RT)
        u = mm(h_ref[sl, :], wu) + bu_ref[...]
        act, slope = gelu_parts(u)
        act_ref[sl, :] = act.astype(BF16)
        du = mm(g_ref[sl, :], wd, NT) * slope
        part = jnp.sum(du, axis=0, keepdims=True)
        bias_sum = part if bias_sum is None else bias_sum + part
        du_ref[sl, :] = du.astype(BF16)
        acc_ref[sl, :] += mm(act_ref[sl, :], wd)
        dh_ref[sl, :] += mm(du_ref[sl, :], wu, NT)
    dbu_ref[...] = bias_sum
    dwu_ref[...] = mm(ht_ref[...], du_ref[...]).astype(dwu_ref.dtype)
    dwd_ref[...] = mm(gt_ref[...], act_ref[...]).T.astype(dwd_ref.dtype)


def mlp(h, ht, g, gt, wu, bu, wd):
    rows, d = h.shape
    ff = wu.shape[1]
    one = pl.Buffered(1)
    whole = pl.BlockSpec((rows, d), lambda c: (0, 0), pipeline_mode=one)
    whole_t = pl.BlockSpec((d, rows), lambda c: (0, 0), pipeline_mode=one)
    return pl.pallas_call(
        mlp_body,
        grid=(ff // FC,),
        in_specs=[
            whole,
            whole_t,
            whole,
            whole_t,
            pl.BlockSpec((d, FC), lambda c: (0, c)),
            pl.BlockSpec((1, FC), lambda c: (0, c)),
            pl.BlockSpec((FC, d), lambda c: (c, 0)),
        ],
        out_specs=[
            whole,
            whole,
            pl.BlockSpec((d, FC), lambda c: (0, c)),
            pl.BlockSpec((FC, d), lambda c: (c, 0)),
            pl.BlockSpec((1, FC), lambda c: (0, c)),
        ],
        out_shape=[
            jax.ShapeDtypeStruct((rows, d), F32),
            jax.ShapeDtypeStruct((rows, d), F32),
            jax.ShapeDtypeStruct((d, ff), BF16),
            jax.ShapeDtypeStruct((ff, d), BF16),
            jax.ShapeDtypeStruct((1, ff), F32),
        ],
        scratch_shapes=[pltpu.VMEM((rows, FC), BF16), pltpu.VMEM((rows, FC), BF16)],
        compiler_params=params(),
        name="mlp",
        cost_estimate=pl.CostEstimate(
            flops=12 * rows * d * ff, bytes_accessed=rows * d * 20 + 8 * d * ff, transcendentals=3 * rows * ff
        ),
    )(h, ht, g, gt, wu, bu, wd)


def fold(ref, row, step, value):
    part = jnp.sum(value, axis=0, keepdims=True)

    @pl.when(step == 0)
    def _():
        ref[row : row + 1, :] = part

    @pl.when(step != 0)
    def _():
        ref[row : row + 1, :] += part


def norm_pull(grad, n, inv, gain):
    dn = grad * gain
    plain = jnp.mean(dn, axis=-1, keepdims=True)
    cross = jnp.mean(dn * n, axis=-1, keepdims=True)
    return inv * (dn - plain - n * cross)


def mid_body(resid_ref, acc_ref, dh_ref, g_ref, mixed_ref, w_ref, vec_ref,
             y_ref, dr_ref, dm_ref, dw_ref, dvec_ref, sum_ref, low_ref):
    step = pl.program_id(0)

    @pl.when(step == 0)
    def _():
        dvec_ref[...] = jnp.zeros_like(dvec_ref)

    size = 128

    for t in range(resid_ref.shape[0] // size):
        sl = pl.ds(t * size, size)
        resid = resid_ref[sl, :]
        y_ref[sl, :] = (resid + acc_ref[sl, :] + vec_ref[7:8, :]).astype(BF16)
        g = g_ref[sl, :].astype(F32)
        n, inv = norm_stats(resid)
        dh = dh_ref[sl, :]
        dr = g + norm_pull(dh, n, inv, vec_ref[5:6, :])
        dr_ref[sl, :] = dr
        for row, value in ((4, dr), (5, dh * n), (6, dh), (7, g)):
            dvec_ref[row : row + 1, :] += jnp.sum(value, axis=0, keepdims=True)
        low_ref[sl, :] = dr.astype(BF16)
        dm_ref[sl, :] = mm(low_ref[sl, :], w_ref[...], NT).astype(BF16)
    low = low_ref[...]
    dw = mm(mixed_ref[...].T, low)

    @pl.when(step == 0)
    def _():
        sum_ref[...] = dw

    @pl.when(step != 0)
    def _():
        sum_ref[...] += dw

    @pl.when(step == pl.num_programs(0) - 1)
    def _():
        dw_ref[...] = sum_ref[...].astype(dw_ref.dtype)


def middle(resid, acc, dh, g, mixed, w, vec):
    rows, d = resid.shape
    tile = 512
    blk = pl.BlockSpec((tile, d), lambda i: (i, 0))
    mat = pl.BlockSpec((d, d), lambda i: (0, 0))
    eight = pl.BlockSpec((8, d), lambda i: (0, 0))
    return pl.pallas_call(
        mid_body,
        grid=(rows // tile,),
        in_specs=[blk, blk, blk, blk, blk, mat, eight],
        out_specs=[blk, blk, blk, mat, eight],
        out_shape=[
            jax.ShapeDtypeStruct((rows, d), BF16),
            jax.ShapeDtypeStruct((rows, d), F32),
            jax.ShapeDtypeStruct((rows, d), BF16),
            jax.ShapeDtypeStruct((d, d), BF16),
            jax.ShapeDtypeStruct((8, d), F32),
        ],
        scratch_shapes=[pltpu.VMEM((d, d), F32), pltpu.VMEM((tile, d), BF16)],
        compiler_params=params(),
        name="middle",
        cost_estimate=pl.CostEstimate(
            flops=4 * rows * d * d, bytes_accessed=rows * d * 24, transcendentals=0
        ),
    )(resid, acc, dh, g, mixed, w, vec)


PHASES = 3
FINAL_TILE = 256


def finish_body(plan, ht_ref, part_ref, tile_ref, x_ref, dr_ref, w_hbm, vec_ref, dvec_ref, dbu_ref, dx_ref, *refs):
    step = pl.program_id(0)
    d = x_ref.shape[1]
    if plan is None:
        dw_ref, sums_ref, w_ref, w_sem = refs
    else:
        out_ref, small_ref, w_ref, w_sem, sums_ref, grad_ref, tall_ref = refs[:7]
        places = [(grad_ref.at[j], out_ref, (col, j * d + col)) for j in range(PHASES) for col, _ in PIECES]
        places.append((tall_ref, small_ref, (0, 0)))
        work = reduce_work(plan, places, refs[7:])
        vectors = len(places) - 1
        last = vectors - 1 + ht_ref.shape[1] // FINAL_TILE
        moves = FINISH_MOVES

    fetch = pltpu.make_async_copy(w_hbm, w_ref, w_sem)

    @pl.when(step == 0)
    def _():
        if plan is not None:
            greet(wait=False)
        fetch.start()
        sums_ref[...] = dvec_ref[...]

    for i, (col, n) in enumerate(PIECES):

        @pl.when(step < PHASES)
        def _():
            cols = pl.ds(col, n)
            dw = mm(ht_ref[...], part_ref[0, :, cols]).astype(BF16)
            if plan is None:
                dw_ref[:, cols] = dw
            else:
                grad_ref[step, :, :, :, :, cols] = dw.reshape(4, 2, 2, d // 16, n)

        if plan is not None:
            for j in range(PHASES):

                @pl.when(step == j)
                def _():
                    if i == 0 and j == 0:
                        greet(signal=False)
                    at_hook(2 * j + i, moves, work, True)

    for j, row in ((0, 2), (2, 3)):

        @pl.when(step == j)
        def _():
            sums_ref[row : row + 1, :] = jnp.sum(part_ref[0].astype(F32), axis=0, keepdims=True)

    @pl.when(step == PHASES)
    def _():
        fetch.wait()

    @pl.when(step >= PHASES)
    def _():
        n, inv = norm_stats(x_ref[...].astype(F32))
        dh = None
        for j in range(3):
            term = mm(tile_ref[j], w_ref[:, pl.ds(j * d, d)], NT)
            dh = term if dh is None else dh + term
        fold(sums_ref, 0, step - PHASES, dh * n)
        fold(sums_ref, 1, step - PHASES, dh)
        dx_ref[...] = (dr_ref[...] + norm_pull(dh, n, inv, vec_ref[0:1, :])).astype(BF16)

    if plan is not None:
        for k in range(2 * PHASES, last + 1):

            @pl.when(step == k - PHASES)
            def _():
                if k == last:
                    pack(tall_ref, sums_ref, dbu_ref)
                    for hook in range(last, 1 + max(max(m) for m in moves)):
                        at_hook(hook, moves, work, True)
                else:
                    at_hook(k, moves, work, True)


FINISH_MOVES = [
    [0, 1, 5, 8, 12, 14, 18],
    [1, 2, 6, 9, 12, 14, 18],
    [2, 3, 7, 10, 13, 15, 18],
    [3, 4, 8, 11, 14, 16, 18],
    [4, 5, 9, 12, 14, 16, 18],
    [5, 6, 11, 13, 15, 17, 18],
    [13, 14, 14, 15, 16, 17, 18],
]


def pack(tall_ref, sums_ref, dbu_ref):
    d = sums_ref.shape[1] // 16
    f = dbu_ref.shape[1] // 16
    for i in range(16):
        tile = tall_ref.at[i // 4, (i // 2) % 2, i % 2]
        tile[0:8, 0:d] = sums_ref[:, i * d : (i + 1) * d]
        tile[8:9, 0:128] = dbu_ref[:, i * f : i * f + 128]
        tile[9:10, 0 : f - 128] = dbu_ref[:, i * f + 128 : (i + 1) * f]


def finish(x, dr, ht, dqkv, w, vec, dvec, dbu, near):
    rows, d = x.shape
    tiles = rows // FINAL_TILE
    row = lambda s: jnp.maximum(s - PHASES, 0)
    one = pl.Buffered(1)
    eight = pl.BlockSpec((8, d), lambda s: (0, 0))
    if near:
        plan = [(d // 16, n, BF16, True) for _ in range(PHASES) for _, n in PIECES] + [(16, 128, F32, False)]
        shapes = [jax.ShapeDtypeStruct((d // 16, 3 * d), F32), jax.ShapeDtypeStruct((16, 128), F32)]
        specs = [pl.BlockSpec(s.shape, lambda s: (0, 0)) for s in shapes]
        scratch = [
            pltpu.VMEM((8, d), F32),
            pltpu.VMEM((PHASES, 4, 2, 2, d // 16, d), BF16),
            pltpu.VMEM((4, 2, 2, 16, 128), F32),
        ] + reduce_scratch(plan)
        extra = dict(collective_id=3, has_side_effects=True)
    else:
        plan = None
        shapes = [jax.ShapeDtypeStruct((d, 3 * d), BF16), jax.ShapeDtypeStruct((8, d), F32)]
        specs = [pl.BlockSpec((d, d), lambda s: (0, jnp.minimum(s, PHASES - 1))), eight]
        scratch = []
        extra = {}
    return pl.pallas_call(
        functools.partial(finish_body, plan),
        grid=(PHASES + tiles,),
        in_specs=[
            pl.BlockSpec((d, rows), lambda s: (0, 0), pipeline_mode=one),
            pl.BlockSpec((1, rows, d), lambda s: (jnp.minimum(s, PHASES - 1), 0, 0)),
            pl.BlockSpec((3, FINAL_TILE, d), lambda s: (0, row(s), 0)),
            pl.BlockSpec((FINAL_TILE, d), lambda s: (row(s), 0)),
            pl.BlockSpec((FINAL_TILE, d), lambda s: (row(s), 0)),
            ANY,
            eight,
            eight,
            pl.BlockSpec(dbu.shape, lambda s: (0, 0)),
        ],
        out_specs=[pl.BlockSpec((FINAL_TILE, d), lambda s: (row(s), 0)), *specs],
        out_shape=[jax.ShapeDtypeStruct((rows, d), BF16), *shapes],
        scratch_shapes=[pltpu.VMEM((d, 3 * d), BF16), pltpu.SemaphoreType.DMA(()), *scratch],
        compiler_params=params(**extra),
        name="finish",
        cost_estimate=pl.CostEstimate(
            flops=12 * rows * d * d, bytes_accessed=rows * d * 20, transcendentals=0
        ),
    )(ht, dqkv, dqkv, x, dr, w, vec, dvec, dbu)


def publish_body(splits, small_ref, *refs):
    n = len(splits)
    arrays, outs = refs[:n], refs[n : 2 * n]
    vectors = refs[2 * n : 2 * n + 9]
    holds = refs[2 * n + 9 : 3 * n + 9]
    get_sem, put_sem = refs[3 * n + 9 :]
    gets, puts = [], []
    for src, out, hold, parts in zip(arrays, outs, holds, splits):
        size = src.shape[0] // parts
        for p in range(parts):
            rows = pl.ds(p * size, size)
            i = len(gets)
            gets.append(pltpu.make_async_copy(src.at[rows], hold.at[rows], get_sem.at[i]))
            puts.append(pltpu.make_async_copy(hold.at[rows], out.at[rows], put_sem.at[i]))
    for get in gets:
        get.start()
    for i, ref in enumerate(vectors[:8]):
        ref[...] = small_ref[i, 0 : ref.shape[0]]
    up = vectors[8]
    up[0:128] = small_ref[8, :]
    up[128:] = small_ref[9, 0 : up.shape[0] - 128]
    for get, put in zip(gets, puts):
        get.wait()
        put.start()
    for put in puts:
        put.wait()


def publish(small, lengths, arrays):
    splits = [8 if a.dtype == BF16 else 2 for a in arrays]
    total = sum(splits)
    vmem = pl.BlockSpec(memory_space=pltpu.VMEM)
    return pl.pallas_call(
        functools.partial(publish_body, splits),
        in_specs=[vmem] + [ANY] * len(arrays),
        out_specs=[ANY] * len(arrays) + [vmem] * 9,
        out_shape=[jax.ShapeDtypeStruct(a.shape, a.dtype) for a in arrays]
        + [jax.ShapeDtypeStruct((n,), F32) for n in lengths],
        scratch_shapes=[pltpu.VMEM(a.shape, a.dtype) for a in arrays]
        + [pltpu.SemaphoreType.DMA((total,)), pltpu.SemaphoreType.DMA((total,))],
        compiler_params=params(),
        name="publish",
    )(small, *arrays)


def on_device(tokens, cotangent, segment_ids, *shards):
    gather = lambda s: lax.all_gather(s, "fsdp", axis=0, tiled=True)
    n = lax.axis_size("fsdp")
    near = n == 16 and lax.axis_size("dp") == 2
    triple_s, out_s, up_s, down_s = (s for s in shards if s.ndim == 2)
    rows, d = tokens.shape
    up_bias_s = shards[10]
    eights = [s for i, s in enumerate(shards) if s.ndim == 1 and i != 10]
    flat = lambda w: w.reshape(-1, w.shape[-1])
    if near:
        triple_weight, vec, up_bias, qkv, first_t, cot_t = first(eights + [up_bias_s], triple_s, tokens, cotangent)
        triple_weight = flat(triple_weight)
    else:
        triple_weight = gather(triple_s)
        packed = gather(jnp.concatenate(eights + [up_bias_s]).reshape(1, -1)).astype(F32)
        m = eights[0].shape[0]
        vec = jnp.stack([packed[:, i * m : (i + 1) * m].reshape(-1) for i in range(8)])
        up_bias = packed[:, 8 * m :].reshape(1, -1)
        qkv, first_t = project(tokens, vec, triple_weight)
        cot_t = cotangent.T

    segr = segment_ids.reshape(rows // ROWS, 1, ROWS)
    if near:
        mixed, soft, inv, *full = attend(qkv, segr, (out_s, up_s, down_s))
        out_weight, up_weight, down_weight = (flat(w) for w in full)
    else:
        mixed, soft, inv = attend(qkv, segr)
        out_weight, up_weight, down_weight = gather(out_s), gather(up_s), gather(down_s)
    resid, h, ht = out_project(tokens, mixed, out_weight, vec)
    acc, dh, dwu, dwd, dbu = mlp(h, ht, cotangent, cot_t, up_weight, up_bias, down_weight)
    y, dr, dm, dwo, dvec = middle(resid, acc, dh, cotangent, mixed, out_weight, vec)
    if near:
        dqkv, out_grad, up_grad, down_grad = attend_back(qkv, soft, mixed, dm, inv, (dwo, dwu, dwd))
        dx, triple_grad, small = finish(tokens, dr, first_t, dqkv, triple_weight, vec, dvec, dbu, True)
        lengths = [d // n] * 8 + [up_bias_s.shape[0]]
        dx, triple_grad, out_grad, up_grad, down_grad, *small_grads, up_bias_grad = publish(
            small, lengths, (dx, triple_grad, out_grad, up_grad, down_grad)
        )
    else:
        (dqkv,) = attend_back(qkv, soft, mixed, dm, inv)
        dx, dwt, dvec = finish(tokens, dr, first_t, dqkv, triple_weight, vec, dvec, dbu, False)
        small = jnp.concatenate([dvec[i].reshape(n, -1) for i in range(8)] + [dbu.reshape(n, -1)], axis=1)
        small = lax.psum_scatter(small, "fsdp", scatter_dimension=0, tiled=True).reshape(-1)
        small = lax.psum(small, "dp")
        total = lambda p: lax.psum(lax.psum_scatter(p, "fsdp", scatter_dimension=0, tiled=True), "dp").astype(F32)
        triple_grad, out_grad, up_grad, down_grad = total(dwt), total(dwo), total(dwu), total(dwd)
        m = d // n
        small_grads = [small[i * m : (i + 1) * m] for i in range(8)]
        up_bias_grad = small[8 * m :]
    dg1, ds1, dqb, dvb, dob, dg2, ds2, ddb = small_grads
    return (
        y, dx, dg1, ds1, triple_grad, dqb, dvb, out_grad, dob, dg2, ds2, up_grad, up_bias_grad, down_grad, ddb,
    )


def solution(mesh):
    tok = P(("dp", "fsdp"), None)
    vec = P("fsdp")
    mat = P("fsdp", None)
    weights = (vec, vec, mat, vec, vec, mat, vec, vec, vec, mat, vec, mat, vec)
    return jax.shard_map(
        on_device,
        mesh=mesh,
        in_specs=(tok, tok, P(("dp", "fsdp")), *weights),
        out_specs=(tok, tok, *weights),
        check_vma=False,
    )
```

```python
import functools

import jax
import jax.numpy as jnp
from jax import lax
from jax.experimental import pallas as pl
from jax.experimental.pallas import tpu as pltpu
from jax.sharding import PartitionSpec as P

H = 12
HD = 64
ROWS = 1024
EPS = 1e-06
F32 = jnp.float32
BF16 = jnp.bfloat16
VMEM_LIMIT = 60 * 1024 * 1024

ROOT_HALF = 0.7071067811865476
ROOT_INV_TWO_PI = 0.3989422804014327

NN = (((1,), (0,)), ((), ()))
NT = (((1,), (1,)), ((), ()))


def mm(a, b, dims=NN):
    return lax.dot_general(a, b, dims, preferred_element_type=F32)


def params(**kw):
    return pltpu.CompilerParams(vmem_limit_bytes=VMEM_LIMIT, **kw)


def norm_stats(x):
    mean = jnp.mean(x, axis=-1, keepdims=True)
    cen = x - mean
    var = jnp.mean(cen * cen, axis=-1, keepdims=True)
    inv = lax.rsqrt(var + EPS)
    return cen * inv, inv


MESH = pl.DeviceIdType.MESH
ANY = pl.BlockSpec(memory_space=pl.ANY)


def whereabouts():
    y = lax.axis_index("dp")
    f = lax.axis_index("fsdp")
    return y, f // 4, (f // 2) % 2, f % 2


def spot(z, x, c):
    return z * 4 + x * 2 + c


def greet(signal=True, wait=True):
    y, z, x, c = whereabouts()
    barrier = pltpu.get_barrier_semaphore()
    peers = [(1 - y, spot(z, x, c)), (y, spot(z, 1 - x, c)), (y, spot(z, x, 1 - c))]
    peers += [(y, spot((z + d) % 4, x, c)) for d in (1, 2, 3)]
    if signal:
        for peer in peers:
            pl.semaphore_signal(barrier, inc=1, device_id=peer, device_id_type=MESH)
    if wait:
        pl.semaphore_wait(barrier, len(peers))


class Mover:
    def __init__(self, send, recv, local, per):
        self.send, self.recv, self.local, self.per = send, recv, local, per
        self.y, self.z, self.x, self.c = whereabouts()

    def wide(self, r, split, y):
        return pl.ds(pl.multiple_of(y * (r // 3), 8), 2 * (r // 3)) if split else pl.ds(0, r)

    def thin(self, r, y):
        return pl.ds(pl.multiple_of(y * 2 * (r // 3), 8), r // 3)

    def copy(self, u, slot, src, dst, z=None, x=None, c=None, y=None):
        i = u * self.per + slot
        pick = lambda v, own: own if v is None else v
        peer = (pick(y, self.y), spot(pick(z, self.z), pick(x, self.x), pick(c, self.c)))
        return pltpu.make_async_remote_copy(
            src_ref=src, dst_ref=dst, send_sem=self.send.at[i], recv_sem=self.recv.at[i],
            device_id=peer, device_id_type=MESH,
        )


class Gather(Mover):
    def __init__(self, units, send, recv, local):
        super().__init__(send, recv, local, 6)
        self.units = units

    def mine(self, u):
        src, _, _, col, n, split = self.units[u]
        return src.at[self.wide(src.shape[0], split, self.y), pl.ds(col, n)]

    def held(self, u):
        src, _, hold, col, n, split = self.units[u]
        return hold.at[self.wide(src.shape[0], split, self.y), pl.ds(col, n)]

    def part(self, u, z, x, c, rows):
        _, dst, _, col, n, _ = self.units[u]
        every = slice(None)
        pick = lambda v: every if v is None else v
        return dst.at[pick(z), pick(x), pick(c), rows, pl.ds(col, n)]

    def broad(self, u):
        src, _, _, _, _, split = self.units[u]
        return self.wide(src.shape[0], split, self.y)

    def load(self, u):
        return pltpu.make_async_copy(self.mine(u), self.held(u), self.local.at[2 * u])

    def store(self, u):
        dst = self.part(u, self.z, self.x, self.c, self.broad(u))
        return pltpu.make_async_copy(self.held(u), dst, self.local.at[2 * u + 1])

    def along_z(self, u, d, out=True):
        here, there = (self.z + 4 - d) % 4, (self.z + d) % 4
        dst = self.part(u, self.z if out else here, self.x, self.c, self.broad(u))
        return self.copy(u, d - 1, self.mine(u), dst, z=there)

    def along_x(self, u, out=True):
        src = self.part(u, None, self.x, self.c, self.broad(u))
        dst = src if out else self.part(u, None, 1 - self.x, self.c, self.broad(u))
        return self.copy(u, 3, src, dst, x=1 - self.x)

    def along_y(self, u, out=True):
        r = self.units[u][0].shape[0]
        src = self.part(u, None, None, self.c, self.thin(r, self.y))
        dst = src if out else self.part(u, None, None, self.c, self.thin(r, 1 - self.y))
        return self.copy(u, 4, src, dst, y=1 - self.y)

    def along_c(self, u, out=True):
        every = pl.ds(0, self.units[u][0].shape[0])
        src = self.part(u, None, None, self.c, every)
        dst = src if out else self.part(u, None, None, 1 - self.c, every)
        return self.copy(u, 5, src, dst, c=1 - self.c)

    def stage(self, s, u):
        split = self.units[u][5]
        if s == 0:
            for d in (1, 2, 3):
                self.along_z(u, d).start()
            self.load(u).start()
        if s == 1:
            self.load(u).wait()
            self.store(u).start()
        if s == 2:
            self.store(u).wait()
            for d in (1, 2, 3):
                self.along_z(u, d, False).wait_recv()
            self.along_x(u).start()
        if s == 3:
            self.along_x(u, False).wait_recv()
            if split:
                self.along_y(u).start()
            else:
                self.along_c(u).start()
        if s == 4 and split:
            self.along_y(u, False).wait_recv()
            self.along_c(u).start()
        if s == 5:
            self.along_c(u, False).wait_recv()
            for d in (1, 2, 3):
                self.along_z(u, d).wait_send()
            self.along_x(u).wait_send()
            if split:
                self.along_y(u).wait_send()
            self.along_c(u).wait_send()


def gather_sems(units):
    return [
        pltpu.SemaphoreType.DMA((units * 6,)),
        pltpu.SemaphoreType.DMA((units * 6,)),
        pltpu.SemaphoreType.DMA((2 * units,)),
    ]


def whole(shard):
    return jax.ShapeDtypeStruct((4, 2, 2, *shard.shape), shard.dtype)


class Reduce(Mover):
    def __init__(self, units, send, recv, local):
        super().__init__(send, recv, local, 7)
        self.units = units

    def size(self, u):
        return self.units[u][0].shape[3]

    def partial(self, u, c):
        src, _, (col, _), n, _, _ = self.units[u]
        return src.at[:, :, c, :, pl.ds(col, n)]

    def load(self, u):
        return pltpu.make_async_copy(self.partial(u, self.c), self.units[u][5][0], self.local.at[u])

    def over_c(self, u):
        return self.copy(u, 0, self.partial(u, 1 - self.c), self.units[u][5][1], c=1 - self.c)

    def over_y(self, u):
        own, from_y = self.units[u][5][0], self.units[u][5][5]
        return self.copy(u, 1, own.at[:, :, self.thin(self.size(u), 1 - self.y), :], from_y, y=1 - self.y)

    def over_x(self, u):
        own, from_x = self.units[u][5][0], self.units[u][5][2]
        rows = self.wide(self.size(u), self.units[u][4], self.y)
        return self.copy(u, 2, own.at[:, 1 - self.x, rows, :], from_x, x=1 - self.x)

    def over_z(self, u, d):
        own, from_z = self.units[u][5][0], self.units[u][5][3]
        rows = self.wide(self.size(u), self.units[u][4], self.y)
        to = (self.z + d) % 4
        return self.copy(u, 2 + d, own.at[to, self.x, rows, :], from_z.at[d - 1], z=to)

    def over_last(self, u):
        last = self.units[u][5][4]
        return self.copy(u, 6, last.at[0], last.at[1], y=1 - self.y)

    def stage(self, s, u):
        _, out, (_, col), n, split, (own, from_c, from_x, from_z, last, *rest) = self.units[u]
        y, z, x = self.y, self.z, self.x
        r = self.size(u)
        rows = self.wide(r, split, y)
        if s == 0:
            self.over_c(u).start()
            self.load(u).start()
        if s == 1:
            self.load(u).wait()
            self.over_c(u).wait_recv()
            own[...] = own[...] + from_c[...]
            if split:
                self.over_y(u).start()
        if s == 2:
            if split:
                self.over_y(u).wait_recv()
                mine = self.thin(r, y)
                own[:, :, mine, :] = own[:, :, mine, :] + rest[0][...]
            self.over_x(u).start()
        if s == 3:
            self.over_x(u).wait_recv()
            for k in range(4):
                own[k, x, rows, :] = own[k, x, rows, :] + from_x[k]
            for d in (1, 2, 3):
                self.over_z(u, d).start()
        if s == 4:
            total = own[z, x, rows, :].astype(F32)
            for d in (1, 2, 3):
                self.over_z(u, d).wait_recv()
                total = total + from_z[d - 1].astype(F32)
            last[0] = total.astype(last.dtype)
            self.over_last(u).start()
        if s == 5:
            self.over_last(u).wait_recv()
            cols = pl.ds(col, n)
            if split:
                t = r // 3
                at = lambda k: pl.ds(pl.multiple_of(k * t, 8), t)
                put = lambda k, v: out.__setitem__((at(k), cols), v.astype(F32))
                put(1, last[0, at(1 - y), :].astype(F32) + last[1, at(y), :].astype(F32))
                put(2 * y, last[0, at(y), :])
                put(2 * (1 - y), last[1, at(1 - y), :])
            else:
                out[:, cols] = last[0].astype(F32) + last[1].astype(F32)
        if s == 6:
            self.over_c(u).wait_send()
            if split:
                self.over_y(u).wait_send()
            self.over_x(u).wait_send()
            for d in (1, 2, 3):
                self.over_z(u, d).wait_send()
            self.over_last(u).wait_send()


def reduce_buffers(r, n, dtype, split):
    wide = 2 * r // 3 if split else r
    shapes = [(4, 2, r, n), (4, 2, r, n), (4, wide, n), (3, wide, n), (2, wide, n)]
    if split:
        shapes.append((4, 2, r // 3, n))
    return [pltpu.VMEM(shape, dtype) for shape in shapes]


def reduce_scratch(plan):
    flat = []
    for p in plan:
        flat += reduce_buffers(*p)
    units = len(plan)
    return flat + [
        pltpu.SemaphoreType.DMA((units * 7,)),
        pltpu.SemaphoreType.DMA((units * 7,)),
        pltpu.SemaphoreType.DMA((units,)),
    ]


def reduce_work(plan, places, scratch):
    units = []
    at = 0
    for (_, n, _, split), (src, out, col) in zip(plan, places):
        count = 6 if split else 5
        units.append((src, out, col, n, split, scratch[at : at + count]))
        at += count
    return Reduce(units, *scratch[at:])


def at_hook(hook, moves, work, newest=False):
    for u, hooks in list(enumerate(moves))[:: -1 if newest else 1]:
        for s, when in enumerate(hooks):
            if when == hook:
                work.stage(s, u)


def hooked(step, per_step, which, steps, moves, work, late=False):
    if late and which == 0:

        @pl.when(step == 0)
        def _():
            greet(wait=False)

    for k in range(steps):
        if any(k * per_step + which in hooks for hooks in moves):

            @pl.when(step == k)
            def _():
                if which == 0 and k == late:
                    greet(signal=not late)
                at_hook(k * per_step + which, moves, work)


def unpack(vec_ref, ub_ref, tall_ref):
    d = vec_ref.shape[1] // 16
    f = ub_ref.shape[1] // 16
    for i in range(16):
        tile = tall_ref[i // 4, (i // 2) % 2, i % 2].astype(F32)
        vec_ref[:, i * d : (i + 1) * d] = tile[0:8, 0:d]
        ub_ref[:, i * f : i * f + 128] = tile[8:9, 0:128]
        ub_ref[:, i * f + 128 : (i + 1) * f] = tile[9:10, 0 : f - 128]


PIECES = ((0, 512), (512, 256))
FIRST_LAGS = (0, 1, 2, 4, 6, 8)


def first_body(*refs):
    vectors = refs[:9]
    t_ref, x_hbm, g_hbm = refs[9:12]
    w_hbm, vec_ref, ub_ref, qkv_hbm, ht_hbm, gt_hbm = refs[12:18]
    row_ref, tile_ref, tall_ref, vh_ref, w_ref, th_ref, x_ref, g_ref, h_ref, ht_ref, gt_ref, out_ref = refs[18:30]
    move_sem, out_sem, w_sem, *sems = refs[30:]
    rows, d = x_ref.shape
    columns = [(j, j * d + col, n) for j in range(3) for col, n in PIECES]
    units = [(tile_ref, tall_ref, vh_ref, 0, 128, False)]
    units += [(t_ref, w_ref, th_ref, col, n, True) for _, col, n in columns]
    work = Gather(units, *sems)
    moves = [[0, 1, 2, 3, 4, 5]] + [[u + lag for lag in FIRST_LAGS] for u in range(len(columns))]
    local = lambda i, src, dst: pltpu.make_async_copy(src, dst, move_sem.at[i])
    get_x, get_g = local(0, x_hbm, x_ref), local(1, g_hbm, g_ref)
    put_h, put_g = local(2, ht_ref, ht_hbm), local(3, gt_ref, gt_hbm)

    greet(wait=False)
    get_g.start()
    get_x.start()
    for i, ref in enumerate(vectors[:8]):
        row_ref[i : i + 1, 0 : ref.shape[0]] = ref[...].astype(F32).reshape(1, -1)
    up = vectors[8][...].astype(F32).reshape(1, -1)
    row_ref[8:9, :] = up[:, :128]
    row_ref[9:10, 0 : up.shape[1] - 128] = up[:, 128:]
    tile_ref[...] = row_ref[...].astype(BF16)
    greet(signal=False)
    at_hook(0, moves, work)
    get_g.wait()
    for t in range(4):

        @pl.loop(0, rows // 4 // 128)
        def _(i):
            part = pl.ds(pl.multiple_of(t * (rows // 4) + i * 128, 128), 128)
            gt_ref[:, part] = g_ref[part, :].T

        at_hook(1 + t, moves, work)
    put_g.start()
    get_x.wait()
    at_hook(5, moves, work)
    unpack(vec_ref, ub_ref, tall_ref)
    for t in range(4):

        @pl.loop(0, rows // 4 // 128)
        def _(i):
            part = pl.ds(pl.multiple_of(t * (rows // 4) + i * 128, 128), 128)
            n, _ = norm_stats(x_ref[part, :].astype(F32))
            h = (n * vec_ref[0:1, :] + vec_ref[1:2, :]).astype(BF16)
            h_ref[part, :] = h
            ht_ref[:, part] = h.T

        at_hook(6 + t, moves, work)
    put_h.start()

    def place(u):
        _, col, n = columns[u]
        return pltpu.make_async_copy(out_ref.at[u % 2, :, pl.ds(0, n)], qkv_hbm.at[:, pl.ds(col, n)], out_sem.at[u])

    def keep(u):
        _, col, n = columns[u]
        cols = pl.ds(col, n)
        return pltpu.make_async_copy(w_ref.at[:, :, :, :, cols], w_hbm.at[:, :, :, :, cols], w_sem.at[u])

    for u, (j, col, n) in enumerate(columns):
        if u:
            at_hook(9 + u, moves, work)
        keep(u).start()
        if u >= 2:
            place(u - 2).wait()
        own = slice(col - j * d, col - j * d + n)

        @pl.loop(0, 4)
        def _(t):
            part = pl.ds(pl.multiple_of(t * (rows // 4), 8), rows // 4)
            p = mm(h_ref[part, :], w_ref[:, :, :, :, col : col + n].reshape(d, n))
            if j == 0:
                p = (p + vec_ref[2:3, own]) * 0.125
            if j == 2:
                p = p + vec_ref[3:4, own]
            out_ref[u % 2, part, 0:n] = p.astype(BF16)

        place(u).start()
    put_g.wait()
    put_h.wait()
    for u in range(len(columns)):
        keep(u).wait()
        if u >= len(columns) - 2:
            place(u).wait()


def first(vectors, triple, x, g):
    rows, d = x.shape
    vmem = pl.BlockSpec(memory_space=pltpu.VMEM)
    across = pltpu.VMEM((d, rows), BF16)
    down = pltpu.VMEM((rows, d), BF16)
    pieces = 3 * len(PIECES)
    return pl.pallas_call(
        first_body,
        in_specs=[vmem] * 9 + [ANY] * 3,
        out_specs=[ANY, vmem, vmem, ANY, ANY, ANY],
        out_shape=[
            whole(triple),
            jax.ShapeDtypeStruct((8, d), F32),
            jax.ShapeDtypeStruct((1, 4 * d), F32),
            jax.ShapeDtypeStruct((rows, 3 * d), BF16),
            jax.ShapeDtypeStruct((d, rows), BF16),
            jax.ShapeDtypeStruct((d, rows), BF16),
        ],
        scratch_shapes=[
            pltpu.VMEM((16, 128), F32),
            pltpu.VMEM((16, 128), BF16),
            pltpu.VMEM((4, 2, 2, 16, 128), BF16),
            pltpu.VMEM((16, 128), BF16),
            pltpu.VMEM((4, 2, 2, *triple.shape), BF16),
            pltpu.VMEM(triple.shape, BF16),
            down,
            down,
            down,
            across,
            across,
            pltpu.VMEM((2, rows, PIECES[0][1]), BF16),
            pltpu.SemaphoreType.DMA((4,)),
            pltpu.SemaphoreType.DMA((pieces,)),
            pltpu.SemaphoreType.DMA((pieces,)),
            *gather_sems(1 + pieces),
        ],
        compiler_params=params(collective_id=0, has_side_effects=True),
        name="first",
    )(*vectors, triple, x, g)


def proj_body(x_ref, vec_ref, w_ref, qkv_ref, ht_ref):
    d = x_ref.shape[1]
    n, _ = norm_stats(x_ref[...].astype(F32))
    h = (n * vec_ref[0:1, :] + vec_ref[1:2, :]).astype(BF16)
    ht_ref[...] = h.T
    for j in range(3):
        cols = pl.ds(j * d, d)
        p = mm(h, w_ref[:, cols])
        if j == 0:
            p = (p + vec_ref[2:3, :]) * 0.125
        if j == 2:
            p = p + vec_ref[3:4, :]
        qkv_ref[:, cols] = p.astype(BF16)


def project(x, vec, w):
    rows, d = x.shape
    cols = w.shape[1]
    tile = 512
    return pl.pallas_call(
        proj_body,
        grid=(rows // tile,),
        in_specs=[
            pl.BlockSpec((tile, d), lambda i: (i, 0)),
            pl.BlockSpec((8, d), lambda i: (0, 0)),
            pl.BlockSpec((d, cols), lambda i: (0, 0)),
        ],
        out_specs=[
            pl.BlockSpec((tile, cols), lambda i: (i, 0)),
            pl.BlockSpec((d, tile), lambda i: (0, i)),
        ],
        out_shape=[jax.ShapeDtypeStruct((rows, cols), BF16), jax.ShapeDtypeStruct((d, rows), BF16)],
        compiler_params=params(),
        name="project",
        cost_estimate=pl.CostEstimate(
            flops=2 * rows * d * cols, bytes_accessed=2 * rows * (d + cols), transcendentals=0
        ),
    )(x, vec, w)


QT = 256
GATHER_CUT = (2, 8, 6)
REDUCE_CUT = (1, 3, 3)
GATHER_LAGS = (0, 1, 2, 4, 6, 8)
REDUCE_LAGS = (0, 1, 4, 7, 10, 12, 12)


LOG2E = 1.4426950408889634


def swap(value):
    return jnp.concatenate([value[:, HD:], value[:, :HD]], axis=1)


def twice(value, own):
    return jnp.where(own, value, swap(value))


def unit_list(widths, cuts):
    return [(i, j * (w // cut), w // cut) for i, (w, cut) in enumerate(zip(widths, cuts)) for j in range(cut)]


def attend_body(hosting, *refs):
    q_ref, k_ref, v_ref, seg_ref = refs[:4]
    if hosting:
        shards = refs[4:7]
        o_ref, p_ref, inv_ref = refs[7:10]
        full = refs[10:13]
        bias_ref, pair_ref = refs[13:15]
        hold = refs[15:18]
        units = [(shards[i], full[i], hold[i], col, n, True) for i, col, n in unit_list([s.shape[1] for s in shards], GATHER_CUT)]
        work = Gather(units, *refs[18:])
        moves = [[u + lag for lag in GATHER_LAGS] for u in range(len(units))]
    else:
        o_ref, p_ref, inv_ref, bias_ref, pair_ref = refs[4:]
    step = pl.program_id(0) * pl.num_programs(1) + pl.program_id(1)
    rows = q_ref.shape[0]

    @pl.when(pl.program_id(1) == 0)
    def _():
        seg = seg_ref[...].astype(F32)
        column = jnp.broadcast_to(seg, (8, rows)).T[:, 0:1]
        bias_ref[...] = jnp.where(column == seg, 0.0, -1e30)

    lower = lax.broadcasted_iota(jnp.int32, (1, 128), 1) < HD
    lower = lax.broadcasted_iota(jnp.int32, (1, 128), 1) < HD
    lower = lax.broadcasted_iota(jnp.int32, (1, 128), 1) < HD
    sums = []
    for hh in range(2):
        if hosting:
            hooked(step, 2, hh, 12, moves, work)
        own = lower if hh == 0 else ~lower
        q = q_ref[...].astype(F32) * LOG2E
        high = q.astype(BF16)
        low = (q - high.astype(F32)).astype(BF16)
        pair_ref[0, hh] = jnp.where(own, high, swap(low))
        pair_ref[1, hh] = twice(k_ref[...], own)
        pair_ref[2, hh] = jnp.where(own, v_ref[...], jnp.ones_like(v_ref[...]))
        if hh == 1:
            sums.append(mm(p_ref[0], pair_ref[2, 0]))
        for t in range(rows // QT):
            sl = pl.ds(t * QT, QT)
            s = mm(pair_ref[0, hh, sl, :], pair_ref[1, hh], NT) + bias_ref[sl, :]
            p_ref[hh, sl, :] = jnp.exp2(s - jnp.max(s, axis=-1, keepdims=True)).astype(BF16)
    sums.append(mm(p_ref[1], pair_ref[2, 1]))
    inv = 1.0 / swap(jnp.where(lower, sums[1], sums[0]))
    inv_ref[...] = inv
    o_ref[...] = (jnp.where(lower, sums[0], sums[1]) * inv).astype(BF16)


def attend(qkv, segr, shards=()):
    rows = qkv.shape[0]
    d = qkv.shape[1] // 3
    mb = rows // ROWS
    pairs = d // 128
    extra = dict(collective_id=1, has_side_effects=True) if shards else {}
    return pl.pallas_call(
        functools.partial(attend_body, bool(shards)),
        grid=(mb, pairs),
        in_specs=[
            pl.BlockSpec((ROWS, 128), lambda m, h: (m, h)),
            pl.BlockSpec((ROWS, 128), lambda m, h: (m, pairs + h)),
            pl.BlockSpec((ROWS, 128), lambda m, h: (m, 2 * pairs + h)),
            pl.BlockSpec((None, 1, ROWS), lambda m, h: (m, 0, 0)),
            *[ANY for _ in shards],
        ],
        out_specs=[
            pl.BlockSpec((ROWS, 128), lambda m, h: (m, h)),
            pl.BlockSpec((None, 2, ROWS, ROWS), lambda m, h: (m, h, 0, 0)),
            pl.BlockSpec((ROWS, 128), lambda m, h: (m, h)),
            *[ANY for _ in shards],
        ],
        out_shape=[
            jax.ShapeDtypeStruct((rows, d), BF16),
            jax.ShapeDtypeStruct((mb, 2 * pairs, ROWS, ROWS), BF16),
            jax.ShapeDtypeStruct((rows, d), F32),
            *[whole(s) for s in shards],
        ],
        scratch_shapes=[pltpu.VMEM((ROWS, ROWS), F32), pltpu.VMEM((3, 2, ROWS, 128), BF16)]
        + ([pltpu.VMEM(s.shape, s.dtype) for s in shards] + gather_sems(sum(GATHER_CUT)) if shards else []),
        compiler_params=params(**extra),
        name="attend",
        cost_estimate=pl.CostEstimate(
            flops=mb * pairs * 2 * 4 * ROWS * ROWS * 256,
            bytes_accessed=mb * pairs * 2 * ROWS * ROWS * 2,
            transcendentals=mb * pairs * 2 * ROWS * ROWS,
        ),
    )(qkv, qkv, qkv, segr, *shards)


def attend_back_body(plan, *refs):
    q_ref, k_ref, v_ref, p_ref, o_ref, g_ref, inv_ref = refs[:7]
    hosting = plan is not None
    if hosting:
        parts = refs[7:10]
        d_ref = refs[10]
        results = refs[11:14]
        ds_ref = refs[14]
        places = [(parts[i], results[i], (col, col)) for i, col, _ in unit_list([p.shape[4] for p in parts], REDUCE_CUT)]
        work = reduce_work(plan, places, refs[15:])
        moves = [[max(0, 2 * u - 1) + lag for lag in REDUCE_LAGS] for u in range(len(places))]
    else:
        d_ref, ds_ref = refs[7:]
    step = pl.program_id(0) * pl.num_programs(1) + pl.program_id(1)
    rows = q_ref.shape[0]
    lower = lax.broadcasted_iota(jnp.int32, (1, 128), 1) < HD
    dk_parts = []
    dv_parts = []
    dq_parts = []
    for hh in range(2):
        if hosting:
            hooked(step, 2, hh, 12, moves, work)
        own = lower if hh == 0 else ~lower
        half = slice(hh * HD, (hh + 1) * HD)
        g = g_ref[...].astype(F32) * inv_ref[...]
        high = g.astype(BF16)
        low = (g - high.astype(F32)).astype(BF16)
        pair = jnp.where(own, high, swap(low))
        center = jnp.sum(jnp.where(own, g * o_ref[...].astype(F32), 0.0), axis=-1, keepdims=True)
        v = twice(v_ref[...], own)
        for t in range(rows // QT):
            sl = pl.ds(t * QT, QT)
            ts = slice(t * QT, (t + 1) * QT)
            d_soft = mm(pair[ts, :], v, NT)
            ds_ref[hh, sl, :] = (p_ref[hh, sl, :].astype(F32) * (d_soft - center[ts, :])).astype(BF16)
        dv = mm(pair.T, p_ref[hh])
        dv_parts.append(dv[:HD, :] + dv[HD:, :])
        dk_parts.append(mm(q_ref[...].T[half, :], ds_ref[hh]))
        dq_parts.append(mm(ds_ref[hh], k_ref[...]))
    d_ref[0] = (jnp.where(lower, dq_parts[0], dq_parts[1]) * 0.125).astype(BF16)
    d_ref[1] = jnp.concatenate(dk_parts, axis=0).T.astype(BF16)
    d_ref[2] = jnp.concatenate(dv_parts, axis=0).T.astype(BF16)


def attend_back(qkv, soft, mixed, d_mixed, inv, grads=()):
    rows = qkv.shape[0]
    d = qkv.shape[1] // 3
    mb = rows // ROWS
    pairs = d // 128
    blk = pl.BlockSpec((ROWS, 128), lambda m, h: (m, h))
    plan = None
    results = []
    extra = {}
    grads = [g.reshape(4, 2, 2, g.shape[0] // 16, g.shape[1]) for g in grads]
    if grads:
        plan = [(grads[i].shape[3], n, BF16, True) for i, _, n in unit_list([g.shape[4] for g in grads], REDUCE_CUT)]
        results = [jax.ShapeDtypeStruct(g.shape[3:], F32) for g in grads]
        extra = dict(collective_id=2, has_side_effects=True)
    return pl.pallas_call(
        functools.partial(attend_back_body, plan),
        grid=(mb, pairs),
        in_specs=[
            blk,
            pl.BlockSpec((ROWS, 128), lambda m, h: (m, pairs + h)),
            pl.BlockSpec((ROWS, 128), lambda m, h: (m, 2 * pairs + h)),
            pl.BlockSpec((None, 2, ROWS, ROWS), lambda m, h: (m, h, 0, 0)),
            blk,
            blk,
            blk,
            *[ANY for _ in grads],
        ],
        out_specs=[
            pl.BlockSpec((3, ROWS, 128), lambda m, h: (0, m, h)),
            *[pl.BlockSpec(r.shape, lambda m, h: (0, 0)) for r in results],
        ],
        out_shape=[jax.ShapeDtypeStruct((3, rows, d), BF16), *results],
        scratch_shapes=[pltpu.VMEM((2, ROWS, ROWS), BF16)] + (reduce_scratch(plan) if grads else []),
        compiler_params=params(**extra),
        name="attend_back",
        cost_estimate=pl.CostEstimate(
            flops=mb * pairs * 2 * 8 * ROWS * ROWS * 256,
            bytes_accessed=mb * pairs * 2 * ROWS * ROWS * 2,
            transcendentals=0,
        ),
    )(qkv, qkv, qkv, soft, mixed, d_mixed, inv, *grads)


def out_body(x_ref, m_ref, w_ref, vec_ref, resid_ref, h_ref, ht_ref):
    size = 256
    for t in range(x_ref.shape[0] // size):
        sl = pl.ds(t * size, size)
        resid = x_ref[sl, :].astype(F32) + mm(m_ref[sl, :], w_ref[...]) + vec_ref[4:5, :]
        resid_ref[sl, :] = resid
        n, _ = norm_stats(resid)
        h = (n * vec_ref[5:6, :] + vec_ref[6:7, :]).astype(BF16)
        h_ref[sl, :] = h
        ht_ref[:, t * size : (t + 1) * size] = h.T


def out_project(x, mixed, w, vec):
    rows, d = x.shape
    tile = 512
    blk = pl.BlockSpec((tile, d), lambda i: (i, 0))
    return pl.pallas_call(
        out_body,
        grid=(rows // tile,),
        in_specs=[blk, blk, pl.BlockSpec((d, d), lambda i: (0, 0)), pl.BlockSpec((8, d), lambda i: (0, 0))],
        out_specs=[blk, blk, pl.BlockSpec((d, tile), lambda i: (0, i))],
        out_shape=[
            jax.ShapeDtypeStruct((rows, d), F32),
            jax.ShapeDtypeStruct((rows, d), BF16),
            jax.ShapeDtypeStruct((d, rows), BF16),
        ],
        compiler_params=params(),
        name="out_project",
        cost_estimate=pl.CostEstimate(
            flops=2 * rows * d * d, bytes_accessed=rows * d * 12, transcendentals=0
        ),
    )(x, mixed, w, vec)


FC = 512
RT = 1024


def gelu_parts(u):
    cdf = 0.5 * (1.0 + lax.erf(u * ROOT_HALF))
    bell = jnp.exp(-0.5 * u * u) * ROOT_INV_TWO_PI
    return u * cdf, cdf + u * bell


def mlp_body(h_ref, ht_ref, g_ref, gt_ref, wu_ref, bu_ref, wd_ref, acc_ref, dh_ref, dwu_ref, dwd_ref, dbu_ref,
             act_ref, du_ref):
    rows = h_ref.shape[0]

    @pl.when(pl.program_id(0) == 0)
    def _():
        acc_ref[...] = jnp.zeros_like(acc_ref)
        dh_ref[...] = jnp.zeros_like(dh_ref)

    wu = wu_ref[...]
    wd = wd_ref[...]
    bias_sum = None
    for t in range(rows // RT):
        sl = pl.ds(t * RT, RT)
        u = mm(h_ref[sl, :], wu) + bu_ref[...]
        act, slope = gelu_parts(u)
        act_ref[sl, :] = act.astype(BF16)
        du = mm(g_ref[sl, :], wd, NT) * slope
        part = jnp.sum(du, axis=0, keepdims=True)
        bias_sum = part if bias_sum is None else bias_sum + part
        du_ref[sl, :] = du.astype(BF16)
        acc_ref[sl, :] += mm(act_ref[sl, :], wd)
        dh_ref[sl, :] += mm(du_ref[sl, :], wu, NT)
    dbu_ref[...] = bias_sum
    dwu_ref[...] = mm(ht_ref[...], du_ref[...]).astype(dwu_ref.dtype)
    dwd_ref[...] = mm(gt_ref[...], act_ref[...]).T.astype(dwd_ref.dtype)


def mlp(h, ht, g, gt, wu, bu, wd):
    rows, d = h.shape
    ff = wu.shape[1]
    one = pl.Buffered(1)
    whole = pl.BlockSpec((rows, d), lambda c: (0, 0), pipeline_mode=one)
    whole_t = pl.BlockSpec((d, rows), lambda c: (0, 0), pipeline_mode=one)
    return pl.pallas_call(
        mlp_body,
        grid=(ff // FC,),
        in_specs=[
            whole,
            whole_t,
            whole,
            whole_t,
            pl.BlockSpec((d, FC), lambda c: (0, c)),
            pl.BlockSpec((1, FC), lambda c: (0, c)),
            pl.BlockSpec((FC, d), lambda c: (c, 0)),
        ],
        out_specs=[
            whole,
            whole,
            pl.BlockSpec((d, FC), lambda c: (0, c)),
            pl.BlockSpec((FC, d), lambda c: (c, 0)),
            pl.BlockSpec((1, FC), lambda c: (0, c)),
        ],
        out_shape=[
            jax.ShapeDtypeStruct((rows, d), F32),
            jax.ShapeDtypeStruct((rows, d), F32),
            jax.ShapeDtypeStruct((d, ff), BF16),
            jax.ShapeDtypeStruct((ff, d), BF16),
            jax.ShapeDtypeStruct((1, ff), F32),
        ],
        scratch_shapes=[pltpu.VMEM((rows, FC), BF16), pltpu.VMEM((rows, FC), BF16)],
        compiler_params=params(),
        name="mlp",
        cost_estimate=pl.CostEstimate(
            flops=12 * rows * d * ff, bytes_accessed=rows * d * 20 + 8 * d * ff, transcendentals=3 * rows * ff
        ),
    )(h, ht, g, gt, wu, bu, wd)


def fold(ref, row, step, value):
    part = jnp.sum(value, axis=0, keepdims=True)

    @pl.when(step == 0)
    def _():
        ref[row : row + 1, :] = part

    @pl.when(step != 0)
    def _():
        ref[row : row + 1, :] += part


def norm_pull(grad, n, inv, gain):
    dn = grad * gain
    plain = jnp.mean(dn, axis=-1, keepdims=True)
    cross = jnp.mean(dn * n, axis=-1, keepdims=True)
    return inv * (dn - plain - n * cross)


def mid_body(resid_ref, acc_ref, dh_ref, g_ref, mixed_ref, w_ref, vec_ref,
             y_ref, dr_ref, dm_ref, dw_ref, dvec_ref, sum_ref, low_ref):
    step = pl.program_id(0)

    @pl.when(step == 0)
    def _():
        dvec_ref[...] = jnp.zeros_like(dvec_ref)

    size = 128

    for t in range(resid_ref.shape[0] // size):
        sl = pl.ds(t * size, size)
        resid = resid_ref[sl, :]
        y_ref[sl, :] = (resid + acc_ref[sl, :] + vec_ref[7:8, :]).astype(BF16)
        g = g_ref[sl, :].astype(F32)
        n, inv = norm_stats(resid)
        dh = dh_ref[sl, :]
        dr = g + norm_pull(dh, n, inv, vec_ref[5:6, :])
        dr_ref[sl, :] = dr
        for row, value in ((4, dr), (5, dh * n), (6, dh), (7, g)):
            dvec_ref[row : row + 1, :] += jnp.sum(value, axis=0, keepdims=True)
        low_ref[sl, :] = dr.astype(BF16)
        dm_ref[sl, :] = mm(low_ref[sl, :], w_ref[...], NT).astype(BF16)
    low = low_ref[...]
    dw = mm(mixed_ref[...].T, low)

    @pl.when(step == 0)
    def _():
        sum_ref[...] = dw

    @pl.when(step != 0)
    def _():
        sum_ref[...] += dw

    @pl.when(step == pl.num_programs(0) - 1)
    def _():
        dw_ref[...] = sum_ref[...].astype(dw_ref.dtype)


def middle(resid, acc, dh, g, mixed, w, vec):
    rows, d = resid.shape
    tile = 512
    blk = pl.BlockSpec((tile, d), lambda i: (i, 0))
    mat = pl.BlockSpec((d, d), lambda i: (0, 0))
    eight = pl.BlockSpec((8, d), lambda i: (0, 0))
    return pl.pallas_call(
        mid_body,
        grid=(rows // tile,),
        in_specs=[blk, blk, blk, blk, blk, mat, eight],
        out_specs=[blk, blk, blk, mat, eight],
        out_shape=[
            jax.ShapeDtypeStruct((rows, d), BF16),
            jax.ShapeDtypeStruct((rows, d), F32),
            jax.ShapeDtypeStruct((rows, d), BF16),
            jax.ShapeDtypeStruct((d, d), BF16),
            jax.ShapeDtypeStruct((8, d), F32),
        ],
        scratch_shapes=[pltpu.VMEM((d, d), F32), pltpu.VMEM((tile, d), BF16)],
        compiler_params=params(),
        name="middle",
        cost_estimate=pl.CostEstimate(
            flops=4 * rows * d * d, bytes_accessed=rows * d * 24, transcendentals=0
        ),
    )(resid, acc, dh, g, mixed, w, vec)


PHASES = 3
FINAL_TILE = 256


def finish_body(plan, ht_ref, part_ref, tile_ref, x_ref, dr_ref, w_hbm, vec_ref, dvec_ref, dbu_ref, dx_ref, *refs):
    step = pl.program_id(0)
    d = x_ref.shape[1]
    if plan is None:
        dw_ref, sums_ref, w_ref, w_sem = refs
    else:
        out_ref, small_ref, w_ref, w_sem, sums_ref, grad_ref, tall_ref = refs[:7]
        places = [(grad_ref.at[j], out_ref, (col, j * d + col)) for j in range(PHASES) for col, _ in PIECES]
        places.append((tall_ref, small_ref, (0, 0)))
        work = reduce_work(plan, places, refs[7:])
        vectors = len(places) - 1
        last = vectors - 1 + ht_ref.shape[1] // FINAL_TILE
        moves = FINISH_MOVES

    fetch = pltpu.make_async_copy(w_hbm, w_ref, w_sem)

    @pl.when(step == 0)
    def _():
        if plan is not None:
            greet(wait=False)
        fetch.start()
        sums_ref[...] = dvec_ref[...]

    for i, (col, n) in enumerate(PIECES):

        @pl.when(step < PHASES)
        def _():
            cols = pl.ds(col, n)
            dw = mm(ht_ref[...], part_ref[0, :, cols]).astype(BF16)
            if plan is None:
                dw_ref[:, cols] = dw
            else:
                grad_ref[step, :, :, :, :, cols] = dw.reshape(4, 2, 2, d // 16, n)

        if plan is not None:
            for j in range(PHASES):

                @pl.when(step == j)
                def _():
                    if i == 0 and j == 0:
                        greet(signal=False)
                    at_hook(2 * j + i, moves, work, True)

    for j, row in ((0, 2), (2, 3)):

        @pl.when(step == j)
        def _():
            sums_ref[row : row + 1, :] = jnp.sum(part_ref[0].astype(F32), axis=0, keepdims=True)

    @pl.when(step == PHASES)
    def _():
        fetch.wait()

    @pl.when(step >= PHASES)
    def _():
        n, inv = norm_stats(x_ref[...].astype(F32))
        dh = None
        for j in range(3):
            term = mm(tile_ref[j], w_ref[:, pl.ds(j * d, d)], NT)
            dh = term if dh is None else dh + term
        fold(sums_ref, 0, step - PHASES, dh * n)
        fold(sums_ref, 1, step - PHASES, dh)
        dx_ref[...] = (dr_ref[...] + norm_pull(dh, n, inv, vec_ref[0:1, :])).astype(BF16)

    if plan is not None:
        for k in range(2 * PHASES, last + 1):

            @pl.when(step == k - PHASES)
            def _():
                if k == last:
                    pack(tall_ref, sums_ref, dbu_ref)
                    for hook in range(last, 1 + max(max(m) for m in moves)):
                        at_hook(hook, moves, work, True)
                else:
                    at_hook(k, moves, work, True)


FINISH_MOVES = [
    [0, 1, 5, 8, 12, 14, 18],
    [1, 2, 6, 9, 12, 14, 18],
    [2, 3, 7, 10, 13, 15, 18],
    [3, 4, 8, 11, 14, 16, 18],
    [4, 5, 9, 12, 14, 16, 18],
    [5, 6, 11, 13, 15, 17, 18],
    [13, 14, 14, 15, 16, 17, 18],
]


def pack(tall_ref, sums_ref, dbu_ref):
    d = sums_ref.shape[1] // 16
    f = dbu_ref.shape[1] // 16
    for i in range(16):
        tile = tall_ref.at[i // 4, (i // 2) % 2, i % 2]
        tile[0:8, 0:d] = sums_ref[:, i * d : (i + 1) * d]
        tile[8:9, 0:128] = dbu_ref[:, i * f : i * f + 128]
        tile[9:10, 0 : f - 128] = dbu_ref[:, i * f + 128 : (i + 1) * f]


def finish(x, dr, ht, dqkv, w, vec, dvec, dbu, near):
    rows, d = x.shape
    tiles = rows // FINAL_TILE
    row = lambda s: jnp.maximum(s - PHASES, 0)
    one = pl.Buffered(1)
    eight = pl.BlockSpec((8, d), lambda s: (0, 0))
    if near:
        plan = [(d // 16, n, BF16, True) for _ in range(PHASES) for _, n in PIECES] + [(16, 128, F32, False)]
        shapes = [jax.ShapeDtypeStruct((d // 16, 3 * d), F32), jax.ShapeDtypeStruct((16, 128), F32)]
        specs = [pl.BlockSpec(s.shape, lambda s: (0, 0)) for s in shapes]
        scratch = [
            pltpu.VMEM((8, d), F32),
            pltpu.VMEM((PHASES, 4, 2, 2, d // 16, d), BF16),
            pltpu.VMEM((4, 2, 2, 16, 128), F32),
        ] + reduce_scratch(plan)
        extra = dict(collective_id=3, has_side_effects=True)
    else:
        plan = None
        shapes = [jax.ShapeDtypeStruct((d, 3 * d), BF16), jax.ShapeDtypeStruct((8, d), F32)]
        specs = [pl.BlockSpec((d, d), lambda s: (0, jnp.minimum(s, PHASES - 1))), eight]
        scratch = []
        extra = {}
    return pl.pallas_call(
        functools.partial(finish_body, plan),
        grid=(PHASES + tiles,),
        in_specs=[
            pl.BlockSpec((d, rows), lambda s: (0, 0), pipeline_mode=one),
            pl.BlockSpec((1, rows, d), lambda s: (jnp.minimum(s, PHASES - 1), 0, 0)),
            pl.BlockSpec((3, FINAL_TILE, d), lambda s: (0, row(s), 0)),
            pl.BlockSpec((FINAL_TILE, d), lambda s: (row(s), 0)),
            pl.BlockSpec((FINAL_TILE, d), lambda s: (row(s), 0)),
            ANY,
            eight,
            eight,
            pl.BlockSpec(dbu.shape, lambda s: (0, 0)),
        ],
        out_specs=[pl.BlockSpec((FINAL_TILE, d), lambda s: (row(s), 0)), *specs],
        out_shape=[jax.ShapeDtypeStruct((rows, d), BF16), *shapes],
        scratch_shapes=[pltpu.VMEM((d, 3 * d), BF16), pltpu.SemaphoreType.DMA(()), *scratch],
        compiler_params=params(**extra),
        name="finish",
        cost_estimate=pl.CostEstimate(
            flops=12 * rows * d * d, bytes_accessed=rows * d * 20, transcendentals=0
        ),
    )(ht, dqkv, dqkv, x, dr, w, vec, dvec, dbu)


def publish_body(splits, small_ref, *refs):
    n = len(splits)
    arrays, outs = refs[:n], refs[n : 2 * n]
    vectors = refs[2 * n : 2 * n + 9]
    holds = refs[2 * n + 9 : 3 * n + 9]
    get_sem, put_sem = refs[3 * n + 9 :]
    gets, puts = [], []
    for src, out, hold, parts in zip(arrays, outs, holds, splits):
        size = src.shape[0] // parts
        for p in range(parts):
            rows = pl.ds(p * size, size)
            i = len(gets)
            gets.append(pltpu.make_async_copy(src.at[rows], hold.at[rows], get_sem.at[i]))
            puts.append(pltpu.make_async_copy(hold.at[rows], out.at[rows], put_sem.at[i]))
    for get in gets:
        get.start()
    for i, ref in enumerate(vectors[:8]):
        ref[...] = small_ref[i, 0 : ref.shape[0]]
    up = vectors[8]
    up[0:128] = small_ref[8, :]
    up[128:] = small_ref[9, 0 : up.shape[0] - 128]
    for get, put in zip(gets, puts):
        get.wait()
        put.start()
    for put in puts:
        put.wait()


def publish(small, lengths, arrays):
    splits = [2 if a.dtype == BF16 else 1 for a in arrays]
    total = sum(splits)
    vmem = pl.BlockSpec(memory_space=pltpu.VMEM)
    return pl.pallas_call(
        functools.partial(publish_body, splits),
        in_specs=[vmem] + [ANY] * len(arrays),
        out_specs=[ANY] * len(arrays) + [vmem] * 9,
        out_shape=[jax.ShapeDtypeStruct(a.shape, a.dtype) for a in arrays]
        + [jax.ShapeDtypeStruct((n,), F32) for n in lengths],
        scratch_shapes=[pltpu.VMEM(a.shape, a.dtype) for a in arrays]
        + [pltpu.SemaphoreType.DMA((total,)), pltpu.SemaphoreType.DMA((total,))],
        compiler_params=params(),
        name="publish",
    )(small, *arrays)


def on_device(tokens, cotangent, segment_ids, *shards):
    gather = lambda s: lax.all_gather(s, "fsdp", axis=0, tiled=True)
    n = lax.axis_size("fsdp")
    near = n == 16 and lax.axis_size("dp") == 2
    triple_s, out_s, up_s, down_s = (s for s in shards if s.ndim == 2)
    rows, d = tokens.shape
    up_bias_s = shards[10]
    eights = [s for i, s in enumerate(shards) if s.ndim == 1 and i != 10]
    flat = lambda w: w.reshape(-1, w.shape[-1])
    if near:
        triple_weight, vec, up_bias, qkv, first_t, cot_t = first(eights + [up_bias_s], triple_s, tokens, cotangent)
        triple_weight = flat(triple_weight)
    else:
        triple_weight = gather(triple_s)
        packed = gather(jnp.concatenate(eights + [up_bias_s]).reshape(1, -1)).astype(F32)
        m = eights[0].shape[0]
        vec = jnp.stack([packed[:, i * m : (i + 1) * m].reshape(-1) for i in range(8)])
        up_bias = packed[:, 8 * m :].reshape(1, -1)
        qkv, first_t = project(tokens, vec, triple_weight)
        cot_t = cotangent.T

    segr = segment_ids.reshape(rows // ROWS, 1, ROWS)
    if near:
        mixed, soft, inv, *full = attend(qkv, segr, (out_s, up_s, down_s))
        out_weight, up_weight, down_weight = (flat(w) for w in full)
    else:
        mixed, soft, inv = attend(qkv, segr)
        out_weight, up_weight, down_weight = gather(out_s), gather(up_s), gather(down_s)
    resid, h, ht = out_project(tokens, mixed, out_weight, vec)
    acc, dh, dwu, dwd, dbu = mlp(h, ht, cotangent, cot_t, up_weight, up_bias, down_weight)
    y, dr, dm, dwo, dvec = middle(resid, acc, dh, cotangent, mixed, out_weight, vec)
    if near:
        dqkv, out_grad, up_grad, down_grad = attend_back(qkv, soft, mixed, dm, inv, (dwo, dwu, dwd))
        dx, triple_grad, small = finish(tokens, dr, first_t, dqkv, triple_weight, vec, dvec, dbu, True)
        lengths = [d // n] * 8 + [up_bias_s.shape[0]]
        dx, triple_grad, out_grad, up_grad, down_grad, *small_grads, up_bias_grad = publish(
            small, lengths, (dx, triple_grad, out_grad, up_grad, down_grad)
        )
    else:
        (dqkv,) = attend_back(qkv, soft, mixed, dm, inv)
        dx, dwt, dvec = finish(tokens, dr, first_t, dqkv, triple_weight, vec, dvec, dbu, False)
        small = jnp.concatenate([dvec[i].reshape(n, -1) for i in range(8)] + [dbu.reshape(n, -1)], axis=1)
        small = lax.psum_scatter(small, "fsdp", scatter_dimension=0, tiled=True).reshape(-1)
        small = lax.psum(small, "dp")
        total = lambda p: lax.psum(lax.psum_scatter(p, "fsdp", scatter_dimension=0, tiled=True), "dp").astype(F32)
        triple_grad, out_grad, up_grad, down_grad = total(dwt), total(dwo), total(dwu), total(dwd)
        m = d // n
        small_grads = [small[i * m : (i + 1) * m] for i in range(8)]
        up_bias_grad = small[8 * m :]
    dg1, ds1, dqb, dvb, dob, dg2, ds2, ddb = small_grads
    return (
        y, dx, dg1, ds1, triple_grad, dqb, dvb, out_grad, dob, dg2, ds2, up_grad, up_bias_grad, down_grad, ddb,
    )


def solution(mesh):
    tok = P(("dp", "fsdp"), None)
    vec = P("fsdp")
    mat = P("fsdp", None)
    weights = (vec, vec, mat, vec, vec, mat, vec, vec, vec, mat, vec, mat, vec)
    return jax.shard_map(
        on_device,
        mesh=mesh,
        in_specs=(tok, tok, P(("dp", "fsdp")), *weights),
        out_specs=(tok, tok, *weights),
        check_vma=False,
    )
```

```python
import functools

import jax
import jax.numpy as jnp
from jax import lax
from jax.experimental import pallas as pl
from jax.experimental.pallas import tpu as pltpu
from jax.sharding import PartitionSpec as P

H = 12
HD = 64
ROWS = 1024
EPS = 1e-06
F32 = jnp.float32
BF16 = jnp.bfloat16
VMEM_LIMIT = 60 * 1024 * 1024

ROOT_HALF = 0.7071067811865476
ROOT_INV_TWO_PI = 0.3989422804014327

NN = (((1,), (0,)), ((), ()))
NT = (((1,), (1,)), ((), ()))


def mm(a, b, dims=NN):
    return lax.dot_general(a, b, dims, preferred_element_type=F32)


def params(**kw):
    return pltpu.CompilerParams(vmem_limit_bytes=VMEM_LIMIT, **kw)


def norm_stats(x):
    mean = jnp.mean(x, axis=-1, keepdims=True)
    cen = x - mean
    var = jnp.mean(cen * cen, axis=-1, keepdims=True)
    inv = lax.rsqrt(var + EPS)
    return cen * inv, inv


MESH = pl.DeviceIdType.MESH
ANY = pl.BlockSpec(memory_space=pl.ANY)


def whereabouts():
    y = lax.axis_index("dp")
    f = lax.axis_index("fsdp")
    return y, f // 4, (f // 2) % 2, f % 2


def spot(z, x, c):
    return z * 4 + x * 2 + c


def greet(signal=True, wait=True):
    y, z, x, c = whereabouts()
    barrier = pltpu.get_barrier_semaphore()
    peers = [(1 - y, spot(z, x, c)), (y, spot(z, 1 - x, c)), (y, spot(z, x, 1 - c))]
    peers += [(y, spot((z + d) % 4, x, c)) for d in (1, 2, 3)]
    if signal:
        for peer in peers:
            pl.semaphore_signal(barrier, inc=1, device_id=peer, device_id_type=MESH)
    if wait:
        pl.semaphore_wait(barrier, len(peers))


class Mover:
    def __init__(self, send, recv, local, per):
        self.send, self.recv, self.local, self.per = send, recv, local, per
        self.y, self.z, self.x, self.c = whereabouts()

    def wide(self, r, split, y):
        return pl.ds(pl.multiple_of(y * (r // 3), 8), 2 * (r // 3)) if split else pl.ds(0, r)

    def thin(self, r, y):
        return pl.ds(pl.multiple_of(y * 2 * (r // 3), 8), r // 3)

    def copy(self, u, slot, src, dst, z=None, x=None, c=None, y=None):
        i = u * self.per + slot
        pick = lambda v, own: own if v is None else v
        peer = (pick(y, self.y), spot(pick(z, self.z), pick(x, self.x), pick(c, self.c)))
        return pltpu.make_async_remote_copy(
            src_ref=src, dst_ref=dst, send_sem=self.send.at[i], recv_sem=self.recv.at[i],
            device_id=peer, device_id_type=MESH,
        )


class Gather(Mover):
    def __init__(self, units, send, recv, local):
        super().__init__(send, recv, local, 6)
        self.units = units

    def mine(self, u):
        src, _, _, col, n, split = self.units[u]
        return src.at[self.wide(src.shape[0], split, self.y), pl.ds(col, n)]

    def held(self, u):
        src, _, hold, col, n, split = self.units[u]
        return hold.at[self.wide(src.shape[0], split, self.y), pl.ds(col, n)]

    def part(self, u, z, x, c, rows):
        _, dst, _, col, n, _ = self.units[u]
        every = slice(None)
        pick = lambda v: every if v is None else v
        return dst.at[pick(z), pick(x), pick(c), rows, pl.ds(col, n)]

    def broad(self, u):
        src, _, _, _, _, split = self.units[u]
        return self.wide(src.shape[0], split, self.y)

    def load(self, u):
        return pltpu.make_async_copy(self.mine(u), self.held(u), self.local.at[2 * u])

    def store(self, u):
        dst = self.part(u, self.z, self.x, self.c, self.broad(u))
        return pltpu.make_async_copy(self.held(u), dst, self.local.at[2 * u + 1])

    def along_z(self, u, d, out=True):
        here, there = (self.z + 4 - d) % 4, (self.z + d) % 4
        dst = self.part(u, self.z if out else here, self.x, self.c, self.broad(u))
        return self.copy(u, d - 1, self.mine(u), dst, z=there)

    def along_x(self, u, out=True):
        src = self.part(u, None, self.x, self.c, self.broad(u))
        dst = src if out else self.part(u, None, 1 - self.x, self.c, self.broad(u))
        return self.copy(u, 3, src, dst, x=1 - self.x)

    def along_y(self, u, out=True):
        r = self.units[u][0].shape[0]
        src = self.part(u, None, None, self.c, self.thin(r, self.y))
        dst = src if out else self.part(u, None, None, self.c, self.thin(r, 1 - self.y))
        return self.copy(u, 4, src, dst, y=1 - self.y)

    def along_c(self, u, out=True):
        every = pl.ds(0, self.units[u][0].shape[0])
        src = self.part(u, None, None, self.c, every)
        dst = src if out else self.part(u, None, None, 1 - self.c, every)
        return self.copy(u, 5, src, dst, c=1 - self.c)

    def stage(self, s, u):
        split = self.units[u][5]
        if s == 0:
            for d in (1, 2, 3):
                self.along_z(u, d).start()
            self.load(u).start()
        if s == 1:
            self.load(u).wait()
            self.store(u).start()
        if s == 2:
            self.store(u).wait()
            for d in (1, 2, 3):
                self.along_z(u, d, False).wait_recv()
            self.along_x(u).start()
        if s == 3:
            self.along_x(u, False).wait_recv()
            if split:
                self.along_y(u).start()
            else:
                self.along_c(u).start()
        if s == 4 and split:
            self.along_y(u, False).wait_recv()
            self.along_c(u).start()
        if s == 5:
            self.along_c(u, False).wait_recv()
            for d in (1, 2, 3):
                self.along_z(u, d).wait_send()
            self.along_x(u).wait_send()
            if split:
                self.along_y(u).wait_send()
            self.along_c(u).wait_send()


def gather_sems(units):
    return [
        pltpu.SemaphoreType.DMA((units * 6,)),
        pltpu.SemaphoreType.DMA((units * 6,)),
        pltpu.SemaphoreType.DMA((2 * units,)),
    ]


def whole(shard):
    return jax.ShapeDtypeStruct((4, 2, 2, *shard.shape), shard.dtype)


class Reduce(Mover):
    def __init__(self, units, send, recv, local):
        super().__init__(send, recv, local, 7)
        self.units = units

    def size(self, u):
        return self.units[u][0].shape[3]

    def partial(self, u, c):
        src, _, (col, _), n, _, _ = self.units[u]
        return src.at[:, :, c, :, pl.ds(col, n)]

    def load(self, u):
        return pltpu.make_async_copy(self.partial(u, self.c), self.units[u][5][0], self.local.at[u])

    def over_c(self, u):
        return self.copy(u, 0, self.partial(u, 1 - self.c), self.units[u][5][1], c=1 - self.c)

    def over_y(self, u):
        own, from_y = self.units[u][5][0], self.units[u][5][5]
        return self.copy(u, 1, own.at[:, :, self.thin(self.size(u), 1 - self.y), :], from_y, y=1 - self.y)

    def over_x(self, u):
        own, from_x = self.units[u][5][0], self.units[u][5][2]
        rows = self.wide(self.size(u), self.units[u][4], self.y)
        return self.copy(u, 2, own.at[:, 1 - self.x, rows, :], from_x, x=1 - self.x)

    def over_z(self, u, d):
        own, from_z = self.units[u][5][0], self.units[u][5][3]
        rows = self.wide(self.size(u), self.units[u][4], self.y)
        to = (self.z + d) % 4
        return self.copy(u, 2 + d, own.at[to, self.x, rows, :], from_z.at[d - 1], z=to)

    def over_last(self, u):
        last = self.units[u][5][4]
        return self.copy(u, 6, last.at[0], last.at[1], y=1 - self.y)

    def stage(self, s, u):
        _, out, (_, col), n, split, (own, from_c, from_x, from_z, last, *rest) = self.units[u]
        y, z, x = self.y, self.z, self.x
        r = self.size(u)
        rows = self.wide(r, split, y)
        if s == 0:
            self.over_c(u).start()
            self.load(u).start()
        if s == 1:
            self.load(u).wait()
            self.over_c(u).wait_recv()
            own[...] = own[...] + from_c[...]
            if split:
                self.over_y(u).start()
        if s == 2:
            if split:
                self.over_y(u).wait_recv()
                mine = self.thin(r, y)
                own[:, :, mine, :] = own[:, :, mine, :] + rest[0][...]
            self.over_x(u).start()
        if s == 3:
            self.over_x(u).wait_recv()
            for k in range(4):
                own[k, x, rows, :] = own[k, x, rows, :] + from_x[k]
            for d in (1, 2, 3):
                self.over_z(u, d).start()
        if s == 4:
            total = own[z, x, rows, :].astype(F32)
            for d in (1, 2, 3):
                self.over_z(u, d).wait_recv()
                total = total + from_z[d - 1].astype(F32)
            last[0] = total.astype(last.dtype)
            self.over_last(u).start()
        if s == 5:
            self.over_last(u).wait_recv()
            cols = pl.ds(col, n)
            if split:
                t = r // 3
                at = lambda k: pl.ds(pl.multiple_of(k * t, 8), t)
                put = lambda k, v: out.__setitem__((at(k), cols), v.astype(F32))
                put(1, last[0, at(1 - y), :].astype(F32) + last[1, at(y), :].astype(F32))
                put(2 * y, last[0, at(y), :])
                put(2 * (1 - y), last[1, at(1 - y), :])
            else:
                out[:, cols] = last[0].astype(F32) + last[1].astype(F32)
        if s == 6:
            self.over_c(u).wait_send()
            if split:
                self.over_y(u).wait_send()
            self.over_x(u).wait_send()
            for d in (1, 2, 3):
                self.over_z(u, d).wait_send()
            self.over_last(u).wait_send()


def reduce_buffers(r, n, dtype, split):
    wide = 2 * r // 3 if split else r
    shapes = [(4, 2, r, n), (4, 2, r, n), (4, wide, n), (3, wide, n), (2, wide, n)]
    if split:
        shapes.append((4, 2, r // 3, n))
    return [pltpu.VMEM(shape, dtype) for shape in shapes]


def reduce_scratch(plan):
    flat = []
    for p in plan:
        flat += reduce_buffers(*p)
    units = len(plan)
    return flat + [
        pltpu.SemaphoreType.DMA((units * 7,)),
        pltpu.SemaphoreType.DMA((units * 7,)),
        pltpu.SemaphoreType.DMA((units,)),
    ]


def reduce_work(plan, places, scratch):
    units = []
    at = 0
    for (_, n, _, split), (src, out, col) in zip(plan, places):
        count = 6 if split else 5
        units.append((src, out, col, n, split, scratch[at : at + count]))
        at += count
    return Reduce(units, *scratch[at:])


def at_hook(hook, moves, work, newest=False):
    for u, hooks in list(enumerate(moves))[:: -1 if newest else 1]:
        for s, when in enumerate(hooks):
            if when == hook:
                work.stage(s, u)


def hooked(step, per_step, which, steps, moves, work, late=False):
    if late and which == 0:

        @pl.when(step == 0)
        def _():
            greet(wait=False)

    for k in range(steps):
        if any(k * per_step + which in hooks for hooks in moves):

            @pl.when(step == k)
            def _():
                if which == 0 and k == late:
                    greet(signal=not late)
                at_hook(k * per_step + which, moves, work)


def unpack(vec_ref, ub_ref, tall_ref):
    d = vec_ref.shape[1] // 16
    f = ub_ref.shape[1] // 16
    for i in range(16):
        tile = tall_ref[i // 4, (i // 2) % 2, i % 2].astype(F32)
        vec_ref[:, i * d : (i + 1) * d] = tile[0:8, 0:d]
        ub_ref[:, i * f : i * f + 128] = tile[8:9, 0:128]
        ub_ref[:, i * f + 128 : (i + 1) * f] = tile[9:10, 0 : f - 128]


PIECES = ((0, 512), (512, 256))
FIRST_LAGS = (0, 1, 2, 4, 6, 8)


def first_body(*refs):
    vectors = refs[:9]
    t_ref, x_hbm, g_hbm = refs[9:12]
    w_hbm, vec_ref, ub_ref, qkv_hbm, ht_hbm, gt_hbm = refs[12:18]
    row_ref, tile_ref, tall_ref, vh_ref, w_ref, th_ref, x_ref, g_ref, h_ref, ht_ref, gt_ref, out_ref = refs[18:30]
    move_sem, out_sem, w_sem, *sems = refs[30:]
    rows, d = x_ref.shape
    columns = [(j, j * d + col, n) for j in range(3) for col, n in PIECES]
    units = [(tile_ref, tall_ref, vh_ref, 0, 128, False)]
    units += [(t_ref, w_ref, th_ref, col, n, True) for _, col, n in columns]
    work = Gather(units, *sems)
    moves = [[0, 1, 2, 3, 4, 5]] + [[u + lag for lag in FIRST_LAGS] for u in range(len(columns))]
    local = lambda i, src, dst: pltpu.make_async_copy(src, dst, move_sem.at[i])
    get_x, get_g = local(0, x_hbm, x_ref), local(1, g_hbm, g_ref)
    put_h, put_g = local(2, ht_ref, ht_hbm), local(3, gt_ref, gt_hbm)

    greet(wait=False)
    get_g.start()
    get_x.start()
    for i, ref in enumerate(vectors[:8]):
        row_ref[i : i + 1, 0 : ref.shape[0]] = ref[...].astype(F32).reshape(1, -1)
    up = vectors[8][...].astype(F32).reshape(1, -1)
    row_ref[8:9, :] = up[:, :128]
    row_ref[9:10, 0 : up.shape[1] - 128] = up[:, 128:]
    tile_ref[...] = row_ref[...].astype(BF16)
    greet(signal=False)
    at_hook(0, moves, work)
    get_g.wait()
    for t in range(4):

        @pl.loop(0, rows // 4 // 128)
        def _(i):
            part = pl.ds(pl.multiple_of(t * (rows // 4) + i * 128, 128), 128)
            gt_ref[:, part] = g_ref[part, :].T

        at_hook(1 + t, moves, work)
    put_g.start()
    get_x.wait()
    at_hook(5, moves, work)
    unpack(vec_ref, ub_ref, tall_ref)
    for t in range(4):

        @pl.loop(0, rows // 4 // 128)
        def _(i):
            part = pl.ds(pl.multiple_of(t * (rows // 4) + i * 128, 128), 128)
            n, _ = norm_stats(x_ref[part, :].astype(F32))
            h = (n * vec_ref[0:1, :] + vec_ref[1:2, :]).astype(BF16)
            h_ref[part, :] = h
            ht_ref[:, part] = h.T

        at_hook(6 + t, moves, work)
    put_h.start()

    def place(u):
        _, col, n = columns[u]
        return pltpu.make_async_copy(out_ref.at[u % 2, :, pl.ds(0, n)], qkv_hbm.at[:, pl.ds(col, n)], out_sem.at[u])

    def keep(u):
        _, col, n = columns[u]
        cols = pl.ds(col, n)
        return pltpu.make_async_copy(w_ref.at[:, :, :, :, cols], w_hbm.at[:, :, :, :, cols], w_sem.at[u])

    for u, (j, col, n) in enumerate(columns):
        if u:
            at_hook(9 + u, moves, work)
        keep(u).start()
        if u >= 2:
            place(u - 2).wait()
        own = slice(col - j * d, col - j * d + n)

        @pl.loop(0, 4)
        def _(t):
            part = pl.ds(pl.multiple_of(t * (rows // 4), 8), rows // 4)
            p = mm(h_ref[part, :], w_ref[:, :, :, :, col : col + n].reshape(d, n))
            if j == 0:
                p = (p + vec_ref[2:3, own]) * 0.125
            if j == 2:
                p = p + vec_ref[3:4, own]
            out_ref[u % 2, part, 0:n] = p.astype(BF16)

        place(u).start()
    put_g.wait()
    put_h.wait()
    for u in range(len(columns)):
        keep(u).wait()
        if u >= len(columns) - 2:
            place(u).wait()


def first(vectors, triple, x, g):
    rows, d = x.shape
    vmem = pl.BlockSpec(memory_space=pltpu.VMEM)
    across = pltpu.VMEM((d, rows), BF16)
    down = pltpu.VMEM((rows, d), BF16)
    pieces = 3 * len(PIECES)
    return pl.pallas_call(
        first_body,
        in_specs=[vmem] * 9 + [ANY] * 3,
        out_specs=[ANY, vmem, vmem, ANY, ANY, ANY],
        out_shape=[
            whole(triple),
            jax.ShapeDtypeStruct((8, d), F32),
            jax.ShapeDtypeStruct((1, 4 * d), F32),
            jax.ShapeDtypeStruct((rows, 3 * d), BF16),
            jax.ShapeDtypeStruct((d, rows), BF16),
            jax.ShapeDtypeStruct((d, rows), BF16),
        ],
        scratch_shapes=[
            pltpu.VMEM((16, 128), F32),
            pltpu.VMEM((16, 128), BF16),
            pltpu.VMEM((4, 2, 2, 16, 128), BF16),
            pltpu.VMEM((16, 128), BF16),
            pltpu.VMEM((4, 2, 2, *triple.shape), BF16),
            pltpu.VMEM(triple.shape, BF16),
            down,
            down,
            down,
            across,
            across,
            pltpu.VMEM((2, rows, PIECES[0][1]), BF16),
            pltpu.SemaphoreType.DMA((4,)),
            pltpu.SemaphoreType.DMA((pieces,)),
            pltpu.SemaphoreType.DMA((pieces,)),
            *gather_sems(1 + pieces),
        ],
        compiler_params=params(collective_id=0, has_side_effects=True),
        name="first",
    )(*vectors, triple, x, g)


def proj_body(x_ref, vec_ref, w_ref, qkv_ref, ht_ref):
    d = x_ref.shape[1]
    n, _ = norm_stats(x_ref[...].astype(F32))
    h = (n * vec_ref[0:1, :] + vec_ref[1:2, :]).astype(BF16)
    ht_ref[...] = h.T
    for j in range(3):
        cols = pl.ds(j * d, d)
        p = mm(h, w_ref[:, cols])
        if j == 0:
            p = (p + vec_ref[2:3, :]) * 0.125
        if j == 2:
            p = p + vec_ref[3:4, :]
        qkv_ref[:, cols] = p.astype(BF16)


def project(x, vec, w):
    rows, d = x.shape
    cols = w.shape[1]
    tile = 512
    return pl.pallas_call(
        proj_body,
        grid=(rows // tile,),
        in_specs=[
            pl.BlockSpec((tile, d), lambda i: (i, 0)),
            pl.BlockSpec((8, d), lambda i: (0, 0)),
            pl.BlockSpec((d, cols), lambda i: (0, 0)),
        ],
        out_specs=[
            pl.BlockSpec((tile, cols), lambda i: (i, 0)),
            pl.BlockSpec((d, tile), lambda i: (0, i)),
        ],
        out_shape=[jax.ShapeDtypeStruct((rows, cols), BF16), jax.ShapeDtypeStruct((d, rows), BF16)],
        compiler_params=params(),
        name="project",
        cost_estimate=pl.CostEstimate(
            flops=2 * rows * d * cols, bytes_accessed=2 * rows * (d + cols), transcendentals=0
        ),
    )(x, vec, w)


QT = 256
BACK_TILE = 512
GATHER_CUT = (2, 8, 6)
REDUCE_CUT = (1, 3, 3)
GATHER_LAGS = (0, 1, 2, 4, 6, 8)
REDUCE_LAGS = (0, 1, 4, 7, 10, 12, 12)


LOG2E = 1.4426950408889634


def swap(value):
    return jnp.concatenate([value[:, HD:], value[:, :HD]], axis=1)


def twice(value, own):
    return jnp.where(own, value, swap(value))


def unit_list(widths, cuts):
    return [(i, j * (w // cut), w // cut) for i, (w, cut) in enumerate(zip(widths, cuts)) for j in range(cut)]


def attend_body(hosting, *refs):
    q_ref, k_ref, v_ref, seg_ref = refs[:4]
    if hosting:
        shards = refs[4:7]
        o_ref, p_ref, inv_ref = refs[7:10]
        full = refs[10:13]
        bias_ref, pair_ref = refs[13:15]
        hold = refs[15:18]
        units = [(shards[i], full[i], hold[i], col, n, True) for i, col, n in unit_list([s.shape[1] for s in shards], GATHER_CUT)]
        work = Gather(units, *refs[18:])
        moves = [[u + lag for lag in GATHER_LAGS] for u in range(len(units))]
    else:
        o_ref, p_ref, inv_ref, bias_ref, pair_ref = refs[4:]
    step = pl.program_id(0) * pl.num_programs(1) + pl.program_id(1)
    rows = q_ref.shape[0]

    @pl.when(pl.program_id(1) == 0)
    def _():
        seg = seg_ref[...].astype(F32)
        column = jnp.broadcast_to(seg, (8, rows)).T[:, 0:1]
        bias_ref[...] = jnp.where(column == seg, 0.0, -1e30)

    lower = lax.broadcasted_iota(jnp.int32, (1, 128), 1) < HD
    lower = lax.broadcasted_iota(jnp.int32, (1, 128), 1) < HD
    lower = lax.broadcasted_iota(jnp.int32, (1, 128), 1) < HD
    sums = []
    for hh in range(2):
        if hosting:
            hooked(step, 2, hh, 12, moves, work)
        own = lower if hh == 0 else ~lower
        q = q_ref[...].astype(F32) * LOG2E
        high = q.astype(BF16)
        low = (q - high.astype(F32)).astype(BF16)
        pair_ref[0, hh] = jnp.where(own, high, swap(low))
        pair_ref[1, hh] = twice(k_ref[...], own)
        pair_ref[2, hh] = jnp.where(own, v_ref[...], jnp.ones_like(v_ref[...]))
        if hh == 1:
            sums.append(mm(p_ref[0], pair_ref[2, 0]))
        for t in range(rows // QT):
            sl = pl.ds(t * QT, QT)
            s = mm(pair_ref[0, hh, sl, :], pair_ref[1, hh], NT) + bias_ref[sl, :]
            p_ref[hh, sl, :] = jnp.exp2(s - jnp.max(s, axis=-1, keepdims=True)).astype(BF16)
    sums.append(mm(p_ref[1], pair_ref[2, 1]))
    inv = 1.0 / swap(jnp.where(lower, sums[1], sums[0]))
    inv_ref[...] = inv
    o_ref[...] = (jnp.where(lower, sums[0], sums[1]) * inv).astype(BF16)


def attend(qkv, segr, shards=()):
    rows = qkv.shape[0]
    d = qkv.shape[1] // 3
    mb = rows // ROWS
    pairs = d // 128
    extra = dict(collective_id=1, has_side_effects=True) if shards else {}
    return pl.pallas_call(
        functools.partial(attend_body, bool(shards)),
        grid=(mb, pairs),
        in_specs=[
            pl.BlockSpec((ROWS, 128), lambda m, h: (m, h)),
            pl.BlockSpec((ROWS, 128), lambda m, h: (m, pairs + h)),
            pl.BlockSpec((ROWS, 128), lambda m, h: (m, 2 * pairs + h)),
            pl.BlockSpec((None, 1, ROWS), lambda m, h: (m, 0, 0)),
            *[ANY for _ in shards],
        ],
        out_specs=[
            pl.BlockSpec((ROWS, 128), lambda m, h: (m, h)),
            pl.BlockSpec((None, 2, ROWS, ROWS), lambda m, h: (m, h, 0, 0)),
            pl.BlockSpec((ROWS, 128), lambda m, h: (m, h)),
            *[ANY for _ in shards],
        ],
        out_shape=[
            jax.ShapeDtypeStruct((rows, d), BF16),
            jax.ShapeDtypeStruct((mb, 2 * pairs, ROWS, ROWS), BF16),
            jax.ShapeDtypeStruct((rows, d), F32),
            *[whole(s) for s in shards],
        ],
        scratch_shapes=[pltpu.VMEM((ROWS, ROWS), F32), pltpu.VMEM((3, 2, ROWS, 128), BF16)]
        + ([pltpu.VMEM(s.shape, s.dtype) for s in shards] + gather_sems(sum(GATHER_CUT)) if shards else []),
        compiler_params=params(**extra),
        name="attend",
        cost_estimate=pl.CostEstimate(
            flops=mb * pairs * 2 * 4 * ROWS * ROWS * 256,
            bytes_accessed=mb * pairs * 2 * ROWS * ROWS * 2,
            transcendentals=mb * pairs * 2 * ROWS * ROWS,
        ),
    )(qkv, qkv, qkv, segr, *shards)


def attend_back_body(plan, *refs):
    q_ref, k_ref, v_ref, p_ref, o_ref, g_ref, inv_ref = refs[:7]
    hosting = plan is not None
    if hosting:
        parts = refs[7:10]
        d_ref = refs[10]
        results = refs[11:14]
        ds_ref = refs[14]
        places = [(parts[i], results[i], (col, col)) for i, col, _ in unit_list([p.shape[4] for p in parts], REDUCE_CUT)]
        work = reduce_work(plan, places, refs[15:])
        moves = [[max(0, 2 * u - 1) + lag for lag in REDUCE_LAGS] for u in range(len(places))]
    else:
        d_ref, ds_ref = refs[7:]
    step = pl.program_id(0) * pl.num_programs(1) + pl.program_id(1)
    rows = q_ref.shape[0]
    lower = lax.broadcasted_iota(jnp.int32, (1, 128), 1) < HD
    dk_parts = []
    dv_parts = []
    dq_parts = []
    for hh in range(2):
        if hosting:
            hooked(step, 2, hh, 12, moves, work)
        own = lower if hh == 0 else ~lower
        half = slice(hh * HD, (hh + 1) * HD)
        g = g_ref[...].astype(F32) * inv_ref[...]
        high = g.astype(BF16)
        low = (g - high.astype(F32)).astype(BF16)
        pair = jnp.where(own, high, swap(low))
        center = jnp.sum(jnp.where(own, g * o_ref[...].astype(F32), 0.0), axis=-1, keepdims=True)
        v = twice(v_ref[...], own)
        for t in range(rows // BACK_TILE):
            sl = pl.ds(t * BACK_TILE, BACK_TILE)
            ts = slice(t * BACK_TILE, (t + 1) * BACK_TILE)
            d_soft = mm(pair[ts, :], v, NT)
            ds_ref[hh, sl, :] = (p_ref[hh, sl, :].astype(F32) * (d_soft - center[ts, :])).astype(BF16)
        dv = mm(pair.T, p_ref[hh])
        dv_parts.append(dv[:HD, :] + dv[HD:, :])
        dk_parts.append(mm(q_ref[...].T[half, :], ds_ref[hh]))
        dq_parts.append(mm(ds_ref[hh], k_ref[...]))
    d_ref[0] = (jnp.where(lower, dq_parts[0], dq_parts[1]) * 0.125).astype(BF16)
    d_ref[1] = jnp.concatenate(dk_parts, axis=0).T.astype(BF16)
    d_ref[2] = jnp.concatenate(dv_parts, axis=0).T.astype(BF16)


def attend_back(qkv, soft, mixed, d_mixed, inv, grads=()):
    rows = qkv.shape[0]
    d = qkv.shape[1] // 3
    mb = rows // ROWS
    pairs = d // 128
    blk = pl.BlockSpec((ROWS, 128), lambda m, h: (m, h))
    plan = None
    results = []
    extra = {}
    grads = [g.reshape(4, 2, 2, g.shape[0] // 16, g.shape[1]) for g in grads]
    if grads:
        plan = [(grads[i].shape[3], n, BF16, True) for i, _, n in unit_list([g.shape[4] for g in grads], REDUCE_CUT)]
        results = [jax.ShapeDtypeStruct(g.shape[3:], F32) for g in grads]
        extra = dict(collective_id=2, has_side_effects=True)
    return pl.pallas_call(
        functools.partial(attend_back_body, plan),
        grid=(mb, pairs),
        in_specs=[
            blk,
            pl.BlockSpec((ROWS, 128), lambda m, h: (m, pairs + h)),
            pl.BlockSpec((ROWS, 128), lambda m, h: (m, 2 * pairs + h)),
            pl.BlockSpec((None, 2, ROWS, ROWS), lambda m, h: (m, h, 0, 0)),
            blk,
            blk,
            blk,
            *[ANY for _ in grads],
        ],
        out_specs=[
            pl.BlockSpec((3, ROWS, 128), lambda m, h: (0, m, h)),
            *[pl.BlockSpec(r.shape, lambda m, h: (0, 0)) for r in results],
        ],
        out_shape=[jax.ShapeDtypeStruct((3, rows, d), BF16), *results],
        scratch_shapes=[pltpu.VMEM((2, ROWS, ROWS), BF16)] + (reduce_scratch(plan) if grads else []),
        compiler_params=params(**extra),
        name="attend_back",
        cost_estimate=pl.CostEstimate(
            flops=mb * pairs * 2 * 8 * ROWS * ROWS * 256,
            bytes_accessed=mb * pairs * 2 * ROWS * ROWS * 2,
            transcendentals=0,
        ),
    )(qkv, qkv, qkv, soft, mixed, d_mixed, inv, *grads)


def out_body(x_ref, m_ref, w_ref, vec_ref, resid_ref, h_ref, ht_ref):
    size = 256
    for t in range(x_ref.shape[0] // size):
        sl = pl.ds(t * size, size)
        resid = x_ref[sl, :].astype(F32) + mm(m_ref[sl, :], w_ref[...]) + vec_ref[4:5, :]
        resid_ref[sl, :] = resid
        n, _ = norm_stats(resid)
        h = (n * vec_ref[5:6, :] + vec_ref[6:7, :]).astype(BF16)
        h_ref[sl, :] = h
        ht_ref[:, t * size : (t + 1) * size] = h.T


def out_project(x, mixed, w, vec):
    rows, d = x.shape
    tile = 512
    blk = pl.BlockSpec((tile, d), lambda i: (i, 0))
    return pl.pallas_call(
        out_body,
        grid=(rows // tile,),
        in_specs=[blk, blk, pl.BlockSpec((d, d), lambda i: (0, 0)), pl.BlockSpec((8, d), lambda i: (0, 0))],
        out_specs=[blk, blk, pl.BlockSpec((d, tile), lambda i: (0, i))],
        out_shape=[
            jax.ShapeDtypeStruct((rows, d), F32),
            jax.ShapeDtypeStruct((rows, d), BF16),
            jax.ShapeDtypeStruct((d, rows), BF16),
        ],
        compiler_params=params(),
        name="out_project",
        cost_estimate=pl.CostEstimate(
            flops=2 * rows * d * d, bytes_accessed=rows * d * 12, transcendentals=0
        ),
    )(x, mixed, w, vec)


FC = 512
RT = 1024


def gelu_parts(u):
    cdf = 0.5 * (1.0 + lax.erf(u * ROOT_HALF))
    bell = jnp.exp(-0.5 * u * u) * ROOT_INV_TWO_PI
    return u * cdf, cdf + u * bell


def mlp_body(h_ref, ht_ref, g_ref, gt_ref, wu_ref, bu_ref, wd_ref, acc_ref, dh_ref, dwu_ref, dwd_ref, dbu_ref,
             act_ref, du_ref):
    rows = h_ref.shape[0]

    @pl.when(pl.program_id(0) == 0)
    def _():
        acc_ref[...] = jnp.zeros_like(acc_ref)
        dh_ref[...] = jnp.zeros_like(dh_ref)

    wu = wu_ref[...]
    wd = wd_ref[...]
    bias_sum = None
    for t in range(rows // RT):
        sl = pl.ds(t * RT, RT)
        u = mm(h_ref[sl, :], wu) + bu_ref[...]
        act, slope = gelu_parts(u)
        act_ref[sl, :] = act.astype(BF16)
        du = mm(g_ref[sl, :], wd, NT) * slope
        part = jnp.sum(du, axis=0, keepdims=True)
        bias_sum = part if bias_sum is None else bias_sum + part
        du_ref[sl, :] = du.astype(BF16)
        acc_ref[sl, :] += mm(act_ref[sl, :], wd)
        dh_ref[sl, :] += mm(du_ref[sl, :], wu, NT)
    dbu_ref[...] = bias_sum
    dwu_ref[...] = mm(ht_ref[...], du_ref[...]).astype(dwu_ref.dtype)
    dwd_ref[...] = mm(gt_ref[...], act_ref[...]).T.astype(dwd_ref.dtype)


def mlp(h, ht, g, gt, wu, bu, wd):
    rows, d = h.shape
    ff = wu.shape[1]
    one = pl.Buffered(1)
    whole = pl.BlockSpec((rows, d), lambda c: (0, 0), pipeline_mode=one)
    whole_t = pl.BlockSpec((d, rows), lambda c: (0, 0), pipeline_mode=one)
    return pl.pallas_call(
        mlp_body,
        grid=(ff // FC,),
        in_specs=[
            whole,
            whole_t,
            whole,
            whole_t,
            pl.BlockSpec((d, FC), lambda c: (0, c)),
            pl.BlockSpec((1, FC), lambda c: (0, c)),
            pl.BlockSpec((FC, d), lambda c: (c, 0)),
        ],
        out_specs=[
            whole,
            whole,
            pl.BlockSpec((d, FC), lambda c: (0, c)),
            pl.BlockSpec((FC, d), lambda c: (c, 0)),
            pl.BlockSpec((1, FC), lambda c: (0, c)),
        ],
        out_shape=[
            jax.ShapeDtypeStruct((rows, d), F32),
            jax.ShapeDtypeStruct((rows, d), F32),
            jax.ShapeDtypeStruct((d, ff), BF16),
            jax.ShapeDtypeStruct((ff, d), BF16),
            jax.ShapeDtypeStruct((1, ff), F32),
        ],
        scratch_shapes=[pltpu.VMEM((rows, FC), BF16), pltpu.VMEM((rows, FC), BF16)],
        compiler_params=params(),
        name="mlp",
        cost_estimate=pl.CostEstimate(
            flops=12 * rows * d * ff, bytes_accessed=rows * d * 20 + 8 * d * ff, transcendentals=3 * rows * ff
        ),
    )(h, ht, g, gt, wu, bu, wd)


def fold(ref, row, step, value):
    part = jnp.sum(value, axis=0, keepdims=True)

    @pl.when(step == 0)
    def _():
        ref[row : row + 1, :] = part

    @pl.when(step != 0)
    def _():
        ref[row : row + 1, :] += part


def norm_pull(grad, n, inv, gain):
    dn = grad * gain
    plain = jnp.mean(dn, axis=-1, keepdims=True)
    cross = jnp.mean(dn * n, axis=-1, keepdims=True)
    return inv * (dn - plain - n * cross)


def mid_body(resid_ref, acc_ref, dh_ref, g_ref, mixed_ref, w_ref, vec_ref,
             y_ref, dr_ref, dm_ref, dw_ref, dvec_ref, sum_ref, low_ref):
    step = pl.program_id(0)

    @pl.when(step == 0)
    def _():
        dvec_ref[...] = jnp.zeros_like(dvec_ref)

    size = 128

    for t in range(resid_ref.shape[0] // size):
        sl = pl.ds(t * size, size)
        resid = resid_ref[sl, :]
        y_ref[sl, :] = (resid + acc_ref[sl, :] + vec_ref[7:8, :]).astype(BF16)
        g = g_ref[sl, :].astype(F32)
        n, inv = norm_stats(resid)
        dh = dh_ref[sl, :]
        dr = g + norm_pull(dh, n, inv, vec_ref[5:6, :])
        dr_ref[sl, :] = dr
        for row, value in ((4, dr), (5, dh * n), (6, dh), (7, g)):
            dvec_ref[row : row + 1, :] += jnp.sum(value, axis=0, keepdims=True)
        low_ref[sl, :] = dr.astype(BF16)
        dm_ref[sl, :] = mm(low_ref[sl, :], w_ref[...], NT).astype(BF16)
    low = low_ref[...]
    dw = mm(mixed_ref[...].T, low)

    @pl.when(step == 0)
    def _():
        sum_ref[...] = dw

    @pl.when(step != 0)
    def _():
        sum_ref[...] += dw

    @pl.when(step == pl.num_programs(0) - 1)
    def _():
        dw_ref[...] = sum_ref[...].astype(dw_ref.dtype)


def middle(resid, acc, dh, g, mixed, w, vec):
    rows, d = resid.shape
    tile = 512
    blk = pl.BlockSpec((tile, d), lambda i: (i, 0))
    mat = pl.BlockSpec((d, d), lambda i: (0, 0))
    eight = pl.BlockSpec((8, d), lambda i: (0, 0))
    return pl.pallas_call(
        mid_body,
        grid=(rows // tile,),
        in_specs=[blk, blk, blk, blk, blk, mat, eight],
        out_specs=[blk, blk, blk, mat, eight],
        out_shape=[
            jax.ShapeDtypeStruct((rows, d), BF16),
            jax.ShapeDtypeStruct((rows, d), F32),
            jax.ShapeDtypeStruct((rows, d), BF16),
            jax.ShapeDtypeStruct((d, d), BF16),
            jax.ShapeDtypeStruct((8, d), F32),
        ],
        scratch_shapes=[pltpu.VMEM((d, d), F32), pltpu.VMEM((tile, d), BF16)],
        compiler_params=params(),
        name="middle",
        cost_estimate=pl.CostEstimate(
            flops=4 * rows * d * d, bytes_accessed=rows * d * 24, transcendentals=0
        ),
    )(resid, acc, dh, g, mixed, w, vec)


PHASES = 3
FINAL_TILE = 256


def finish_body(plan, ht_ref, part_ref, tile_ref, x_ref, dr_ref, w_hbm, vec_ref, dvec_ref, dbu_ref, dx_ref, *refs):
    step = pl.program_id(0)
    d = x_ref.shape[1]
    if plan is None:
        dw_ref, sums_ref, w_ref, w_sem = refs
    else:
        out_ref, small_ref, w_ref, w_sem, sums_ref, grad_ref, tall_ref = refs[:7]
        places = [(grad_ref.at[j], out_ref, (col, j * d + col)) for j in range(PHASES) for col, _ in PIECES]
        places.append((tall_ref, small_ref, (0, 0)))
        work = reduce_work(plan, places, refs[7:])
        vectors = len(places) - 1
        last = vectors - 1 + ht_ref.shape[1] // FINAL_TILE
        moves = FINISH_MOVES

    fetch = pltpu.make_async_copy(w_hbm, w_ref, w_sem)

    @pl.when(step == 0)
    def _():
        if plan is not None:
            greet(wait=False)
        fetch.start()
        sums_ref[...] = dvec_ref[...]

    for i, (col, n) in enumerate(PIECES):

        @pl.when(step < PHASES)
        def _():
            cols = pl.ds(col, n)
            dw = mm(ht_ref[...], part_ref[0, :, cols]).astype(BF16)
            if plan is None:
                dw_ref[:, cols] = dw
            else:
                grad_ref[step, :, :, :, :, cols] = dw.reshape(4, 2, 2, d // 16, n)

        if plan is not None:
            for j in range(PHASES):

                @pl.when(step == j)
                def _():
                    if i == 0 and j == 0:
                        greet(signal=False)
                    at_hook(2 * j + i, moves, work, True)

    for j, row in ((0, 2), (2, 3)):

        @pl.when(step == j)
        def _():
            sums_ref[row : row + 1, :] = jnp.sum(part_ref[0].astype(F32), axis=0, keepdims=True)

    @pl.when(step == PHASES)
    def _():
        fetch.wait()

    @pl.when(step >= PHASES)
    def _():
        n, inv = norm_stats(x_ref[...].astype(F32))
        dh = None
        for j in range(3):
            term = mm(tile_ref[j], w_ref[:, pl.ds(j * d, d)], NT)
            dh = term if dh is None else dh + term
        fold(sums_ref, 0, step - PHASES, dh * n)
        fold(sums_ref, 1, step - PHASES, dh)
        dx_ref[...] = (dr_ref[...] + norm_pull(dh, n, inv, vec_ref[0:1, :])).astype(BF16)

    if plan is not None:
        for k in range(2 * PHASES, last + 1):

            @pl.when(step == k - PHASES)
            def _():
                if k == last:
                    pack(tall_ref, sums_ref, dbu_ref)
                    for hook in range(last, 1 + max(max(m) for m in moves)):
                        at_hook(hook, moves, work, True)
                else:
                    at_hook(k, moves, work, True)


FINISH_MOVES = [
    [0, 1, 5, 8, 12, 14, 18],
    [1, 2, 6, 9, 12, 14, 18],
    [2, 3, 7, 10, 13, 15, 18],
    [3, 4, 8, 11, 14, 16, 18],
    [4, 5, 9, 12, 14, 16, 18],
    [5, 6, 11, 13, 15, 17, 18],
    [13, 14, 14, 15, 16, 17, 18],
]


def pack(tall_ref, sums_ref, dbu_ref):
    d = sums_ref.shape[1] // 16
    f = dbu_ref.shape[1] // 16
    for i in range(16):
        tile = tall_ref.at[i // 4, (i // 2) % 2, i % 2]
        tile[0:8, 0:d] = sums_ref[:, i * d : (i + 1) * d]
        tile[8:9, 0:128] = dbu_ref[:, i * f : i * f + 128]
        tile[9:10, 0 : f - 128] = dbu_ref[:, i * f + 128 : (i + 1) * f]


def finish(x, dr, ht, dqkv, w, vec, dvec, dbu, near):
    rows, d = x.shape
    tiles = rows // FINAL_TILE
    row = lambda s: jnp.maximum(s - PHASES, 0)
    one = pl.Buffered(1)
    eight = pl.BlockSpec((8, d), lambda s: (0, 0))
    if near:
        plan = [(d // 16, n, BF16, True) for _ in range(PHASES) for _, n in PIECES] + [(16, 128, F32, False)]
        shapes = [jax.ShapeDtypeStruct((d // 16, 3 * d), F32), jax.ShapeDtypeStruct((16, 128), F32)]
        specs = [pl.BlockSpec(s.shape, lambda s: (0, 0)) for s in shapes]
        scratch = [
            pltpu.VMEM((8, d), F32),
            pltpu.VMEM((PHASES, 4, 2, 2, d // 16, d), BF16),
            pltpu.VMEM((4, 2, 2, 16, 128), F32),
        ] + reduce_scratch(plan)
        extra = dict(collective_id=3, has_side_effects=True)
    else:
        plan = None
        shapes = [jax.ShapeDtypeStruct((d, 3 * d), BF16), jax.ShapeDtypeStruct((8, d), F32)]
        specs = [pl.BlockSpec((d, d), lambda s: (0, jnp.minimum(s, PHASES - 1))), eight]
        scratch = []
        extra = {}
    return pl.pallas_call(
        functools.partial(finish_body, plan),
        grid=(PHASES + tiles,),
        in_specs=[
            pl.BlockSpec((d, rows), lambda s: (0, 0), pipeline_mode=one),
            pl.BlockSpec((1, rows, d), lambda s: (jnp.minimum(s, PHASES - 1), 0, 0)),
            pl.BlockSpec((3, FINAL_TILE, d), lambda s: (0, row(s), 0)),
            pl.BlockSpec((FINAL_TILE, d), lambda s: (row(s), 0)),
            pl.BlockSpec((FINAL_TILE, d), lambda s: (row(s), 0)),
            ANY,
            eight,
            eight,
            pl.BlockSpec(dbu.shape, lambda s: (0, 0)),
        ],
        out_specs=[pl.BlockSpec((FINAL_TILE, d), lambda s: (row(s), 0)), *specs],
        out_shape=[jax.ShapeDtypeStruct((rows, d), BF16), *shapes],
        scratch_shapes=[pltpu.VMEM((d, 3 * d), BF16), pltpu.SemaphoreType.DMA(()), *scratch],
        compiler_params=params(**extra),
        name="finish",
        cost_estimate=pl.CostEstimate(
            flops=12 * rows * d * d, bytes_accessed=rows * d * 20, transcendentals=0
        ),
    )(ht, dqkv, dqkv, x, dr, w, vec, dvec, dbu)


def publish_body(splits, small_ref, *refs):
    n = len(splits)
    arrays, outs = refs[:n], refs[n : 2 * n]
    vectors = refs[2 * n : 2 * n + 9]
    holds = refs[2 * n + 9 : 3 * n + 9]
    get_sem, put_sem = refs[3 * n + 9 :]
    gets, puts = [], []
    for src, out, hold, parts in zip(arrays, outs, holds, splits):
        size = src.shape[0] // parts
        for p in range(parts):
            rows = pl.ds(p * size, size)
            i = len(gets)
            gets.append(pltpu.make_async_copy(src.at[rows], hold.at[rows], get_sem.at[i]))
            puts.append(pltpu.make_async_copy(hold.at[rows], out.at[rows], put_sem.at[i]))
    for get in gets:
        get.start()
    for i, ref in enumerate(vectors[:8]):
        ref[...] = small_ref[i, 0 : ref.shape[0]]
    up = vectors[8]
    up[0:128] = small_ref[8, :]
    up[128:] = small_ref[9, 0 : up.shape[0] - 128]
    for get, put in zip(gets, puts):
        get.wait()
        put.start()
    for put in puts:
        put.wait()


def publish(small, lengths, arrays):
    splits = [2 if a.dtype == BF16 else 1 for a in arrays]
    total = sum(splits)
    vmem = pl.BlockSpec(memory_space=pltpu.VMEM)
    return pl.pallas_call(
        functools.partial(publish_body, splits),
        in_specs=[vmem] + [ANY] * len(arrays),
        out_specs=[ANY] * len(arrays) + [vmem] * 9,
        out_shape=[jax.ShapeDtypeStruct(a.shape, a.dtype) for a in arrays]
        + [jax.ShapeDtypeStruct((n,), F32) for n in lengths],
        scratch_shapes=[pltpu.VMEM(a.shape, a.dtype) for a in arrays]
        + [pltpu.SemaphoreType.DMA((total,)), pltpu.SemaphoreType.DMA((total,))],
        compiler_params=params(),
        name="publish",
    )(small, *arrays)


def on_device(tokens, cotangent, segment_ids, *shards):
    gather = lambda s: lax.all_gather(s, "fsdp", axis=0, tiled=True)
    n = lax.axis_size("fsdp")
    near = n == 16 and lax.axis_size("dp") == 2
    triple_s, out_s, up_s, down_s = (s for s in shards if s.ndim == 2)
    rows, d = tokens.shape
    up_bias_s = shards[10]
    eights = [s for i, s in enumerate(shards) if s.ndim == 1 and i != 10]
    flat = lambda w: w.reshape(-1, w.shape[-1])
    if near:
        triple_weight, vec, up_bias, qkv, first_t, cot_t = first(eights + [up_bias_s], triple_s, tokens, cotangent)
        triple_weight = flat(triple_weight)
    else:
        triple_weight = gather(triple_s)
        packed = gather(jnp.concatenate(eights + [up_bias_s]).reshape(1, -1)).astype(F32)
        m = eights[0].shape[0]
        vec = jnp.stack([packed[:, i * m : (i + 1) * m].reshape(-1) for i in range(8)])
        up_bias = packed[:, 8 * m :].reshape(1, -1)
        qkv, first_t = project(tokens, vec, triple_weight)
        cot_t = cotangent.T

    segr = segment_ids.reshape(rows // ROWS, 1, ROWS)
    if near:
        mixed, soft, inv, *full = attend(qkv, segr, (out_s, up_s, down_s))
        out_weight, up_weight, down_weight = (flat(w) for w in full)
    else:
        mixed, soft, inv = attend(qkv, segr)
        out_weight, up_weight, down_weight = gather(out_s), gather(up_s), gather(down_s)
    resid, h, ht = out_project(tokens, mixed, out_weight, vec)
    acc, dh, dwu, dwd, dbu = mlp(h, ht, cotangent, cot_t, up_weight, up_bias, down_weight)
    y, dr, dm, dwo, dvec = middle(resid, acc, dh, cotangent, mixed, out_weight, vec)
    if near:
        dqkv, out_grad, up_grad, down_grad = attend_back(qkv, soft, mixed, dm, inv, (dwo, dwu, dwd))
        dx, triple_grad, small = finish(tokens, dr, first_t, dqkv, triple_weight, vec, dvec, dbu, True)
        lengths = [d // n] * 8 + [up_bias_s.shape[0]]
        dx, triple_grad, out_grad, up_grad, down_grad, *small_grads, up_bias_grad = publish(
            small, lengths, (dx, triple_grad, out_grad, up_grad, down_grad)
        )
    else:
        (dqkv,) = attend_back(qkv, soft, mixed, dm, inv)
        dx, dwt, dvec = finish(tokens, dr, first_t, dqkv, triple_weight, vec, dvec, dbu, False)
        small = jnp.concatenate([dvec[i].reshape(n, -1) for i in range(8)] + [dbu.reshape(n, -1)], axis=1)
        small = lax.psum_scatter(small, "fsdp", scatter_dimension=0, tiled=True).reshape(-1)
        small = lax.psum(small, "dp")
        total = lambda p: lax.psum(lax.psum_scatter(p, "fsdp", scatter_dimension=0, tiled=True), "dp").astype(F32)
        triple_grad, out_grad, up_grad, down_grad = total(dwt), total(dwo), total(dwu), total(dwd)
        m = d // n
        small_grads = [small[i * m : (i + 1) * m] for i in range(8)]
        up_bias_grad = small[8 * m :]
    dg1, ds1, dqb, dvb, dob, dg2, ds2, ddb = small_grads
    return (
        y, dx, dg1, ds1, triple_grad, dqb, dvb, out_grad, dob, dg2, ds2, up_grad, up_bias_grad, down_grad, ddb,
    )


def solution(mesh):
    tok = P(("dp", "fsdp"), None)
    vec = P("fsdp")
    mat = P("fsdp", None)
    weights = (vec, vec, mat, vec, vec, mat, vec, vec, vec, mat, vec, mat, vec)
    return jax.shard_map(
        on_device,
        mesh=mesh,
        in_specs=(tok, tok, P(("dp", "fsdp")), *weights),
        out_specs=(tok, tok, *weights),
        check_vma=False,
    )
```
